256 devices in a mesh: group: 16 (over z, x_hi), expert: 16 (over x_lo, y, core).
Axes of the slice: x: 4 (x_hi: 2, x_lo: 2; x = x_hi * 2 + x_lo), y: 4, z: 8, core: 2. Of those that a mesh axis runs over, the one named last changes fastest.
Arguments:
- hidden_in: bfloat16 [16384, 2048], P(('group', 'expert')), may hold values from -54 to 54
- norm_attention: float32 [2048], replicated, may hold values from 0.5 to 1.5
- norm_experts: float32 [2048], replicated, may hold values from 0.5 to 1.5
- query_master: float32 [2048, 4096], P('group', 'expert'), may hold values from -0.125 to 0.125
- trainer_key_value_weight: float32 [2, 2048, 512], P(None, 'group'), may hold values from -0.125 to 0.125
- output_master: float32 [4096, 2048], P('expert', 'group'), may hold values from -0.09375 to 0.09375
- query_gain: float32 [128], replicated, may hold values from 0.5 to 1.5
- key_gain: float32 [128], replicated, may hold values from 0.5 to 1.5
- lengths: int32 [8], replicated, may hold values from 1 to 2048, as said below
- router: bfloat16 [2048, 128], replicated, may hold values from -0.125 to 0.125
- expert_gateup: bfloat16 [16, 2048, 1536], P('expert'), may hold values from -0.125 to 0.125
- expert_down: bfloat16 [16, 768, 2048], P('expert'), may hold values from -0.21875 to 0.21875
- routes: int32 [16384, 8], P(('group', 'expert')), may hold values from 0 to 127, as said below
Outputs:
- hidden: bfloat16 [16384, 2048], P(('group', 'expert'))
- expert_mix: bfloat16 [16384, 2048], P(('group', 'expert'))
The draws below stay inside these ranges and needn't reach their ends.
Inputs may be any that keep to these rules, and one draw needn't show every extreme that they name: `lengths`: one request has exactly 2048 valid tokens. `routes`: A row's 8 experts are different, and at most one of them is below 16. In the 64 rows of one device, each expert below 16 is named by at most 4 rows; in every such block some expert is named by exactly 4 rows, and one expert is named by exactly 4 rows in every block.
All inputs are finite; a program needn't handle non-finite values.
Results may differ from the reference program's by a relative error of at most 0.02.
Values may be sent and summed in bfloat16 or wider, within the bound.
A program may use at most 64 MiB of HBM per device.

```python
import math
import jax
import jax.numpy as jnp
from jax import lax

MODEL_DIMENSION = 2048
QUERY_HEADS = 32
KEY_VALUE_HEADS = 4
HEAD_DIMENSION = 128
EXPERTS = 128
FFE = 768
TOPK = 8
SEQ_G = 1024
ROWS_DEV = 64
CAP = 4
EXPERTS_WIN = 16
PAIRS = 8
TOKENS = 16384
N_GROUP = 16
N_EXPERT = 16


def draw_hidden_in(key, part):
    subkeys = jax.random.split(key, 3)
    lowest = math.log(0.3)
    highest = math.log(3.0)
    row_scale = jnp.exp(jax.random.uniform(subkeys[0], (TOKENS, 1), jnp.float32, lowest, highest))
    column_scale = jnp.exp(jax.random.uniform(subkeys[1], (1, MODEL_DIMENSION), jnp.float32, lowest, highest))
    noise = jnp.clip(jax.random.normal(subkeys[2], (TOKENS, MODEL_DIMENSION), jnp.float32), -6.0, 6.0)
    return (noise * row_scale * column_scale).astype(jnp.bfloat16)


def draw_lengths(key, part):
    subkeys = jax.random.split(key, 2)
    drawn = jax.random.randint(subkeys[0], (PAIRS,), 1, 2 * SEQ_G + 1)
    longest = jax.random.randint(subkeys[1], (), 0, PAIRS)
    return jnp.where(jnp.arange(PAIRS) == longest, 2 * SEQ_G, drawn).astype(jnp.int32)


def draw_routes(key, part):
    subkeys = jax.random.split(key, 7)
    block_count = TOKENS // ROWS_DEV
    window = EXPERTS_WIN
    ceiling = jax.random.randint(subkeys[0], (window,), CAP // 2, CAP + 1)
    counts = ceiling[None, :] - jax.random.randint(subkeys[1], (block_count, window), 0, CAP // 2 + 1)
    busiest = jax.random.randint(subkeys[2], (block_count,), 0, window)
    hottest = jax.random.randint(subkeys[6], (), 0, window)
    columns = jnp.arange(window)[None, :]
    counts = jnp.where((columns == busiest[:, None]) | (columns == hottest), CAP, counts)
    bounds = jnp.cumsum(counts, axis=1)
    ranking = jax.vmap(lambda subkey: jax.random.permutation(subkey, ROWS_DEV))(jax.random.split(subkeys[3], block_count))
    chosen = jnp.sum((ranking[:, :, None] >= bounds[:, None, :]).astype(jnp.int32), axis=2).reshape(TOKENS)
    outside = EXPERTS - window
    scores = jax.random.randint(subkeys[4], (TOKENS, outside), 0, 1 << 20) * outside + jnp.arange(outside)[None, :]
    _, others = lax.top_k(scores, TOPK)
    others = others + window
    position = jax.random.randint(subkeys[5], (TOKENS, 1), 0, TOPK)
    place_here = (jnp.arange(TOPK)[None, :] == position) & (chosen[:, None] < window)
    return jnp.where(place_here, chosen[:, None], others).astype(jnp.int32)


def shard_levels(rng, extent, pieces, low, largest):
    level, own = 1.0, jax.random.fold_in(rng, 6)
    for dim, blocks in pieces:
        draws = jnp.exp(jax.random.uniform(jax.random.fold_in(own, dim), (blocks,), jnp.float32, low / len(pieces), largest / len(pieces)))
        level = level * jnp.repeat(draws, extent[dim] // blocks).reshape([-1 if axis == dim else 1 for axis in range(len(extent))])
    return level


def gaussian(own_key, dims, scale, reach, cuts=(), kind=jnp.bfloat16):
    array = scale * jax.random.normal(own_key, dims, jnp.float32)
    if cuts:
        array = array * shard_levels(own_key, dims, cuts, -0.22, 0.18)
    return jnp.clip(array, -reach, reach).astype(kind)


def setup_inputs(seed: int = 0) -> dict:
    key_list = jax.random.split(jax.random.key(seed), 14)
    return {
        "hidden_in": draw_hidden_in(jax.random.fold_in(key_list[13], 71), 0),
        "norm_attention": jnp.clip(jax.random.uniform(key_list[1], (MODEL_DIMENSION,), jnp.float32, 0.5, 1.5), 0.5, 1.5),
        "norm_experts": jnp.clip(jax.random.uniform(key_list[2], (MODEL_DIMENSION,), jnp.float32, 0.5, 1.5), 0.5, 1.5),
        "query_master": gaussian(key_list[3], (MODEL_DIMENSION, QUERY_HEADS * HEAD_DIMENSION), MODEL_DIMENSION ** -0.5, 0.125, ((0, 16), (1, 16)), jnp.float32),
        "trainer_key_value_weight": gaussian(key_list[4], (2, MODEL_DIMENSION, KEY_VALUE_HEADS * HEAD_DIMENSION), MODEL_DIMENSION ** -0.5, 0.125, ((1, 16),), jnp.float32),
        "output_master": gaussian(key_list[5], (QUERY_HEADS * HEAD_DIMENSION, MODEL_DIMENSION), (QUERY_HEADS * HEAD_DIMENSION) ** -0.5, 0.09375, ((0, 16), (1, 16)), jnp.float32),
        "query_gain": jnp.clip(jax.random.uniform(key_list[6], (HEAD_DIMENSION,), jnp.float32, 0.5, 1.5), 0.5, 1.5),
        "key_gain": jnp.clip(jax.random.uniform(key_list[7], (HEAD_DIMENSION,), jnp.float32, 0.5, 1.5), 0.5, 1.5),
        "lengths": draw_lengths(jax.random.fold_in(key_list[13], 71), 0),
        "router": gaussian(key_list[9], (MODEL_DIMENSION, EXPERTS), MODEL_DIMENSION ** -0.5, 0.125),
        "expert_gateup": gaussian(key_list[10], (EXPERTS_WIN, MODEL_DIMENSION, 2 * FFE), MODEL_DIMENSION ** -0.5, 0.125, ((0, 16),)),
        "expert_down": gaussian(key_list[11], (EXPERTS_WIN, FFE, MODEL_DIMENSION), FFE ** -0.5, 0.21875, ((0, 16),)),
        "routes": draw_routes(jax.random.fold_in(key_list[13], 71), 0),
    }


epsilon = 1e-06
rope_theta = 1000000.0

def norm_rows(values, gain_vector):
    widened = values.astype(jnp.float32)
    inverse_rms = lax.rsqrt(lax.optimization_barrier(jnp.mean(widened * widened, axis=-1, keepdims=True)) + epsilon)
    return widened * inverse_rms * gain_vector

def rotate(values, positions):
    half_width = values.shape[-1] // 2
    exponents = jnp.arange(half_width).astype(jnp.float32)
    inverse = jnp.exp(exponents * (-2.0 * math.log(rope_theta) / values.shape[-1]))
    angles = positions[:, None, None] * inverse[None, None, :]
    cosine_values = jnp.cos(angles)
    sine_values = jnp.sin(angles)
    first_half = values[..., :half_width]
    second = values[..., half_width:]
    return jnp.concatenate([first_half * cosine_values - second * sine_values, second * cosine_values + first_half * sine_values], axis=-1)

def local_positions(parity, row_count):
    indices = jnp.arange(row_count).astype(jnp.int32)
    quarter = row_count // 2
    offset = jnp.where(parity == 0, jnp.where(indices < quarter, 0, 2 * quarter), quarter)
    return indices + offset

def reference(hidden_in, norm_attention, norm_experts, query_master, trainer_key_value_weight, output_master, query_gain, key_gain, lengths, router, expert_gateup, expert_down, routes):
    query_weight = query_master.astype(jnp.bfloat16)
    key_matrix = trainer_key_value_weight[0].astype(jnp.bfloat16)
    value_matrix = trainer_key_value_weight[1].astype(jnp.bfloat16)
    output_weight = output_master.astype(jnp.bfloat16)
    normed = norm_rows(hidden_in, norm_attention).astype(jnp.bfloat16)
    group_member_count = QUERY_HEADS // KEY_VALUE_HEADS
    paired_rows = 2 * SEQ_G
    score_scale = HEAD_DIMENSION ** (-0.5)

    def one_pair(pair_index):
        paired_states = lax.dynamic_slice_in_dim(normed, pair_index * paired_rows, paired_rows, 0)
        query_rows_list = jnp.dot(paired_states, query_weight, preferred_element_type=jnp.float32).astype(jnp.bfloat16).reshape(paired_rows, QUERY_HEADS, HEAD_DIMENSION)
        paired_keys = jnp.dot(paired_states, key_matrix, preferred_element_type=jnp.float32).astype(jnp.bfloat16).reshape(paired_rows, KEY_VALUE_HEADS, HEAD_DIMENSION)
        paired_values = jnp.dot(paired_states, value_matrix, preferred_element_type=jnp.float32).astype(jnp.bfloat16).reshape(paired_rows, KEY_VALUE_HEADS, HEAD_DIMENSION)
        positions = jnp.concatenate([local_positions(0, SEQ_G), local_positions(1, SEQ_G)])
        places = positions.astype(jnp.float32)
        query_rows_list = rotate(norm_rows(query_rows_list, query_gain), places).astype(jnp.bfloat16)
        paired_keys = rotate(norm_rows(paired_keys, key_gain), places).astype(jnp.bfloat16)
        length = lengths[pair_index]
        allowed = (positions[None, :] <= positions[:, None]) & (positions[None, :] < length)
        query_broad = query_rows_list.astype(jnp.float32).reshape(paired_rows, KEY_VALUE_HEADS, group_member_count, HEAD_DIMENSION)
        key_wide = paired_keys.astype(jnp.float32)
        value_wide = paired_values.astype(jnp.float32)

        def single_group(head_index):
            query_head = lax.dynamic_index_in_dim(query_broad, head_index, 1, keepdims=False)
            key_head = lax.dynamic_index_in_dim(key_wide, head_index, 1, keepdims=False)
            value_head = lax.dynamic_index_in_dim(value_wide, head_index, 1, keepdims=False)
            scores = jnp.einsum('qgd,kd->gqk', query_head, key_head) * score_scale
            weights = jnp.where(allowed[None], jnp.exp(scores), 0.0)
            denominators = lax.optimization_barrier(jnp.sum(weights, axis=-1))
            rounded = lax.optimization_barrier(weights.astype(jnp.bfloat16)).astype(jnp.float32)
            output = jnp.einsum('gqk,kd->qgd', rounded, value_head) / jnp.transpose(denominators)[:, :, None]
            return output.astype(jnp.bfloat16)
        grouped_heads = lax.map(single_group, jnp.arange(KEY_VALUE_HEADS))
        return jnp.transpose(grouped_heads, (1, 0, 2, 3)).reshape(paired_rows, QUERY_HEADS * HEAD_DIMENSION)
    attended = lax.map(one_pair, jnp.arange(N_GROUP // 2)).reshape(TOKENS, QUERY_HEADS * HEAD_DIMENSION)
    block_width = QUERY_HEADS * HEAD_DIMENSION // N_EXPERT

    def add_block(total, block_index):
        columns = lax.dynamic_slice_in_dim(attended, block_index * block_width, block_width, 1)
        rows = lax.dynamic_slice_in_dim(output_weight, block_index * block_width, block_width, 0)
        partial_block = lax.optimization_barrier(jnp.dot(columns, rows, preferred_element_type=jnp.float32).astype(jnp.bfloat16)).astype(jnp.float32)
        return (total + partial_block, None)
    summed, _ = lax.scan(add_block, jnp.zeros((TOKENS, MODEL_DIMENSION), jnp.float32), jnp.arange(N_EXPERT))
    hidden = (hidden_in.astype(jnp.float32) + summed).astype(jnp.bfloat16)
    normed_second = norm_rows(hidden, norm_experts).astype(jnp.bfloat16)
    logits = jnp.dot(normed_second, router, preferred_element_type=jnp.float32)
    picked = jnp.take_along_axis(logits, routes, axis=1)
    raised = jnp.exp(picked)
    gate_values = raised / lax.optimization_barrier(jnp.sum(raised, axis=1, keepdims=True))
    inside = routes < EXPERTS_WIN
    gate_window = lax.optimization_barrier(jnp.sum(jnp.where(inside, gate_values, 0.0), axis=1))
    expert_window = lax.optimization_barrier(jnp.sum(jnp.where(inside, routes, 0), axis=1))
    present = jnp.any(inside, axis=1)
    slot_count = N_GROUP * N_EXPERT * CAP

    def one_expert(accumulated, expert):
        missing = jnp.where(present & (expert_window == expert), 0, 1).astype(jnp.int32)
        ordering = jnp.argsort(missing, stable=True)[:slot_count]
        chosen_rows = normed_second[ordering]
        gate_up = jnp.dot(chosen_rows, expert_gateup[expert], preferred_element_type=jnp.float32)
        active = (jax.nn.silu(gate_up[:, :FFE]) * gate_up[:, FFE:]).astype(jnp.bfloat16)
        output = lax.optimization_barrier(jnp.dot(active, expert_down[expert], preferred_element_type=jnp.float32).astype(jnp.bfloat16)).astype(jnp.float32)
        valid_slots = (missing[ordering] == 0)[:, None]
        accumulated = accumulated.at[ordering].add(jnp.where(valid_slots, output, 0.0))
        return (accumulated, None)
    combined, _ = lax.scan(one_expert, jnp.zeros((TOKENS, MODEL_DIMENSION), jnp.float32), jnp.arange(EXPERTS_WIN))
    expert_mix = (gate_window[:, None] * combined).astype(jnp.bfloat16)
    return (hidden, expert_mix)
```

```python
import functools
import math

import jax
import jax.numpy as jnp
from jax import lax
from jax.experimental import pallas as pl
from jax.experimental.pallas import tpu as pltpu
from jax.sharding import PartitionSpec as P

MESH = pl.DeviceIdType.MESH

QUERY_HEADS = 32
KEY_VALUE_HEADS = 4
HEAD_DIMENSION = 128


epsilon = 1e-06
rope_theta = 1000000.0


def from_partner(block, axis, stride):
    count = lax.axis_size(axis)
    route = []
    for low in range(count):
        high = low | 1 << stride
        if high != low and high < count:
            route += [(low, high), (high, low)]
    return lax.ppermute(block, axis, route)


def gather_kernel(n_group, n_expert, wq, wk, wv, wo, xn, oq, ok, ov, oo, oxn, send, recv, local):
    g = lax.axis_index("group")
    e = lax.axis_index("expert")
    barrier = pltpu.get_barrier_semaphore()
    for j in range(1, n_group):
        pl.semaphore_signal(barrier, 1, device_id=(lax.rem(g + j, n_group), e), device_id_type=MESH)
    for j in range(1, n_expert):
        pl.semaphore_signal(barrier, 1, device_id=(g, lax.rem(e + j, n_expert)), device_id_type=MESH)
    pl.semaphore_wait(barrier, n_group - 1 + n_expert - 1)
    copies = []
    for j in range(1, n_expert):
        copy = pltpu.make_async_remote_copy(
            src_ref=xn,
            dst_ref=oxn.at[e],
            send_sem=send.at[4, j],
            recv_sem=recv.at[4, j],
            device_id=(g, lax.rem(e + j, n_expert)),
            device_id_type=MESH,
        )
        copy.start()
        copies.append(copy)
    pieces = [(wq, oq), (wk, ok), (wv, ov), (wo, oo)]
    for j in range(1, n_group):
        for k, (src, dst) in enumerate(pieces):
            copy = pltpu.make_async_remote_copy(
                src_ref=src,
                dst_ref=dst.at[g],
                send_sem=send.at[k, j],
                recv_sem=recv.at[k, j],
                device_id=(lax.rem(g + j, n_group), e),
                device_id_type=MESH,
            )
            copy.start()
            copies.append(copy)
    own = [pltpu.make_async_copy(xn, oxn.at[e], local.at[4])]
    own += [pltpu.make_async_copy(src, dst.at[g], local.at[k]) for k, (src, dst) in enumerate(pieces)]
    for copy in own:
        copy.start()
    for copy in copies:
        copy.wait()
    for copy in own:
        copy.wait()


def gather_all(wq, wk, wv, wo, xn, n_group, n_expert):
    any_spec = pl.BlockSpec(memory_space=pl.ANY)
    shapes = [
        jax.ShapeDtypeStruct((n_group,) + a.shape, a.dtype) for a in (wq, wk, wv, wo)
    ] + [jax.ShapeDtypeStruct((n_expert,) + xn.shape, xn.dtype)]
    return pl.pallas_call(
        functools.partial(gather_kernel, n_group, n_expert),
        out_shape=tuple(shapes),
        in_specs=[any_spec] * 5,
        out_specs=tuple([any_spec] * 5),
        scratch_shapes=[
            pltpu.SemaphoreType.DMA((5, max(n_group, n_expert))),
            pltpu.SemaphoreType.DMA((5, max(n_group, n_expert))),
            pltpu.SemaphoreType.DMA((5,)),
        ],
        compiler_params=pltpu.CompilerParams(collective_id=0, has_side_effects=True),
    )(wq, wk, wv, wo, xn)


def scatter_kernel(n_expert, part, out, send, recv, local):
    g = lax.axis_index("group")
    e = lax.axis_index("expert")
    barrier = pltpu.get_barrier_semaphore()
    for j in range(1, n_expert):
        pl.semaphore_signal(barrier, 1, device_id=(g, lax.rem(e + j, n_expert)), device_id_type=MESH)
    pl.semaphore_wait(barrier, n_expert - 1)
    copies = []
    for j in range(1, n_expert):
        peer = lax.rem(e + j, n_expert)
        copy = pltpu.make_async_remote_copy(
            src_ref=part.at[peer],
            dst_ref=out.at[e],
            send_sem=send.at[j],
            recv_sem=recv.at[j],
            device_id=(g, peer),
            device_id_type=MESH,
        )
        copy.start()
        copies.append(copy)
    own = pltpu.make_async_copy(part.at[e], out.at[e], local.at[0])
    own.start()
    for copy in copies:
        copy.wait()
    own.wait()


def scatter_blocks(part, n_expert):
    any_spec = pl.BlockSpec(memory_space=pl.ANY)
    return pl.pallas_call(
        functools.partial(scatter_kernel, n_expert),
        out_shape=jax.ShapeDtypeStruct(part.shape, part.dtype),
        in_specs=[any_spec],
        out_specs=any_spec,
        scratch_shapes=[
            pltpu.SemaphoreType.DMA((n_expert,)),
            pltpu.SemaphoreType.DMA((n_expert,)),
            pltpu.SemaphoreType.DMA((1,)),
        ],
        compiler_params=pltpu.CompilerParams(collective_id=1, has_side_effects=True),
    )(part)


def norm_rows(values, gain_vector):
    widened = values.astype(jnp.float32)
    inverse_rms = lax.rsqrt(jnp.mean(widened * widened, axis=-1, keepdims=True) + epsilon)
    return widened * inverse_rms * gain_vector


def rotate(values, positions):
    half_width = values.shape[-1] // 2
    exponents = jnp.arange(half_width).astype(jnp.float32)
    inverse = jnp.exp(exponents * (-2.0 * math.log(rope_theta) / values.shape[-1]))
    angles = positions[:, None, None] * inverse[None, None, :]
    cosine_values = jnp.cos(angles)
    sine_values = jnp.sin(angles)
    first_half = values[..., :half_width]
    second = values[..., half_width:]
    return jnp.concatenate(
        [
            first_half * cosine_values - second * sine_values,
            second * cosine_values + first_half * sine_values,
        ],
        axis=-1,
    )


def local_positions(parity, row_count):
    indices = jnp.arange(row_count)
    quarter = row_count // 2
    offset = jnp.where(parity == 0, jnp.where(indices < quarter, 0, 2 * quarter), quarter)
    return indices + offset


def per_device(
    hidden_in,
    norm_attention,
    norm_experts,
    query_master,
    trainer_key_value_weight,
    output_master,
    query_gain,
    key_gain,
    lengths,
    router,
    expert_gateup,
    expert_down,
    routes,
):
    experts_axis = lax.axis_size("expert")
    group_member = lax.axis_index("expert")
    group_index = lax.axis_index("group")
    local_head_count = QUERY_HEADS // experts_axis
    width_here = local_head_count * HEAD_DIMENSION
    common_head = group_member * local_head_count // (QUERY_HEADS // KEY_VALUE_HEADS)
    groups_axis = lax.axis_size("group")
    keyvalue_slice = lax.dynamic_slice_in_dim(
        trainer_key_value_weight, common_head * HEAD_DIMENSION, HEAD_DIMENSION, 2
    ).astype(jnp.bfloat16)
    normed = norm_rows(hidden_in, norm_attention).astype(jnp.bfloat16)
    query_parts, key_parts, value_parts, output_parts, normed_parts = gather_all(
        query_master.astype(jnp.bfloat16),
        keyvalue_slice[0],
        keyvalue_slice[1],
        output_master.astype(jnp.bfloat16),
        normed,
        groups_axis,
        experts_axis,
    )
    model_width = hidden_in.shape[1]
    joined_weights = jnp.concatenate(
        [
            query_parts.reshape(model_width, -1),
            key_parts.reshape(model_width, -1),
            value_parts.reshape(model_width, -1),
        ],
        axis=1,
    )
    projected = jnp.dot(
        normed_parts.reshape(-1, model_width),
        joined_weights,
        preferred_element_type=jnp.float32,
    ).astype(jnp.bfloat16)
    local_rows = projected.shape[0]
    query_rows_list = projected[:, :width_here].reshape(
        local_rows, local_head_count, HEAD_DIMENSION
    )
    key_rows = projected[:, width_here : width_here + HEAD_DIMENSION]
    value_rows = projected[:, width_here + HEAD_DIMENSION :]
    parity = group_index % 2
    own_places = local_positions(parity, local_rows)
    partner_places = local_positions(1 - parity, local_rows)
    query_rows_list = rotate(
        norm_rows(query_rows_list, query_gain), own_places.astype(jnp.float32)
    ).astype(jnp.bfloat16)
    key_rows = rotate(norm_rows(key_rows[:, None, :], key_gain), own_places.astype(jnp.float32))[
        :, 0, :
    ].astype(jnp.bfloat16)
    partner = from_partner(jnp.stack([key_rows, value_rows]), "group", 0)
    all_keys = jnp.concatenate([key_rows, partner[0]], axis=0)
    all_values = jnp.concatenate([value_rows, partner[1]], axis=0)
    key_places = jnp.concatenate([own_places, partner_places])
    valid_length = jnp.sum(jnp.where(jnp.arange(lengths.shape[0]) == group_index // 2, lengths, 0))
    block_rows = min(512, local_rows)
    block_count = local_rows // block_rows
    score_scale = HEAD_DIMENSION ** (-0.5)

    def attend(block_index):
        block_start = block_index * block_rows
        query_block = lax.dynamic_slice_in_dim(query_rows_list, block_start, block_rows, 0)
        query_places = lax.dynamic_slice_in_dim(own_places, block_start, block_rows, 0)
        scores = (
            jnp.einsum("qhd,kd->hqk", query_block, all_keys, preferred_element_type=jnp.float32)
            * score_scale
        )
        allowed = (key_places[None, :] <= query_places[:, None]) & (
            key_places[None, :] < valid_length
        )
        weights = jnp.where(allowed[None], jnp.exp(scores), 0.0)
        denominators = jnp.sum(weights, axis=-1)
        weighted = jnp.einsum(
            "hqk,kd->qhd",
            weights.astype(jnp.bfloat16),
            all_values,
            preferred_element_type=jnp.float32,
        )
        return (weighted / jnp.transpose(denominators)[:, :, None]).astype(jnp.bfloat16)

    attended = lax.map(attend, jnp.arange(block_count)).reshape(local_rows, width_here)
    head_partials = jnp.einsum(
        "tk,gkn->tgn", attended, output_parts, preferred_element_type=jnp.float32
    ).astype(jnp.bfloat16)
    owned = scatter_blocks(head_partials.reshape(experts_axis, -1, model_width), experts_axis)
    summed = jnp.sum(owned.astype(jnp.float32), axis=0)
    hidden = (hidden_in.astype(jnp.float32) + summed).astype(jnp.bfloat16)
    normed_second = norm_rows(hidden, norm_experts).astype(jnp.bfloat16)
    logits = jnp.dot(normed_second, router, preferred_element_type=jnp.float32)
    route_table = routes[:, :, None] == jnp.arange(logits.shape[1])[None, None, :]
    picked = jnp.sum(jnp.where(route_table, logits[:, None, :], 0.0), axis=-1)
    raised = jnp.exp(picked)
    gate_values = raised / jnp.sum(raised, axis=1, keepdims=True)
    inside = routes < experts_axis
    gate_window = jnp.sum(jnp.where(inside, gate_values, 0.0), axis=1)
    expert_window = jnp.sum(jnp.where(inside, routes, 0), axis=1)
    present = jnp.any(inside, axis=1)
    capacity = local_rows // (experts_axis * experts_axis)
    member_table = (
        present[:, None] & (expert_window[:, None] == jnp.arange(experts_axis)[None, :])
    ).astype(jnp.int32)
    ranking = jnp.sum(jnp.cumsum(member_table, axis=0) * member_table, axis=1) - 1
    slot_index = expert_window * capacity + ranking
    select = (
        (jnp.arange(experts_axis * capacity)[:, None] == slot_index[None, :]) & present[None, :]
    ).astype(jnp.bfloat16)
    outgoing = (
        jnp.dot(select, normed_second, preferred_element_type=jnp.float32)
        .astype(jnp.bfloat16)
        .reshape(experts_axis, capacity, model_width)
    )
    gateup_here = expert_gateup[0]
    down_here = expert_down[0]
    hidden_units = down_here.shape[0]
    slot_items = lax.all_to_all(outgoing, "expert", split_axis=0, concat_axis=0, tiled=True)
    flattened = slot_items.reshape(-1, slot_items.shape[-1])
    gate_up = jnp.dot(flattened, gateup_here, preferred_element_type=jnp.float32)
    active = (jax.nn.silu(gate_up[:, :hidden_units]) * gate_up[:, hidden_units:]).astype(
        jnp.bfloat16
    )
    result = (
        jnp.dot(active, down_here, preferred_element_type=jnp.float32)
        .astype(jnp.bfloat16)
        .reshape(slot_items.shape)
    )
    returned = lax.all_to_all(result, "expert", split_axis=0, concat_axis=0, tiled=True)
    combined = jnp.dot(
        jnp.transpose(select), returned.reshape(-1, model_width), preferred_element_type=jnp.float32
    )
    expert_mix = (gate_window[:, None] * combined).astype(jnp.bfloat16)
    return (hidden, expert_mix)


def solution(mesh):
    return jax.shard_map(
        per_device,
        mesh=mesh,
        in_specs=(
            P(("group", "expert"), None),
            P(),
            P(),
            P("group", "expert"),
            P(None, "group", None),
            P("expert", "group"),
            P(),
            P(),
            P(),
            P(),
            P("expert", None, None),
            P("expert", None, None),
            P(("group", "expert"), None),
        ),
        out_specs=(P(("group", "expert"), None), P(("group", "expert"), None)),
        check_vma=False,
    )
```

```python
import functools
import math

import jax
import jax.numpy as jnp
from jax import lax
from jax.experimental import pallas as pl
from jax.experimental.pallas import tpu as pltpu
from jax.sharding import PartitionSpec as P

MESH = pl.DeviceIdType.MESH

QUERY_HEADS = 32
KEY_VALUE_HEADS = 4
HEAD_DIMENSION = 128


epsilon = 1e-06
rope_theta = 1000000.0


def from_partner(block, axis, stride):
    count = lax.axis_size(axis)
    route = []
    for low in range(count):
        high = low | 1 << stride
        if high != low and high < count:
            route += [(low, high), (high, low)]
    return lax.ppermute(block, axis, route)


def gather_kernel(n_group, n_expert, wq, wk, wv, wo, xn, oq, ok, ov, oo, oxn, send, recv, local):
    g = lax.axis_index("group")
    e = lax.axis_index("expert")
    barrier = pltpu.get_barrier_semaphore()
    for j in range(1, n_group):
        pl.semaphore_signal(barrier, 1, device_id=(lax.rem(g + j, n_group), e), device_id_type=MESH)
    for j in range(1, n_expert):
        pl.semaphore_signal(barrier, 1, device_id=(g, lax.rem(e + j, n_expert)), device_id_type=MESH)
    pl.semaphore_wait(barrier, n_group - 1 + n_expert - 1)
    copies = []
    for j in range(1, n_expert):
        copy = pltpu.make_async_remote_copy(
            src_ref=xn,
            dst_ref=oxn.at[e],
            send_sem=send.at[4, j],
            recv_sem=recv.at[4, j],
            device_id=(g, lax.rem(e + j, n_expert)),
            device_id_type=MESH,
        )
        copy.start()
        copies.append(copy)
    pieces = [(wq, oq), (wk, ok), (wv, ov), (wo, oo)]
    width = wo.shape[1]

    def slot(dst, k):
        if k == 3:
            return dst.at[:, pl.ds(pl.multiple_of(g * width, width), width)]
        return dst.at[g]

    for j in range(1, n_group):
        for k, (src, dst) in enumerate(pieces):
            copy = pltpu.make_async_remote_copy(
                src_ref=src,
                dst_ref=slot(dst, k),
                send_sem=send.at[k, j],
                recv_sem=recv.at[k, j],
                device_id=(lax.rem(g + j, n_group), e),
                device_id_type=MESH,
            )
            copy.start()
            copies.append(copy)
    own = [pltpu.make_async_copy(xn, oxn.at[e], local.at[4])]
    own += [pltpu.make_async_copy(src, slot(dst, k), local.at[k]) for k, (src, dst) in enumerate(pieces)]
    for copy in own:
        copy.start()
    for copy in copies:
        copy.wait()
    for copy in own:
        copy.wait()


def gather_all(wq, wk, wv, wo, xn, n_group, n_expert):
    any_spec = pl.BlockSpec(memory_space=pl.ANY)
    shapes = [jax.ShapeDtypeStruct((n_group,) + a.shape, a.dtype) for a in (wq, wk, wv)]
    shapes += [jax.ShapeDtypeStruct((wo.shape[0], n_group * wo.shape[1]), wo.dtype)]
    shapes += [jax.ShapeDtypeStruct((n_expert,) + xn.shape, xn.dtype)]
    return pl.pallas_call(
        functools.partial(gather_kernel, n_group, n_expert),
        out_shape=tuple(shapes),
        in_specs=[any_spec] * 5,
        out_specs=tuple([any_spec] * 5),
        scratch_shapes=[
            pltpu.SemaphoreType.DMA((5, max(n_group, n_expert))),
            pltpu.SemaphoreType.DMA((5, max(n_group, n_expert))),
            pltpu.SemaphoreType.DMA((5,)),
        ],
        compiler_params=pltpu.CompilerParams(collective_id=0, has_side_effects=True),
    )(wq, wk, wv, wo, xn)


def scatter_kernel(n_expert, part, out, send, recv, local):
    g = lax.axis_index("group")
    e = lax.axis_index("expert")
    barrier = pltpu.get_barrier_semaphore()
    for j in range(1, n_expert):
        pl.semaphore_signal(barrier, 1, device_id=(g, lax.rem(e + j, n_expert)), device_id_type=MESH)
    pl.semaphore_wait(barrier, n_expert - 1)
    copies = []
    for j in range(1, n_expert):
        peer = lax.rem(e + j, n_expert)
        copy = pltpu.make_async_remote_copy(
            src_ref=part.at[peer],
            dst_ref=out.at[e],
            send_sem=send.at[j],
            recv_sem=recv.at[j],
            device_id=(g, peer),
            device_id_type=MESH,
        )
        copy.start()
        copies.append(copy)
    own = pltpu.make_async_copy(part.at[e], out.at[e], local.at[0])
    own.start()
    for copy in copies:
        copy.wait()
    own.wait()


def scatter_blocks(part, n_expert, collective_id):
    any_spec = pl.BlockSpec(memory_space=pl.ANY)
    return pl.pallas_call(
        functools.partial(scatter_kernel, n_expert),
        out_shape=jax.ShapeDtypeStruct(part.shape, part.dtype),
        in_specs=[any_spec],
        out_specs=any_spec,
        scratch_shapes=[
            pltpu.SemaphoreType.DMA((n_expert,)),
            pltpu.SemaphoreType.DMA((n_expert,)),
            pltpu.SemaphoreType.DMA((1,)),
        ],
        compiler_params=pltpu.CompilerParams(collective_id=collective_id, has_side_effects=True),
    )(part)


def norm_rows(values, gain_vector):
    widened = values.astype(jnp.float32)
    inverse_rms = lax.rsqrt(jnp.mean(widened * widened, axis=-1, keepdims=True) + epsilon)
    return widened * inverse_rms * gain_vector


def rotate(values, positions):
    half_width = values.shape[-1] // 2
    exponents = jnp.arange(half_width).astype(jnp.float32)
    inverse = jnp.exp(exponents * (-2.0 * math.log(rope_theta) / values.shape[-1]))
    angles = positions[:, None, None] * inverse[None, None, :]
    cosine_values = jnp.cos(angles)
    sine_values = jnp.sin(angles)
    first_half = values[..., :half_width]
    second = values[..., half_width:]
    return jnp.concatenate(
        [
            first_half * cosine_values - second * sine_values,
            second * cosine_values + first_half * sine_values,
        ],
        axis=-1,
    )


def local_positions(parity, row_count):
    indices = jnp.arange(row_count)
    quarter = row_count // 2
    offset = jnp.where(parity == 0, jnp.where(indices < quarter, 0, 2 * quarter), quarter)
    return indices + offset


def per_device(
    hidden_in,
    norm_attention,
    norm_experts,
    query_master,
    trainer_key_value_weight,
    output_master,
    query_gain,
    key_gain,
    lengths,
    router,
    expert_gateup,
    expert_down,
    routes,
):
    experts_axis = lax.axis_size("expert")
    group_member = lax.axis_index("expert")
    group_index = lax.axis_index("group")
    local_head_count = QUERY_HEADS // experts_axis
    width_here = local_head_count * HEAD_DIMENSION
    common_head = group_member * local_head_count // (QUERY_HEADS // KEY_VALUE_HEADS)
    groups_axis = lax.axis_size("group")
    keyvalue_slice = lax.dynamic_slice_in_dim(
        trainer_key_value_weight, common_head * HEAD_DIMENSION, HEAD_DIMENSION, 2
    ).astype(jnp.bfloat16)
    normed = norm_rows(hidden_in, norm_attention).astype(jnp.bfloat16)
    query_parts, key_parts, value_parts, output_parts, normed_parts = gather_all(
        query_master.astype(jnp.bfloat16),
        keyvalue_slice[0],
        keyvalue_slice[1],
        output_master.astype(jnp.bfloat16),
        normed,
        groups_axis,
        experts_axis,
    )
    model_width = hidden_in.shape[1]
    joined_weights = jnp.concatenate(
        [
            query_parts.reshape(model_width, -1),
            key_parts.reshape(model_width, -1),
            value_parts.reshape(model_width, -1),
        ],
        axis=1,
    )
    projected = jnp.dot(
        normed_parts.reshape(-1, model_width),
        joined_weights,
        preferred_element_type=jnp.float32,
    ).astype(jnp.bfloat16)
    local_rows = projected.shape[0]
    query_rows_list = projected[:, :width_here].reshape(
        local_rows, local_head_count, HEAD_DIMENSION
    )
    key_rows = projected[:, width_here : width_here + HEAD_DIMENSION]
    value_rows = projected[:, width_here + HEAD_DIMENSION :]
    parity = group_index % 2
    own_places = local_positions(parity, local_rows)
    partner_places = local_positions(1 - parity, local_rows)
    query_rows_list = rotate(
        norm_rows(query_rows_list, query_gain), own_places.astype(jnp.float32)
    ).astype(jnp.bfloat16)
    key_rows = rotate(norm_rows(key_rows[:, None, :], key_gain), own_places.astype(jnp.float32))[
        :, 0, :
    ].astype(jnp.bfloat16)
    partner = from_partner(jnp.stack([key_rows, value_rows]), "group", 0)
    all_keys = jnp.concatenate([key_rows, partner[0]], axis=0)
    all_values = jnp.concatenate([value_rows, partner[1]], axis=0)
    key_places = jnp.concatenate([own_places, partner_places])
    valid_length = jnp.sum(jnp.where(jnp.arange(lengths.shape[0]) == group_index // 2, lengths, 0))
    block_rows = min(512, local_rows)
    block_count = local_rows // block_rows
    score_scale = HEAD_DIMENSION ** (-0.5)

    def attend(block_index):
        block_start = block_index * block_rows
        query_block = lax.dynamic_slice_in_dim(query_rows_list, block_start, block_rows, 0)
        query_places = lax.dynamic_slice_in_dim(own_places, block_start, block_rows, 0)
        scores = (
            jnp.einsum("qhd,kd->hqk", query_block, all_keys, preferred_element_type=jnp.float32)
            * score_scale
        )
        allowed = (key_places[None, :] <= query_places[:, None]) & (
            key_places[None, :] < valid_length
        )
        weights = jnp.where(allowed[None], jnp.exp(scores), 0.0)
        denominators = jnp.sum(weights, axis=-1)
        weighted = jnp.einsum(
            "hqk,kd->qhd",
            weights.astype(jnp.bfloat16),
            all_values,
            preferred_element_type=jnp.float32,
        )
        return (weighted / jnp.transpose(denominators)[:, :, None]).astype(jnp.bfloat16)

    attended = lax.map(attend, jnp.arange(block_count)).reshape(local_rows, width_here)
    head_partials = jnp.dot(
        attended, output_parts, preferred_element_type=jnp.float32
    ).astype(jnp.bfloat16)
    owned = scatter_blocks(head_partials.reshape(experts_axis, -1, model_width), experts_axis, 1)
    summed = jnp.sum(owned.astype(jnp.float32), axis=0)
    hidden = (hidden_in.astype(jnp.float32) + summed).astype(jnp.bfloat16)
    normed_second = norm_rows(hidden, norm_experts).astype(jnp.bfloat16)
    logits = jnp.dot(normed_second, router, preferred_element_type=jnp.float32)
    route_table = routes[:, :, None] == jnp.arange(logits.shape[1])[None, None, :]
    picked = jnp.sum(jnp.where(route_table, logits[:, None, :], 0.0), axis=-1)
    raised = jnp.exp(picked)
    gate_values = raised / jnp.sum(raised, axis=1, keepdims=True)
    inside = routes < experts_axis
    gate_window = jnp.sum(jnp.where(inside, gate_values, 0.0), axis=1)
    expert_window = jnp.sum(jnp.where(inside, routes, 0), axis=1)
    present = jnp.any(inside, axis=1)
    capacity = local_rows // (experts_axis * experts_axis)
    member_table = (
        present[:, None] & (expert_window[:, None] == jnp.arange(experts_axis)[None, :])
    ).astype(jnp.int32)
    ranking = jnp.sum(jnp.cumsum(member_table, axis=0) * member_table, axis=1) - 1
    slot_index = expert_window * capacity + ranking
    select = (
        (jnp.arange(experts_axis * capacity)[:, None] == slot_index[None, :]) & present[None, :]
    ).astype(jnp.bfloat16)
    outgoing = (
        jnp.dot(select, normed_second, preferred_element_type=jnp.float32)
        .astype(jnp.bfloat16)
        .reshape(experts_axis, capacity, model_width)
    )
    gateup_here = expert_gateup[0]
    down_here = expert_down[0]
    hidden_units = down_here.shape[0]
    slot_items = scatter_blocks(outgoing, experts_axis, 2)
    flattened = slot_items.reshape(-1, slot_items.shape[-1])
    gate_up = jnp.dot(flattened, gateup_here, preferred_element_type=jnp.float32)
    active = (jax.nn.silu(gate_up[:, :hidden_units]) * gate_up[:, hidden_units:]).astype(
        jnp.bfloat16
    )
    result = (
        jnp.dot(active, down_here, preferred_element_type=jnp.float32)
        .astype(jnp.bfloat16)
        .reshape(slot_items.shape)
    )
    returned = scatter_blocks(result, experts_axis, 3)
    combined = jnp.dot(
        jnp.transpose(select), returned.reshape(-1, model_width), preferred_element_type=jnp.float32
    )
    expert_mix = (gate_window[:, None] * combined).astype(jnp.bfloat16)
    return (hidden, expert_mix)


def solution(mesh):
    return jax.shard_map(
        per_device,
        mesh=mesh,
        in_specs=(
            P(("group", "expert"), None),
            P(),
            P(),
            P("group", "expert"),
            P(None, "group", None),
            P("expert", "group"),
            P(),
            P(),
            P(),
            P(),
            P("expert", None, None),
            P("expert", None, None),
            P(("group", "expert"), None),
        ),
        out_specs=(P(("group", "expert"), None), P(("group", "expert"), None)),
        check_vma=False,
    )
```

```python
import functools
import math

import jax
import jax.numpy as jnp
from jax import lax
from jax.experimental import pallas as pl
from jax.experimental.pallas import tpu as pltpu
from jax.sharding import PartitionSpec as P

MESH = pl.DeviceIdType.MESH

QUERY_HEADS = 32
KEY_VALUE_HEADS = 4
HEAD_DIMENSION = 128


epsilon = 1e-06
rope_theta = 1000000.0


def from_partner(block, axis, stride):
    count = lax.axis_size(axis)
    route = []
    for low in range(count):
        high = low | 1 << stride
        if high != low and high < count:
            route += [(low, high), (high, low)]
    return lax.ppermute(block, axis, route)


def gather_kernel(n_group, n_expert, wq, wk, wv, wo, xn, oq, ok, ov, oo, oxn, send, recv, xsend, xrecv, local):
    g = lax.axis_index("group")
    e = lax.axis_index("expert")
    columns = n_group // 2
    z = lax.div(g, 2)
    xh = lax.rem(g, 2)
    zp = lax.rem(z + 1, columns)
    zm = lax.rem(z + columns - 1, columns)
    plus_dev = (2 * zp + xh, e)
    minus_dev = (2 * zm + xh, e)
    pair_dev = (g + 1 - 2 * xh, e)
    core = lax.rem(e, 2)
    chip = lax.div(e, 2)
    chips = n_expert // 2
    mate_dev = (g, e + 1 - 2 * core)
    chip_devs = [(g, 2 * lax.rem(chip + j, chips) + core) for j in range(1, chips)]
    barrier = pltpu.get_barrier_semaphore()
    peers = [plus_dev, minus_dev, pair_dev, mate_dev] + chip_devs
    for dev in peers:
        pl.semaphore_signal(barrier, 1, device_id=dev, device_id_type=MESH)
    pl.semaphore_wait(barrier, len(peers))

    width = wo.shape[1]

    def slot(k, origin):
        if k == 3:
            return oo.at[:, pl.ds(pl.multiple_of(origin * width, width), width)]
        return (oq, ok, ov)[k].at[origin]

    sends = []

    def push(k, origin, src, dev):
        copy = pltpu.make_async_remote_copy(
            src_ref=src,
            dst_ref=slot(k, origin),
            send_sem=send.at[len(sends)],
            recv_sem=recv.at[k, origin],
            device_id=dev,
            device_id_type=MESH,
        )
        copy.start()
        sends.append(copy)

    def forward(origin, dev):
        for k in range(4):
            push(k, origin, slot(k, origin), dev)

    def arrive(origin):
        for k in range(4):
            pltpu.make_async_remote_copy(
                src_ref=slot(k, origin),
                dst_ref=slot(k, origin),
                send_sem=send.at[0],
                recv_sem=recv.at[k, origin],
                device_id=pair_dev,
                device_id_type=MESH,
            ).wait_recv()

    xsends = []

    def xpush(src, origin, dev):
        copy = pltpu.make_async_remote_copy(
            src_ref=src,
            dst_ref=oxn.at[origin],
            send_sem=xsend.at[len(xsends)],
            recv_sem=xrecv.at[origin],
            device_id=dev,
            device_id_type=MESH,
        )
        copy.start()
        xsends.append(copy)

    def xarrive(origin):
        pltpu.make_async_remote_copy(
            src_ref=oxn.at[origin],
            dst_ref=oxn.at[origin],
            send_sem=xsend.at[0],
            recv_sem=xrecv.at[origin],
            device_id=mate_dev,
            device_id_type=MESH,
        ).wait_recv()

    inputs = (wq, wk, wv, wo)
    own = [pltpu.make_async_copy(xn, oxn.at[e], local.at[4])]
    own += [pltpu.make_async_copy(inputs[k], slot(k, g), local.at[k]) for k in range(4)]
    for copy in own:
        copy.start()
    xpush(xn, e, mate_dev)
    for dev in chip_devs:
        xpush(xn, e, dev)
    for dev in (pair_dev, plus_dev, minus_dev):
        for k in range(4):
            push(k, g, inputs[k], dev)
    partner = g + 1 - 2 * xh
    arrive(partner)
    forward(partner, plus_dev)
    forward(partner, minus_dev)
    chip_origins = [2 * lax.rem(chip + j, chips) + core for j in range(1, chips)]
    normed_order = [chip_origins[0:2], chip_origins[2:5], chip_origins[5:]]
    for step in range(1, 4):
        behind = lax.rem(z - step + columns, columns)
        ahead = lax.rem(z + step, columns)
        for origin in (2 * behind, 2 * behind + 1):
            arrive(origin)
        for origin in ((2 * behind, 2 * behind + 1) if step < 3 else (2 * behind,)):
            forward(origin, plus_dev)
        for origin in (2 * ahead, 2 * ahead + 1):
            arrive(origin)
        for origin in ((2 * ahead, 2 * ahead + 1) if step < 3 else (2 * ahead + 1,)):
            forward(origin, minus_dev)
        for origin in normed_order[step - 1]:
            xarrive(origin)
            xpush(oxn.at[origin], origin, mate_dev)
    across = lax.rem(z + columns // 2, columns)
    arrive(2 * across)
    arrive(2 * across + 1)
    mate_core = 1 - core
    xarrive(e + 1 - 2 * core)
    for j in range(1, chips):
        xarrive(2 * lax.rem(chip + j, chips) + mate_core)
    for copy in sends + xsends:
        copy.wait_send()
    for copy in own:
        copy.wait()


def gather_all(wq, wk, wv, wo, xn, n_group, n_expert):
    any_spec = pl.BlockSpec(memory_space=pl.ANY)
    shapes = [jax.ShapeDtypeStruct((n_group,) + a.shape, a.dtype) for a in (wq, wk, wv)]
    shapes += [jax.ShapeDtypeStruct((wo.shape[0], n_group * wo.shape[1]), wo.dtype)]
    shapes += [jax.ShapeDtypeStruct((n_expert,) + xn.shape, xn.dtype)]
    return pl.pallas_call(
        functools.partial(gather_kernel, n_group, n_expert),
        out_shape=tuple(shapes),
        in_specs=[any_spec] * 5,
        out_specs=tuple([any_spec] * 5),
        scratch_shapes=[
            pltpu.SemaphoreType.DMA((64,)),
            pltpu.SemaphoreType.DMA((4, n_group)),
            pltpu.SemaphoreType.DMA((n_expert,)),
            pltpu.SemaphoreType.DMA((n_expert,)),
            pltpu.SemaphoreType.DMA((5,)),
        ],
        compiler_params=pltpu.CompilerParams(collective_id=0, has_side_effects=True),
    )(wq, wk, wv, wo, xn)


def mate_kernel(part, out, send, recv):
    g = lax.axis_index("group")
    e = lax.axis_index("expert")
    core = lax.rem(e, 2)
    mate_dev = (g, e + 1 - 2 * core)
    barrier = pltpu.get_barrier_semaphore()
    pl.semaphore_signal(barrier, 1, device_id=mate_dev, device_id_type=MESH)
    pl.semaphore_wait(barrier, 1)
    copy = pltpu.make_async_remote_copy(
        src_ref=part.at[:, 1 - core],
        dst_ref=out,
        send_sem=send.at[0],
        recv_sem=recv.at[0],
        device_id=mate_dev,
        device_id_type=MESH,
    )
    copy.start()
    copy.wait()


def exchange_with_mate(part):
    any_spec = pl.BlockSpec(memory_space=pl.ANY)
    shape = (part.shape[0],) + part.shape[2:]
    return pl.pallas_call(
        mate_kernel,
        out_shape=jax.ShapeDtypeStruct(shape, part.dtype),
        in_specs=[any_spec],
        out_specs=any_spec,
        scratch_shapes=[pltpu.SemaphoreType.DMA((1,)), pltpu.SemaphoreType.DMA((1,))],
        compiler_params=pltpu.CompilerParams(collective_id=4, has_side_effects=True),
    )(part)


def chip_scatter_kernel(chips, part, out, send, recv, local):
    g = lax.axis_index("group")
    e = lax.axis_index("expert")
    core = lax.rem(e, 2)
    chip = lax.div(e, 2)
    devs = [(g, 2 * lax.rem(chip + j, chips) + core) for j in range(1, chips)]
    barrier = pltpu.get_barrier_semaphore()
    for dev in devs:
        pl.semaphore_signal(barrier, 1, device_id=dev, device_id_type=MESH)
    pl.semaphore_wait(barrier, len(devs))
    copies = []
    for j in range(1, chips):
        copy = pltpu.make_async_remote_copy(
            src_ref=part.at[lax.rem(chip + j, chips)],
            dst_ref=out.at[chip],
            send_sem=send.at[j],
            recv_sem=recv.at[j],
            device_id=devs[j - 1],
            device_id_type=MESH,
        )
        copy.start()
        copies.append(copy)
    own = pltpu.make_async_copy(part.at[chip], out.at[chip], local.at[0])
    own.start()
    for copy in copies:
        copy.wait()
    own.wait()


def scatter_to_chips(part):
    chips = part.shape[0]
    any_spec = pl.BlockSpec(memory_space=pl.ANY)
    return pl.pallas_call(
        functools.partial(chip_scatter_kernel, chips),
        out_shape=jax.ShapeDtypeStruct(part.shape, part.dtype),
        in_specs=[any_spec],
        out_specs=any_spec,
        scratch_shapes=[
            pltpu.SemaphoreType.DMA((chips,)),
            pltpu.SemaphoreType.DMA((chips,)),
            pltpu.SemaphoreType.DMA((1,)),
        ],
        compiler_params=pltpu.CompilerParams(collective_id=5, has_side_effects=True),
    )(part)


def scatter_kernel(n_expert, part, out, send, recv, local):
    g = lax.axis_index("group")
    e = lax.axis_index("expert")
    barrier = pltpu.get_barrier_semaphore()
    for j in range(1, n_expert):
        pl.semaphore_signal(barrier, 1, device_id=(g, lax.rem(e + j, n_expert)), device_id_type=MESH)
    pl.semaphore_wait(barrier, n_expert - 1)
    copies = []
    for j in range(1, n_expert):
        peer = lax.rem(e + j, n_expert)
        copy = pltpu.make_async_remote_copy(
            src_ref=part.at[peer],
            dst_ref=out.at[e],
            send_sem=send.at[j],
            recv_sem=recv.at[j],
            device_id=(g, peer),
            device_id_type=MESH,
        )
        copy.start()
        copies.append(copy)
    own = pltpu.make_async_copy(part.at[e], out.at[e], local.at[0])
    own.start()
    for copy in copies:
        copy.wait()
    own.wait()


def scatter_blocks(part, n_expert, collective_id):
    any_spec = pl.BlockSpec(memory_space=pl.ANY)
    return pl.pallas_call(
        functools.partial(scatter_kernel, n_expert),
        out_shape=jax.ShapeDtypeStruct(part.shape, part.dtype),
        in_specs=[any_spec],
        out_specs=any_spec,
        scratch_shapes=[
            pltpu.SemaphoreType.DMA((n_expert,)),
            pltpu.SemaphoreType.DMA((n_expert,)),
            pltpu.SemaphoreType.DMA((1,)),
        ],
        compiler_params=pltpu.CompilerParams(collective_id=collective_id, has_side_effects=True),
    )(part)


def norm_rows(values, gain_vector):
    widened = values.astype(jnp.float32)
    inverse_rms = lax.rsqrt(jnp.mean(widened * widened, axis=-1, keepdims=True) + epsilon)
    return widened * inverse_rms * gain_vector


def rotate(values, positions):
    half_width = values.shape[-1] // 2
    exponents = jnp.arange(half_width).astype(jnp.float32)
    inverse = jnp.exp(exponents * (-2.0 * math.log(rope_theta) / values.shape[-1]))
    angles = positions[:, None, None] * inverse[None, None, :]
    cosine_values = jnp.cos(angles)
    sine_values = jnp.sin(angles)
    first_half = values[..., :half_width]
    second = values[..., half_width:]
    return jnp.concatenate(
        [
            first_half * cosine_values - second * sine_values,
            second * cosine_values + first_half * sine_values,
        ],
        axis=-1,
    )


def local_positions(parity, row_count):
    indices = jnp.arange(row_count)
    quarter = row_count // 2
    offset = jnp.where(parity == 0, jnp.where(indices < quarter, 0, 2 * quarter), quarter)
    return indices + offset


def per_device(
    hidden_in,
    norm_attention,
    norm_experts,
    query_master,
    trainer_key_value_weight,
    output_master,
    query_gain,
    key_gain,
    lengths,
    router,
    expert_gateup,
    expert_down,
    routes,
):
    experts_axis = lax.axis_size("expert")
    group_member = lax.axis_index("expert")
    group_index = lax.axis_index("group")
    local_head_count = QUERY_HEADS // experts_axis
    width_here = local_head_count * HEAD_DIMENSION
    common_head = group_member * local_head_count // (QUERY_HEADS // KEY_VALUE_HEADS)
    groups_axis = lax.axis_size("group")
    keyvalue_slice = lax.dynamic_slice_in_dim(
        trainer_key_value_weight, common_head * HEAD_DIMENSION, HEAD_DIMENSION, 2
    ).astype(jnp.bfloat16)
    normed = norm_rows(hidden_in, norm_attention).astype(jnp.bfloat16)
    query_parts, key_parts, value_parts, output_parts, normed_parts = gather_all(
        query_master.astype(jnp.bfloat16),
        keyvalue_slice[0],
        keyvalue_slice[1],
        output_master.astype(jnp.bfloat16),
        normed,
        groups_axis,
        experts_axis,
    )
    model_width = hidden_in.shape[1]
    joined_weights = jnp.concatenate(
        [
            query_parts.reshape(model_width, -1),
            key_parts.reshape(model_width, -1),
            value_parts.reshape(model_width, -1),
        ],
        axis=1,
    )
    projected = jnp.dot(
        normed_parts.reshape(-1, model_width),
        joined_weights,
        preferred_element_type=jnp.float32,
    ).astype(jnp.bfloat16)
    local_rows = projected.shape[0]
    query_rows_list = projected[:, :width_here].reshape(
        local_rows, local_head_count, HEAD_DIMENSION
    )
    key_rows = projected[:, width_here : width_here + HEAD_DIMENSION]
    value_rows = projected[:, width_here + HEAD_DIMENSION :]
    parity = group_index % 2
    own_places = local_positions(parity, local_rows)
    partner_places = local_positions(1 - parity, local_rows)
    query_rows_list = rotate(
        norm_rows(query_rows_list, query_gain), own_places.astype(jnp.float32)
    ).astype(jnp.bfloat16)
    key_rows = rotate(norm_rows(key_rows[:, None, :], key_gain), own_places.astype(jnp.float32))[
        :, 0, :
    ].astype(jnp.bfloat16)
    partner = from_partner(jnp.stack([key_rows, value_rows]), "group", 0)
    all_keys = jnp.concatenate([key_rows, partner[0]], axis=0)
    all_values = jnp.concatenate([value_rows, partner[1]], axis=0)
    key_places = jnp.concatenate([own_places, partner_places])
    valid_length = jnp.sum(jnp.where(jnp.arange(lengths.shape[0]) == group_index // 2, lengths, 0))
    block_rows = min(512, local_rows)
    block_count = local_rows // block_rows
    score_scale = HEAD_DIMENSION ** (-0.5)

    def attend(block_index):
        block_start = block_index * block_rows
        query_block = lax.dynamic_slice_in_dim(query_rows_list, block_start, block_rows, 0)
        query_places = lax.dynamic_slice_in_dim(own_places, block_start, block_rows, 0)
        scores = (
            jnp.einsum("qhd,kd->hqk", query_block, all_keys, preferred_element_type=jnp.float32)
            * score_scale
        )
        allowed = (key_places[None, :] <= query_places[:, None]) & (
            key_places[None, :] < valid_length
        )
        weights = jnp.where(allowed[None], jnp.exp(scores), 0.0)
        denominators = jnp.sum(weights, axis=-1)
        weighted = jnp.einsum(
            "hqk,kd->qhd",
            weights.astype(jnp.bfloat16),
            all_values,
            preferred_element_type=jnp.float32,
        )
        return (weighted / jnp.transpose(denominators)[:, :, None]).astype(jnp.bfloat16)

    attended = lax.map(attend, jnp.arange(block_count)).reshape(local_rows, width_here)
    head_partials = jnp.dot(
        attended, output_parts, preferred_element_type=jnp.float32
    ).astype(jnp.bfloat16)
    paired = head_partials.reshape(experts_axis // 2, 2, -1, model_width)
    from_mate = exchange_with_mate(paired)
    own_parity = lax.dynamic_index_in_dim(paired, group_member % 2, 1, keepdims=False)
    chip_sums = (own_parity.astype(jnp.float32) + from_mate.astype(jnp.float32)).astype(jnp.bfloat16)
    owned = scatter_to_chips(chip_sums)
    summed = jnp.sum(owned.astype(jnp.float32), axis=0)
    hidden = (hidden_in.astype(jnp.float32) + summed).astype(jnp.bfloat16)
    normed_second = norm_rows(hidden, norm_experts).astype(jnp.bfloat16)
    logits = jnp.dot(normed_second, router, preferred_element_type=jnp.float32)
    route_table = routes[:, :, None] == jnp.arange(logits.shape[1])[None, None, :]
    picked = jnp.sum(jnp.where(route_table, logits[:, None, :], 0.0), axis=-1)
    raised = jnp.exp(picked)
    gate_values = raised / jnp.sum(raised, axis=1, keepdims=True)
    inside = routes < experts_axis
    gate_window = jnp.sum(jnp.where(inside, gate_values, 0.0), axis=1)
    expert_window = jnp.sum(jnp.where(inside, routes, 0), axis=1)
    present = jnp.any(inside, axis=1)
    capacity = local_rows // (experts_axis * experts_axis)
    member_table = (
        present[:, None] & (expert_window[:, None] == jnp.arange(experts_axis)[None, :])
    ).astype(jnp.int32)
    ranking = jnp.sum(jnp.cumsum(member_table, axis=0) * member_table, axis=1) - 1
    slot_index = expert_window * capacity + ranking
    select = (
        (jnp.arange(experts_axis * capacity)[:, None] == slot_index[None, :]) & present[None, :]
    ).astype(jnp.bfloat16)
    outgoing = (
        jnp.dot(select, normed_second, preferred_element_type=jnp.float32)
        .astype(jnp.bfloat16)
        .reshape(experts_axis, capacity, model_width)
    )
    gateup_here = expert_gateup[0]
    down_here = expert_down[0]
    hidden_units = down_here.shape[0]
    slot_items = scatter_blocks(outgoing, experts_axis, 2)
    flattened = slot_items.reshape(-1, slot_items.shape[-1])
    gate_up = jnp.dot(flattened, gateup_here, preferred_element_type=jnp.float32)
    active = (jax.nn.silu(gate_up[:, :hidden_units]) * gate_up[:, hidden_units:]).astype(
        jnp.bfloat16
    )
    result = (
        jnp.dot(active, down_here, preferred_element_type=jnp.float32)
        .astype(jnp.bfloat16)
        .reshape(slot_items.shape)
    )
    returned = scatter_blocks(result, experts_axis, 3)
    combined = jnp.dot(
        jnp.transpose(select), returned.reshape(-1, model_width), preferred_element_type=jnp.float32
    )
    expert_mix = (gate_window[:, None] * combined).astype(jnp.bfloat16)
    return (hidden, expert_mix)


def solution(mesh):
    return jax.shard_map(
        per_device,
        mesh=mesh,
        in_specs=(
            P(("group", "expert"), None),
            P(),
            P(),
            P("group", "expert"),
            P(None, "group", None),
            P("expert", "group"),
            P(),
            P(),
            P(),
            P(),
            P("expert", None, None),
            P("expert", None, None),
            P(("group", "expert"), None),
        ),
        out_specs=(P(("group", "expert"), None), P(("group", "expert"), None)),
        check_vma=False,
    )
```

```python
import functools
import math

import jax
import jax.numpy as jnp
from jax import lax
from jax.experimental import pallas as pl
from jax.experimental.pallas import tpu as pltpu
from jax.sharding import PartitionSpec as P

MESH = pl.DeviceIdType.MESH

QUERY_HEADS = 32
KEY_VALUE_HEADS = 4
HEAD_DIMENSION = 128


epsilon = 1e-06
rope_theta = 1000000.0


def from_partner(block, axis, stride):
    count = lax.axis_size(axis)
    route = []
    for low in range(count):
        high = low | 1 << stride
        if high != low and high < count:
            route += [(low, high), (high, low)]
    return lax.ppermute(block, axis, route)


def gather_kernel(n_group, n_expert, wq, wk, wv, wo, xn, oq, ok, ov, oo, oxn, send, recv, xsend, xrecv, local):
    g = lax.axis_index("group")
    e = lax.axis_index("expert")
    columns = n_group // 2
    z = lax.div(g, 2)
    xh = lax.rem(g, 2)
    zp = lax.rem(z + 1, columns)
    zm = lax.rem(z + columns - 1, columns)
    plus_dev = (2 * zp + xh, e)
    minus_dev = (2 * zm + xh, e)
    pair_dev = (g + 1 - 2 * xh, e)
    core = lax.rem(e, 2)
    chip = lax.div(e, 2)
    chips = n_expert // 2
    mate_dev = (g, e + 1 - 2 * core)
    chip_devs = [(g, 2 * lax.rem(chip + j, chips) + core) for j in range(1, chips)]
    barrier = pltpu.get_barrier_semaphore()
    peers = [plus_dev, minus_dev, pair_dev, mate_dev] + chip_devs
    for dev in peers:
        pl.semaphore_signal(barrier, 1, device_id=dev, device_id_type=MESH)
    pl.semaphore_wait(barrier, len(peers))

    width = wo.shape[1]

    def slot(k, origin):
        if k == 3:
            return oo.at[:, pl.ds(pl.multiple_of(origin * width, width), width)]
        return (oq, ok, ov)[k].at[origin]

    sends = []

    def push(k, origin, src, dev):
        copy = pltpu.make_async_remote_copy(
            src_ref=src,
            dst_ref=slot(k, origin),
            send_sem=send.at[len(sends)],
            recv_sem=recv.at[k, origin],
            device_id=dev,
            device_id_type=MESH,
        )
        copy.start()
        sends.append(copy)

    def forward(origin, dev):
        for k in range(4):
            push(k, origin, slot(k, origin), dev)

    def arrive(origin):
        for k in range(4):
            pltpu.make_async_remote_copy(
                src_ref=slot(k, origin),
                dst_ref=slot(k, origin),
                send_sem=send.at[0],
                recv_sem=recv.at[k, origin],
                device_id=pair_dev,
                device_id_type=MESH,
            ).wait_recv()

    xsends = []

    def xpush(src, origin, dev):
        copy = pltpu.make_async_remote_copy(
            src_ref=src,
            dst_ref=oxn.at[origin],
            send_sem=xsend.at[len(xsends)],
            recv_sem=xrecv.at[origin],
            device_id=dev,
            device_id_type=MESH,
        )
        copy.start()
        xsends.append(copy)

    def xarrive(origin):
        pltpu.make_async_remote_copy(
            src_ref=oxn.at[origin],
            dst_ref=oxn.at[origin],
            send_sem=xsend.at[0],
            recv_sem=xrecv.at[origin],
            device_id=mate_dev,
            device_id_type=MESH,
        ).wait_recv()

    inputs = (wq, wk, wv, wo)
    own = [pltpu.make_async_copy(xn, oxn.at[e], local.at[4])]
    own += [pltpu.make_async_copy(inputs[k], slot(k, g), local.at[k]) for k in range(4)]
    for copy in own:
        copy.start()
    xpush(xn, e, mate_dev)
    for dev in chip_devs:
        xpush(xn, e, dev)
    for dev in (pair_dev, plus_dev, minus_dev):
        for k in range(4):
            push(k, g, inputs[k], dev)
    partner = g + 1 - 2 * xh
    arrive(partner)
    forward(partner, plus_dev)
    forward(partner, minus_dev)
    chip_origins = [2 * lax.rem(chip + j, chips) + core for j in range(1, chips)]
    normed_order = [chip_origins[0:2], chip_origins[2:5], chip_origins[5:]]
    for step in range(1, 4):
        behind = lax.rem(z - step + columns, columns)
        ahead = lax.rem(z + step, columns)
        for origin in (2 * behind, 2 * behind + 1):
            arrive(origin)
        for origin in ((2 * behind, 2 * behind + 1) if step < 3 else (2 * behind,)):
            forward(origin, plus_dev)
        for origin in (2 * ahead, 2 * ahead + 1):
            arrive(origin)
        for origin in ((2 * ahead, 2 * ahead + 1) if step < 3 else (2 * ahead + 1,)):
            forward(origin, minus_dev)
        for origin in normed_order[step - 1]:
            xarrive(origin)
            xpush(oxn.at[origin], origin, mate_dev)
    across = lax.rem(z + columns // 2, columns)
    arrive(2 * across)
    arrive(2 * across + 1)
    mate_core = 1 - core
    xarrive(e + 1 - 2 * core)
    for j in range(1, chips):
        xarrive(2 * lax.rem(chip + j, chips) + mate_core)
    for copy in sends + xsends:
        copy.wait_send()
    for copy in own:
        copy.wait()


def gather_all(wq, wk, wv, wo, xn, n_group, n_expert):
    any_spec = pl.BlockSpec(memory_space=pl.ANY)
    shapes = [jax.ShapeDtypeStruct((n_group,) + a.shape, a.dtype) for a in (wq, wk, wv)]
    shapes += [jax.ShapeDtypeStruct((wo.shape[0], n_group * wo.shape[1]), wo.dtype)]
    shapes += [jax.ShapeDtypeStruct((n_expert,) + xn.shape, xn.dtype)]
    return pl.pallas_call(
        functools.partial(gather_kernel, n_group, n_expert),
        out_shape=tuple(shapes),
        in_specs=[any_spec] * 5,
        out_specs=tuple([any_spec] * 5),
        scratch_shapes=[
            pltpu.SemaphoreType.DMA((64,)),
            pltpu.SemaphoreType.DMA((4, n_group)),
            pltpu.SemaphoreType.DMA((n_expert,)),
            pltpu.SemaphoreType.DMA((n_expert,)),
            pltpu.SemaphoreType.DMA((5,)),
        ],
        compiler_params=pltpu.CompilerParams(collective_id=0, has_side_effects=True),
    )(wq, wk, wv, wo, xn)


def mate_kernel(part, out, send, recv):
    g = lax.axis_index("group")
    e = lax.axis_index("expert")
    core = lax.rem(e, 2)
    mate_dev = (g, e + 1 - 2 * core)
    barrier = pltpu.get_barrier_semaphore()
    pl.semaphore_signal(barrier, 1, device_id=mate_dev, device_id_type=MESH)
    pl.semaphore_wait(barrier, 1)
    copy = pltpu.make_async_remote_copy(
        src_ref=part.at[:, 1 - core],
        dst_ref=out,
        send_sem=send.at[0],
        recv_sem=recv.at[0],
        device_id=mate_dev,
        device_id_type=MESH,
    )
    copy.start()
    copy.wait()


def exchange_with_mate(part):
    any_spec = pl.BlockSpec(memory_space=pl.ANY)
    shape = (part.shape[0],) + part.shape[2:]
    return pl.pallas_call(
        mate_kernel,
        out_shape=jax.ShapeDtypeStruct(shape, part.dtype),
        in_specs=[any_spec],
        out_specs=any_spec,
        scratch_shapes=[pltpu.SemaphoreType.DMA((1,)), pltpu.SemaphoreType.DMA((1,))],
        compiler_params=pltpu.CompilerParams(collective_id=4, has_side_effects=True),
    )(part)


def chip_scatter_kernel(chips, part, out, send, recv, local):
    g = lax.axis_index("group")
    e = lax.axis_index("expert")
    core = lax.rem(e, 2)
    chip = lax.div(e, 2)
    devs = [(g, 2 * lax.rem(chip + j, chips) + core) for j in range(1, chips)]
    barrier = pltpu.get_barrier_semaphore()
    for dev in devs:
        pl.semaphore_signal(barrier, 1, device_id=dev, device_id_type=MESH)
    pl.semaphore_wait(barrier, len(devs))
    copies = []
    for j in range(1, chips):
        copy = pltpu.make_async_remote_copy(
            src_ref=part.at[lax.rem(chip + j, chips)],
            dst_ref=out.at[chip],
            send_sem=send.at[j],
            recv_sem=recv.at[j],
            device_id=devs[j - 1],
            device_id_type=MESH,
        )
        copy.start()
        copies.append(copy)
    own = pltpu.make_async_copy(part.at[chip], out.at[chip], local.at[0])
    own.start()
    for copy in copies:
        copy.wait()
    own.wait()


def scatter_to_chips(part):
    chips = part.shape[0]
    any_spec = pl.BlockSpec(memory_space=pl.ANY)
    return pl.pallas_call(
        functools.partial(chip_scatter_kernel, chips),
        out_shape=jax.ShapeDtypeStruct(part.shape, part.dtype),
        in_specs=[any_spec],
        out_specs=any_spec,
        scratch_shapes=[
            pltpu.SemaphoreType.DMA((chips,)),
            pltpu.SemaphoreType.DMA((chips,)),
            pltpu.SemaphoreType.DMA((1,)),
        ],
        compiler_params=pltpu.CompilerParams(collective_id=5, has_side_effects=True),
    )(part)


def scatter_kernel(n_expert, part, out, send, recv, local):
    g = lax.axis_index("group")
    e = lax.axis_index("expert")
    barrier = pltpu.get_barrier_semaphore()
    for j in range(1, n_expert):
        pl.semaphore_signal(barrier, 1, device_id=(g, lax.rem(e + j, n_expert)), device_id_type=MESH)
    pl.semaphore_wait(barrier, n_expert - 1)
    copies = []
    for j in range(1, n_expert):
        peer = lax.rem(e + j, n_expert)
        copy = pltpu.make_async_remote_copy(
            src_ref=part.at[peer],
            dst_ref=out.at[e],
            send_sem=send.at[j],
            recv_sem=recv.at[j],
            device_id=(g, peer),
            device_id_type=MESH,
        )
        copy.start()
        copies.append(copy)
    own = pltpu.make_async_copy(part.at[e], out.at[e], local.at[0])
    own.start()
    for copy in copies:
        copy.wait()
    own.wait()


def scatter_blocks(part, n_expert, collective_id):
    any_spec = pl.BlockSpec(memory_space=pl.ANY)
    return pl.pallas_call(
        functools.partial(scatter_kernel, n_expert),
        out_shape=jax.ShapeDtypeStruct(part.shape, part.dtype),
        in_specs=[any_spec],
        out_specs=any_spec,
        scratch_shapes=[
            pltpu.SemaphoreType.DMA((n_expert,)),
            pltpu.SemaphoreType.DMA((n_expert,)),
            pltpu.SemaphoreType.DMA((1,)),
        ],
        compiler_params=pltpu.CompilerParams(collective_id=collective_id, has_side_effects=True),
    )(part)


def attention_kernel(scale, heads, q_ref, k_ref, v_ref, qpos_ref, kpos_ref, o_ref):
    allowed = kpos_ref[...] <= qpos_ref[...]
    keys = k_ref[...]
    values = v_ref[...]
    depth = keys.shape[1]
    for h in range(heads):
        query = q_ref[:, h * depth : (h + 1) * depth]
        scores = (
            lax.dot_general(
                query, keys, (((1,), (1,)), ((), ())), preferred_element_type=jnp.float32
            )
            * scale
        )
        weights = jnp.where(allowed, jnp.exp(scores), 0.0)
        denominators = jnp.sum(weights, axis=-1, keepdims=True)
        weighted = jnp.dot(
            weights.astype(jnp.bfloat16), values, preferred_element_type=jnp.float32
        )
        o_ref[:, h * depth : (h + 1) * depth] = (weighted / denominators).astype(o_ref.dtype)


def attention(queries, keys, values, query_places, key_places, scale):
    rows, width = queries.shape
    key_rows, depth = keys.shape
    block = min(256, rows)
    return pl.pallas_call(
        functools.partial(attention_kernel, scale, width // depth),
        out_shape=jax.ShapeDtypeStruct((rows, width), jnp.bfloat16),
        grid=(rows // block,),
        in_specs=[
            pl.BlockSpec((block, width), lambda i: (i, 0)),
            pl.BlockSpec((key_rows, depth), lambda i: (0, 0)),
            pl.BlockSpec((key_rows, depth), lambda i: (0, 0)),
            pl.BlockSpec((block, 1), lambda i: (i, 0)),
            pl.BlockSpec((1, key_rows), lambda i: (0, 0)),
        ],
        out_specs=pl.BlockSpec((block, width), lambda i: (i, 0)),
        cost_estimate=pl.CostEstimate(
            flops=4 * rows * key_rows * width,
            transcendentals=rows * key_rows * (width // depth),
            bytes_accessed=2 * (2 * rows * width + 2 * key_rows * depth),
        ),
    )(queries, keys, values, query_places.reshape(rows, 1), key_places.reshape(1, key_rows))


def norm_rows(values, gain_vector):
    widened = values.astype(jnp.float32)
    inverse_rms = lax.rsqrt(jnp.mean(widened * widened, axis=-1, keepdims=True) + epsilon)
    return widened * inverse_rms * gain_vector


def rotate(values, positions):
    half_width = values.shape[-1] // 2
    exponents = jnp.arange(half_width).astype(jnp.float32)
    inverse = jnp.exp(exponents * (-2.0 * math.log(rope_theta) / values.shape[-1]))
    angles = positions[:, None, None] * inverse[None, None, :]
    cosine_values = jnp.cos(angles)
    sine_values = jnp.sin(angles)
    first_half = values[..., :half_width]
    second = values[..., half_width:]
    return jnp.concatenate(
        [
            first_half * cosine_values - second * sine_values,
            second * cosine_values + first_half * sine_values,
        ],
        axis=-1,
    )


def local_positions(parity, row_count):
    indices = jnp.arange(row_count)
    quarter = row_count // 2
    offset = jnp.where(parity == 0, jnp.where(indices < quarter, 0, 2 * quarter), quarter)
    return indices + offset


def per_device(
    hidden_in,
    norm_attention,
    norm_experts,
    query_master,
    trainer_key_value_weight,
    output_master,
    query_gain,
    key_gain,
    lengths,
    router,
    expert_gateup,
    expert_down,
    routes,
):
    experts_axis = lax.axis_size("expert")
    group_member = lax.axis_index("expert")
    group_index = lax.axis_index("group")
    local_head_count = QUERY_HEADS // experts_axis
    width_here = local_head_count * HEAD_DIMENSION
    common_head = group_member * local_head_count // (QUERY_HEADS // KEY_VALUE_HEADS)
    groups_axis = lax.axis_size("group")
    keyvalue_slice = lax.dynamic_slice_in_dim(
        trainer_key_value_weight, common_head * HEAD_DIMENSION, HEAD_DIMENSION, 2
    ).astype(jnp.bfloat16)
    normed = norm_rows(hidden_in, norm_attention).astype(jnp.bfloat16)
    query_parts, key_parts, value_parts, output_parts, normed_parts = gather_all(
        query_master.astype(jnp.bfloat16),
        keyvalue_slice[0],
        keyvalue_slice[1],
        output_master.astype(jnp.bfloat16),
        normed,
        groups_axis,
        experts_axis,
    )
    model_width = hidden_in.shape[1]
    joined_weights = jnp.concatenate(
        [
            query_parts.reshape(model_width, -1),
            key_parts.reshape(model_width, -1),
            value_parts.reshape(model_width, -1),
        ],
        axis=1,
    )
    projected = jnp.dot(
        normed_parts.reshape(-1, model_width),
        joined_weights,
        preferred_element_type=jnp.float32,
    ).astype(jnp.bfloat16)
    local_rows = projected.shape[0]
    query_rows_list = projected[:, :width_here].reshape(
        local_rows, local_head_count, HEAD_DIMENSION
    )
    key_rows = projected[:, width_here : width_here + HEAD_DIMENSION]
    value_rows = projected[:, width_here + HEAD_DIMENSION :]
    parity = group_index % 2
    own_places = local_positions(parity, local_rows)
    partner_places = local_positions(1 - parity, local_rows)
    query_rows_list = rotate(
        norm_rows(query_rows_list, query_gain), own_places.astype(jnp.float32)
    ).astype(jnp.bfloat16)
    key_rows = rotate(norm_rows(key_rows[:, None, :], key_gain), own_places.astype(jnp.float32))[
        :, 0, :
    ].astype(jnp.bfloat16)
    partner = from_partner(jnp.stack([key_rows, value_rows]), "group", 0)
    all_keys = jnp.concatenate([key_rows, partner[0]], axis=0)
    all_values = jnp.concatenate([value_rows, partner[1]], axis=0)
    key_places = jnp.concatenate([own_places, partner_places])
    valid_length = jnp.sum(jnp.where(jnp.arange(lengths.shape[0]) == group_index // 2, lengths, 0))
    past_end = jnp.full_like(key_places, 4 * key_places.shape[0])
    key_limits = jnp.where(key_places < valid_length, key_places, past_end)
    attended = attention(
        query_rows_list.reshape(local_rows, width_here),
        all_keys,
        all_values,
        own_places,
        key_limits,
        HEAD_DIMENSION ** (-0.5),
    )
    head_partials = jnp.dot(
        attended, output_parts, preferred_element_type=jnp.float32
    ).astype(jnp.bfloat16)
    paired = head_partials.reshape(experts_axis // 2, 2, -1, model_width)
    from_mate = exchange_with_mate(paired)
    own_parity = lax.dynamic_index_in_dim(paired, group_member % 2, 1, keepdims=False)
    chip_sums = (own_parity.astype(jnp.float32) + from_mate.astype(jnp.float32)).astype(jnp.bfloat16)
    owned = scatter_to_chips(chip_sums)
    summed = jnp.sum(owned.astype(jnp.float32), axis=0)
    hidden = (hidden_in.astype(jnp.float32) + summed).astype(jnp.bfloat16)
    normed_second = norm_rows(hidden, norm_experts).astype(jnp.bfloat16)
    logits = jnp.dot(normed_second, router, preferred_element_type=jnp.float32)
    route_table = routes[:, :, None] == jnp.arange(logits.shape[1])[None, None, :]
    picked = jnp.sum(jnp.where(route_table, logits[:, None, :], 0.0), axis=-1)
    raised = jnp.exp(picked)
    gate_values = raised / jnp.sum(raised, axis=1, keepdims=True)
    inside = routes < experts_axis
    gate_window = jnp.sum(jnp.where(inside, gate_values, 0.0), axis=1)
    expert_window = jnp.sum(jnp.where(inside, routes, 0), axis=1)
    present = jnp.any(inside, axis=1)
    capacity = local_rows // (experts_axis * experts_axis)
    member_table = (
        present[:, None] & (expert_window[:, None] == jnp.arange(experts_axis)[None, :])
    ).astype(jnp.int32)
    ranking = jnp.sum(jnp.cumsum(member_table, axis=0) * member_table, axis=1) - 1
    slot_index = expert_window * capacity + ranking
    select = (
        (jnp.arange(experts_axis * capacity)[:, None] == slot_index[None, :]) & present[None, :]
    ).astype(jnp.bfloat16)
    outgoing = (
        jnp.dot(select, normed_second, preferred_element_type=jnp.float32)
        .astype(jnp.bfloat16)
        .reshape(experts_axis, capacity, model_width)
    )
    gateup_here = expert_gateup[0]
    down_here = expert_down[0]
    hidden_units = down_here.shape[0]
    slot_items = scatter_blocks(outgoing, experts_axis, 2)
    flattened = slot_items.reshape(-1, slot_items.shape[-1])
    gate_up = jnp.dot(flattened, gateup_here, preferred_element_type=jnp.float32)
    active = (jax.nn.silu(gate_up[:, :hidden_units]) * gate_up[:, hidden_units:]).astype(
        jnp.bfloat16
    )
    result = (
        jnp.dot(active, down_here, preferred_element_type=jnp.float32)
        .astype(jnp.bfloat16)
        .reshape(slot_items.shape)
    )
    returned = scatter_blocks(result, experts_axis, 3)
    combined = jnp.dot(
        jnp.transpose(select), returned.reshape(-1, model_width), preferred_element_type=jnp.float32
    )
    expert_mix = (gate_window[:, None] * combined).astype(jnp.bfloat16)
    return (hidden, expert_mix)


def solution(mesh):
    return jax.shard_map(
        per_device,
        mesh=mesh,
        in_specs=(
            P(("group", "expert"), None),
            P(),
            P(),
            P("group", "expert"),
            P(None, "group", None),
            P("expert", "group"),
            P(),
            P(),
            P(),
            P(),
            P("expert", None, None),
            P("expert", None, None),
            P(("group", "expert"), None),
        ),
        out_specs=(P(("group", "expert"), None), P(("group", "expert"), None)),
        check_vma=False,
    )
```

```python
import functools
import math

import jax
import numpy as np
import jax.numpy as jnp
from jax import lax
from jax.experimental import pallas as pl
from jax.experimental.pallas import tpu as pltpu
from jax.sharding import PartitionSpec as P

MESH = pl.DeviceIdType.MESH

QUERY_HEADS = 32
KEY_VALUE_HEADS = 4
HEAD_DIMENSION = 128


epsilon = 1e-06
rope_theta = 1000000.0


def from_partner(block, axis, stride):
    count = lax.axis_size(axis)
    route = []
    for low in range(count):
        high = low | 1 << stride
        if high != low and high < count:
            route += [(low, high), (high, low)]
    return lax.ppermute(block, axis, route)


def gather_kernel(n_group, n_expert, wq, wk, wv, wo, xn, oq, ok, ov, oo, oxn, send, recv, xsend, xrecv, local):
    g = lax.axis_index("group")
    e = lax.axis_index("expert")
    columns = n_group // 2
    z = lax.div(g, 2)
    xh = lax.rem(g, 2)
    zp = lax.rem(z + 1, columns)
    zm = lax.rem(z + columns - 1, columns)
    plus_dev = (2 * zp + xh, e)
    minus_dev = (2 * zm + xh, e)
    pair_dev = (g + 1 - 2 * xh, e)
    core = lax.rem(e, 2)
    chip = lax.div(e, 2)
    chips = n_expert // 2
    mate_dev = (g, e + 1 - 2 * core)
    chip_devs = [(g, 2 * lax.rem(chip + j, chips) + core) for j in range(1, chips)]
    barrier = pltpu.get_barrier_semaphore()
    peers = [plus_dev, minus_dev, pair_dev, mate_dev] + chip_devs
    for dev in peers:
        pl.semaphore_signal(barrier, 1, device_id=dev, device_id_type=MESH)
    pl.semaphore_wait(barrier, len(peers))

    width = wo.shape[1]

    def slot(k, origin):
        if k == 3:
            return oo.at[:, pl.ds(pl.multiple_of(origin * width, width), width)]
        return (oq, ok, ov)[k].at[origin]

    sends = []

    def push(k, origin, src, dev):
        copy = pltpu.make_async_remote_copy(
            src_ref=src,
            dst_ref=slot(k, origin),
            send_sem=send.at[len(sends)],
            recv_sem=recv.at[k, origin],
            device_id=dev,
            device_id_type=MESH,
        )
        copy.start()
        sends.append(copy)

    def forward(origin, dev):
        for k in range(4):
            push(k, origin, slot(k, origin), dev)

    def arrive(origin):
        for k in range(4):
            pltpu.make_async_remote_copy(
                src_ref=slot(k, origin),
                dst_ref=slot(k, origin),
                send_sem=send.at[0],
                recv_sem=recv.at[k, origin],
                device_id=pair_dev,
                device_id_type=MESH,
            ).wait_recv()

    xsends = []

    def xpush(src, origin, dev):
        copy = pltpu.make_async_remote_copy(
            src_ref=src,
            dst_ref=oxn.at[origin],
            send_sem=xsend.at[len(xsends)],
            recv_sem=xrecv.at[origin],
            device_id=dev,
            device_id_type=MESH,
        )
        copy.start()
        xsends.append(copy)

    def xarrive(origin):
        pltpu.make_async_remote_copy(
            src_ref=oxn.at[origin],
            dst_ref=oxn.at[origin],
            send_sem=xsend.at[0],
            recv_sem=xrecv.at[origin],
            device_id=mate_dev,
            device_id_type=MESH,
        ).wait_recv()

    inputs = (wq, wk, wv, wo)
    own = [pltpu.make_async_copy(xn, oxn.at[e], local.at[4])]
    own += [pltpu.make_async_copy(inputs[k], slot(k, g), local.at[k]) for k in range(4)]
    for copy in own:
        copy.start()
    xpush(xn, e, mate_dev)
    for dev in chip_devs:
        xpush(xn, e, dev)
    for dev in (pair_dev, plus_dev, minus_dev):
        for k in range(4):
            push(k, g, inputs[k], dev)
    partner = g + 1 - 2 * xh
    arrive(partner)
    forward(partner, plus_dev)
    forward(partner, minus_dev)
    chip_origins = [2 * lax.rem(chip + j, chips) + core for j in range(1, chips)]
    normed_order = [chip_origins[0:2], chip_origins[2:5], chip_origins[5:]]
    for step in range(1, 4):
        behind = lax.rem(z - step + columns, columns)
        ahead = lax.rem(z + step, columns)
        for origin in (2 * behind, 2 * behind + 1):
            arrive(origin)
        for origin in ((2 * behind, 2 * behind + 1) if step < 3 else (2 * behind,)):
            forward(origin, plus_dev)
        for origin in (2 * ahead, 2 * ahead + 1):
            arrive(origin)
        for origin in ((2 * ahead, 2 * ahead + 1) if step < 3 else (2 * ahead + 1,)):
            forward(origin, minus_dev)
        for origin in normed_order[step - 1]:
            xarrive(origin)
            xpush(oxn.at[origin], origin, mate_dev)
    across = lax.rem(z + columns // 2, columns)
    arrive(2 * across)
    arrive(2 * across + 1)
    mate_core = 1 - core
    xarrive(e + 1 - 2 * core)
    for j in range(1, chips):
        xarrive(2 * lax.rem(chip + j, chips) + mate_core)
    for copy in sends + xsends:
        copy.wait_send()
    for copy in own:
        copy.wait()


def gather_all(wq, wk, wv, wo, xn, n_group, n_expert):
    any_spec = pl.BlockSpec(memory_space=pl.ANY)
    shapes = [jax.ShapeDtypeStruct((n_group,) + a.shape, a.dtype) for a in (wq, wk, wv)]
    shapes += [jax.ShapeDtypeStruct((wo.shape[0], n_group * wo.shape[1]), wo.dtype)]
    shapes += [jax.ShapeDtypeStruct((n_expert,) + xn.shape, xn.dtype)]
    return pl.pallas_call(
        functools.partial(gather_kernel, n_group, n_expert),
        out_shape=tuple(shapes),
        in_specs=[any_spec] * 5,
        out_specs=tuple([any_spec] * 5),
        scratch_shapes=[
            pltpu.SemaphoreType.DMA((64,)),
            pltpu.SemaphoreType.DMA((4, n_group)),
            pltpu.SemaphoreType.DMA((n_expert,)),
            pltpu.SemaphoreType.DMA((n_expert,)),
            pltpu.SemaphoreType.DMA((5,)),
        ],
        compiler_params=pltpu.CompilerParams(collective_id=0, has_side_effects=True),
    )(wq, wk, wv, wo, xn)


def mate_kernel(part, out, send, recv):
    g = lax.axis_index("group")
    e = lax.axis_index("expert")
    core = lax.rem(e, 2)
    mate_dev = (g, e + 1 - 2 * core)
    barrier = pltpu.get_barrier_semaphore()
    pl.semaphore_signal(barrier, 1, device_id=mate_dev, device_id_type=MESH)
    pl.semaphore_wait(barrier, 1)
    copy = pltpu.make_async_remote_copy(
        src_ref=part.at[:, 1 - core],
        dst_ref=out,
        send_sem=send.at[0],
        recv_sem=recv.at[0],
        device_id=mate_dev,
        device_id_type=MESH,
    )
    copy.start()
    copy.wait()


def exchange_with_mate(part):
    any_spec = pl.BlockSpec(memory_space=pl.ANY)
    shape = (part.shape[0],) + part.shape[2:]
    return pl.pallas_call(
        mate_kernel,
        out_shape=jax.ShapeDtypeStruct(shape, part.dtype),
        in_specs=[any_spec],
        out_specs=any_spec,
        scratch_shapes=[pltpu.SemaphoreType.DMA((1,)), pltpu.SemaphoreType.DMA((1,))],
        compiler_params=pltpu.CompilerParams(collective_id=4, has_side_effects=True),
    )(part)


def chip_scatter_kernel(chips, part, out, send, recv, local):
    g = lax.axis_index("group")
    e = lax.axis_index("expert")
    core = lax.rem(e, 2)
    chip = lax.div(e, 2)
    devs = [(g, 2 * lax.rem(chip + j, chips) + core) for j in range(1, chips)]
    barrier = pltpu.get_barrier_semaphore()
    for dev in devs:
        pl.semaphore_signal(barrier, 1, device_id=dev, device_id_type=MESH)
    pl.semaphore_wait(barrier, len(devs))
    copies = []
    for j in range(1, chips):
        copy = pltpu.make_async_remote_copy(
            src_ref=part.at[lax.rem(chip + j, chips)],
            dst_ref=out.at[chip],
            send_sem=send.at[j],
            recv_sem=recv.at[j],
            device_id=devs[j - 1],
            device_id_type=MESH,
        )
        copy.start()
        copies.append(copy)
    own = pltpu.make_async_copy(part.at[chip], out.at[chip], local.at[0])
    own.start()
    for copy in copies:
        copy.wait()
    own.wait()


def scatter_to_chips(part):
    chips = part.shape[0]
    any_spec = pl.BlockSpec(memory_space=pl.ANY)
    return pl.pallas_call(
        functools.partial(chip_scatter_kernel, chips),
        out_shape=jax.ShapeDtypeStruct(part.shape, part.dtype),
        in_specs=[any_spec],
        out_specs=any_spec,
        scratch_shapes=[
            pltpu.SemaphoreType.DMA((chips,)),
            pltpu.SemaphoreType.DMA((chips,)),
            pltpu.SemaphoreType.DMA((1,)),
        ],
        compiler_params=pltpu.CompilerParams(collective_id=5, has_side_effects=True),
    )(part)


def scatter_kernel(n_expert, part, out, send, recv, local):
    g = lax.axis_index("group")
    e = lax.axis_index("expert")
    barrier = pltpu.get_barrier_semaphore()
    for j in range(1, n_expert):
        pl.semaphore_signal(barrier, 1, device_id=(g, lax.rem(e + j, n_expert)), device_id_type=MESH)
    pl.semaphore_wait(barrier, n_expert - 1)
    copies = []
    for j in range(1, n_expert):
        peer = lax.rem(e + j, n_expert)
        copy = pltpu.make_async_remote_copy(
            src_ref=part.at[peer],
            dst_ref=out.at[e],
            send_sem=send.at[j],
            recv_sem=recv.at[j],
            device_id=(g, peer),
            device_id_type=MESH,
        )
        copy.start()
        copies.append(copy)
    own = pltpu.make_async_copy(part.at[e], out.at[e], local.at[0])
    own.start()
    for copy in copies:
        copy.wait()
    own.wait()


def scatter_blocks(part, n_expert, collective_id):
    any_spec = pl.BlockSpec(memory_space=pl.ANY)
    return pl.pallas_call(
        functools.partial(scatter_kernel, n_expert),
        out_shape=jax.ShapeDtypeStruct(part.shape, part.dtype),
        in_specs=[any_spec],
        out_specs=any_spec,
        scratch_shapes=[
            pltpu.SemaphoreType.DMA((n_expert,)),
            pltpu.SemaphoreType.DMA((n_expert,)),
            pltpu.SemaphoreType.DMA((1,)),
        ],
        compiler_params=pltpu.CompilerParams(collective_id=collective_id, has_side_effects=True),
    )(part)


def attention_kernel(scale, heads, q_ref, k_ref, v_ref, qpos_ref, kpos_ref, o_ref):
    allowed = kpos_ref[...] <= qpos_ref[...]
    keys = k_ref[...]
    values = v_ref[...]
    depth = keys.shape[1]
    for h in range(heads):
        query = q_ref[:, h * depth : (h + 1) * depth]
        scores = (
            lax.dot_general(
                query, keys, (((1,), (1,)), ((), ())), preferred_element_type=jnp.float32
            )
            * scale
        )
        weights = jnp.where(allowed, jnp.exp(scores), 0.0)
        denominators = jnp.sum(weights, axis=-1, keepdims=True)
        weighted = jnp.dot(
            weights.astype(jnp.bfloat16), values, preferred_element_type=jnp.float32
        )
        o_ref[:, h * depth : (h + 1) * depth] = (weighted / denominators).astype(o_ref.dtype)


def attention(queries, keys, values, query_places, key_places, scale):
    rows, width = queries.shape
    key_rows, depth = keys.shape
    block = min(256, rows)
    return pl.pallas_call(
        functools.partial(attention_kernel, scale, width // depth),
        out_shape=jax.ShapeDtypeStruct((rows, width), jnp.bfloat16),
        grid=(rows // block,),
        in_specs=[
            pl.BlockSpec((block, width), lambda i: (i, 0)),
            pl.BlockSpec((key_rows, depth), lambda i: (0, 0)),
            pl.BlockSpec((key_rows, depth), lambda i: (0, 0)),
            pl.BlockSpec((block, 1), lambda i: (i, 0)),
            pl.BlockSpec((1, key_rows), lambda i: (0, 0)),
        ],
        out_specs=pl.BlockSpec((block, width), lambda i: (i, 0)),
        cost_estimate=pl.CostEstimate(
            flops=4 * rows * key_rows * width,
            transcendentals=rows * key_rows * (width // depth),
            bytes_accessed=2 * (2 * rows * width + 2 * key_rows * depth),
        ),
    )(queries, keys, values, query_places.reshape(rows, 1), key_places.reshape(1, key_rows))


def norm_rows(values, gain_vector):
    widened = values.astype(jnp.float32)
    inverse_rms = lax.rsqrt(jnp.mean(widened * widened, axis=-1, keepdims=True) + epsilon)
    return widened * inverse_rms * gain_vector


def rotate(values, positions):
    half_width = values.shape[-1] // 2
    exponents = jnp.arange(half_width).astype(jnp.float32)
    inverse = jnp.exp(exponents * (-2.0 * math.log(rope_theta) / values.shape[-1]))
    angles = positions[:, None, None] * inverse[None, None, :]
    cosine_values = jnp.cos(angles)
    sine_values = jnp.sin(angles)
    first_half = values[..., :half_width]
    second = values[..., half_width:]
    return jnp.concatenate(
        [
            first_half * cosine_values - second * sine_values,
            second * cosine_values + first_half * sine_values,
        ],
        axis=-1,
    )


def local_positions(parity, row_count):
    indices = jnp.arange(row_count)
    quarter = row_count // 2
    offset = jnp.where(parity == 0, jnp.where(indices < quarter, 0, 2 * quarter), quarter)
    return indices + offset


def prep_kernel(x_ref, wq_ref, wk_ref, wv_ref, cos_ref, sin_ref, qg_ref, kg_ref, q_out, k_out, v_out):
    x = x_ref[...]
    cosines = cos_ref[...]
    sines = sin_ref[...]
    depth = cosines.shape[1]

    def project(w_ref):
        return jnp.dot(x, w_ref[...], preferred_element_type=jnp.float32).astype(jnp.bfloat16)

    def norm_rope(values, gain):
        values = values.astype(jnp.float32)
        inverse_rms = lax.rsqrt(jnp.mean(values * values, axis=-1, keepdims=True) + epsilon)
        normed = values * inverse_rms * gain
        return (normed * cosines + pltpu.roll(normed, depth // 2, 1) * sines).astype(jnp.bfloat16)

    queries = project(wq_ref)
    for h in range(queries.shape[1] // depth):
        q_out[:, h * depth : (h + 1) * depth] = norm_rope(
            queries[:, h * depth : (h + 1) * depth], qg_ref[...]
        )
    k_out[...] = norm_rope(project(wk_ref), kg_ref[...])
    v_out[...] = project(wv_ref)


def prep(normed_rows, wq, wk, wv, cosines, sines, query_gain, key_gain):
    rows, width = normed_rows.shape
    depth = wk.shape[1]
    block = min(256, rows)
    whole = lambda shape: pl.BlockSpec(shape, lambda i: (0, 0))
    per_row = lambda cols: pl.BlockSpec((block, cols), lambda i: (i, 0))
    return pl.pallas_call(
        prep_kernel,
        out_shape=(
            jax.ShapeDtypeStruct((rows, wq.shape[1]), jnp.bfloat16),
            jax.ShapeDtypeStruct((rows, depth), jnp.bfloat16),
            jax.ShapeDtypeStruct((rows, depth), jnp.bfloat16),
        ),
        grid=(rows // block,),
        in_specs=[
            per_row(width),
            whole(wq.shape),
            whole(wk.shape),
            whole(wv.shape),
            per_row(depth),
            per_row(depth),
            whole((1, depth)),
            whole((1, depth)),
        ],
        out_specs=(per_row(wq.shape[1]), per_row(depth), per_row(depth)),
        cost_estimate=pl.CostEstimate(
            flops=2 * rows * width * (wq.shape[1] + 2 * depth),
            transcendentals=rows * (wq.shape[1] // depth + 1),
            bytes_accessed=2 * (rows * width + width * (wq.shape[1] + 2 * depth) + rows * (wq.shape[1] + 2 * depth)),
        ),
    )(normed_rows, wq, wk, wv, cosines, sines, query_gain.reshape(1, depth), key_gain.reshape(1, depth))


def rope_tables(parity, row_count, depth):
    half = depth // 2
    frequencies = rope_theta ** (-2.0 * np.arange(half) / depth)
    indices = np.arange(row_count)
    quarter = row_count // 2
    places = np.concatenate([np.where(indices < quarter, indices, indices + 2 * quarter), indices + quarter])
    angles = places[:, None].astype(np.float64) * frequencies[None, :]
    cosines = jnp.asarray(np.cos(angles), jnp.float32)
    sines = jnp.asarray(np.sin(angles), jnp.float32)
    cosines = lax.dynamic_slice_in_dim(cosines, parity * row_count, row_count, 0)
    sines = lax.dynamic_slice_in_dim(sines, parity * row_count, row_count, 0)
    return (
        jnp.concatenate([cosines, cosines], axis=1),
        jnp.concatenate([-sines, sines], axis=1),
    )


def per_device(
    hidden_in,
    norm_attention,
    norm_experts,
    query_master,
    trainer_key_value_weight,
    output_master,
    query_gain,
    key_gain,
    lengths,
    router,
    expert_gateup,
    expert_down,
    routes,
):
    experts_axis = lax.axis_size("expert")
    group_member = lax.axis_index("expert")
    group_index = lax.axis_index("group")
    local_head_count = QUERY_HEADS // experts_axis
    width_here = local_head_count * HEAD_DIMENSION
    common_head = group_member * local_head_count // (QUERY_HEADS // KEY_VALUE_HEADS)
    groups_axis = lax.axis_size("group")
    keyvalue_slice = lax.dynamic_slice_in_dim(
        trainer_key_value_weight, common_head * HEAD_DIMENSION, HEAD_DIMENSION, 2
    ).astype(jnp.bfloat16)
    normed = norm_rows(hidden_in, norm_attention).astype(jnp.bfloat16)
    query_parts, key_parts, value_parts, output_parts, normed_parts = gather_all(
        query_master.astype(jnp.bfloat16),
        keyvalue_slice[0],
        keyvalue_slice[1],
        output_master.astype(jnp.bfloat16),
        normed,
        groups_axis,
        experts_axis,
    )
    model_width = hidden_in.shape[1]
    local_rows = normed_parts.shape[0] * normed_parts.shape[1]
    parity = group_index % 2
    own_places = local_positions(parity, local_rows)
    partner_places = local_positions(1 - parity, local_rows)
    cosines, sines = rope_tables(parity, local_rows, HEAD_DIMENSION)
    query_rows_list, key_rows, value_rows = prep(
        normed_parts.reshape(local_rows, model_width),
        query_parts.reshape(model_width, -1),
        key_parts.reshape(model_width, -1),
        value_parts.reshape(model_width, -1),
        cosines,
        sines,
        query_gain,
        key_gain,
    )
    partner = from_partner(jnp.stack([key_rows, value_rows]), "group", 0)
    all_keys = jnp.concatenate([key_rows, partner[0]], axis=0)
    all_values = jnp.concatenate([value_rows, partner[1]], axis=0)
    key_places = jnp.concatenate([own_places, partner_places])
    valid_length = jnp.sum(jnp.where(jnp.arange(lengths.shape[0]) == group_index // 2, lengths, 0))
    past_end = jnp.full_like(key_places, 4 * key_places.shape[0])
    key_limits = jnp.where(key_places < valid_length, key_places, past_end)
    attended = attention(
        query_rows_list,
        all_keys,
        all_values,
        own_places,
        key_limits,
        HEAD_DIMENSION ** (-0.5),
    )
    head_partials = jnp.dot(
        attended, output_parts, preferred_element_type=jnp.float32
    ).astype(jnp.bfloat16)
    paired = head_partials.reshape(experts_axis // 2, 2, -1, model_width)
    from_mate = exchange_with_mate(paired)
    own_parity = lax.dynamic_index_in_dim(paired, group_member % 2, 1, keepdims=False)
    chip_sums = (own_parity.astype(jnp.float32) + from_mate.astype(jnp.float32)).astype(jnp.bfloat16)
    owned = scatter_to_chips(chip_sums)
    summed = jnp.sum(owned.astype(jnp.float32), axis=0)
    hidden = (hidden_in.astype(jnp.float32) + summed).astype(jnp.bfloat16)
    normed_second = norm_rows(hidden, norm_experts).astype(jnp.bfloat16)
    logits = jnp.dot(normed_second, router, preferred_element_type=jnp.float32)
    route_table = routes[:, :, None] == jnp.arange(logits.shape[1])[None, None, :]
    picked = jnp.sum(jnp.where(route_table, logits[:, None, :], 0.0), axis=-1)
    raised = jnp.exp(picked)
    gate_values = raised / jnp.sum(raised, axis=1, keepdims=True)
    inside = routes < experts_axis
    gate_window = jnp.sum(jnp.where(inside, gate_values, 0.0), axis=1)
    expert_window = jnp.sum(jnp.where(inside, routes, 0), axis=1)
    present = jnp.any(inside, axis=1)
    capacity = local_rows // (experts_axis * experts_axis)
    member_table = (
        present[:, None] & (expert_window[:, None] == jnp.arange(experts_axis)[None, :])
    ).astype(jnp.int32)
    ranking = jnp.sum(jnp.cumsum(member_table, axis=0) * member_table, axis=1) - 1
    slot_index = expert_window * capacity + ranking
    select = (
        (jnp.arange(experts_axis * capacity)[:, None] == slot_index[None, :]) & present[None, :]
    ).astype(jnp.bfloat16)
    outgoing = (
        jnp.dot(select, normed_second, preferred_element_type=jnp.float32)
        .astype(jnp.bfloat16)
        .reshape(experts_axis, capacity, model_width)
    )
    gateup_here = expert_gateup[0]
    down_here = expert_down[0]
    hidden_units = down_here.shape[0]
    slot_items = scatter_blocks(outgoing, experts_axis, 2)
    flattened = slot_items.reshape(-1, slot_items.shape[-1])
    gate_up = jnp.dot(flattened, gateup_here, preferred_element_type=jnp.float32)
    active = (jax.nn.silu(gate_up[:, :hidden_units]) * gate_up[:, hidden_units:]).astype(
        jnp.bfloat16
    )
    result = (
        jnp.dot(active, down_here, preferred_element_type=jnp.float32)
        .astype(jnp.bfloat16)
        .reshape(slot_items.shape)
    )
    returned = scatter_blocks(result, experts_axis, 3)
    combined = jnp.dot(
        jnp.transpose(select), returned.reshape(-1, model_width), preferred_element_type=jnp.float32
    )
    expert_mix = (gate_window[:, None] * combined).astype(jnp.bfloat16)
    return (hidden, expert_mix)


def solution(mesh):
    return jax.shard_map(
        per_device,
        mesh=mesh,
        in_specs=(
            P(("group", "expert"), None),
            P(),
            P(),
            P("group", "expert"),
            P(None, "group", None),
            P("expert", "group"),
            P(),
            P(),
            P(),
            P(),
            P("expert", None, None),
            P("expert", None, None),
            P(("group", "expert"), None),
        ),
        out_specs=(P(("group", "expert"), None), P(("group", "expert"), None)),
        check_vma=False,
    )
```

```python
import functools
import math

import jax
import numpy as np
import jax.numpy as jnp
from jax import lax
from jax.experimental import pallas as pl
from jax.experimental.pallas import tpu as pltpu
from jax.sharding import PartitionSpec as P

MESH = pl.DeviceIdType.MESH

QUERY_HEADS = 32
KEY_VALUE_HEADS = 4
HEAD_DIMENSION = 128


epsilon = 1e-06
rope_theta = 1000000.0


def from_partner(block, axis, stride):
    count = lax.axis_size(axis)
    route = []
    for low in range(count):
        high = low | 1 << stride
        if high != low and high < count:
            route += [(low, high), (high, low)]
    return lax.ppermute(block, axis, route)


def gather_kernel(n_group, n_expert, wq, wk, wv, wo, xn, oq, ok, ov, oo, oxn, send, recv, xsend, xrecv, local):
    g = lax.axis_index("group")
    e = lax.axis_index("expert")
    columns = n_group // 2
    z = lax.div(g, 2)
    xh = lax.rem(g, 2)
    zp = lax.rem(z + 1, columns)
    zm = lax.rem(z + columns - 1, columns)
    plus_dev = (2 * zp + xh, e)
    minus_dev = (2 * zm + xh, e)
    pair_dev = (g + 1 - 2 * xh, e)
    core = lax.rem(e, 2)
    chip = lax.div(e, 2)
    chips = n_expert // 2
    mate_dev = (g, e + 1 - 2 * core)
    chip_devs = [(g, 2 * lax.rem(chip + j, chips) + core) for j in range(1, chips)]
    barrier = pltpu.get_barrier_semaphore()
    peers = [plus_dev, minus_dev, pair_dev, mate_dev] + chip_devs
    for dev in peers:
        pl.semaphore_signal(barrier, 1, device_id=dev, device_id_type=MESH)
    pl.semaphore_wait(barrier, len(peers))

    width = wo.shape[1]

    def slot(k, origin):
        if k == 3:
            return oo.at[:, pl.ds(pl.multiple_of(origin * width, width), width)]
        return (oq, ok, ov)[k].at[origin]

    sends = []

    def push(k, origin, src, dev):
        copy = pltpu.make_async_remote_copy(
            src_ref=src,
            dst_ref=slot(k, origin),
            send_sem=send.at[len(sends)],
            recv_sem=recv.at[k, origin],
            device_id=dev,
            device_id_type=MESH,
        )
        copy.start()
        sends.append(copy)

    def forward(origin, dev):
        for k in range(4):
            push(k, origin, slot(k, origin), dev)

    def arrive(origin):
        for k in range(4):
            pltpu.make_async_remote_copy(
                src_ref=slot(k, origin),
                dst_ref=slot(k, origin),
                send_sem=send.at[0],
                recv_sem=recv.at[k, origin],
                device_id=pair_dev,
                device_id_type=MESH,
            ).wait_recv()

    xsends = []

    def xpush(src, origin, dev):
        copy = pltpu.make_async_remote_copy(
            src_ref=src,
            dst_ref=oxn.at[origin],
            send_sem=xsend.at[len(xsends)],
            recv_sem=xrecv.at[origin],
            device_id=dev,
            device_id_type=MESH,
        )
        copy.start()
        xsends.append(copy)

    def xarrive(origin):
        pltpu.make_async_remote_copy(
            src_ref=oxn.at[origin],
            dst_ref=oxn.at[origin],
            send_sem=xsend.at[0],
            recv_sem=xrecv.at[origin],
            device_id=mate_dev,
            device_id_type=MESH,
        ).wait_recv()

    inputs = (wq, wk, wv, wo)
    own = [pltpu.make_async_copy(xn, oxn.at[e], local.at[4])]
    own += [pltpu.make_async_copy(inputs[k], slot(k, g), local.at[k]) for k in range(4)]
    for copy in own:
        copy.start()
    xpush(xn, e, mate_dev)
    for dev in chip_devs:
        xpush(xn, e, dev)
    for dev in (pair_dev, plus_dev, minus_dev):
        for k in range(4):
            push(k, g, inputs[k], dev)
    partner = g + 1 - 2 * xh
    arrive(partner)
    forward(partner, plus_dev)
    forward(partner, minus_dev)
    chip_origins = [2 * lax.rem(chip + j, chips) + core for j in range(1, chips)]
    normed_order = [chip_origins[0:2], chip_origins[2:5], chip_origins[5:]]
    for step in range(1, 4):
        behind = lax.rem(z - step + columns, columns)
        ahead = lax.rem(z + step, columns)
        for origin in (2 * behind, 2 * behind + 1):
            arrive(origin)
        for origin in ((2 * behind, 2 * behind + 1) if step < 3 else (2 * behind,)):
            forward(origin, plus_dev)
        for origin in (2 * ahead, 2 * ahead + 1):
            arrive(origin)
        for origin in ((2 * ahead, 2 * ahead + 1) if step < 3 else (2 * ahead + 1,)):
            forward(origin, minus_dev)
        for origin in normed_order[step - 1]:
            xarrive(origin)
            xpush(oxn.at[origin], origin, mate_dev)
    across = lax.rem(z + columns // 2, columns)
    arrive(2 * across)
    arrive(2 * across + 1)
    mate_core = 1 - core
    xarrive(e + 1 - 2 * core)
    for j in range(1, chips):
        xarrive(2 * lax.rem(chip + j, chips) + mate_core)
    for copy in sends + xsends:
        copy.wait_send()
    for copy in own:
        copy.wait()


def gather_all(wq, wk, wv, wo, xn, n_group, n_expert):
    any_spec = pl.BlockSpec(memory_space=pl.ANY)
    shapes = [jax.ShapeDtypeStruct((n_group,) + a.shape, a.dtype) for a in (wq, wk, wv)]
    shapes += [jax.ShapeDtypeStruct((wo.shape[0], n_group * wo.shape[1]), wo.dtype)]
    shapes += [jax.ShapeDtypeStruct((n_expert,) + xn.shape, xn.dtype)]
    return pl.pallas_call(
        functools.partial(gather_kernel, n_group, n_expert),
        out_shape=tuple(shapes),
        in_specs=[any_spec] * 5,
        out_specs=tuple([any_spec] * 5),
        scratch_shapes=[
            pltpu.SemaphoreType.DMA((64,)),
            pltpu.SemaphoreType.DMA((4, n_group)),
            pltpu.SemaphoreType.DMA((n_expert,)),
            pltpu.SemaphoreType.DMA((n_expert,)),
            pltpu.SemaphoreType.DMA((5,)),
        ],
        compiler_params=pltpu.CompilerParams(collective_id=0, has_side_effects=True),
    )(wq, wk, wv, wo, xn)


def mate_kernel(part, out, send, recv):
    g = lax.axis_index("group")
    e = lax.axis_index("expert")
    core = lax.rem(e, 2)
    mate_dev = (g, e + 1 - 2 * core)
    barrier = pltpu.get_barrier_semaphore()
    pl.semaphore_signal(barrier, 1, device_id=mate_dev, device_id_type=MESH)
    pl.semaphore_wait(barrier, 1)
    copy = pltpu.make_async_remote_copy(
        src_ref=part.at[:, 1 - core],
        dst_ref=out,
        send_sem=send.at[0],
        recv_sem=recv.at[0],
        device_id=mate_dev,
        device_id_type=MESH,
    )
    copy.start()
    copy.wait()


def exchange_with_mate(part):
    any_spec = pl.BlockSpec(memory_space=pl.ANY)
    shape = (part.shape[0],) + part.shape[2:]
    return pl.pallas_call(
        mate_kernel,
        out_shape=jax.ShapeDtypeStruct(shape, part.dtype),
        in_specs=[any_spec],
        out_specs=any_spec,
        scratch_shapes=[pltpu.SemaphoreType.DMA((1,)), pltpu.SemaphoreType.DMA((1,))],
        compiler_params=pltpu.CompilerParams(collective_id=4, has_side_effects=True),
    )(part)


def chip_scatter_kernel(chips, part, out, send, recv, local):
    g = lax.axis_index("group")
    e = lax.axis_index("expert")
    core = lax.rem(e, 2)
    chip = lax.div(e, 2)
    devs = [(g, 2 * lax.rem(chip + j, chips) + core) for j in range(1, chips)]
    barrier = pltpu.get_barrier_semaphore()
    for dev in devs:
        pl.semaphore_signal(barrier, 1, device_id=dev, device_id_type=MESH)
    pl.semaphore_wait(barrier, len(devs))
    copies = []
    for j in range(1, chips):
        copy = pltpu.make_async_remote_copy(
            src_ref=part.at[lax.rem(chip + j, chips)],
            dst_ref=out.at[chip],
            send_sem=send.at[j],
            recv_sem=recv.at[j],
            device_id=devs[j - 1],
            device_id_type=MESH,
        )
        copy.start()
        copies.append(copy)
    own = pltpu.make_async_copy(part.at[chip], out.at[chip], local.at[0])
    own.start()
    for copy in copies:
        copy.wait()
    own.wait()


def scatter_to_chips(part):
    chips = part.shape[0]
    any_spec = pl.BlockSpec(memory_space=pl.ANY)
    return pl.pallas_call(
        functools.partial(chip_scatter_kernel, chips),
        out_shape=jax.ShapeDtypeStruct(part.shape, part.dtype),
        in_specs=[any_spec],
        out_specs=any_spec,
        scratch_shapes=[
            pltpu.SemaphoreType.DMA((chips,)),
            pltpu.SemaphoreType.DMA((chips,)),
            pltpu.SemaphoreType.DMA((1,)),
        ],
        compiler_params=pltpu.CompilerParams(collective_id=5, has_side_effects=True),
    )(part)


def scatter_kernel(n_expert, part, out, send, recv, local):
    g = lax.axis_index("group")
    e = lax.axis_index("expert")
    barrier = pltpu.get_barrier_semaphore()
    for j in range(1, n_expert):
        pl.semaphore_signal(barrier, 1, device_id=(g, lax.rem(e + j, n_expert)), device_id_type=MESH)
    pl.semaphore_wait(barrier, n_expert - 1)
    copies = []
    for j in range(1, n_expert):
        peer = lax.rem(e + j, n_expert)
        copy = pltpu.make_async_remote_copy(
            src_ref=part.at[peer],
            dst_ref=out.at[e],
            send_sem=send.at[j],
            recv_sem=recv.at[j],
            device_id=(g, peer),
            device_id_type=MESH,
        )
        copy.start()
        copies.append(copy)
    own = pltpu.make_async_copy(part.at[e], out.at[e], local.at[0])
    own.start()
    for copy in copies:
        copy.wait()
    own.wait()


def scatter_blocks(part, n_expert, collective_id):
    any_spec = pl.BlockSpec(memory_space=pl.ANY)
    return pl.pallas_call(
        functools.partial(scatter_kernel, n_expert),
        out_shape=jax.ShapeDtypeStruct(part.shape, part.dtype),
        in_specs=[any_spec],
        out_specs=any_spec,
        scratch_shapes=[
            pltpu.SemaphoreType.DMA((n_expert,)),
            pltpu.SemaphoreType.DMA((n_expert,)),
            pltpu.SemaphoreType.DMA((1,)),
        ],
        compiler_params=pltpu.CompilerParams(collective_id=collective_id, has_side_effects=True),
    )(part)


def attention_kernel(scale, heads, q_ref, k_ref, v_ref, qpos_ref, kpos_ref, o_ref):
    allowed = kpos_ref[...] <= qpos_ref[...]
    keys = k_ref[...]
    values = v_ref[...]
    depth = keys.shape[1]
    for h in range(heads):
        query = q_ref[:, h * depth : (h + 1) * depth]
        scores = (
            lax.dot_general(
                query, keys, (((1,), (1,)), ((), ())), preferred_element_type=jnp.float32
            )
            * scale
        )
        weights = jnp.where(allowed, jnp.exp(scores), 0.0)
        denominators = jnp.sum(weights, axis=-1, keepdims=True)
        weighted = jnp.dot(
            weights.astype(jnp.bfloat16), values, preferred_element_type=jnp.float32
        )
        o_ref[:, h * depth : (h + 1) * depth] = (weighted / denominators).astype(o_ref.dtype)


def attention(queries, keys, values, query_places, key_places, scale):
    rows, width = queries.shape
    key_rows, depth = keys.shape
    block = min(256, rows)
    return pl.pallas_call(
        functools.partial(attention_kernel, scale, width // depth),
        out_shape=jax.ShapeDtypeStruct((rows, width), jnp.bfloat16),
        grid=(rows // block,),
        in_specs=[
            pl.BlockSpec((block, width), lambda i: (i, 0)),
            pl.BlockSpec((key_rows, depth), lambda i: (0, 0)),
            pl.BlockSpec((key_rows, depth), lambda i: (0, 0)),
            pl.BlockSpec((block, 1), lambda i: (i, 0)),
            pl.BlockSpec((1, key_rows), lambda i: (0, 0)),
        ],
        out_specs=pl.BlockSpec((block, width), lambda i: (i, 0)),
        cost_estimate=pl.CostEstimate(
            flops=4 * rows * key_rows * width,
            transcendentals=rows * key_rows * (width // depth),
            bytes_accessed=2 * (2 * rows * width + 2 * key_rows * depth),
        ),
    )(queries, keys, values, query_places.reshape(rows, 1), key_places.reshape(1, key_rows))


def norm_rows(values, gain_vector):
    widened = values.astype(jnp.float32)
    inverse_rms = lax.rsqrt(jnp.mean(widened * widened, axis=-1, keepdims=True) + epsilon)
    return widened * inverse_rms * gain_vector


def rotate(values, positions):
    half_width = values.shape[-1] // 2
    exponents = jnp.arange(half_width).astype(jnp.float32)
    inverse = jnp.exp(exponents * (-2.0 * math.log(rope_theta) / values.shape[-1]))
    angles = positions[:, None, None] * inverse[None, None, :]
    cosine_values = jnp.cos(angles)
    sine_values = jnp.sin(angles)
    first_half = values[..., :half_width]
    second = values[..., half_width:]
    return jnp.concatenate(
        [
            first_half * cosine_values - second * sine_values,
            second * cosine_values + first_half * sine_values,
        ],
        axis=-1,
    )


def local_positions(parity, row_count):
    indices = jnp.arange(row_count)
    quarter = row_count // 2
    offset = jnp.where(parity == 0, jnp.where(indices < quarter, 0, 2 * quarter), quarter)
    return indices + offset


def pair_keys_kernel(k_ref, v_ref, k_all, v_all, send, recv, local):
    g = lax.axis_index("group")
    e = lax.axis_index("expert")
    pair_dev = (g + 1 - 2 * lax.rem(g, 2), e)
    rows = k_ref.shape[0]
    barrier = pltpu.get_barrier_semaphore()
    pl.semaphore_signal(barrier, 1, device_id=pair_dev, device_id_type=MESH)
    pl.semaphore_wait(barrier, 1)
    copies = []
    for i, (src, dst) in enumerate(((k_ref, k_all), (v_ref, v_all))):
        copy = pltpu.make_async_remote_copy(
            src_ref=src,
            dst_ref=dst.at[pl.ds(rows, rows)],
            send_sem=send.at[i],
            recv_sem=recv.at[i],
            device_id=pair_dev,
            device_id_type=MESH,
        )
        copy.start()
        copies.append(copy)
    own = [
        pltpu.make_async_copy(src, dst.at[pl.ds(0, rows)], local.at[i])
        for i, (src, dst) in enumerate(((k_ref, k_all), (v_ref, v_all)))
    ]
    for copy in own:
        copy.start()
    for copy in copies + own:
        copy.wait()


def pair_keys(keys, values):
    any_spec = pl.BlockSpec(memory_space=pl.ANY)
    shape = jax.ShapeDtypeStruct((2 * keys.shape[0], keys.shape[1]), keys.dtype)
    return pl.pallas_call(
        pair_keys_kernel,
        out_shape=(shape, shape),
        in_specs=[any_spec, any_spec],
        out_specs=(any_spec, any_spec),
        scratch_shapes=[pltpu.SemaphoreType.DMA((2,))] * 3,
        compiler_params=pltpu.CompilerParams(collective_id=6, has_side_effects=True),
    )(keys, values)


def prep_kernel(x_ref, wq_ref, wk_ref, wv_ref, cos_ref, sin_ref, qg_ref, kg_ref, q_out, k_out, v_out):
    x = x_ref[...]
    cosines = cos_ref[...]
    sines = sin_ref[...]
    depth = cosines.shape[1]

    def project(w_ref):
        return jnp.dot(x, w_ref[...], preferred_element_type=jnp.float32).astype(jnp.bfloat16)

    def norm_rope(values, gain):
        values = values.astype(jnp.float32)
        inverse_rms = lax.rsqrt(jnp.mean(values * values, axis=-1, keepdims=True) + epsilon)
        normed = values * inverse_rms * gain
        return (normed * cosines + pltpu.roll(normed, depth // 2, 1) * sines).astype(jnp.bfloat16)

    queries = project(wq_ref)
    for h in range(queries.shape[1] // depth):
        q_out[:, h * depth : (h + 1) * depth] = norm_rope(
            queries[:, h * depth : (h + 1) * depth], qg_ref[...]
        )
    k_out[...] = norm_rope(project(wk_ref), kg_ref[...])
    v_out[...] = project(wv_ref)


def prep(normed_rows, wq, wk, wv, cosines, sines, query_gain, key_gain):
    rows, width = normed_rows.shape
    depth = wk.shape[1]
    block = min(256, rows)
    whole = lambda shape: pl.BlockSpec(shape, lambda i: (0, 0))
    per_row = lambda cols: pl.BlockSpec((block, cols), lambda i: (i, 0))
    return pl.pallas_call(
        prep_kernel,
        out_shape=(
            jax.ShapeDtypeStruct((rows, wq.shape[1]), jnp.bfloat16),
            jax.ShapeDtypeStruct((rows, depth), jnp.bfloat16),
            jax.ShapeDtypeStruct((rows, depth), jnp.bfloat16),
        ),
        grid=(rows // block,),
        in_specs=[
            per_row(width),
            whole(wq.shape),
            whole(wk.shape),
            whole(wv.shape),
            per_row(depth),
            per_row(depth),
            whole((1, depth)),
            whole((1, depth)),
        ],
        out_specs=(per_row(wq.shape[1]), per_row(depth), per_row(depth)),
        cost_estimate=pl.CostEstimate(
            flops=2 * rows * width * (wq.shape[1] + 2 * depth),
            transcendentals=rows * (wq.shape[1] // depth + 1),
            bytes_accessed=2 * (rows * width + width * (wq.shape[1] + 2 * depth) + rows * (wq.shape[1] + 2 * depth)),
        ),
    )(normed_rows, wq, wk, wv, cosines, sines, query_gain.reshape(1, depth), key_gain.reshape(1, depth))


def rope_tables(parity, row_count, depth):
    half = depth // 2
    frequencies = rope_theta ** (-2.0 * np.arange(half) / depth)
    indices = np.arange(row_count)
    quarter = row_count // 2
    places = np.concatenate([np.where(indices < quarter, indices, indices + 2 * quarter), indices + quarter])
    angles = places[:, None].astype(np.float64) * frequencies[None, :]
    cosines = jnp.asarray(np.cos(angles), jnp.float32)
    sines = jnp.asarray(np.sin(angles), jnp.float32)
    cosines = lax.dynamic_slice_in_dim(cosines, parity * row_count, row_count, 0)
    sines = lax.dynamic_slice_in_dim(sines, parity * row_count, row_count, 0)
    return (
        jnp.concatenate([cosines, cosines], axis=1),
        jnp.concatenate([-sines, sines], axis=1),
    )


def per_device(
    hidden_in,
    norm_attention,
    norm_experts,
    query_master,
    trainer_key_value_weight,
    output_master,
    query_gain,
    key_gain,
    lengths,
    router,
    expert_gateup,
    expert_down,
    routes,
):
    experts_axis = lax.axis_size("expert")
    group_member = lax.axis_index("expert")
    group_index = lax.axis_index("group")
    local_head_count = QUERY_HEADS // experts_axis
    width_here = local_head_count * HEAD_DIMENSION
    common_head = group_member * local_head_count // (QUERY_HEADS // KEY_VALUE_HEADS)
    groups_axis = lax.axis_size("group")
    keyvalue_slice = lax.dynamic_slice_in_dim(
        trainer_key_value_weight, common_head * HEAD_DIMENSION, HEAD_DIMENSION, 2
    ).astype(jnp.bfloat16)
    normed = norm_rows(hidden_in, norm_attention).astype(jnp.bfloat16)
    query_parts, key_parts, value_parts, output_parts, normed_parts = gather_all(
        query_master.astype(jnp.bfloat16),
        keyvalue_slice[0],
        keyvalue_slice[1],
        output_master.astype(jnp.bfloat16),
        normed,
        groups_axis,
        experts_axis,
    )
    model_width = hidden_in.shape[1]
    local_rows = normed_parts.shape[0] * normed_parts.shape[1]
    parity = group_index % 2
    own_places = local_positions(parity, local_rows)
    partner_places = local_positions(1 - parity, local_rows)
    cosines, sines = rope_tables(parity, local_rows, HEAD_DIMENSION)
    query_rows_list, key_rows, value_rows = prep(
        normed_parts.reshape(local_rows, model_width),
        query_parts.reshape(model_width, -1),
        key_parts.reshape(model_width, -1),
        value_parts.reshape(model_width, -1),
        cosines,
        sines,
        query_gain,
        key_gain,
    )
    all_keys, all_values = pair_keys(key_rows, value_rows)
    key_places = jnp.concatenate([own_places, partner_places])
    valid_length = jnp.sum(jnp.where(jnp.arange(lengths.shape[0]) == group_index // 2, lengths, 0))
    past_end = jnp.full_like(key_places, 4 * key_places.shape[0])
    key_limits = jnp.where(key_places < valid_length, key_places, past_end)
    attended = attention(
        query_rows_list,
        all_keys,
        all_values,
        own_places,
        key_limits,
        HEAD_DIMENSION ** (-0.5),
    )
    head_partials = jnp.dot(
        attended, output_parts, preferred_element_type=jnp.float32
    ).astype(jnp.bfloat16)
    paired = head_partials.reshape(experts_axis // 2, 2, -1, model_width)
    from_mate = exchange_with_mate(paired)
    own_parity = lax.dynamic_index_in_dim(paired, group_member % 2, 1, keepdims=False)
    chip_sums = (own_parity.astype(jnp.float32) + from_mate.astype(jnp.float32)).astype(jnp.bfloat16)
    owned = scatter_to_chips(chip_sums)
    summed = jnp.sum(owned.astype(jnp.float32), axis=0)
    hidden = (hidden_in.astype(jnp.float32) + summed).astype(jnp.bfloat16)
    normed_second = norm_rows(hidden, norm_experts).astype(jnp.bfloat16)
    logits = jnp.dot(normed_second, router, preferred_element_type=jnp.float32)
    route_table = routes[:, :, None] == jnp.arange(logits.shape[1])[None, None, :]
    picked = jnp.sum(jnp.where(route_table, logits[:, None, :], 0.0), axis=-1)
    raised = jnp.exp(picked)
    gate_values = raised / jnp.sum(raised, axis=1, keepdims=True)
    inside = routes < experts_axis
    gate_window = jnp.sum(jnp.where(inside, gate_values, 0.0), axis=1)
    expert_window = jnp.sum(jnp.where(inside, routes, 0), axis=1)
    present = jnp.any(inside, axis=1)
    capacity = local_rows // (experts_axis * experts_axis)
    member_table = (
        present[:, None] & (expert_window[:, None] == jnp.arange(experts_axis)[None, :])
    ).astype(jnp.int32)
    ranking = jnp.sum(jnp.cumsum(member_table, axis=0) * member_table, axis=1) - 1
    slot_index = expert_window * capacity + ranking
    select = (
        (jnp.arange(experts_axis * capacity)[:, None] == slot_index[None, :]) & present[None, :]
    ).astype(jnp.bfloat16)
    outgoing = (
        jnp.dot(select, normed_second, preferred_element_type=jnp.float32)
        .astype(jnp.bfloat16)
        .reshape(experts_axis, capacity, model_width)
    )
    gateup_here = expert_gateup[0]
    down_here = expert_down[0]
    hidden_units = down_here.shape[0]
    slot_items = scatter_blocks(outgoing, experts_axis, 2)
    flattened = slot_items.reshape(-1, slot_items.shape[-1])
    gate_up = jnp.dot(flattened, gateup_here, preferred_element_type=jnp.float32)
    active = (jax.nn.silu(gate_up[:, :hidden_units]) * gate_up[:, hidden_units:]).astype(
        jnp.bfloat16
    )
    result = (
        jnp.dot(active, down_here, preferred_element_type=jnp.float32)
        .astype(jnp.bfloat16)
        .reshape(slot_items.shape)
    )
    returned = scatter_blocks(result, experts_axis, 3)
    combined = jnp.dot(
        jnp.transpose(select), returned.reshape(-1, model_width), preferred_element_type=jnp.float32
    )
    expert_mix = (gate_window[:, None] * combined).astype(jnp.bfloat16)
    return (hidden, expert_mix)


def solution(mesh):
    return jax.shard_map(
        per_device,
        mesh=mesh,
        in_specs=(
            P(("group", "expert"), None),
            P(),
            P(),
            P("group", "expert"),
            P(None, "group", None),
            P("expert", "group"),
            P(),
            P(),
            P(),
            P(),
            P("expert", None, None),
            P("expert", None, None),
            P(("group", "expert"), None),
        ),
        out_specs=(P(("group", "expert"), None), P(("group", "expert"), None)),
        check_vma=False,
    )
```

```python
import functools
import math

import jax
import numpy as np
import jax.numpy as jnp
from jax import lax
from jax.experimental import pallas as pl
from jax.experimental.pallas import tpu as pltpu
from jax.sharding import PartitionSpec as P

MESH = pl.DeviceIdType.MESH

QUERY_HEADS = 32
KEY_VALUE_HEADS = 4
HEAD_DIMENSION = 128


epsilon = 1e-06
rope_theta = 1000000.0


def from_partner(block, axis, stride):
    count = lax.axis_size(axis)
    route = []
    for low in range(count):
        high = low | 1 << stride
        if high != low and high < count:
            route += [(low, high), (high, low)]
    return lax.ppermute(block, axis, route)


def gather_kernel(n_group, n_expert, wqkv, wo, xn, oqkv, oo, oxn, send, recv, xsend, xrecv, local):
    g = lax.axis_index("group")
    e = lax.axis_index("expert")
    columns = n_group // 2
    z = lax.div(g, 2)
    xh = lax.rem(g, 2)
    zp = lax.rem(z + 1, columns)
    zm = lax.rem(z + columns - 1, columns)
    plus_dev = (2 * zp + xh, e)
    minus_dev = (2 * zm + xh, e)
    pair_dev = (g + 1 - 2 * xh, e)
    core = lax.rem(e, 2)
    chip = lax.div(e, 2)
    chips = n_expert // 2
    mate_dev = (g, e + 1 - 2 * core)
    chip_devs = [(g, 2 * lax.rem(chip + j, chips) + core) for j in range(1, chips)]
    barrier = pltpu.get_barrier_semaphore()
    peers = [plus_dev, minus_dev, pair_dev, mate_dev] + chip_devs
    for dev in peers:
        pl.semaphore_signal(barrier, 1, device_id=dev, device_id_type=MESH)
    pl.semaphore_wait(barrier, len(peers))

    def slot(k, origin):
        return (oqkv, oo)[k].at[origin]

    sends = []

    def push(k, origin, src, dev):
        copy = pltpu.make_async_remote_copy(
            src_ref=src,
            dst_ref=slot(k, origin),
            send_sem=send.at[len(sends)],
            recv_sem=recv.at[k, origin],
            device_id=dev,
            device_id_type=MESH,
        )
        copy.start()
        sends.append(copy)

    def forward(origin, dev):
        for k in range(2):
            push(k, origin, slot(k, origin), dev)

    def arrive(origin):
        for k in range(2):
            pltpu.make_async_remote_copy(
                src_ref=slot(k, origin),
                dst_ref=slot(k, origin),
                send_sem=send.at[0],
                recv_sem=recv.at[k, origin],
                device_id=pair_dev,
                device_id_type=MESH,
            ).wait_recv()

    xsends = []

    def xpush(src, origin, dev):
        copy = pltpu.make_async_remote_copy(
            src_ref=src,
            dst_ref=oxn.at[origin],
            send_sem=xsend.at[len(xsends)],
            recv_sem=xrecv.at[origin],
            device_id=dev,
            device_id_type=MESH,
        )
        copy.start()
        xsends.append(copy)

    def xarrive(origin):
        pltpu.make_async_remote_copy(
            src_ref=oxn.at[origin],
            dst_ref=oxn.at[origin],
            send_sem=xsend.at[0],
            recv_sem=xrecv.at[origin],
            device_id=mate_dev,
            device_id_type=MESH,
        ).wait_recv()

    inputs = (wqkv, wo)
    own = [pltpu.make_async_copy(xn, oxn.at[e], local.at[2])]
    own += [pltpu.make_async_copy(inputs[k], slot(k, g), local.at[k]) for k in range(2)]
    for copy in own:
        copy.start()
    xpush(xn, e, mate_dev)
    for dev in chip_devs:
        xpush(xn, e, dev)
    for dev in (pair_dev, plus_dev, minus_dev):
        for k in range(2):
            push(k, g, inputs[k], dev)
    partner = g + 1 - 2 * xh
    arrive(partner)
    forward(partner, plus_dev)
    forward(partner, minus_dev)
    chip_origins = [2 * lax.rem(chip + j, chips) + core for j in range(1, chips)]
    normed_order = [chip_origins[0:2], chip_origins[2:5], chip_origins[5:]]
    for step in range(1, 4):
        behind = lax.rem(z - step + columns, columns)
        ahead = lax.rem(z + step, columns)
        for origin in (2 * behind, 2 * behind + 1):
            arrive(origin)
        for origin in ((2 * behind, 2 * behind + 1) if step < 3 else (2 * behind,)):
            forward(origin, plus_dev)
        for origin in (2 * ahead, 2 * ahead + 1):
            arrive(origin)
        for origin in ((2 * ahead, 2 * ahead + 1) if step < 3 else (2 * ahead + 1,)):
            forward(origin, minus_dev)
        for origin in normed_order[step - 1]:
            xarrive(origin)
            xpush(oxn.at[origin], origin, mate_dev)
    across = lax.rem(z + columns // 2, columns)
    arrive(2 * across)
    arrive(2 * across + 1)
    mate_core = 1 - core
    xarrive(e + 1 - 2 * core)
    for j in range(1, chips):
        xarrive(2 * lax.rem(chip + j, chips) + mate_core)
    for copy in sends + xsends:
        copy.wait_send()
    for copy in own:
        copy.wait()


def gather_all(wqkv, wo, xn, n_group, n_expert):
    any_spec = pl.BlockSpec(memory_space=pl.ANY)
    shapes = [jax.ShapeDtypeStruct((n_group,) + a.shape, a.dtype) for a in (wqkv, wo)]
    shapes += [jax.ShapeDtypeStruct((n_expert,) + xn.shape, xn.dtype)]
    return pl.pallas_call(
        functools.partial(gather_kernel, n_group, n_expert),
        out_shape=tuple(shapes),
        in_specs=[any_spec] * 3,
        out_specs=tuple([any_spec] * 3),
        scratch_shapes=[
            pltpu.SemaphoreType.DMA((32,)),
            pltpu.SemaphoreType.DMA((2, n_group)),
            pltpu.SemaphoreType.DMA((n_expert,)),
            pltpu.SemaphoreType.DMA((n_expert,)),
            pltpu.SemaphoreType.DMA((3,)),
        ],
        compiler_params=pltpu.CompilerParams(collective_id=0, has_side_effects=True),
    )(wqkv, wo, xn)


def mate_kernel(part, out, send, recv):
    g = lax.axis_index("group")
    e = lax.axis_index("expert")
    core = lax.rem(e, 2)
    mate_dev = (g, e + 1 - 2 * core)
    barrier = pltpu.get_barrier_semaphore()
    pl.semaphore_signal(barrier, 1, device_id=mate_dev, device_id_type=MESH)
    pl.semaphore_wait(barrier, 1)
    copy = pltpu.make_async_remote_copy(
        src_ref=part.at[:, 1 - core],
        dst_ref=out,
        send_sem=send.at[0],
        recv_sem=recv.at[0],
        device_id=mate_dev,
        device_id_type=MESH,
    )
    copy.start()
    copy.wait()


def exchange_with_mate(part):
    any_spec = pl.BlockSpec(memory_space=pl.ANY)
    shape = (part.shape[0],) + part.shape[2:]
    return pl.pallas_call(
        mate_kernel,
        out_shape=jax.ShapeDtypeStruct(shape, part.dtype),
        in_specs=[any_spec],
        out_specs=any_spec,
        scratch_shapes=[pltpu.SemaphoreType.DMA((1,)), pltpu.SemaphoreType.DMA((1,))],
        compiler_params=pltpu.CompilerParams(collective_id=4, has_side_effects=True),
    )(part)


def chip_scatter_kernel(chips, part, out, send, recv, local):
    g = lax.axis_index("group")
    e = lax.axis_index("expert")
    core = lax.rem(e, 2)
    chip = lax.div(e, 2)
    devs = [(g, 2 * lax.rem(chip + j, chips) + core) for j in range(1, chips)]
    barrier = pltpu.get_barrier_semaphore()
    for dev in devs:
        pl.semaphore_signal(barrier, 1, device_id=dev, device_id_type=MESH)
    pl.semaphore_wait(barrier, len(devs))
    copies = []
    for j in range(1, chips):
        copy = pltpu.make_async_remote_copy(
            src_ref=part.at[lax.rem(chip + j, chips)],
            dst_ref=out.at[chip],
            send_sem=send.at[j],
            recv_sem=recv.at[j],
            device_id=devs[j - 1],
            device_id_type=MESH,
        )
        copy.start()
        copies.append(copy)
    own = pltpu.make_async_copy(part.at[chip], out.at[chip], local.at[0])
    own.start()
    for copy in copies:
        copy.wait()
    own.wait()


def scatter_to_chips(part):
    chips = part.shape[0]
    any_spec = pl.BlockSpec(memory_space=pl.ANY)
    return pl.pallas_call(
        functools.partial(chip_scatter_kernel, chips),
        out_shape=jax.ShapeDtypeStruct(part.shape, part.dtype),
        in_specs=[any_spec],
        out_specs=any_spec,
        scratch_shapes=[
            pltpu.SemaphoreType.DMA((chips,)),
            pltpu.SemaphoreType.DMA((chips,)),
            pltpu.SemaphoreType.DMA((1,)),
        ],
        compiler_params=pltpu.CompilerParams(collective_id=5, has_side_effects=True),
    )(part)


def scatter_kernel(n_expert, part, out, send, recv, local):
    g = lax.axis_index("group")
    e = lax.axis_index("expert")
    barrier = pltpu.get_barrier_semaphore()
    for j in range(1, n_expert):
        pl.semaphore_signal(barrier, 1, device_id=(g, lax.rem(e + j, n_expert)), device_id_type=MESH)
    pl.semaphore_wait(barrier, n_expert - 1)
    copies = []
    for j in range(1, n_expert):
        peer = lax.rem(e + j, n_expert)
        copy = pltpu.make_async_remote_copy(
            src_ref=part.at[peer],
            dst_ref=out.at[e],
            send_sem=send.at[j],
            recv_sem=recv.at[j],
            device_id=(g, peer),
            device_id_type=MESH,
        )
        copy.start()
        copies.append(copy)
    own = pltpu.make_async_copy(part.at[e], out.at[e], local.at[0])
    own.start()
    for copy in copies:
        copy.wait()
    own.wait()


def scatter_blocks(part, n_expert, collective_id):
    any_spec = pl.BlockSpec(memory_space=pl.ANY)
    return pl.pallas_call(
        functools.partial(scatter_kernel, n_expert),
        out_shape=jax.ShapeDtypeStruct(part.shape, part.dtype),
        in_specs=[any_spec],
        out_specs=any_spec,
        scratch_shapes=[
            pltpu.SemaphoreType.DMA((n_expert,)),
            pltpu.SemaphoreType.DMA((n_expert,)),
            pltpu.SemaphoreType.DMA((1,)),
        ],
        compiler_params=pltpu.CompilerParams(collective_id=collective_id, has_side_effects=True),
    )(part)


def attention_kernel(scale, heads, q_ref, k_ref, v_ref, qpos_ref, kpos_ref, o_ref):
    allowed = kpos_ref[...] <= qpos_ref[...]
    keys = k_ref[...]
    values = v_ref[...]
    depth = keys.shape[1]
    for h in range(heads):
        query = q_ref[:, h * depth : (h + 1) * depth]
        scores = (
            lax.dot_general(
                query, keys, (((1,), (1,)), ((), ())), preferred_element_type=jnp.float32
            )
            * scale
        )
        weights = jnp.where(allowed, jnp.exp(scores), 0.0)
        denominators = jnp.sum(weights, axis=-1, keepdims=True)
        weighted = jnp.dot(
            weights.astype(jnp.bfloat16), values, preferred_element_type=jnp.float32
        )
        o_ref[:, h * depth : (h + 1) * depth] = (weighted / denominators).astype(o_ref.dtype)


def attention(queries, keys, values, query_places, key_places, scale):
    rows, width = queries.shape
    key_rows, depth = keys.shape
    block = min(256, rows)
    return pl.pallas_call(
        functools.partial(attention_kernel, scale, width // depth),
        out_shape=jax.ShapeDtypeStruct((rows, width), jnp.bfloat16),
        grid=(rows // block,),
        in_specs=[
            pl.BlockSpec((block, width), lambda i: (i, 0)),
            pl.BlockSpec((key_rows, depth), lambda i: (0, 0)),
            pl.BlockSpec((key_rows, depth), lambda i: (0, 0)),
            pl.BlockSpec((block, 1), lambda i: (i, 0)),
            pl.BlockSpec((1, key_rows), lambda i: (0, 0)),
        ],
        out_specs=pl.BlockSpec((block, width), lambda i: (i, 0)),
        cost_estimate=pl.CostEstimate(
            flops=4 * rows * key_rows * width,
            transcendentals=rows * key_rows * (width // depth),
            bytes_accessed=2 * (2 * rows * width + 2 * key_rows * depth),
        ),
    )(queries, keys, values, query_places.reshape(rows, 1), key_places.reshape(1, key_rows))


def norm_rows(values, gain_vector):
    widened = values.astype(jnp.float32)
    inverse_rms = lax.rsqrt(jnp.mean(widened * widened, axis=-1, keepdims=True) + epsilon)
    return widened * inverse_rms * gain_vector


def rotate(values, positions):
    half_width = values.shape[-1] // 2
    exponents = jnp.arange(half_width).astype(jnp.float32)
    inverse = jnp.exp(exponents * (-2.0 * math.log(rope_theta) / values.shape[-1]))
    angles = positions[:, None, None] * inverse[None, None, :]
    cosine_values = jnp.cos(angles)
    sine_values = jnp.sin(angles)
    first_half = values[..., :half_width]
    second = values[..., half_width:]
    return jnp.concatenate(
        [
            first_half * cosine_values - second * sine_values,
            second * cosine_values + first_half * sine_values,
        ],
        axis=-1,
    )


def local_positions(parity, row_count):
    indices = jnp.arange(row_count)
    quarter = row_count // 2
    offset = jnp.where(parity == 0, jnp.where(indices < quarter, 0, 2 * quarter), quarter)
    return indices + offset


def prep_kernel(query_width, x_ref, w_ref, cos_ref, sin_ref, qg_ref, kg_ref, q_out, k_out, v_out):
    x = x_ref[...]
    cosines = cos_ref[...]
    sines = sin_ref[...]
    depth = cosines.shape[1]

    def project(start, stop):
        return jnp.dot(x, w_ref[:, start:stop], preferred_element_type=jnp.float32).astype(jnp.bfloat16)

    def norm_rope(values, gain):
        values = values.astype(jnp.float32)
        inverse_rms = lax.rsqrt(jnp.mean(values * values, axis=-1, keepdims=True) + epsilon)
        normed = values * inverse_rms * gain
        return (normed * cosines + pltpu.roll(normed, depth // 2, 1) * sines).astype(jnp.bfloat16)

    queries = project(0, query_width)
    for h in range(queries.shape[1] // depth):
        q_out[:, h * depth : (h + 1) * depth] = norm_rope(
            queries[:, h * depth : (h + 1) * depth], qg_ref[...]
        )
    k_out[...] = norm_rope(project(query_width, query_width + depth), kg_ref[...])
    v_out[...] = project(query_width + depth, query_width + 2 * depth)


def prep(normed_rows, joined, cosines, sines, query_gain, key_gain):
    rows, width = normed_rows.shape
    depth = cosines.shape[1]
    query_width = joined.shape[1] - 2 * depth
    block = min(256, rows)
    whole = lambda shape: pl.BlockSpec(shape, lambda i: (0, 0))
    per_row = lambda cols: pl.BlockSpec((block, cols), lambda i: (i, 0))
    return pl.pallas_call(
        functools.partial(prep_kernel, query_width),
        out_shape=(
            jax.ShapeDtypeStruct((rows, query_width), jnp.bfloat16),
            jax.ShapeDtypeStruct((rows, depth), jnp.bfloat16),
            jax.ShapeDtypeStruct((rows, depth), jnp.bfloat16),
        ),
        grid=(rows // block,),
        in_specs=[
            per_row(width),
            whole(joined.shape),
            per_row(depth),
            per_row(depth),
            whole((1, depth)),
            whole((1, depth)),
        ],
        out_specs=(per_row(query_width), per_row(depth), per_row(depth)),
        cost_estimate=pl.CostEstimate(
            flops=2 * rows * width * joined.shape[1],
            transcendentals=rows * (query_width // depth + 1),
            bytes_accessed=2 * (rows * width + width * joined.shape[1] + rows * joined.shape[1]),
        ),
    )(normed_rows, joined, cosines, sines, query_gain.reshape(1, depth), key_gain.reshape(1, depth))


def rope_tables(parity, row_count, depth):
    half = depth // 2
    frequencies = rope_theta ** (-2.0 * np.arange(half) / depth)
    indices = np.arange(row_count)
    quarter = row_count // 2
    places = np.concatenate([np.where(indices < quarter, indices, indices + 2 * quarter), indices + quarter])
    angles = places[:, None].astype(np.float64) * frequencies[None, :]
    cosines = jnp.asarray(np.cos(angles), jnp.float32)
    sines = jnp.asarray(np.sin(angles), jnp.float32)
    cosines = lax.dynamic_slice_in_dim(cosines, parity * row_count, row_count, 0)
    sines = lax.dynamic_slice_in_dim(sines, parity * row_count, row_count, 0)
    return (
        jnp.concatenate([cosines, cosines], axis=1),
        jnp.concatenate([-sines, sines], axis=1),
    )


def per_device(
    hidden_in,
    norm_attention,
    norm_experts,
    query_master,
    trainer_key_value_weight,
    output_master,
    query_gain,
    key_gain,
    lengths,
    router,
    expert_gateup,
    expert_down,
    routes,
):
    experts_axis = lax.axis_size("expert")
    group_member = lax.axis_index("expert")
    group_index = lax.axis_index("group")
    local_head_count = QUERY_HEADS // experts_axis
    width_here = local_head_count * HEAD_DIMENSION
    common_head = group_member * local_head_count // (QUERY_HEADS // KEY_VALUE_HEADS)
    groups_axis = lax.axis_size("group")
    keyvalue_slice = lax.dynamic_slice_in_dim(
        trainer_key_value_weight, common_head * HEAD_DIMENSION, HEAD_DIMENSION, 2
    ).astype(jnp.bfloat16)
    normed = norm_rows(hidden_in, norm_attention).astype(jnp.bfloat16)
    joined_parts, output_parts, normed_parts = gather_all(
        jnp.concatenate(
            [query_master.astype(jnp.bfloat16), keyvalue_slice[0], keyvalue_slice[1]], axis=1
        ),
        output_master.astype(jnp.bfloat16),
        normed,
        groups_axis,
        experts_axis,
    )
    model_width = hidden_in.shape[1]
    local_rows = normed_parts.shape[0] * normed_parts.shape[1]
    parity = group_index % 2
    own_places = local_positions(parity, local_rows)
    partner_places = local_positions(1 - parity, local_rows)
    cosines, sines = rope_tables(parity, local_rows, HEAD_DIMENSION)
    query_rows_list, key_rows, value_rows = prep(
        normed_parts.reshape(local_rows, model_width),
        joined_parts.reshape(model_width, -1),
        cosines,
        sines,
        query_gain,
        key_gain,
    )
    partner = from_partner(jnp.stack([key_rows, value_rows]), "group", 0)
    all_keys = jnp.concatenate([key_rows, partner[0]], axis=0)
    all_values = jnp.concatenate([value_rows, partner[1]], axis=0)
    key_places = jnp.concatenate([own_places, partner_places])
    valid_length = jnp.sum(jnp.where(jnp.arange(lengths.shape[0]) == group_index // 2, lengths, 0))
    past_end = jnp.full_like(key_places, 4 * key_places.shape[0])
    key_limits = jnp.where(key_places < valid_length, key_places, past_end)
    attended = attention(
        query_rows_list,
        all_keys,
        all_values,
        own_places,
        key_limits,
        HEAD_DIMENSION ** (-0.5),
    )
    output_weight = jnp.transpose(output_parts, (1, 0, 2)).reshape(output_parts.shape[1], -1)
    head_partials = jnp.dot(
        attended, output_weight, preferred_element_type=jnp.float32
    ).astype(jnp.bfloat16)
    paired = head_partials.reshape(experts_axis // 2, 2, -1, model_width)
    from_mate = exchange_with_mate(paired)
    own_parity = lax.dynamic_index_in_dim(paired, group_member % 2, 1, keepdims=False)
    chip_sums = (own_parity.astype(jnp.float32) + from_mate.astype(jnp.float32)).astype(jnp.bfloat16)
    owned = scatter_to_chips(chip_sums)
    summed = jnp.sum(owned.astype(jnp.float32), axis=0)
    hidden = (hidden_in.astype(jnp.float32) + summed).astype(jnp.bfloat16)
    normed_second = norm_rows(hidden, norm_experts).astype(jnp.bfloat16)
    logits = jnp.dot(normed_second, router, preferred_element_type=jnp.float32)
    route_table = routes[:, :, None] == jnp.arange(logits.shape[1])[None, None, :]
    picked = jnp.sum(jnp.where(route_table, logits[:, None, :], 0.0), axis=-1)
    raised = jnp.exp(picked)
    gate_values = raised / jnp.sum(raised, axis=1, keepdims=True)
    inside = routes < experts_axis
    gate_window = jnp.sum(jnp.where(inside, gate_values, 0.0), axis=1)
    expert_window = jnp.sum(jnp.where(inside, routes, 0), axis=1)
    present = jnp.any(inside, axis=1)
    capacity = local_rows // (experts_axis * experts_axis)
    member_table = (
        present[:, None] & (expert_window[:, None] == jnp.arange(experts_axis)[None, :])
    ).astype(jnp.int32)
    ranking = jnp.sum(jnp.cumsum(member_table, axis=0) * member_table, axis=1) - 1
    slot_index = expert_window * capacity + ranking
    select = (
        (jnp.arange(experts_axis * capacity)[:, None] == slot_index[None, :]) & present[None, :]
    ).astype(jnp.bfloat16)
    outgoing = (
        jnp.dot(select, normed_second, preferred_element_type=jnp.float32)
        .astype(jnp.bfloat16)
        .reshape(experts_axis, capacity, model_width)
    )
    gateup_here = expert_gateup[0]
    down_here = expert_down[0]
    hidden_units = down_here.shape[0]
    slot_items = scatter_blocks(outgoing, experts_axis, 2)
    flattened = slot_items.reshape(-1, slot_items.shape[-1])
    gate_up = jnp.dot(flattened, gateup_here, preferred_element_type=jnp.float32)
    active = (jax.nn.silu(gate_up[:, :hidden_units]) * gate_up[:, hidden_units:]).astype(
        jnp.bfloat16
    )
    result = (
        jnp.dot(active, down_here, preferred_element_type=jnp.float32)
        .astype(jnp.bfloat16)
        .reshape(slot_items.shape)
    )
    returned = scatter_blocks(result, experts_axis, 3)
    combined = jnp.dot(
        jnp.transpose(select), returned.reshape(-1, model_width), preferred_element_type=jnp.float32
    )
    expert_mix = (gate_window[:, None] * combined).astype(jnp.bfloat16)
    return (hidden, expert_mix)


def solution(mesh):
    return jax.shard_map(
        per_device,
        mesh=mesh,
        in_specs=(
            P(("group", "expert"), None),
            P(),
            P(),
            P("group", "expert"),
            P(None, "group", None),
            P("expert", "group"),
            P(),
            P(),
            P(),
            P(),
            P("expert", None, None),
            P("expert", None, None),
            P(("group", "expert"), None),
        ),
        out_specs=(P(("group", "expert"), None), P(("group", "expert"), None)),
        check_vma=False,
    )
```

```python
import functools
import math

import jax
import numpy as np
import jax.numpy as jnp
from jax import lax
from jax.experimental import pallas as pl
from jax.experimental.pallas import tpu as pltpu
from jax.sharding import PartitionSpec as P

MESH = pl.DeviceIdType.MESH

QUERY_HEADS = 32
KEY_VALUE_HEADS = 4
HEAD_DIMENSION = 128


epsilon = 1e-06
rope_theta = 1000000.0


def from_partner(block, axis, stride):
    count = lax.axis_size(axis)
    route = []
    for low in range(count):
        high = low | 1 << stride
        if high != low and high < count:
            route += [(low, high), (high, low)]
    return lax.ppermute(block, axis, route)


def gather_kernel(n_group, n_expert, wqkv, wo, xn, oqkv, oo, oxn, send, recv, xsend, xrecv, local):
    g = lax.axis_index("group")
    e = lax.axis_index("expert")
    columns = n_group // 2
    z = lax.div(g, 2)
    xh = lax.rem(g, 2)
    zp = lax.rem(z + 1, columns)
    zm = lax.rem(z + columns - 1, columns)
    plus_dev = (2 * zp + xh, e)
    minus_dev = (2 * zm + xh, e)
    pair_dev = (g + 1 - 2 * xh, e)
    core = lax.rem(e, 2)
    chip = lax.div(e, 2)
    chips = n_expert // 2
    mate_dev = (g, e + 1 - 2 * core)
    chip_devs = [(g, 2 * lax.rem(chip + j, chips) + core) for j in range(1, chips)]
    barrier = pltpu.get_barrier_semaphore()
    peers = [plus_dev, minus_dev, pair_dev, mate_dev] + chip_devs
    for dev in peers:
        pl.semaphore_signal(barrier, 1, device_id=dev, device_id_type=MESH)
    pl.semaphore_wait(barrier, len(peers))

    def slot(k, origin):
        return (oqkv, oo)[k].at[origin]

    sends = []

    def push(k, origin, src, dev):
        copy = pltpu.make_async_remote_copy(
            src_ref=src,
            dst_ref=slot(k, origin),
            send_sem=send.at[len(sends)],
            recv_sem=recv.at[k, origin],
            device_id=dev,
            device_id_type=MESH,
        )
        copy.start()
        sends.append(copy)

    def forward(origin, dev):
        for k in range(2):
            push(k, origin, slot(k, origin), dev)

    def arrive(origin):
        for k in range(2):
            pltpu.make_async_remote_copy(
                src_ref=slot(k, origin),
                dst_ref=slot(k, origin),
                send_sem=send.at[0],
                recv_sem=recv.at[k, origin],
                device_id=pair_dev,
                device_id_type=MESH,
            ).wait_recv()

    xsends = []

    def xpush(src, origin, dev):
        copy = pltpu.make_async_remote_copy(
            src_ref=src,
            dst_ref=oxn.at[origin],
            send_sem=xsend.at[len(xsends)],
            recv_sem=xrecv.at[origin],
            device_id=dev,
            device_id_type=MESH,
        )
        copy.start()
        xsends.append(copy)

    def xarrive(origin):
        pltpu.make_async_remote_copy(
            src_ref=oxn.at[origin],
            dst_ref=oxn.at[origin],
            send_sem=xsend.at[0],
            recv_sem=xrecv.at[origin],
            device_id=mate_dev,
            device_id_type=MESH,
        ).wait_recv()

    inputs = (wqkv, wo)
    own = [pltpu.make_async_copy(xn, oxn.at[e], local.at[2])]
    own += [pltpu.make_async_copy(inputs[k], slot(k, g), local.at[k]) for k in range(2)]
    for copy in own:
        copy.start()
    xpush(xn, e, mate_dev)
    for dev in chip_devs:
        xpush(xn, e, dev)
    for dev in (pair_dev, plus_dev, minus_dev):
        for k in range(2):
            push(k, g, inputs[k], dev)
    partner = g + 1 - 2 * xh
    arrive(partner)
    forward(partner, plus_dev)
    forward(partner, minus_dev)
    chip_origins = [2 * lax.rem(chip + j, chips) + core for j in range(1, chips)]
    normed_order = [chip_origins[0:2], chip_origins[2:5], chip_origins[5:]]
    for step in range(1, 4):
        behind = lax.rem(z - step + columns, columns)
        ahead = lax.rem(z + step, columns)
        for origin in (2 * behind, 2 * behind + 1):
            arrive(origin)
        for origin in ((2 * behind, 2 * behind + 1) if step < 3 else (2 * behind,)):
            forward(origin, plus_dev)
        for origin in (2 * ahead, 2 * ahead + 1):
            arrive(origin)
        for origin in ((2 * ahead, 2 * ahead + 1) if step < 3 else (2 * ahead + 1,)):
            forward(origin, minus_dev)
        for origin in normed_order[step - 1]:
            xarrive(origin)
            xpush(oxn.at[origin], origin, mate_dev)
    across = lax.rem(z + columns // 2, columns)
    arrive(2 * across)
    arrive(2 * across + 1)
    mate_core = 1 - core
    xarrive(e + 1 - 2 * core)
    for j in range(1, chips):
        xarrive(2 * lax.rem(chip + j, chips) + mate_core)
    for copy in sends + xsends:
        copy.wait_send()
    for copy in own:
        copy.wait()


def gather_all(wqkv, wo, xn, n_group, n_expert):
    any_spec = pl.BlockSpec(memory_space=pl.ANY)
    shapes = [jax.ShapeDtypeStruct((n_group,) + a.shape, a.dtype) for a in (wqkv, wo)]
    shapes += [jax.ShapeDtypeStruct((n_expert,) + xn.shape, xn.dtype)]
    return pl.pallas_call(
        functools.partial(gather_kernel, n_group, n_expert),
        out_shape=tuple(shapes),
        in_specs=[any_spec] * 3,
        out_specs=tuple([any_spec] * 3),
        scratch_shapes=[
            pltpu.SemaphoreType.DMA((32,)),
            pltpu.SemaphoreType.DMA((2, n_group)),
            pltpu.SemaphoreType.DMA((n_expert,)),
            pltpu.SemaphoreType.DMA((n_expert,)),
            pltpu.SemaphoreType.DMA((3,)),
        ],
        compiler_params=pltpu.CompilerParams(collective_id=0, has_side_effects=True),
    )(wqkv, wo, xn)


def combine_kernel(blocks, attended_ref, weight_ref, out_ref, outgoing, incoming, send, recv):
    g = lax.axis_index("group")
    e = lax.axis_index("expert")
    core = lax.rem(e, 2)
    mate_dev = (g, e + 1 - 2 * core)
    rows = out_ref.shape[1]
    barrier = pltpu.get_barrier_semaphore()
    pl.semaphore_signal(barrier, 1, device_id=mate_dev, device_id_type=MESH)
    pl.semaphore_wait(barrier, 1)

    def partial(block):
        start = pl.multiple_of(block * rows, rows)
        return jnp.dot(
            attended_ref[pl.ds(start, rows), :], weight_ref[...], preferred_element_type=jnp.float32
        ).astype(jnp.bfloat16)

    for i in range(blocks):
        outgoing[i] = partial(2 * i + 1 - core)
    copy = pltpu.make_async_remote_copy(
        src_ref=outgoing,
        dst_ref=incoming,
        send_sem=send.at[0],
        recv_sem=recv.at[0],
        device_id=mate_dev,
        device_id_type=MESH,
    )
    copy.start()
    for i in range(blocks):
        out_ref[i] = partial(2 * i + core)
    copy.wait()
    for i in range(blocks):
        out_ref[i] = (out_ref[i].astype(jnp.float32) + incoming[i].astype(jnp.float32)).astype(
            jnp.bfloat16
        )


def project_and_combine(attended, weight, experts_axis):
    rows = attended.shape[0] // experts_axis
    blocks = experts_axis // 2
    shape = (blocks, rows, weight.shape[1])
    vmem = pl.BlockSpec(memory_space=pltpu.VMEM)
    return pl.pallas_call(
        functools.partial(combine_kernel, blocks),
        out_shape=jax.ShapeDtypeStruct(shape, jnp.bfloat16),
        in_specs=[vmem, vmem],
        out_specs=vmem,
        scratch_shapes=[
            pltpu.VMEM(shape, jnp.bfloat16),
            pltpu.VMEM(shape, jnp.bfloat16),
            pltpu.SemaphoreType.DMA((1,)),
            pltpu.SemaphoreType.DMA((1,)),
        ],
        compiler_params=pltpu.CompilerParams(collective_id=4, has_side_effects=True),
    )(attended, weight)


def mate_kernel(part, out, send, recv):
    g = lax.axis_index("group")
    e = lax.axis_index("expert")
    core = lax.rem(e, 2)
    mate_dev = (g, e + 1 - 2 * core)
    barrier = pltpu.get_barrier_semaphore()
    pl.semaphore_signal(barrier, 1, device_id=mate_dev, device_id_type=MESH)
    pl.semaphore_wait(barrier, 1)
    copy = pltpu.make_async_remote_copy(
        src_ref=part.at[:, 1 - core],
        dst_ref=out,
        send_sem=send.at[0],
        recv_sem=recv.at[0],
        device_id=mate_dev,
        device_id_type=MESH,
    )
    copy.start()
    copy.wait()


def exchange_with_mate(part):
    any_spec = pl.BlockSpec(memory_space=pl.ANY)
    shape = (part.shape[0],) + part.shape[2:]
    return pl.pallas_call(
        mate_kernel,
        out_shape=jax.ShapeDtypeStruct(shape, part.dtype),
        in_specs=[any_spec],
        out_specs=any_spec,
        scratch_shapes=[pltpu.SemaphoreType.DMA((1,)), pltpu.SemaphoreType.DMA((1,))],
        compiler_params=pltpu.CompilerParams(collective_id=4, has_side_effects=True),
    )(part)


def chip_scatter_kernel(chips, part, out, send, recv, local):
    g = lax.axis_index("group")
    e = lax.axis_index("expert")
    core = lax.rem(e, 2)
    chip = lax.div(e, 2)
    devs = [(g, 2 * lax.rem(chip + j, chips) + core) for j in range(1, chips)]
    barrier = pltpu.get_barrier_semaphore()
    for dev in devs:
        pl.semaphore_signal(barrier, 1, device_id=dev, device_id_type=MESH)
    pl.semaphore_wait(barrier, len(devs))
    copies = []
    for j in range(1, chips):
        copy = pltpu.make_async_remote_copy(
            src_ref=part.at[lax.rem(chip + j, chips)],
            dst_ref=out.at[chip],
            send_sem=send.at[j],
            recv_sem=recv.at[j],
            device_id=devs[j - 1],
            device_id_type=MESH,
        )
        copy.start()
        copies.append(copy)
    own = pltpu.make_async_copy(part.at[chip], out.at[chip], local.at[0])
    own.start()
    for copy in copies:
        copy.wait()
    own.wait()


def scatter_to_chips(part):
    chips = part.shape[0]
    any_spec = pl.BlockSpec(memory_space=pl.ANY)
    return pl.pallas_call(
        functools.partial(chip_scatter_kernel, chips),
        out_shape=jax.ShapeDtypeStruct(part.shape, part.dtype),
        in_specs=[any_spec],
        out_specs=any_spec,
        scratch_shapes=[
            pltpu.SemaphoreType.DMA((chips,)),
            pltpu.SemaphoreType.DMA((chips,)),
            pltpu.SemaphoreType.DMA((1,)),
        ],
        compiler_params=pltpu.CompilerParams(collective_id=5, has_side_effects=True),
    )(part)


def scatter_kernel(n_expert, part, out, send, recv, local):
    g = lax.axis_index("group")
    e = lax.axis_index("expert")
    barrier = pltpu.get_barrier_semaphore()
    for j in range(1, n_expert):
        pl.semaphore_signal(barrier, 1, device_id=(g, lax.rem(e + j, n_expert)), device_id_type=MESH)
    pl.semaphore_wait(barrier, n_expert - 1)
    copies = []
    for j in range(1, n_expert):
        peer = lax.rem(e + j, n_expert)
        copy = pltpu.make_async_remote_copy(
            src_ref=part.at[peer],
            dst_ref=out.at[e],
            send_sem=send.at[j],
            recv_sem=recv.at[j],
            device_id=(g, peer),
            device_id_type=MESH,
        )
        copy.start()
        copies.append(copy)
    own = pltpu.make_async_copy(part.at[e], out.at[e], local.at[0])
    own.start()
    for copy in copies:
        copy.wait()
    own.wait()


def scatter_blocks(part, n_expert, collective_id):
    any_spec = pl.BlockSpec(memory_space=pl.ANY)
    return pl.pallas_call(
        functools.partial(scatter_kernel, n_expert),
        out_shape=jax.ShapeDtypeStruct(part.shape, part.dtype),
        in_specs=[any_spec],
        out_specs=any_spec,
        scratch_shapes=[
            pltpu.SemaphoreType.DMA((n_expert,)),
            pltpu.SemaphoreType.DMA((n_expert,)),
            pltpu.SemaphoreType.DMA((1,)),
        ],
        compiler_params=pltpu.CompilerParams(collective_id=collective_id, has_side_effects=True),
    )(part)


def attention_kernel(scale, heads, q_ref, k_ref, v_ref, qpos_ref, kpos_ref, o_ref):
    allowed = kpos_ref[...] <= qpos_ref[...]
    keys = k_ref[...]
    values = v_ref[...]
    depth = keys.shape[1]
    for h in range(heads):
        query = q_ref[:, h * depth : (h + 1) * depth]
        scores = (
            lax.dot_general(
                query, keys, (((1,), (1,)), ((), ())), preferred_element_type=jnp.float32
            )
            * scale
        )
        weights = jnp.where(allowed, jnp.exp(scores), 0.0)
        denominators = jnp.sum(weights, axis=-1, keepdims=True)
        weighted = jnp.dot(
            weights.astype(jnp.bfloat16), values, preferred_element_type=jnp.float32
        )
        o_ref[:, h * depth : (h + 1) * depth] = (weighted / denominators).astype(o_ref.dtype)


def attention(queries, keys, values, query_places, key_places, scale):
    rows, width = queries.shape
    key_rows, depth = keys.shape
    block = min(256, rows)
    return pl.pallas_call(
        functools.partial(attention_kernel, scale, width // depth),
        out_shape=jax.ShapeDtypeStruct((rows, width), jnp.bfloat16),
        grid=(rows // block,),
        in_specs=[
            pl.BlockSpec((block, width), lambda i: (i, 0)),
            pl.BlockSpec((key_rows, depth), lambda i: (0, 0)),
            pl.BlockSpec((key_rows, depth), lambda i: (0, 0)),
            pl.BlockSpec((block, 1), lambda i: (i, 0)),
            pl.BlockSpec((1, key_rows), lambda i: (0, 0)),
        ],
        out_specs=pl.BlockSpec((block, width), lambda i: (i, 0)),
        cost_estimate=pl.CostEstimate(
            flops=4 * rows * key_rows * width,
            transcendentals=rows * key_rows * (width // depth),
            bytes_accessed=2 * (2 * rows * width + 2 * key_rows * depth),
        ),
    )(queries, keys, values, query_places.reshape(rows, 1), key_places.reshape(1, key_rows))


def norm_rows(values, gain_vector):
    widened = values.astype(jnp.float32)
    inverse_rms = lax.rsqrt(jnp.mean(widened * widened, axis=-1, keepdims=True) + epsilon)
    return widened * inverse_rms * gain_vector


def rotate(values, positions):
    half_width = values.shape[-1] // 2
    exponents = jnp.arange(half_width).astype(jnp.float32)
    inverse = jnp.exp(exponents * (-2.0 * math.log(rope_theta) / values.shape[-1]))
    angles = positions[:, None, None] * inverse[None, None, :]
    cosine_values = jnp.cos(angles)
    sine_values = jnp.sin(angles)
    first_half = values[..., :half_width]
    second = values[..., half_width:]
    return jnp.concatenate(
        [
            first_half * cosine_values - second * sine_values,
            second * cosine_values + first_half * sine_values,
        ],
        axis=-1,
    )


def local_positions(parity, row_count):
    indices = jnp.arange(row_count)
    quarter = row_count // 2
    offset = jnp.where(parity == 0, jnp.where(indices < quarter, 0, 2 * quarter), quarter)
    return indices + offset


def prep_kernel(query_width, x_ref, w_ref, cos_ref, sin_ref, qg_ref, kg_ref, q_out, k_out, v_out):
    x = x_ref[...]
    cosines = cos_ref[...]
    sines = sin_ref[...]
    depth = cosines.shape[1]

    def project(start, stop):
        return jnp.dot(x, w_ref[:, start:stop], preferred_element_type=jnp.float32).astype(jnp.bfloat16)

    def norm_rope(values, gain):
        values = values.astype(jnp.float32)
        inverse_rms = lax.rsqrt(jnp.mean(values * values, axis=-1, keepdims=True) + epsilon)
        normed = values * inverse_rms * gain
        return (normed * cosines + pltpu.roll(normed, depth // 2, 1) * sines).astype(jnp.bfloat16)

    queries = project(0, query_width)
    for h in range(queries.shape[1] // depth):
        q_out[:, h * depth : (h + 1) * depth] = norm_rope(
            queries[:, h * depth : (h + 1) * depth], qg_ref[...]
        )
    k_out[...] = norm_rope(project(query_width, query_width + depth), kg_ref[...])
    v_out[...] = project(query_width + depth, query_width + 2 * depth)


def prep(normed_rows, joined, cosines, sines, query_gain, key_gain):
    rows, width = normed_rows.shape
    depth = cosines.shape[1]
    query_width = joined.shape[1] - 2 * depth
    block = min(256, rows)
    whole = lambda shape: pl.BlockSpec(shape, lambda i: (0, 0))
    per_row = lambda cols: pl.BlockSpec((block, cols), lambda i: (i, 0))
    return pl.pallas_call(
        functools.partial(prep_kernel, query_width),
        out_shape=(
            jax.ShapeDtypeStruct((rows, query_width), jnp.bfloat16),
            jax.ShapeDtypeStruct((rows, depth), jnp.bfloat16),
            jax.ShapeDtypeStruct((rows, depth), jnp.bfloat16),
        ),
        grid=(rows // block,),
        in_specs=[
            per_row(width),
            whole(joined.shape),
            per_row(depth),
            per_row(depth),
            whole((1, depth)),
            whole((1, depth)),
        ],
        out_specs=(per_row(query_width), per_row(depth), per_row(depth)),
        cost_estimate=pl.CostEstimate(
            flops=2 * rows * width * joined.shape[1],
            transcendentals=rows * (query_width // depth + 1),
            bytes_accessed=2 * (rows * width + width * joined.shape[1] + rows * joined.shape[1]),
        ),
    )(normed_rows, joined, cosines, sines, query_gain.reshape(1, depth), key_gain.reshape(1, depth))


def rope_tables(parity, row_count, depth):
    half = depth // 2
    frequencies = rope_theta ** (-2.0 * np.arange(half) / depth)
    indices = np.arange(row_count)
    quarter = row_count // 2
    places = np.concatenate([np.where(indices < quarter, indices, indices + 2 * quarter), indices + quarter])
    angles = places[:, None].astype(np.float64) * frequencies[None, :]
    cosines = jnp.asarray(np.cos(angles), jnp.float32)
    sines = jnp.asarray(np.sin(angles), jnp.float32)
    cosines = lax.dynamic_slice_in_dim(cosines, parity * row_count, row_count, 0)
    sines = lax.dynamic_slice_in_dim(sines, parity * row_count, row_count, 0)
    return (
        jnp.concatenate([cosines, cosines], axis=1),
        jnp.concatenate([-sines, sines], axis=1),
    )


def per_device(
    hidden_in,
    norm_attention,
    norm_experts,
    query_master,
    trainer_key_value_weight,
    output_master,
    query_gain,
    key_gain,
    lengths,
    router,
    expert_gateup,
    expert_down,
    routes,
):
    experts_axis = lax.axis_size("expert")
    group_member = lax.axis_index("expert")
    group_index = lax.axis_index("group")
    local_head_count = QUERY_HEADS // experts_axis
    width_here = local_head_count * HEAD_DIMENSION
    common_head = group_member * local_head_count // (QUERY_HEADS // KEY_VALUE_HEADS)
    groups_axis = lax.axis_size("group")
    keyvalue_slice = lax.dynamic_slice_in_dim(
        trainer_key_value_weight, common_head * HEAD_DIMENSION, HEAD_DIMENSION, 2
    ).astype(jnp.bfloat16)
    normed = norm_rows(hidden_in, norm_attention).astype(jnp.bfloat16)
    joined_parts, output_parts, normed_parts = gather_all(
        jnp.concatenate(
            [query_master.astype(jnp.bfloat16), keyvalue_slice[0], keyvalue_slice[1]], axis=1
        ),
        output_master.astype(jnp.bfloat16),
        normed,
        groups_axis,
        experts_axis,
    )
    model_width = hidden_in.shape[1]
    local_rows = normed_parts.shape[0] * normed_parts.shape[1]
    parity = group_index % 2
    own_places = local_positions(parity, local_rows)
    partner_places = local_positions(1 - parity, local_rows)
    cosines, sines = rope_tables(parity, local_rows, HEAD_DIMENSION)
    query_rows_list, key_rows, value_rows = prep(
        normed_parts.reshape(local_rows, model_width),
        joined_parts.reshape(model_width, -1),
        cosines,
        sines,
        query_gain,
        key_gain,
    )
    partner = from_partner(jnp.stack([key_rows, value_rows]), "group", 0)
    all_keys = jnp.concatenate([key_rows, partner[0]], axis=0)
    all_values = jnp.concatenate([value_rows, partner[1]], axis=0)
    key_places = jnp.concatenate([own_places, partner_places])
    valid_length = jnp.sum(jnp.where(jnp.arange(lengths.shape[0]) == group_index // 2, lengths, 0))
    past_end = jnp.full_like(key_places, 4 * key_places.shape[0])
    key_limits = jnp.where(key_places < valid_length, key_places, past_end)
    attended = attention(
        query_rows_list,
        all_keys,
        all_values,
        own_places,
        key_limits,
        HEAD_DIMENSION ** (-0.5),
    )
    output_weight = jnp.transpose(output_parts, (1, 0, 2)).reshape(output_parts.shape[1], -1)
    chip_sums = project_and_combine(attended, output_weight, experts_axis)
    owned = scatter_to_chips(chip_sums)
    summed = jnp.sum(owned.astype(jnp.float32), axis=0)
    hidden = (hidden_in.astype(jnp.float32) + summed).astype(jnp.bfloat16)
    normed_second = norm_rows(hidden, norm_experts).astype(jnp.bfloat16)
    logits = jnp.dot(normed_second, router, preferred_element_type=jnp.float32)
    route_table = routes[:, :, None] == jnp.arange(logits.shape[1])[None, None, :]
    picked = jnp.sum(jnp.where(route_table, logits[:, None, :], 0.0), axis=-1)
    raised = jnp.exp(picked)
    gate_values = raised / jnp.sum(raised, axis=1, keepdims=True)
    inside = routes < experts_axis
    gate_window = jnp.sum(jnp.where(inside, gate_values, 0.0), axis=1)
    expert_window = jnp.sum(jnp.where(inside, routes, 0), axis=1)
    present = jnp.any(inside, axis=1)
    capacity = local_rows // (experts_axis * experts_axis)
    member_table = (
        present[:, None] & (expert_window[:, None] == jnp.arange(experts_axis)[None, :])
    ).astype(jnp.int32)
    ranking = jnp.sum(jnp.cumsum(member_table, axis=0) * member_table, axis=1) - 1
    slot_index = expert_window * capacity + ranking
    select = (
        (jnp.arange(experts_axis * capacity)[:, None] == slot_index[None, :]) & present[None, :]
    ).astype(jnp.bfloat16)
    outgoing = (
        jnp.dot(select, normed_second, preferred_element_type=jnp.float32)
        .astype(jnp.bfloat16)
        .reshape(experts_axis, capacity, model_width)
    )
    gateup_here = expert_gateup[0]
    down_here = expert_down[0]
    hidden_units = down_here.shape[0]
    slot_items = scatter_blocks(outgoing, experts_axis, 2)
    flattened = slot_items.reshape(-1, slot_items.shape[-1])
    gate_up = jnp.dot(flattened, gateup_here, preferred_element_type=jnp.float32)
    active = (jax.nn.silu(gate_up[:, :hidden_units]) * gate_up[:, hidden_units:]).astype(
        jnp.bfloat16
    )
    result = (
        jnp.dot(active, down_here, preferred_element_type=jnp.float32)
        .astype(jnp.bfloat16)
        .reshape(slot_items.shape)
    )
    returned = scatter_blocks(result, experts_axis, 3)
    combined = jnp.dot(
        jnp.transpose(select), returned.reshape(-1, model_width), preferred_element_type=jnp.float32
    )
    expert_mix = (gate_window[:, None] * combined).astype(jnp.bfloat16)
    return (hidden, expert_mix)


def solution(mesh):
    return jax.shard_map(
        per_device,
        mesh=mesh,
        in_specs=(
            P(("group", "expert"), None),
            P(),
            P(),
            P("group", "expert"),
            P(None, "group", None),
            P("expert", "group"),
            P(),
            P(),
            P(),
            P(),
            P("expert", None, None),
            P("expert", None, None),
            P(("group", "expert"), None),
        ),
        out_specs=(P(("group", "expert"), None), P(("group", "expert"), None)),
        check_vma=False,
    )
```

```python
import functools
import math

import jax
import numpy as np
import jax.numpy as jnp
from jax import lax
from jax.experimental import pallas as pl
from jax.experimental.pallas import tpu as pltpu
from jax.sharding import PartitionSpec as P

MESH = pl.DeviceIdType.MESH

QUERY_HEADS = 32
KEY_VALUE_HEADS = 4
HEAD_DIMENSION = 128


epsilon = 1e-06
rope_theta = 1000000.0


def from_partner(block, axis, stride):
    count = lax.axis_size(axis)
    route = []
    for low in range(count):
        high = low | 1 << stride
        if high != low and high < count:
            route += [(low, high), (high, low)]
    return lax.ppermute(block, axis, route)


def gather_kernel(n_group, n_expert, wqkv, wo, xn, oqkv, oo, oxn, send, recv, xsend, xrecv, local):
    g = lax.axis_index("group")
    e = lax.axis_index("expert")
    columns = n_group // 2
    z = lax.div(g, 2)
    xh = lax.rem(g, 2)
    zp = lax.rem(z + 1, columns)
    zm = lax.rem(z + columns - 1, columns)
    plus_dev = (2 * zp + xh, e)
    minus_dev = (2 * zm + xh, e)
    pair_dev = (g + 1 - 2 * xh, e)
    core = lax.rem(e, 2)
    chip = lax.div(e, 2)
    chips = n_expert // 2
    mate_dev = (g, e + 1 - 2 * core)
    chip_devs = [(g, 2 * lax.rem(chip + j, chips) + core) for j in range(1, chips)]
    barrier = pltpu.get_barrier_semaphore()
    peers = [plus_dev, minus_dev, pair_dev, mate_dev] + chip_devs
    for dev in peers:
        pl.semaphore_signal(barrier, 1, device_id=dev, device_id_type=MESH)
    pl.semaphore_wait(barrier, len(peers))

    def slot(k, origin):
        return (oqkv, oo)[k].at[origin]

    sends = []

    def push(k, origin, src, dev):
        copy = pltpu.make_async_remote_copy(
            src_ref=src,
            dst_ref=slot(k, origin),
            send_sem=send.at[len(sends)],
            recv_sem=recv.at[k, origin],
            device_id=dev,
            device_id_type=MESH,
        )
        copy.start()
        sends.append(copy)

    def forward(origin, dev):
        for k in range(2):
            push(k, origin, slot(k, origin), dev)

    def arrive(origin):
        for k in range(2):
            pltpu.make_async_remote_copy(
                src_ref=slot(k, origin),
                dst_ref=slot(k, origin),
                send_sem=send.at[0],
                recv_sem=recv.at[k, origin],
                device_id=pair_dev,
                device_id_type=MESH,
            ).wait_recv()

    xsends = []

    def xpush(src, origin, dev):
        copy = pltpu.make_async_remote_copy(
            src_ref=src,
            dst_ref=oxn.at[origin],
            send_sem=xsend.at[len(xsends)],
            recv_sem=xrecv.at[origin],
            device_id=dev,
            device_id_type=MESH,
        )
        copy.start()
        xsends.append(copy)

    def xarrive(origin):
        pltpu.make_async_remote_copy(
            src_ref=oxn.at[origin],
            dst_ref=oxn.at[origin],
            send_sem=xsend.at[0],
            recv_sem=xrecv.at[origin],
            device_id=mate_dev,
            device_id_type=MESH,
        ).wait_recv()

    inputs = (wqkv, wo)
    own = [pltpu.make_async_copy(xn, oxn.at[e], local.at[2])]
    own += [pltpu.make_async_copy(inputs[k], slot(k, g), local.at[k]) for k in range(2)]
    for copy in own:
        copy.start()
    xpush(xn, e, mate_dev)
    for dev in chip_devs:
        xpush(xn, e, dev)
    for dev in (pair_dev, plus_dev, minus_dev):
        for k in range(2):
            push(k, g, inputs[k], dev)
    partner = g + 1 - 2 * xh
    arrive(partner)
    forward(partner, plus_dev)
    forward(partner, minus_dev)
    chip_origins = [2 * lax.rem(chip + j, chips) + core for j in range(1, chips)]
    normed_order = [chip_origins[0:2], chip_origins[2:5], chip_origins[5:]]
    for step in range(1, 4):
        behind = lax.rem(z - step + columns, columns)
        ahead = lax.rem(z + step, columns)
        for origin in (2 * behind, 2 * behind + 1):
            arrive(origin)
        for origin in ((2 * behind, 2 * behind + 1) if step < 3 else (2 * behind,)):
            forward(origin, plus_dev)
        for origin in (2 * ahead, 2 * ahead + 1):
            arrive(origin)
        for origin in ((2 * ahead, 2 * ahead + 1) if step < 3 else (2 * ahead + 1,)):
            forward(origin, minus_dev)
        for origin in normed_order[step - 1]:
            xarrive(origin)
            xpush(oxn.at[origin], origin, mate_dev)
    across = lax.rem(z + columns // 2, columns)
    arrive(2 * across)
    arrive(2 * across + 1)
    mate_core = 1 - core
    xarrive(e + 1 - 2 * core)
    for j in range(1, chips):
        xarrive(2 * lax.rem(chip + j, chips) + mate_core)
    for copy in sends + xsends:
        copy.wait_send()
    for copy in own:
        copy.wait()


def gather_all(wqkv, wo, xn, n_group, n_expert):
    any_spec = pl.BlockSpec(memory_space=pl.ANY)
    shapes = [jax.ShapeDtypeStruct((n_group,) + a.shape, a.dtype) for a in (wqkv, wo)]
    shapes += [jax.ShapeDtypeStruct((n_expert,) + xn.shape, xn.dtype)]
    return pl.pallas_call(
        functools.partial(gather_kernel, n_group, n_expert),
        out_shape=tuple(shapes),
        in_specs=[any_spec] * 3,
        out_specs=tuple([any_spec] * 3),
        scratch_shapes=[
            pltpu.SemaphoreType.DMA((32,)),
            pltpu.SemaphoreType.DMA((2, n_group)),
            pltpu.SemaphoreType.DMA((n_expert,)),
            pltpu.SemaphoreType.DMA((n_expert,)),
            pltpu.SemaphoreType.DMA((3,)),
        ],
        compiler_params=pltpu.CompilerParams(collective_id=0, has_side_effects=True),
    )(wqkv, wo, xn)


def combine_kernel(blocks, attended_ref, weight_ref, out_ref, outgoing, incoming, send, recv):
    g = lax.axis_index("group")
    e = lax.axis_index("expert")
    core = lax.rem(e, 2)
    mate_dev = (g, e + 1 - 2 * core)
    rows = out_ref.shape[1]
    barrier = pltpu.get_barrier_semaphore()
    pl.semaphore_signal(barrier, 1, device_id=mate_dev, device_id_type=MESH)
    pl.semaphore_wait(barrier, 1)

    def partial(block):
        start = pl.multiple_of(block * rows, rows)
        return jnp.dot(
            attended_ref[pl.ds(start, rows), :], weight_ref[...], preferred_element_type=jnp.float32
        ).astype(jnp.bfloat16)

    for i in range(blocks):
        outgoing[i] = partial(2 * i + 1 - core)
    copy = pltpu.make_async_remote_copy(
        src_ref=outgoing,
        dst_ref=incoming,
        send_sem=send.at[0],
        recv_sem=recv.at[0],
        device_id=mate_dev,
        device_id_type=MESH,
    )
    copy.start()
    for i in range(blocks):
        out_ref[i] = partial(2 * i + core)
    copy.wait()
    for i in range(blocks):
        out_ref[i] = (out_ref[i].astype(jnp.float32) + incoming[i].astype(jnp.float32)).astype(
            jnp.bfloat16
        )


def project_and_combine(attended, weight, experts_axis):
    rows = attended.shape[0] // experts_axis
    blocks = experts_axis // 2
    shape = (blocks, rows, weight.shape[1])
    vmem = pl.BlockSpec(memory_space=pltpu.VMEM)
    return pl.pallas_call(
        functools.partial(combine_kernel, blocks),
        out_shape=jax.ShapeDtypeStruct(shape, jnp.bfloat16),
        in_specs=[vmem, vmem],
        out_specs=vmem,
        scratch_shapes=[
            pltpu.VMEM(shape, jnp.bfloat16),
            pltpu.VMEM(shape, jnp.bfloat16),
            pltpu.SemaphoreType.DMA((1,)),
            pltpu.SemaphoreType.DMA((1,)),
        ],
        compiler_params=pltpu.CompilerParams(collective_id=4, has_side_effects=True),
    )(attended, weight)


def combine_scatter_kernel(blocks, attended_ref, weight_ref, out_ref, outgoing, incoming, combined, send, recv, chip_send, chip_recv, local):
    g = lax.axis_index("group")
    e = lax.axis_index("expert")
    core = lax.rem(e, 2)
    chip = lax.div(e, 2)
    mate_dev = (g, e + 1 - 2 * core)
    chip_devs = [(g, 2 * lax.rem(chip + j, blocks) + core) for j in range(1, blocks)]
    rows = out_ref.shape[1]
    barrier = pltpu.get_barrier_semaphore()
    for dev in [mate_dev] + chip_devs:
        pl.semaphore_signal(barrier, 1, device_id=dev, device_id_type=MESH)
    pl.semaphore_wait(barrier, blocks)

    def partial(block):
        start = pl.multiple_of(block * rows, rows)
        return jnp.dot(
            attended_ref[pl.ds(start, rows), :], weight_ref[...], preferred_element_type=jnp.float32
        ).astype(jnp.bfloat16)

    for i in range(blocks):
        outgoing[i] = partial(2 * i + 1 - core)
    copy = pltpu.make_async_remote_copy(
        src_ref=outgoing,
        dst_ref=incoming,
        send_sem=send.at[0],
        recv_sem=recv.at[0],
        device_id=mate_dev,
        device_id_type=MESH,
    )
    copy.start()
    for i in range(blocks):
        combined[i] = partial(2 * i + core)
    copy.wait()
    pushes = []
    for j in range(1, blocks):
        i = lax.rem(chip + j, blocks)
        combined[i] = (combined[i].astype(jnp.float32) + incoming[i].astype(jnp.float32)).astype(
            jnp.bfloat16
        )
        push = pltpu.make_async_remote_copy(
            src_ref=combined.at[i],
            dst_ref=out_ref.at[chip],
            send_sem=chip_send.at[j],
            recv_sem=chip_recv.at[j],
            device_id=chip_devs[j - 1],
            device_id_type=MESH,
        )
        push.start()
        pushes.append(push)
    combined[chip] = (combined[chip].astype(jnp.float32) + incoming[chip].astype(jnp.float32)).astype(
        jnp.bfloat16
    )
    own = pltpu.make_async_copy(combined.at[chip], out_ref.at[chip], local.at[0])
    own.start()
    for push in pushes:
        push.wait()
    own.wait()


def combine_and_scatter(attended, weight, experts_axis):
    rows = attended.shape[0] // experts_axis
    blocks = experts_axis // 2
    shape = (blocks, rows, weight.shape[1])
    vmem = pl.BlockSpec(memory_space=pltpu.VMEM)
    return pl.pallas_call(
        functools.partial(combine_scatter_kernel, blocks),
        out_shape=jax.ShapeDtypeStruct(shape, jnp.bfloat16),
        in_specs=[vmem, vmem],
        out_specs=pl.BlockSpec(memory_space=pl.ANY),
        scratch_shapes=[
            pltpu.VMEM(shape, jnp.bfloat16),
            pltpu.VMEM(shape, jnp.bfloat16),
            pltpu.VMEM(shape, jnp.bfloat16),
            pltpu.SemaphoreType.DMA((1,)),
            pltpu.SemaphoreType.DMA((1,)),
            pltpu.SemaphoreType.DMA((blocks,)),
            pltpu.SemaphoreType.DMA((blocks,)),
            pltpu.SemaphoreType.DMA((1,)),
        ],
        compiler_params=pltpu.CompilerParams(collective_id=7, has_side_effects=True),
    )(attended, weight)


def mate_kernel(part, out, send, recv):
    g = lax.axis_index("group")
    e = lax.axis_index("expert")
    core = lax.rem(e, 2)
    mate_dev = (g, e + 1 - 2 * core)
    barrier = pltpu.get_barrier_semaphore()
    pl.semaphore_signal(barrier, 1, device_id=mate_dev, device_id_type=MESH)
    pl.semaphore_wait(barrier, 1)
    copy = pltpu.make_async_remote_copy(
        src_ref=part.at[:, 1 - core],
        dst_ref=out,
        send_sem=send.at[0],
        recv_sem=recv.at[0],
        device_id=mate_dev,
        device_id_type=MESH,
    )
    copy.start()
    copy.wait()


def exchange_with_mate(part):
    any_spec = pl.BlockSpec(memory_space=pl.ANY)
    shape = (part.shape[0],) + part.shape[2:]
    return pl.pallas_call(
        mate_kernel,
        out_shape=jax.ShapeDtypeStruct(shape, part.dtype),
        in_specs=[any_spec],
        out_specs=any_spec,
        scratch_shapes=[pltpu.SemaphoreType.DMA((1,)), pltpu.SemaphoreType.DMA((1,))],
        compiler_params=pltpu.CompilerParams(collective_id=4, has_side_effects=True),
    )(part)


def chip_scatter_kernel(chips, part, out, send, recv, local):
    g = lax.axis_index("group")
    e = lax.axis_index("expert")
    core = lax.rem(e, 2)
    chip = lax.div(e, 2)
    devs = [(g, 2 * lax.rem(chip + j, chips) + core) for j in range(1, chips)]
    barrier = pltpu.get_barrier_semaphore()
    for dev in devs:
        pl.semaphore_signal(barrier, 1, device_id=dev, device_id_type=MESH)
    pl.semaphore_wait(barrier, len(devs))
    copies = []
    for j in range(1, chips):
        copy = pltpu.make_async_remote_copy(
            src_ref=part.at[lax.rem(chip + j, chips)],
            dst_ref=out.at[chip],
            send_sem=send.at[j],
            recv_sem=recv.at[j],
            device_id=devs[j - 1],
            device_id_type=MESH,
        )
        copy.start()
        copies.append(copy)
    own = pltpu.make_async_copy(part.at[chip], out.at[chip], local.at[0])
    own.start()
    for copy in copies:
        copy.wait()
    own.wait()


def scatter_to_chips(part):
    chips = part.shape[0]
    any_spec = pl.BlockSpec(memory_space=pl.ANY)
    return pl.pallas_call(
        functools.partial(chip_scatter_kernel, chips),
        out_shape=jax.ShapeDtypeStruct(part.shape, part.dtype),
        in_specs=[any_spec],
        out_specs=any_spec,
        scratch_shapes=[
            pltpu.SemaphoreType.DMA((chips,)),
            pltpu.SemaphoreType.DMA((chips,)),
            pltpu.SemaphoreType.DMA((1,)),
        ],
        compiler_params=pltpu.CompilerParams(collective_id=5, has_side_effects=True),
    )(part)


def scatter_kernel(n_expert, part, out, send, recv, local):
    g = lax.axis_index("group")
    e = lax.axis_index("expert")
    barrier = pltpu.get_barrier_semaphore()
    for j in range(1, n_expert):
        pl.semaphore_signal(barrier, 1, device_id=(g, lax.rem(e + j, n_expert)), device_id_type=MESH)
    pl.semaphore_wait(barrier, n_expert - 1)
    copies = []
    for j in range(1, n_expert):
        peer = lax.rem(e + j, n_expert)
        copy = pltpu.make_async_remote_copy(
            src_ref=part.at[peer],
            dst_ref=out.at[e],
            send_sem=send.at[j],
            recv_sem=recv.at[j],
            device_id=(g, peer),
            device_id_type=MESH,
        )
        copy.start()
        copies.append(copy)
    own = pltpu.make_async_copy(part.at[e], out.at[e], local.at[0])
    own.start()
    for copy in copies:
        copy.wait()
    own.wait()


def scatter_blocks(part, n_expert, collective_id):
    any_spec = pl.BlockSpec(memory_space=pl.ANY)
    return pl.pallas_call(
        functools.partial(scatter_kernel, n_expert),
        out_shape=jax.ShapeDtypeStruct(part.shape, part.dtype),
        in_specs=[any_spec],
        out_specs=any_spec,
        scratch_shapes=[
            pltpu.SemaphoreType.DMA((n_expert,)),
            pltpu.SemaphoreType.DMA((n_expert,)),
            pltpu.SemaphoreType.DMA((1,)),
        ],
        compiler_params=pltpu.CompilerParams(collective_id=collective_id, has_side_effects=True),
    )(part)


def attention_kernel(scale, heads, q_ref, k_ref, v_ref, qpos_ref, kpos_ref, o_ref):
    allowed = kpos_ref[...] <= qpos_ref[...]
    keys = k_ref[...]
    values = v_ref[...]
    depth = keys.shape[1]
    for h in range(heads):
        query = q_ref[:, h * depth : (h + 1) * depth]
        scores = (
            lax.dot_general(
                query, keys, (((1,), (1,)), ((), ())), preferred_element_type=jnp.float32
            )
            * scale
        )
        weights = jnp.where(allowed, jnp.exp(scores), 0.0)
        denominators = jnp.sum(weights, axis=-1, keepdims=True)
        weighted = jnp.dot(
            weights.astype(jnp.bfloat16), values, preferred_element_type=jnp.float32
        )
        o_ref[:, h * depth : (h + 1) * depth] = (weighted / denominators).astype(o_ref.dtype)


def attention(queries, keys, values, query_places, key_places, scale):
    rows, width = queries.shape
    key_rows, depth = keys.shape
    block = min(256, rows)
    return pl.pallas_call(
        functools.partial(attention_kernel, scale, width // depth),
        out_shape=jax.ShapeDtypeStruct((rows, width), jnp.bfloat16),
        grid=(rows // block,),
        in_specs=[
            pl.BlockSpec((block, width), lambda i: (i, 0)),
            pl.BlockSpec((key_rows, depth), lambda i: (0, 0)),
            pl.BlockSpec((key_rows, depth), lambda i: (0, 0)),
            pl.BlockSpec((block, 1), lambda i: (i, 0)),
            pl.BlockSpec((1, key_rows), lambda i: (0, 0)),
        ],
        out_specs=pl.BlockSpec((block, width), lambda i: (i, 0)),
        cost_estimate=pl.CostEstimate(
            flops=4 * rows * key_rows * width,
            transcendentals=rows * key_rows * (width // depth),
            bytes_accessed=2 * (2 * rows * width + 2 * key_rows * depth),
        ),
    )(queries, keys, values, query_places.reshape(rows, 1), key_places.reshape(1, key_rows))


def norm_rows(values, gain_vector):
    widened = values.astype(jnp.float32)
    inverse_rms = lax.rsqrt(jnp.mean(widened * widened, axis=-1, keepdims=True) + epsilon)
    return widened * inverse_rms * gain_vector


def rotate(values, positions):
    half_width = values.shape[-1] // 2
    exponents = jnp.arange(half_width).astype(jnp.float32)
    inverse = jnp.exp(exponents * (-2.0 * math.log(rope_theta) / values.shape[-1]))
    angles = positions[:, None, None] * inverse[None, None, :]
    cosine_values = jnp.cos(angles)
    sine_values = jnp.sin(angles)
    first_half = values[..., :half_width]
    second = values[..., half_width:]
    return jnp.concatenate(
        [
            first_half * cosine_values - second * sine_values,
            second * cosine_values + first_half * sine_values,
        ],
        axis=-1,
    )


def local_positions(parity, row_count):
    indices = jnp.arange(row_count)
    quarter = row_count // 2
    offset = jnp.where(parity == 0, jnp.where(indices < quarter, 0, 2 * quarter), quarter)
    return indices + offset


def prep_kernel(query_width, x_ref, w_ref, cos_ref, sin_ref, qg_ref, kg_ref, q_out, k_out, v_out):
    x = x_ref[...]
    cosines = cos_ref[...]
    sines = sin_ref[...]
    depth = cosines.shape[1]

    def project(start, stop):
        return jnp.dot(x, w_ref[:, start:stop], preferred_element_type=jnp.float32).astype(jnp.bfloat16)

    def norm_rope(values, gain):
        values = values.astype(jnp.float32)
        inverse_rms = lax.rsqrt(jnp.mean(values * values, axis=-1, keepdims=True) + epsilon)
        normed = values * inverse_rms * gain
        return (normed * cosines + pltpu.roll(normed, depth // 2, 1) * sines).astype(jnp.bfloat16)

    queries = project(0, query_width)
    for h in range(queries.shape[1] // depth):
        q_out[:, h * depth : (h + 1) * depth] = norm_rope(
            queries[:, h * depth : (h + 1) * depth], qg_ref[...]
        )
    k_out[...] = norm_rope(project(query_width, query_width + depth), kg_ref[...])
    v_out[...] = project(query_width + depth, query_width + 2 * depth)


def prep(normed_rows, joined, cosines, sines, query_gain, key_gain):
    rows, width = normed_rows.shape
    depth = cosines.shape[1]
    query_width = joined.shape[1] - 2 * depth
    block = min(256, rows)
    whole = lambda shape: pl.BlockSpec(shape, lambda i: (0, 0))
    per_row = lambda cols: pl.BlockSpec((block, cols), lambda i: (i, 0))
    return pl.pallas_call(
        functools.partial(prep_kernel, query_width),
        out_shape=(
            jax.ShapeDtypeStruct((rows, query_width), jnp.bfloat16),
            jax.ShapeDtypeStruct((rows, depth), jnp.bfloat16),
            jax.ShapeDtypeStruct((rows, depth), jnp.bfloat16),
        ),
        grid=(rows // block,),
        in_specs=[
            per_row(width),
            whole(joined.shape),
            per_row(depth),
            per_row(depth),
            whole((1, depth)),
            whole((1, depth)),
        ],
        out_specs=(per_row(query_width), per_row(depth), per_row(depth)),
        cost_estimate=pl.CostEstimate(
            flops=2 * rows * width * joined.shape[1],
            transcendentals=rows * (query_width // depth + 1),
            bytes_accessed=2 * (rows * width + width * joined.shape[1] + rows * joined.shape[1]),
        ),
    )(normed_rows, joined, cosines, sines, query_gain.reshape(1, depth), key_gain.reshape(1, depth))


def rope_tables(parity, row_count, depth):
    half = depth // 2
    frequencies = rope_theta ** (-2.0 * np.arange(half) / depth)
    indices = np.arange(row_count)
    quarter = row_count // 2
    places = np.concatenate([np.where(indices < quarter, indices, indices + 2 * quarter), indices + quarter])
    angles = places[:, None].astype(np.float64) * frequencies[None, :]
    cosines = jnp.asarray(np.cos(angles), jnp.float32)
    sines = jnp.asarray(np.sin(angles), jnp.float32)
    cosines = lax.dynamic_slice_in_dim(cosines, parity * row_count, row_count, 0)
    sines = lax.dynamic_slice_in_dim(sines, parity * row_count, row_count, 0)
    return (
        jnp.concatenate([cosines, cosines], axis=1),
        jnp.concatenate([-sines, sines], axis=1),
    )


def per_device(
    hidden_in,
    norm_attention,
    norm_experts,
    query_master,
    trainer_key_value_weight,
    output_master,
    query_gain,
    key_gain,
    lengths,
    router,
    expert_gateup,
    expert_down,
    routes,
):
    experts_axis = lax.axis_size("expert")
    group_member = lax.axis_index("expert")
    group_index = lax.axis_index("group")
    local_head_count = QUERY_HEADS // experts_axis
    width_here = local_head_count * HEAD_DIMENSION
    common_head = group_member * local_head_count // (QUERY_HEADS // KEY_VALUE_HEADS)
    groups_axis = lax.axis_size("group")
    keyvalue_slice = lax.dynamic_slice_in_dim(
        trainer_key_value_weight, common_head * HEAD_DIMENSION, HEAD_DIMENSION, 2
    ).astype(jnp.bfloat16)
    normed = norm_rows(hidden_in, norm_attention).astype(jnp.bfloat16)
    joined_parts, output_parts, normed_parts = gather_all(
        jnp.concatenate(
            [query_master.astype(jnp.bfloat16), keyvalue_slice[0], keyvalue_slice[1]], axis=1
        ),
        output_master.astype(jnp.bfloat16),
        normed,
        groups_axis,
        experts_axis,
    )
    model_width = hidden_in.shape[1]
    local_rows = normed_parts.shape[0] * normed_parts.shape[1]
    parity = group_index % 2
    own_places = local_positions(parity, local_rows)
    partner_places = local_positions(1 - parity, local_rows)
    cosines, sines = rope_tables(parity, local_rows, HEAD_DIMENSION)
    query_rows_list, key_rows, value_rows = prep(
        normed_parts.reshape(local_rows, model_width),
        joined_parts.reshape(model_width, -1),
        cosines,
        sines,
        query_gain,
        key_gain,
    )
    partner = from_partner(jnp.stack([key_rows, value_rows]), "group", 0)
    all_keys = jnp.concatenate([key_rows, partner[0]], axis=0)
    all_values = jnp.concatenate([value_rows, partner[1]], axis=0)
    key_places = jnp.concatenate([own_places, partner_places])
    valid_length = jnp.sum(jnp.where(jnp.arange(lengths.shape[0]) == group_index // 2, lengths, 0))
    past_end = jnp.full_like(key_places, 4 * key_places.shape[0])
    key_limits = jnp.where(key_places < valid_length, key_places, past_end)
    attended = attention(
        query_rows_list,
        all_keys,
        all_values,
        own_places,
        key_limits,
        HEAD_DIMENSION ** (-0.5),
    )
    output_weight = jnp.transpose(output_parts, (1, 0, 2)).reshape(output_parts.shape[1], -1)
    owned = combine_and_scatter(attended, output_weight, experts_axis)
    summed = jnp.sum(owned.astype(jnp.float32), axis=0)
    hidden = (hidden_in.astype(jnp.float32) + summed).astype(jnp.bfloat16)
    normed_second = norm_rows(hidden, norm_experts).astype(jnp.bfloat16)
    logits = jnp.dot(normed_second, router, preferred_element_type=jnp.float32)
    route_table = routes[:, :, None] == jnp.arange(logits.shape[1])[None, None, :]
    picked = jnp.sum(jnp.where(route_table, logits[:, None, :], 0.0), axis=-1)
    raised = jnp.exp(picked)
    gate_values = raised / jnp.sum(raised, axis=1, keepdims=True)
    inside = routes < experts_axis
    gate_window = jnp.sum(jnp.where(inside, gate_values, 0.0), axis=1)
    expert_window = jnp.sum(jnp.where(inside, routes, 0), axis=1)
    present = jnp.any(inside, axis=1)
    capacity = local_rows // (experts_axis * experts_axis)
    member_table = (
        present[:, None] & (expert_window[:, None] == jnp.arange(experts_axis)[None, :])
    ).astype(jnp.int32)
    ranking = jnp.sum(jnp.cumsum(member_table, axis=0) * member_table, axis=1) - 1
    slot_index = expert_window * capacity + ranking
    select = (
        (jnp.arange(experts_axis * capacity)[:, None] == slot_index[None, :]) & present[None, :]
    ).astype(jnp.bfloat16)
    outgoing = (
        jnp.dot(select, normed_second, preferred_element_type=jnp.float32)
        .astype(jnp.bfloat16)
        .reshape(experts_axis, capacity, model_width)
    )
    gateup_here = expert_gateup[0]
    down_here = expert_down[0]
    hidden_units = down_here.shape[0]
    slot_items = scatter_blocks(outgoing, experts_axis, 2)
    flattened = slot_items.reshape(-1, slot_items.shape[-1])
    gate_up = jnp.dot(flattened, gateup_here, preferred_element_type=jnp.float32)
    active = (jax.nn.silu(gate_up[:, :hidden_units]) * gate_up[:, hidden_units:]).astype(
        jnp.bfloat16
    )
    result = (
        jnp.dot(active, down_here, preferred_element_type=jnp.float32)
        .astype(jnp.bfloat16)
        .reshape(slot_items.shape)
    )
    returned = scatter_blocks(result, experts_axis, 3)
    combined = jnp.dot(
        jnp.transpose(select), returned.reshape(-1, model_width), preferred_element_type=jnp.float32
    )
    expert_mix = (gate_window[:, None] * combined).astype(jnp.bfloat16)
    return (hidden, expert_mix)


def solution(mesh):
    return jax.shard_map(
        per_device,
        mesh=mesh,
        in_specs=(
            P(("group", "expert"), None),
            P(),
            P(),
            P("group", "expert"),
            P(None, "group", None),
            P("expert", "group"),
            P(),
            P(),
            P(),
            P(),
            P("expert", None, None),
            P("expert", None, None),
            P(("group", "expert"), None),
        ),
        out_specs=(P(("group", "expert"), None), P(("group", "expert"), None)),
        check_vma=False,
    )
```

```python
import functools
import math

import jax
import numpy as np
import jax.numpy as jnp
from jax import lax
from jax.experimental import pallas as pl
from jax.experimental.pallas import tpu as pltpu
from jax.sharding import PartitionSpec as P

MESH = pl.DeviceIdType.MESH

QUERY_HEADS = 32
KEY_VALUE_HEADS = 4
HEAD_DIMENSION = 128


epsilon = 1e-06
rope_theta = 1000000.0


def from_partner(block, axis, stride):
    count = lax.axis_size(axis)
    route = []
    for low in range(count):
        high = low | 1 << stride
        if high != low and high < count:
            route += [(low, high), (high, low)]
    return lax.ppermute(block, axis, route)


def gather_kernel(n_group, n_expert, heads_here, q_in, kv_in, o_in, h_in, gain_in, oqkv, oo, oxn, send, recv, xsend, xrecv, local, wqkv, wo, xn):
    e_here = lax.axis_index("expert")
    depth = HEAD_DIMENSION
    column = pl.multiple_of(lax.div(e_here * heads_here, QUERY_HEADS // KEY_VALUE_HEADS) * depth, depth)
    query_width = q_in.shape[1]
    wqkv[:, 0:query_width] = q_in[...].astype(jnp.bfloat16)
    wqkv[:, query_width : query_width + depth] = kv_in[0, :, pl.ds(column, depth)].astype(jnp.bfloat16)
    wqkv[:, query_width + depth : query_width + 2 * depth] = kv_in[1, :, pl.ds(column, depth)].astype(
        jnp.bfloat16
    )
    wo[...] = o_in[...].astype(jnp.bfloat16)
    xn[...] = norm_rows(h_in[...], gain_in[...]).astype(jnp.bfloat16)
    g = lax.axis_index("group")
    e = lax.axis_index("expert")
    columns = n_group // 2
    z = lax.div(g, 2)
    xh = lax.rem(g, 2)
    zp = lax.rem(z + 1, columns)
    zm = lax.rem(z + columns - 1, columns)
    plus_dev = (2 * zp + xh, e)
    minus_dev = (2 * zm + xh, e)
    pair_dev = (g + 1 - 2 * xh, e)
    core = lax.rem(e, 2)
    chip = lax.div(e, 2)
    chips = n_expert // 2
    mate_dev = (g, e + 1 - 2 * core)
    chip_devs = [(g, 2 * lax.rem(chip + j, chips) + core) for j in range(1, chips)]
    barrier = pltpu.get_barrier_semaphore()
    peers = [plus_dev, minus_dev, pair_dev, mate_dev] + chip_devs
    for dev in peers:
        pl.semaphore_signal(barrier, 1, device_id=dev, device_id_type=MESH)
    pl.semaphore_wait(barrier, len(peers))

    def slot(k, origin):
        return (oqkv, oo)[k].at[origin]

    sends = []

    def push(k, origin, src, dev):
        copy = pltpu.make_async_remote_copy(
            src_ref=src,
            dst_ref=slot(k, origin),
            send_sem=send.at[len(sends)],
            recv_sem=recv.at[k, origin],
            device_id=dev,
            device_id_type=MESH,
        )
        copy.start()
        sends.append(copy)

    def forward(origin, dev):
        for k in range(2):
            push(k, origin, slot(k, origin), dev)

    def arrive(origin):
        for k in range(2):
            pltpu.make_async_remote_copy(
                src_ref=slot(k, origin),
                dst_ref=slot(k, origin),
                send_sem=send.at[0],
                recv_sem=recv.at[k, origin],
                device_id=pair_dev,
                device_id_type=MESH,
            ).wait_recv()

    xsends = []

    def xpush(src, origin, dev):
        copy = pltpu.make_async_remote_copy(
            src_ref=src,
            dst_ref=oxn.at[origin],
            send_sem=xsend.at[len(xsends)],
            recv_sem=xrecv.at[origin],
            device_id=dev,
            device_id_type=MESH,
        )
        copy.start()
        xsends.append(copy)

    def xarrive(origin):
        pltpu.make_async_remote_copy(
            src_ref=oxn.at[origin],
            dst_ref=oxn.at[origin],
            send_sem=xsend.at[0],
            recv_sem=xrecv.at[origin],
            device_id=mate_dev,
            device_id_type=MESH,
        ).wait_recv()

    inputs = (wqkv, wo)
    own = [pltpu.make_async_copy(xn, oxn.at[e], local.at[2])]
    own += [pltpu.make_async_copy(inputs[k], slot(k, g), local.at[k]) for k in range(2)]
    for copy in own:
        copy.start()
    xpush(xn, e, mate_dev)
    for dev in chip_devs:
        xpush(xn, e, dev)
    for dev in (pair_dev, plus_dev, minus_dev):
        for k in range(2):
            push(k, g, inputs[k], dev)
    partner = g + 1 - 2 * xh
    arrive(partner)
    forward(partner, plus_dev)
    forward(partner, minus_dev)
    chip_origins = [2 * lax.rem(chip + j, chips) + core for j in range(1, chips)]
    normed_order = [chip_origins[0:2], chip_origins[2:5], chip_origins[5:]]
    for step in range(1, 4):
        behind = lax.rem(z - step + columns, columns)
        ahead = lax.rem(z + step, columns)
        for origin in (2 * behind, 2 * behind + 1):
            arrive(origin)
        for origin in ((2 * behind, 2 * behind + 1) if step < 3 else (2 * behind,)):
            forward(origin, plus_dev)
        for origin in (2 * ahead, 2 * ahead + 1):
            arrive(origin)
        for origin in ((2 * ahead, 2 * ahead + 1) if step < 3 else (2 * ahead + 1,)):
            forward(origin, minus_dev)
        for origin in normed_order[step - 1]:
            xarrive(origin)
            xpush(oxn.at[origin], origin, mate_dev)
    across = lax.rem(z + columns // 2, columns)
    arrive(2 * across)
    arrive(2 * across + 1)
    mate_core = 1 - core
    xarrive(e + 1 - 2 * core)
    for j in range(1, chips):
        xarrive(2 * lax.rem(chip + j, chips) + mate_core)
    for copy in sends + xsends:
        copy.wait_send()
    for copy in own:
        copy.wait()


def gather_all(q_in, kv_in, o_in, h_in, gain_in, n_group, n_expert):
    any_spec = pl.BlockSpec(memory_space=pl.ANY)
    vmem = pl.BlockSpec(memory_space=pltpu.VMEM)
    depth = HEAD_DIMENSION
    joined = (q_in.shape[0], q_in.shape[1] + 2 * depth)
    shapes = [
        jax.ShapeDtypeStruct((n_group,) + joined, jnp.bfloat16),
        jax.ShapeDtypeStruct((n_group,) + o_in.shape, jnp.bfloat16),
        jax.ShapeDtypeStruct((n_expert,) + h_in.shape, jnp.bfloat16),
    ]
    return pl.pallas_call(
        functools.partial(gather_kernel, n_group, n_expert, q_in.shape[1] // depth),
        out_shape=tuple(shapes),
        in_specs=[vmem] * 5,
        out_specs=tuple([any_spec] * 3),
        scratch_shapes=[
            pltpu.SemaphoreType.DMA((32,)),
            pltpu.SemaphoreType.DMA((2, n_group)),
            pltpu.SemaphoreType.DMA((n_expert,)),
            pltpu.SemaphoreType.DMA((n_expert,)),
            pltpu.SemaphoreType.DMA((3,)),
            pltpu.VMEM(joined, jnp.bfloat16),
            pltpu.VMEM(o_in.shape, jnp.bfloat16),
            pltpu.VMEM(h_in.shape, jnp.bfloat16),
        ],
        compiler_params=pltpu.CompilerParams(collective_id=0, has_side_effects=True),
    )(q_in, kv_in, o_in, h_in, gain_in)


def combine_kernel(blocks, attended_ref, weight_ref, out_ref, outgoing, incoming, send, recv):
    g = lax.axis_index("group")
    e = lax.axis_index("expert")
    core = lax.rem(e, 2)
    mate_dev = (g, e + 1 - 2 * core)
    rows = out_ref.shape[1]
    barrier = pltpu.get_barrier_semaphore()
    pl.semaphore_signal(barrier, 1, device_id=mate_dev, device_id_type=MESH)
    pl.semaphore_wait(barrier, 1)

    def partial(block):
        start = pl.multiple_of(block * rows, rows)
        return jnp.dot(
            attended_ref[pl.ds(start, rows), :], weight_ref[...], preferred_element_type=jnp.float32
        ).astype(jnp.bfloat16)

    for i in range(blocks):
        outgoing[i] = partial(2 * i + 1 - core)
    copy = pltpu.make_async_remote_copy(
        src_ref=outgoing,
        dst_ref=incoming,
        send_sem=send.at[0],
        recv_sem=recv.at[0],
        device_id=mate_dev,
        device_id_type=MESH,
    )
    copy.start()
    for i in range(blocks):
        out_ref[i] = partial(2 * i + core)
    copy.wait()
    for i in range(blocks):
        out_ref[i] = (out_ref[i].astype(jnp.float32) + incoming[i].astype(jnp.float32)).astype(
            jnp.bfloat16
        )


def project_and_combine(attended, weight, experts_axis):
    rows = attended.shape[0] // experts_axis
    blocks = experts_axis // 2
    shape = (blocks, rows, weight.shape[1])
    vmem = pl.BlockSpec(memory_space=pltpu.VMEM)
    return pl.pallas_call(
        functools.partial(combine_kernel, blocks),
        out_shape=jax.ShapeDtypeStruct(shape, jnp.bfloat16),
        in_specs=[vmem, vmem],
        out_specs=vmem,
        scratch_shapes=[
            pltpu.VMEM(shape, jnp.bfloat16),
            pltpu.VMEM(shape, jnp.bfloat16),
            pltpu.SemaphoreType.DMA((1,)),
            pltpu.SemaphoreType.DMA((1,)),
        ],
        compiler_params=pltpu.CompilerParams(collective_id=4, has_side_effects=True),
    )(attended, weight)


def combine_scatter_kernel(blocks, attended_ref, weight_ref, out_ref, outgoing, incoming, combined, send, recv, chip_send, chip_recv, local):
    g = lax.axis_index("group")
    e = lax.axis_index("expert")
    core = lax.rem(e, 2)
    chip = lax.div(e, 2)
    mate_dev = (g, e + 1 - 2 * core)
    chip_devs = [(g, 2 * lax.rem(chip + j, blocks) + core) for j in range(1, blocks)]
    rows = out_ref.shape[1]
    barrier = pltpu.get_barrier_semaphore()
    for dev in [mate_dev] + chip_devs:
        pl.semaphore_signal(barrier, 1, device_id=dev, device_id_type=MESH)
    pl.semaphore_wait(barrier, blocks)

    def partial(block):
        start = pl.multiple_of(block * rows, rows)
        return jnp.dot(
            attended_ref[pl.ds(start, rows), :], weight_ref[...], preferred_element_type=jnp.float32
        ).astype(jnp.bfloat16)

    for i in range(blocks):
        outgoing[i] = partial(2 * i + 1 - core)
    copy = pltpu.make_async_remote_copy(
        src_ref=outgoing,
        dst_ref=incoming,
        send_sem=send.at[0],
        recv_sem=recv.at[0],
        device_id=mate_dev,
        device_id_type=MESH,
    )
    copy.start()
    for i in range(blocks):
        combined[i] = partial(2 * i + core)
    copy.wait()
    pushes = []
    for j in range(1, blocks):
        i = lax.rem(chip + j, blocks)
        combined[i] = (combined[i].astype(jnp.float32) + incoming[i].astype(jnp.float32)).astype(
            jnp.bfloat16
        )
        push = pltpu.make_async_remote_copy(
            src_ref=combined.at[i],
            dst_ref=out_ref.at[chip],
            send_sem=chip_send.at[j],
            recv_sem=chip_recv.at[j],
            device_id=chip_devs[j - 1],
            device_id_type=MESH,
        )
        push.start()
        pushes.append(push)
    combined[chip] = (combined[chip].astype(jnp.float32) + incoming[chip].astype(jnp.float32)).astype(
        jnp.bfloat16
    )
    own = pltpu.make_async_copy(combined.at[chip], out_ref.at[chip], local.at[0])
    own.start()
    for push in pushes:
        push.wait()
    own.wait()


def combine_and_scatter(attended, weight, experts_axis):
    rows = attended.shape[0] // experts_axis
    blocks = experts_axis // 2
    shape = (blocks, rows, weight.shape[1])
    vmem = pl.BlockSpec(memory_space=pltpu.VMEM)
    return pl.pallas_call(
        functools.partial(combine_scatter_kernel, blocks),
        out_shape=jax.ShapeDtypeStruct(shape, jnp.bfloat16),
        in_specs=[vmem, vmem],
        out_specs=pl.BlockSpec(memory_space=pl.ANY),
        scratch_shapes=[
            pltpu.VMEM(shape, jnp.bfloat16),
            pltpu.VMEM(shape, jnp.bfloat16),
            pltpu.VMEM(shape, jnp.bfloat16),
            pltpu.SemaphoreType.DMA((1,)),
            pltpu.SemaphoreType.DMA((1,)),
            pltpu.SemaphoreType.DMA((blocks,)),
            pltpu.SemaphoreType.DMA((blocks,)),
            pltpu.SemaphoreType.DMA((1,)),
        ],
        compiler_params=pltpu.CompilerParams(collective_id=7, has_side_effects=True),
    )(attended, weight)


def mate_kernel(part, out, send, recv):
    g = lax.axis_index("group")
    e = lax.axis_index("expert")
    core = lax.rem(e, 2)
    mate_dev = (g, e + 1 - 2 * core)
    barrier = pltpu.get_barrier_semaphore()
    pl.semaphore_signal(barrier, 1, device_id=mate_dev, device_id_type=MESH)
    pl.semaphore_wait(barrier, 1)
    copy = pltpu.make_async_remote_copy(
        src_ref=part.at[:, 1 - core],
        dst_ref=out,
        send_sem=send.at[0],
        recv_sem=recv.at[0],
        device_id=mate_dev,
        device_id_type=MESH,
    )
    copy.start()
    copy.wait()


def exchange_with_mate(part):
    any_spec = pl.BlockSpec(memory_space=pl.ANY)
    shape = (part.shape[0],) + part.shape[2:]
    return pl.pallas_call(
        mate_kernel,
        out_shape=jax.ShapeDtypeStruct(shape, part.dtype),
        in_specs=[any_spec],
        out_specs=any_spec,
        scratch_shapes=[pltpu.SemaphoreType.DMA((1,)), pltpu.SemaphoreType.DMA((1,))],
        compiler_params=pltpu.CompilerParams(collective_id=4, has_side_effects=True),
    )(part)


def chip_scatter_kernel(chips, part, out, send, recv, local):
    g = lax.axis_index("group")
    e = lax.axis_index("expert")
    core = lax.rem(e, 2)
    chip = lax.div(e, 2)
    devs = [(g, 2 * lax.rem(chip + j, chips) + core) for j in range(1, chips)]
    barrier = pltpu.get_barrier_semaphore()
    for dev in devs:
        pl.semaphore_signal(barrier, 1, device_id=dev, device_id_type=MESH)
    pl.semaphore_wait(barrier, len(devs))
    copies = []
    for j in range(1, chips):
        copy = pltpu.make_async_remote_copy(
            src_ref=part.at[lax.rem(chip + j, chips)],
            dst_ref=out.at[chip],
            send_sem=send.at[j],
            recv_sem=recv.at[j],
            device_id=devs[j - 1],
            device_id_type=MESH,
        )
        copy.start()
        copies.append(copy)
    own = pltpu.make_async_copy(part.at[chip], out.at[chip], local.at[0])
    own.start()
    for copy in copies:
        copy.wait()
    own.wait()


def scatter_to_chips(part):
    chips = part.shape[0]
    any_spec = pl.BlockSpec(memory_space=pl.ANY)
    return pl.pallas_call(
        functools.partial(chip_scatter_kernel, chips),
        out_shape=jax.ShapeDtypeStruct(part.shape, part.dtype),
        in_specs=[any_spec],
        out_specs=any_spec,
        scratch_shapes=[
            pltpu.SemaphoreType.DMA((chips,)),
            pltpu.SemaphoreType.DMA((chips,)),
            pltpu.SemaphoreType.DMA((1,)),
        ],
        compiler_params=pltpu.CompilerParams(collective_id=5, has_side_effects=True),
    )(part)


def scatter_kernel(n_expert, part, out, send, recv, local):
    g = lax.axis_index("group")
    e = lax.axis_index("expert")
    barrier = pltpu.get_barrier_semaphore()
    for j in range(1, n_expert):
        pl.semaphore_signal(barrier, 1, device_id=(g, lax.rem(e + j, n_expert)), device_id_type=MESH)
    pl.semaphore_wait(barrier, n_expert - 1)
    copies = []
    for j in range(1, n_expert):
        peer = lax.rem(e + j, n_expert)
        copy = pltpu.make_async_remote_copy(
            src_ref=part.at[peer],
            dst_ref=out.at[e],
            send_sem=send.at[j],
            recv_sem=recv.at[j],
            device_id=(g, peer),
            device_id_type=MESH,
        )
        copy.start()
        copies.append(copy)
    own = pltpu.make_async_copy(part.at[e], out.at[e], local.at[0])
    own.start()
    for copy in copies:
        copy.wait()
    own.wait()


def scatter_blocks(part, n_expert, collective_id):
    any_spec = pl.BlockSpec(memory_space=pl.ANY)
    return pl.pallas_call(
        functools.partial(scatter_kernel, n_expert),
        out_shape=jax.ShapeDtypeStruct(part.shape, part.dtype),
        in_specs=[any_spec],
        out_specs=any_spec,
        scratch_shapes=[
            pltpu.SemaphoreType.DMA((n_expert,)),
            pltpu.SemaphoreType.DMA((n_expert,)),
            pltpu.SemaphoreType.DMA((1,)),
        ],
        compiler_params=pltpu.CompilerParams(collective_id=collective_id, has_side_effects=True),
    )(part)


def attention_kernel(scale, heads, q_ref, k_ref, v_ref, qpos_ref, kpos_ref, o_ref):
    allowed = kpos_ref[...] <= qpos_ref[...]
    keys = k_ref[...]
    values = v_ref[...]
    depth = keys.shape[1]
    for h in range(heads):
        query = q_ref[:, h * depth : (h + 1) * depth]
        scores = (
            lax.dot_general(
                query, keys, (((1,), (1,)), ((), ())), preferred_element_type=jnp.float32
            )
            * scale
        )
        weights = jnp.where(allowed, jnp.exp(scores), 0.0)
        denominators = jnp.sum(weights, axis=-1, keepdims=True)
        weighted = jnp.dot(
            weights.astype(jnp.bfloat16), values, preferred_element_type=jnp.float32
        )
        o_ref[:, h * depth : (h + 1) * depth] = (weighted / denominators).astype(o_ref.dtype)


def attention(queries, keys, values, query_places, key_places, scale):
    rows, width = queries.shape
    key_rows, depth = keys.shape
    block = min(256, rows)
    return pl.pallas_call(
        functools.partial(attention_kernel, scale, width // depth),
        out_shape=jax.ShapeDtypeStruct((rows, width), jnp.bfloat16),
        grid=(rows // block,),
        in_specs=[
            pl.BlockSpec((block, width), lambda i: (i, 0)),
            pl.BlockSpec((key_rows, depth), lambda i: (0, 0)),
            pl.BlockSpec((key_rows, depth), lambda i: (0, 0)),
            pl.BlockSpec((block, 1), lambda i: (i, 0)),
            pl.BlockSpec((1, key_rows), lambda i: (0, 0)),
        ],
        out_specs=pl.BlockSpec((block, width), lambda i: (i, 0)),
        cost_estimate=pl.CostEstimate(
            flops=4 * rows * key_rows * width,
            transcendentals=rows * key_rows * (width // depth),
            bytes_accessed=2 * (2 * rows * width + 2 * key_rows * depth),
        ),
    )(queries, keys, values, query_places.reshape(rows, 1), key_places.reshape(1, key_rows))


def norm_rows(values, gain_vector):
    widened = values.astype(jnp.float32)
    inverse_rms = lax.rsqrt(jnp.mean(widened * widened, axis=-1, keepdims=True) + epsilon)
    return widened * inverse_rms * gain_vector


def rotate(values, positions):
    half_width = values.shape[-1] // 2
    exponents = jnp.arange(half_width).astype(jnp.float32)
    inverse = jnp.exp(exponents * (-2.0 * math.log(rope_theta) / values.shape[-1]))
    angles = positions[:, None, None] * inverse[None, None, :]
    cosine_values = jnp.cos(angles)
    sine_values = jnp.sin(angles)
    first_half = values[..., :half_width]
    second = values[..., half_width:]
    return jnp.concatenate(
        [
            first_half * cosine_values - second * sine_values,
            second * cosine_values + first_half * sine_values,
        ],
        axis=-1,
    )


def local_positions(parity, row_count):
    indices = jnp.arange(row_count)
    quarter = row_count // 2
    offset = jnp.where(parity == 0, jnp.where(indices < quarter, 0, 2 * quarter), quarter)
    return indices + offset


def prep_kernel(query_width, x_ref, w_ref, cos_ref, sin_ref, qg_ref, kg_ref, q_out, k_out, v_out):
    x = x_ref[...]
    cosines = cos_ref[...]
    sines = sin_ref[...]
    depth = cosines.shape[1]

    def project(start, stop):
        return jnp.dot(x, w_ref[:, start:stop], preferred_element_type=jnp.float32).astype(jnp.bfloat16)

    def norm_rope(values, gain):
        values = values.astype(jnp.float32)
        inverse_rms = lax.rsqrt(jnp.mean(values * values, axis=-1, keepdims=True) + epsilon)
        normed = values * inverse_rms * gain
        return (normed * cosines + pltpu.roll(normed, depth // 2, 1) * sines).astype(jnp.bfloat16)

    queries = project(0, query_width)
    for h in range(queries.shape[1] // depth):
        q_out[:, h * depth : (h + 1) * depth] = norm_rope(
            queries[:, h * depth : (h + 1) * depth], qg_ref[...]
        )
    k_out[...] = norm_rope(project(query_width, query_width + depth), kg_ref[...])
    v_out[...] = project(query_width + depth, query_width + 2 * depth)


def prep(normed_rows, joined, cosines, sines, query_gain, key_gain):
    rows, width = normed_rows.shape
    depth = cosines.shape[1]
    query_width = joined.shape[1] - 2 * depth
    block = min(256, rows)
    whole = lambda shape: pl.BlockSpec(shape, lambda i: (0, 0))
    per_row = lambda cols: pl.BlockSpec((block, cols), lambda i: (i, 0))
    return pl.pallas_call(
        functools.partial(prep_kernel, query_width),
        out_shape=(
            jax.ShapeDtypeStruct((rows, query_width), jnp.bfloat16),
            jax.ShapeDtypeStruct((rows, depth), jnp.bfloat16),
            jax.ShapeDtypeStruct((rows, depth), jnp.bfloat16),
        ),
        grid=(rows // block,),
        in_specs=[
            per_row(width),
            whole(joined.shape),
            per_row(depth),
            per_row(depth),
            whole((1, depth)),
            whole((1, depth)),
        ],
        out_specs=(per_row(query_width), per_row(depth), per_row(depth)),
        cost_estimate=pl.CostEstimate(
            flops=2 * rows * width * joined.shape[1],
            transcendentals=rows * (query_width // depth + 1),
            bytes_accessed=2 * (rows * width + width * joined.shape[1] + rows * joined.shape[1]),
        ),
    )(normed_rows, joined, cosines, sines, query_gain.reshape(1, depth), key_gain.reshape(1, depth))


def rope_tables(parity, row_count, depth):
    half = depth // 2
    frequencies = rope_theta ** (-2.0 * np.arange(half) / depth)
    indices = np.arange(row_count)
    quarter = row_count // 2
    places = np.concatenate([np.where(indices < quarter, indices, indices + 2 * quarter), indices + quarter])
    angles = places[:, None].astype(np.float64) * frequencies[None, :]
    cosines = jnp.asarray(np.cos(angles), jnp.float32)
    sines = jnp.asarray(np.sin(angles), jnp.float32)
    cosines = lax.dynamic_slice_in_dim(cosines, parity * row_count, row_count, 0)
    sines = lax.dynamic_slice_in_dim(sines, parity * row_count, row_count, 0)
    return (
        jnp.concatenate([cosines, cosines], axis=1),
        jnp.concatenate([-sines, sines], axis=1),
    )


def per_device(
    hidden_in,
    norm_attention,
    norm_experts,
    query_master,
    trainer_key_value_weight,
    output_master,
    query_gain,
    key_gain,
    lengths,
    router,
    expert_gateup,
    expert_down,
    routes,
):
    experts_axis = lax.axis_size("expert")
    group_member = lax.axis_index("expert")
    group_index = lax.axis_index("group")
    local_head_count = QUERY_HEADS // experts_axis
    width_here = local_head_count * HEAD_DIMENSION
    common_head = group_member * local_head_count // (QUERY_HEADS // KEY_VALUE_HEADS)
    groups_axis = lax.axis_size("group")
    joined_parts, output_parts, normed_parts = gather_all(
        query_master,
        trainer_key_value_weight,
        output_master,
        hidden_in,
        norm_attention.reshape(1, -1),
        groups_axis,
        experts_axis,
    )
    model_width = hidden_in.shape[1]
    local_rows = normed_parts.shape[0] * normed_parts.shape[1]
    parity = group_index % 2
    own_places = local_positions(parity, local_rows)
    partner_places = local_positions(1 - parity, local_rows)
    cosines, sines = rope_tables(parity, local_rows, HEAD_DIMENSION)
    query_rows_list, key_rows, value_rows = prep(
        normed_parts.reshape(local_rows, model_width),
        joined_parts.reshape(model_width, -1),
        cosines,
        sines,
        query_gain,
        key_gain,
    )
    partner = from_partner(jnp.stack([key_rows, value_rows]), "group", 0)
    all_keys = jnp.concatenate([key_rows, partner[0]], axis=0)
    all_values = jnp.concatenate([value_rows, partner[1]], axis=0)
    key_places = jnp.concatenate([own_places, partner_places])
    valid_length = jnp.sum(jnp.where(jnp.arange(lengths.shape[0]) == group_index // 2, lengths, 0))
    past_end = jnp.full_like(key_places, 4 * key_places.shape[0])
    key_limits = jnp.where(key_places < valid_length, key_places, past_end)
    attended = attention(
        query_rows_list,
        all_keys,
        all_values,
        own_places,
        key_limits,
        HEAD_DIMENSION ** (-0.5),
    )
    output_weight = jnp.transpose(output_parts, (1, 0, 2)).reshape(output_parts.shape[1], -1)
    owned = combine_and_scatter(attended, output_weight, experts_axis)
    summed = jnp.sum(owned.astype(jnp.float32), axis=0)
    hidden = (hidden_in.astype(jnp.float32) + summed).astype(jnp.bfloat16)
    normed_second = norm_rows(hidden, norm_experts).astype(jnp.bfloat16)
    logits = jnp.dot(normed_second, router, preferred_element_type=jnp.float32)
    route_table = routes[:, :, None] == jnp.arange(logits.shape[1])[None, None, :]
    picked = jnp.sum(jnp.where(route_table, logits[:, None, :], 0.0), axis=-1)
    raised = jnp.exp(picked)
    gate_values = raised / jnp.sum(raised, axis=1, keepdims=True)
    inside = routes < experts_axis
    gate_window = jnp.sum(jnp.where(inside, gate_values, 0.0), axis=1)
    expert_window = jnp.sum(jnp.where(inside, routes, 0), axis=1)
    present = jnp.any(inside, axis=1)
    capacity = local_rows // (experts_axis * experts_axis)
    member_table = (
        present[:, None] & (expert_window[:, None] == jnp.arange(experts_axis)[None, :])
    ).astype(jnp.int32)
    ranking = jnp.sum(jnp.cumsum(member_table, axis=0) * member_table, axis=1) - 1
    slot_index = expert_window * capacity + ranking
    select = (
        (jnp.arange(experts_axis * capacity)[:, None] == slot_index[None, :]) & present[None, :]
    ).astype(jnp.bfloat16)
    outgoing = (
        jnp.dot(select, normed_second, preferred_element_type=jnp.float32)
        .astype(jnp.bfloat16)
        .reshape(experts_axis, capacity, model_width)
    )
    gateup_here = expert_gateup[0]
    down_here = expert_down[0]
    hidden_units = down_here.shape[0]
    slot_items = scatter_blocks(outgoing, experts_axis, 2)
    flattened = slot_items.reshape(-1, slot_items.shape[-1])
    gate_up = jnp.dot(flattened, gateup_here, preferred_element_type=jnp.float32)
    active = (jax.nn.silu(gate_up[:, :hidden_units]) * gate_up[:, hidden_units:]).astype(
        jnp.bfloat16
    )
    result = (
        jnp.dot(active, down_here, preferred_element_type=jnp.float32)
        .astype(jnp.bfloat16)
        .reshape(slot_items.shape)
    )
    returned = scatter_blocks(result, experts_axis, 3)
    combined = jnp.dot(
        jnp.transpose(select), returned.reshape(-1, model_width), preferred_element_type=jnp.float32
    )
    expert_mix = (gate_window[:, None] * combined).astype(jnp.bfloat16)
    return (hidden, expert_mix)


def solution(mesh):
    return jax.shard_map(
        per_device,
        mesh=mesh,
        in_specs=(
            P(("group", "expert"), None),
            P(),
            P(),
            P("group", "expert"),
            P(None, "group", None),
            P("expert", "group"),
            P(),
            P(),
            P(),
            P(),
            P("expert", None, None),
            P("expert", None, None),
            P(("group", "expert"), None),
        ),
        out_specs=(P(("group", "expert"), None), P(("group", "expert"), None)),
        check_vma=False,
    )
```

```python
import functools
import math

import jax
import numpy as np
import jax.numpy as jnp
from jax import lax
from jax.experimental import pallas as pl
from jax.experimental.pallas import tpu as pltpu
from jax.sharding import PartitionSpec as P

MESH = pl.DeviceIdType.MESH

QUERY_HEADS = 32
KEY_VALUE_HEADS = 4
HEAD_DIMENSION = 128


epsilon = 1e-06
rope_theta = 1000000.0


def from_partner(block, axis, stride):
    count = lax.axis_size(axis)
    route = []
    for low in range(count):
        high = low | 1 << stride
        if high != low and high < count:
            route += [(low, high), (high, low)]
    return lax.ppermute(block, axis, route)


def gather_kernel(n_group, n_expert, heads_here, q_in, kv_in, o_in, h_in, gain_in, oqkv, oo, oxn, send, recv, xsend, xrecv, local, wqkv, wo, xn):
    e_here = lax.axis_index("expert")
    depth = HEAD_DIMENSION
    column = pl.multiple_of(lax.div(e_here * heads_here, QUERY_HEADS // KEY_VALUE_HEADS) * depth, depth)
    query_width = q_in.shape[1]
    wqkv[:, 0:query_width] = q_in[...].astype(jnp.bfloat16)
    wqkv[:, query_width : query_width + depth] = kv_in[0, :, pl.ds(column, depth)].astype(jnp.bfloat16)
    wqkv[:, query_width + depth : query_width + 2 * depth] = kv_in[1, :, pl.ds(column, depth)].astype(
        jnp.bfloat16
    )
    wo[...] = o_in[...].astype(jnp.bfloat16)
    xn[...] = norm_rows(h_in[...], gain_in[...]).astype(jnp.bfloat16)
    g = lax.axis_index("group")
    e = lax.axis_index("expert")
    columns = n_group // 2
    z = lax.div(g, 2)
    xh = lax.rem(g, 2)
    zp = lax.rem(z + 1, columns)
    zm = lax.rem(z + columns - 1, columns)
    plus_dev = (2 * zp + xh, e)
    minus_dev = (2 * zm + xh, e)
    pair_dev = (g + 1 - 2 * xh, e)
    core = lax.rem(e, 2)
    chip = lax.div(e, 2)
    chips = n_expert // 2
    mate_dev = (g, e + 1 - 2 * core)
    chip_devs = [(g, 2 * lax.rem(chip + j, chips) + core) for j in range(1, chips)]
    barrier = pltpu.get_barrier_semaphore()
    peers = [plus_dev, minus_dev, pair_dev, mate_dev] + chip_devs
    for dev in peers:
        pl.semaphore_signal(barrier, 1, device_id=dev, device_id_type=MESH)
    pl.semaphore_wait(barrier, len(peers))

    def slot(k, origin):
        return (oqkv, oo)[k].at[origin]

    sends = []

    def push(k, origin, src, dev):
        copy = pltpu.make_async_remote_copy(
            src_ref=src,
            dst_ref=slot(k, origin),
            send_sem=send.at[len(sends)],
            recv_sem=recv.at[k, origin],
            device_id=dev,
            device_id_type=MESH,
        )
        copy.start()
        sends.append(copy)

    def forward(origin, dev):
        for k in range(2):
            push(k, origin, slot(k, origin), dev)

    def arrive(origin):
        for k in range(2):
            pltpu.make_async_remote_copy(
                src_ref=slot(k, origin),
                dst_ref=slot(k, origin),
                send_sem=send.at[0],
                recv_sem=recv.at[k, origin],
                device_id=pair_dev,
                device_id_type=MESH,
            ).wait_recv()

    xsends = []

    def xpush(src, origin, dev):
        copy = pltpu.make_async_remote_copy(
            src_ref=src,
            dst_ref=oxn.at[origin],
            send_sem=xsend.at[len(xsends)],
            recv_sem=xrecv.at[origin],
            device_id=dev,
            device_id_type=MESH,
        )
        copy.start()
        xsends.append(copy)

    def xarrive(origin):
        pltpu.make_async_remote_copy(
            src_ref=oxn.at[origin],
            dst_ref=oxn.at[origin],
            send_sem=xsend.at[0],
            recv_sem=xrecv.at[origin],
            device_id=mate_dev,
            device_id_type=MESH,
        ).wait_recv()

    inputs = (wqkv, wo)
    own = [pltpu.make_async_copy(xn, oxn.at[e], local.at[2])]
    own += [pltpu.make_async_copy(inputs[k], slot(k, g), local.at[k]) for k in range(2)]
    for copy in own:
        copy.start()
    xpush(xn, e, mate_dev)
    for dev in chip_devs:
        xpush(xn, e, dev)
    for dev in (pair_dev, plus_dev, minus_dev):
        for k in range(2):
            push(k, g, inputs[k], dev)
    partner = g + 1 - 2 * xh
    arrive(partner)
    forward(partner, plus_dev)
    forward(partner, minus_dev)
    chip_origins = [2 * lax.rem(chip + j, chips) + core for j in range(1, chips)]
    normed_order = [chip_origins[0:2], chip_origins[2:5], chip_origins[5:]]
    for step in range(1, 4):
        behind = lax.rem(z - step + columns, columns)
        ahead = lax.rem(z + step, columns)
        for origin in (2 * behind, 2 * behind + 1):
            arrive(origin)
        for origin in ((2 * behind, 2 * behind + 1) if step < 3 else (2 * behind,)):
            forward(origin, plus_dev)
        for origin in (2 * ahead, 2 * ahead + 1):
            arrive(origin)
        for origin in ((2 * ahead, 2 * ahead + 1) if step < 3 else (2 * ahead + 1,)):
            forward(origin, minus_dev)
        for origin in normed_order[step - 1]:
            xarrive(origin)
            xpush(oxn.at[origin], origin, mate_dev)
    across = lax.rem(z + columns // 2, columns)
    arrive(2 * across)
    arrive(2 * across + 1)
    mate_core = 1 - core
    xarrive(e + 1 - 2 * core)
    for j in range(1, chips):
        xarrive(2 * lax.rem(chip + j, chips) + mate_core)
    for copy in sends + xsends:
        copy.wait_send()
    for copy in own:
        copy.wait()


def gather_all(q_in, kv_in, o_in, h_in, gain_in, n_group, n_expert):
    any_spec = pl.BlockSpec(memory_space=pl.ANY)
    vmem = pl.BlockSpec(memory_space=pltpu.VMEM)
    depth = HEAD_DIMENSION
    joined = (q_in.shape[0], q_in.shape[1] + 2 * depth)
    shapes = [
        jax.ShapeDtypeStruct((n_group,) + joined, jnp.bfloat16),
        jax.ShapeDtypeStruct((n_group,) + o_in.shape, jnp.bfloat16),
        jax.ShapeDtypeStruct((n_expert,) + h_in.shape, jnp.bfloat16),
    ]
    return pl.pallas_call(
        functools.partial(gather_kernel, n_group, n_expert, q_in.shape[1] // depth),
        out_shape=tuple(shapes),
        in_specs=[vmem] * 5,
        out_specs=tuple([any_spec] * 3),
        scratch_shapes=[
            pltpu.SemaphoreType.DMA((32,)),
            pltpu.SemaphoreType.DMA((2, n_group)),
            pltpu.SemaphoreType.DMA((n_expert,)),
            pltpu.SemaphoreType.DMA((n_expert,)),
            pltpu.SemaphoreType.DMA((3,)),
            pltpu.VMEM(joined, jnp.bfloat16),
            pltpu.VMEM(o_in.shape, jnp.bfloat16),
            pltpu.VMEM(h_in.shape, jnp.bfloat16),
        ],
        compiler_params=pltpu.CompilerParams(collective_id=0, has_side_effects=True),
    )(q_in, kv_in, o_in, h_in, gain_in)


def combine_kernel(blocks, attended_ref, weight_ref, out_ref, outgoing, incoming, send, recv):
    g = lax.axis_index("group")
    e = lax.axis_index("expert")
    core = lax.rem(e, 2)
    mate_dev = (g, e + 1 - 2 * core)
    rows = out_ref.shape[1]
    barrier = pltpu.get_barrier_semaphore()
    pl.semaphore_signal(barrier, 1, device_id=mate_dev, device_id_type=MESH)
    pl.semaphore_wait(barrier, 1)

    def partial(block):
        start = pl.multiple_of(block * rows, rows)
        return jnp.dot(
            attended_ref[pl.ds(start, rows), :], weight_ref[...], preferred_element_type=jnp.float32
        ).astype(jnp.bfloat16)

    for i in range(blocks):
        outgoing[i] = partial(2 * i + 1 - core)
    copy = pltpu.make_async_remote_copy(
        src_ref=outgoing,
        dst_ref=incoming,
        send_sem=send.at[0],
        recv_sem=recv.at[0],
        device_id=mate_dev,
        device_id_type=MESH,
    )
    copy.start()
    for i in range(blocks):
        out_ref[i] = partial(2 * i + core)
    copy.wait()
    for i in range(blocks):
        out_ref[i] = (out_ref[i].astype(jnp.float32) + incoming[i].astype(jnp.float32)).astype(
            jnp.bfloat16
        )


def project_and_combine(attended, weight, experts_axis):
    rows = attended.shape[0] // experts_axis
    blocks = experts_axis // 2
    shape = (blocks, rows, weight.shape[1])
    vmem = pl.BlockSpec(memory_space=pltpu.VMEM)
    return pl.pallas_call(
        functools.partial(combine_kernel, blocks),
        out_shape=jax.ShapeDtypeStruct(shape, jnp.bfloat16),
        in_specs=[vmem, vmem],
        out_specs=vmem,
        scratch_shapes=[
            pltpu.VMEM(shape, jnp.bfloat16),
            pltpu.VMEM(shape, jnp.bfloat16),
            pltpu.SemaphoreType.DMA((1,)),
            pltpu.SemaphoreType.DMA((1,)),
        ],
        compiler_params=pltpu.CompilerParams(collective_id=4, has_side_effects=True),
    )(attended, weight)


def combine_scatter_kernel(blocks, attended_ref, weight_ref, out_ref, outgoing, incoming, combined, send, recv, chip_send, chip_recv, local):
    g = lax.axis_index("group")
    e = lax.axis_index("expert")
    core = lax.rem(e, 2)
    chip = lax.div(e, 2)
    mate_dev = (g, e + 1 - 2 * core)
    chip_devs = [(g, 2 * lax.rem(chip + j, blocks) + core) for j in range(1, blocks)]
    rows = out_ref.shape[1]
    barrier = pltpu.get_barrier_semaphore()
    for dev in [mate_dev] + chip_devs:
        pl.semaphore_signal(barrier, 1, device_id=dev, device_id_type=MESH)
    pl.semaphore_wait(barrier, blocks)

    def partial(block):
        start = pl.multiple_of(block * rows, rows)
        return jnp.dot(
            attended_ref[pl.ds(start, rows), :], weight_ref[...], preferred_element_type=jnp.float32
        ).astype(jnp.bfloat16)

    for i in range(blocks):
        outgoing[i] = partial(2 * i + 1 - core)
    copy = pltpu.make_async_remote_copy(
        src_ref=outgoing,
        dst_ref=incoming,
        send_sem=send.at[0],
        recv_sem=recv.at[0],
        device_id=mate_dev,
        device_id_type=MESH,
    )
    copy.start()
    for i in range(blocks):
        combined[i] = partial(2 * i + core)
    copy.wait()
    pushes = []
    for j in range(1, blocks):
        i = lax.rem(chip + j, blocks)
        combined[i] = (combined[i].astype(jnp.float32) + incoming[i].astype(jnp.float32)).astype(
            jnp.bfloat16
        )
        push = pltpu.make_async_remote_copy(
            src_ref=combined.at[i],
            dst_ref=out_ref.at[chip],
            send_sem=chip_send.at[j],
            recv_sem=chip_recv.at[j],
            device_id=chip_devs[j - 1],
            device_id_type=MESH,
        )
        push.start()
        pushes.append(push)
    combined[chip] = (combined[chip].astype(jnp.float32) + incoming[chip].astype(jnp.float32)).astype(
        jnp.bfloat16
    )
    own = pltpu.make_async_copy(combined.at[chip], out_ref.at[chip], local.at[0])
    own.start()
    for push in pushes:
        push.wait()
    own.wait()


def combine_and_scatter(attended, weight, experts_axis):
    rows = attended.shape[0] // experts_axis
    blocks = experts_axis // 2
    shape = (blocks, rows, weight.shape[1])
    vmem = pl.BlockSpec(memory_space=pltpu.VMEM)
    return pl.pallas_call(
        functools.partial(combine_scatter_kernel, blocks),
        out_shape=jax.ShapeDtypeStruct(shape, jnp.bfloat16),
        in_specs=[vmem, vmem],
        out_specs=pl.BlockSpec(memory_space=pl.ANY),
        scratch_shapes=[
            pltpu.VMEM(shape, jnp.bfloat16),
            pltpu.VMEM(shape, jnp.bfloat16),
            pltpu.VMEM(shape, jnp.bfloat16),
            pltpu.SemaphoreType.DMA((1,)),
            pltpu.SemaphoreType.DMA((1,)),
            pltpu.SemaphoreType.DMA((blocks,)),
            pltpu.SemaphoreType.DMA((blocks,)),
            pltpu.SemaphoreType.DMA((1,)),
        ],
        compiler_params=pltpu.CompilerParams(collective_id=7, has_side_effects=True),
    )(attended, weight)


def mate_kernel(part, out, send, recv):
    g = lax.axis_index("group")
    e = lax.axis_index("expert")
    core = lax.rem(e, 2)
    mate_dev = (g, e + 1 - 2 * core)
    barrier = pltpu.get_barrier_semaphore()
    pl.semaphore_signal(barrier, 1, device_id=mate_dev, device_id_type=MESH)
    pl.semaphore_wait(barrier, 1)
    copy = pltpu.make_async_remote_copy(
        src_ref=part.at[:, 1 - core],
        dst_ref=out,
        send_sem=send.at[0],
        recv_sem=recv.at[0],
        device_id=mate_dev,
        device_id_type=MESH,
    )
    copy.start()
    copy.wait()


def exchange_with_mate(part):
    any_spec = pl.BlockSpec(memory_space=pl.ANY)
    shape = (part.shape[0],) + part.shape[2:]
    return pl.pallas_call(
        mate_kernel,
        out_shape=jax.ShapeDtypeStruct(shape, part.dtype),
        in_specs=[any_spec],
        out_specs=any_spec,
        scratch_shapes=[pltpu.SemaphoreType.DMA((1,)), pltpu.SemaphoreType.DMA((1,))],
        compiler_params=pltpu.CompilerParams(collective_id=4, has_side_effects=True),
    )(part)


def chip_scatter_kernel(chips, part, out, send, recv, local):
    g = lax.axis_index("group")
    e = lax.axis_index("expert")
    core = lax.rem(e, 2)
    chip = lax.div(e, 2)
    devs = [(g, 2 * lax.rem(chip + j, chips) + core) for j in range(1, chips)]
    barrier = pltpu.get_barrier_semaphore()
    for dev in devs:
        pl.semaphore_signal(barrier, 1, device_id=dev, device_id_type=MESH)
    pl.semaphore_wait(barrier, len(devs))
    copies = []
    for j in range(1, chips):
        copy = pltpu.make_async_remote_copy(
            src_ref=part.at[lax.rem(chip + j, chips)],
            dst_ref=out.at[chip],
            send_sem=send.at[j],
            recv_sem=recv.at[j],
            device_id=devs[j - 1],
            device_id_type=MESH,
        )
        copy.start()
        copies.append(copy)
    own = pltpu.make_async_copy(part.at[chip], out.at[chip], local.at[0])
    own.start()
    for copy in copies:
        copy.wait()
    own.wait()


def scatter_to_chips(part):
    chips = part.shape[0]
    any_spec = pl.BlockSpec(memory_space=pl.ANY)
    return pl.pallas_call(
        functools.partial(chip_scatter_kernel, chips),
        out_shape=jax.ShapeDtypeStruct(part.shape, part.dtype),
        in_specs=[any_spec],
        out_specs=any_spec,
        scratch_shapes=[
            pltpu.SemaphoreType.DMA((chips,)),
            pltpu.SemaphoreType.DMA((chips,)),
            pltpu.SemaphoreType.DMA((1,)),
        ],
        compiler_params=pltpu.CompilerParams(collective_id=5, has_side_effects=True),
    )(part)


def scatter_kernel(n_expert, part, out, send, recv, local):
    g = lax.axis_index("group")
    e = lax.axis_index("expert")
    barrier = pltpu.get_barrier_semaphore()
    for j in range(1, n_expert):
        pl.semaphore_signal(barrier, 1, device_id=(g, lax.rem(e + j, n_expert)), device_id_type=MESH)
    pl.semaphore_wait(barrier, n_expert - 1)
    copies = []
    for j in range(1, n_expert):
        peer = lax.rem(e + j, n_expert)
        copy = pltpu.make_async_remote_copy(
            src_ref=part.at[peer],
            dst_ref=out.at[e],
            send_sem=send.at[j],
            recv_sem=recv.at[j],
            device_id=(g, peer),
            device_id_type=MESH,
        )
        copy.start()
        copies.append(copy)
    own = pltpu.make_async_copy(part.at[e], out.at[e], local.at[0])
    own.start()
    for copy in copies:
        copy.wait()
    own.wait()


def scatter_blocks(part, n_expert, collective_id):
    any_spec = pl.BlockSpec(memory_space=pl.ANY)
    return pl.pallas_call(
        functools.partial(scatter_kernel, n_expert),
        out_shape=jax.ShapeDtypeStruct(part.shape, part.dtype),
        in_specs=[any_spec],
        out_specs=any_spec,
        scratch_shapes=[
            pltpu.SemaphoreType.DMA((n_expert,)),
            pltpu.SemaphoreType.DMA((n_expert,)),
            pltpu.SemaphoreType.DMA((1,)),
        ],
        compiler_params=pltpu.CompilerParams(collective_id=collective_id, has_side_effects=True),
    )(part)


def attention_kernel(scale, heads, q_ref, k_ref, v_ref, qpos_ref, kpos_ref, o_ref):
    allowed = kpos_ref[...] <= qpos_ref[...]
    keys = k_ref[...]
    values = v_ref[...]
    depth = keys.shape[1]
    for h in range(heads):
        query = q_ref[:, h * depth : (h + 1) * depth]
        scores = (
            lax.dot_general(
                query, keys, (((1,), (1,)), ((), ())), preferred_element_type=jnp.float32
            )
            * scale
        )
        weights = jnp.where(allowed, jnp.exp(scores), 0.0)
        denominators = jnp.sum(weights, axis=-1, keepdims=True)
        weighted = jnp.dot(
            weights.astype(jnp.bfloat16), values, preferred_element_type=jnp.float32
        )
        o_ref[:, h * depth : (h + 1) * depth] = (weighted / denominators).astype(o_ref.dtype)


def attention(queries, keys, values, query_places, key_places, scale):
    rows, width = queries.shape
    key_rows, depth = keys.shape
    block = min(256, rows)
    return pl.pallas_call(
        functools.partial(attention_kernel, scale, width // depth),
        out_shape=jax.ShapeDtypeStruct((rows, width), jnp.bfloat16),
        grid=(rows // block,),
        in_specs=[
            pl.BlockSpec((block, width), lambda i: (i, 0)),
            pl.BlockSpec((key_rows, depth), lambda i: (0, 0)),
            pl.BlockSpec((key_rows, depth), lambda i: (0, 0)),
            pl.BlockSpec((block, 1), lambda i: (i, 0)),
            pl.BlockSpec((1, key_rows), lambda i: (0, 0)),
        ],
        out_specs=pl.BlockSpec((block, width), lambda i: (i, 0)),
        cost_estimate=pl.CostEstimate(
            flops=4 * rows * key_rows * width,
            transcendentals=rows * key_rows * (width // depth),
            bytes_accessed=2 * (2 * rows * width + 2 * key_rows * depth),
        ),
    )(queries, keys, values, query_places.reshape(rows, 1), key_places.reshape(1, key_rows))


def norm_rows(values, gain_vector):
    widened = values.astype(jnp.float32)
    inverse_rms = lax.rsqrt(jnp.mean(widened * widened, axis=-1, keepdims=True) + epsilon)
    return widened * inverse_rms * gain_vector


def rotate(values, positions):
    half_width = values.shape[-1] // 2
    exponents = jnp.arange(half_width).astype(jnp.float32)
    inverse = jnp.exp(exponents * (-2.0 * math.log(rope_theta) / values.shape[-1]))
    angles = positions[:, None, None] * inverse[None, None, :]
    cosine_values = jnp.cos(angles)
    sine_values = jnp.sin(angles)
    first_half = values[..., :half_width]
    second = values[..., half_width:]
    return jnp.concatenate(
        [
            first_half * cosine_values - second * sine_values,
            second * cosine_values + first_half * sine_values,
        ],
        axis=-1,
    )


def local_positions(parity, row_count):
    indices = jnp.arange(row_count)
    quarter = row_count // 2
    offset = jnp.where(parity == 0, jnp.where(indices < quarter, 0, 2 * quarter), quarter)
    return indices + offset


def prep_kernel(query_width, x_ref, w_ref, cos_ref, sin_ref, qg_ref, kg_ref, q_out, k_out, v_out):
    x = x_ref[...]
    cosines = cos_ref[...]
    sines = sin_ref[...]
    depth = cosines.shape[1]

    def project(start, stop):
        return jnp.dot(x, w_ref[:, start:stop], preferred_element_type=jnp.float32).astype(jnp.bfloat16)

    def norm_rope(values, gain):
        values = values.astype(jnp.float32)
        inverse_rms = lax.rsqrt(jnp.mean(values * values, axis=-1, keepdims=True) + epsilon)
        normed = values * inverse_rms * gain
        return (normed * cosines + pltpu.roll(normed, depth // 2, 1) * sines).astype(jnp.bfloat16)

    queries = project(0, query_width)
    for h in range(queries.shape[1] // depth):
        q_out[:, h * depth : (h + 1) * depth] = norm_rope(
            queries[:, h * depth : (h + 1) * depth], qg_ref[...]
        )
    k_out[...] = norm_rope(project(query_width, query_width + depth), kg_ref[...])
    v_out[...] = project(query_width + depth, query_width + 2 * depth)


def prep(normed_rows, joined, cosines, sines, query_gain, key_gain):
    rows, width = normed_rows.shape
    depth = cosines.shape[1]
    query_width = joined.shape[1] - 2 * depth
    block = min(256, rows)
    whole = lambda shape: pl.BlockSpec(shape, lambda i: (0, 0))
    per_row = lambda cols: pl.BlockSpec((block, cols), lambda i: (i, 0))
    return pl.pallas_call(
        functools.partial(prep_kernel, query_width),
        out_shape=(
            jax.ShapeDtypeStruct((rows, query_width), jnp.bfloat16),
            jax.ShapeDtypeStruct((rows, depth), jnp.bfloat16),
            jax.ShapeDtypeStruct((rows, depth), jnp.bfloat16),
        ),
        grid=(rows // block,),
        in_specs=[
            per_row(width),
            whole(joined.shape),
            per_row(depth),
            per_row(depth),
            whole((1, depth)),
            whole((1, depth)),
        ],
        out_specs=(per_row(query_width), per_row(depth), per_row(depth)),
        cost_estimate=pl.CostEstimate(
            flops=2 * rows * width * joined.shape[1],
            transcendentals=rows * (query_width // depth + 1),
            bytes_accessed=2 * (rows * width + width * joined.shape[1] + rows * joined.shape[1]),
        ),
    )(normed_rows, joined, cosines, sines, query_gain.reshape(1, depth), key_gain.reshape(1, depth))


def rope_tables(parity, row_count, depth):
    half = depth // 2
    frequencies = rope_theta ** (-2.0 * np.arange(half) / depth)
    indices = np.arange(row_count)
    quarter = row_count // 2
    places = np.concatenate([np.where(indices < quarter, indices, indices + 2 * quarter), indices + quarter])
    angles = places[:, None].astype(np.float64) * frequencies[None, :]
    cosines = jnp.asarray(np.cos(angles), jnp.float32)
    sines = jnp.asarray(np.sin(angles), jnp.float32)
    cosines = lax.dynamic_slice_in_dim(cosines, parity * row_count, row_count, 0)
    sines = lax.dynamic_slice_in_dim(sines, parity * row_count, row_count, 0)
    return (
        jnp.concatenate([cosines, cosines], axis=1),
        jnp.concatenate([-sines, sines], axis=1),
    )


def per_device(
    hidden_in,
    norm_attention,
    norm_experts,
    query_master,
    trainer_key_value_weight,
    output_master,
    query_gain,
    key_gain,
    lengths,
    router,
    expert_gateup,
    expert_down,
    routes,
):
    experts_axis = lax.axis_size("expert")
    group_member = lax.axis_index("expert")
    group_index = lax.axis_index("group")
    local_head_count = QUERY_HEADS // experts_axis
    width_here = local_head_count * HEAD_DIMENSION
    common_head = group_member * local_head_count // (QUERY_HEADS // KEY_VALUE_HEADS)
    groups_axis = lax.axis_size("group")
    joined_parts, output_parts, normed_parts = gather_all(
        query_master,
        trainer_key_value_weight,
        output_master,
        hidden_in,
        norm_attention.reshape(1, -1),
        groups_axis,
        experts_axis,
    )
    model_width = hidden_in.shape[1]
    local_rows = normed_parts.shape[0] * normed_parts.shape[1]
    parity = group_index % 2
    own_places = local_positions(parity, local_rows)
    partner_places = local_positions(1 - parity, local_rows)
    cosines, sines = rope_tables(parity, local_rows, HEAD_DIMENSION)
    query_rows_list, key_rows, value_rows = prep(
        normed_parts.reshape(local_rows, model_width),
        joined_parts.reshape(model_width, -1),
        cosines,
        sines,
        query_gain,
        key_gain,
    )
    partner = from_partner(jnp.stack([key_rows, value_rows]), "group", 0)
    all_keys = jnp.concatenate([key_rows, partner[0]], axis=0)
    all_values = jnp.concatenate([value_rows, partner[1]], axis=0)
    key_places = jnp.concatenate([own_places, partner_places])
    valid_length = jnp.sum(jnp.where(jnp.arange(lengths.shape[0]) == group_index // 2, lengths, 0))
    past_end = jnp.full_like(key_places, 4 * key_places.shape[0])
    key_limits = jnp.where(key_places < valid_length, key_places, past_end)
    attended = attention(
        query_rows_list,
        all_keys,
        all_values,
        own_places,
        key_limits,
        HEAD_DIMENSION ** (-0.5),
    )
    output_weight = jnp.transpose(output_parts, (1, 0, 2)).reshape(output_parts.shape[1], -1)
    owned = combine_and_scatter(attended, output_weight, experts_axis)
    summed = jnp.sum(owned.astype(jnp.float32), axis=0)
    hidden = (hidden_in.astype(jnp.float32) + summed).astype(jnp.bfloat16)
    normed_second = norm_rows(hidden, norm_experts).astype(jnp.bfloat16)
    logits = jnp.dot(normed_second, router, preferred_element_type=jnp.float32)
    route_table = routes[:, :, None] == jnp.arange(logits.shape[1])[None, None, :]
    picked = jnp.sum(jnp.where(route_table, logits[:, None, :], 0.0), axis=-1)
    raised = jnp.exp(picked)
    gate_values = raised / jnp.sum(raised, axis=1, keepdims=True)
    inside = routes < experts_axis
    gate_window = jnp.sum(jnp.where(inside, gate_values, 0.0), axis=1)
    expert_window = jnp.sum(jnp.where(inside, routes, 0), axis=1)
    present = jnp.any(inside, axis=1)
    capacity = local_rows // (experts_axis * experts_axis)
    member_table = (
        present[:, None] & (expert_window[:, None] == jnp.arange(experts_axis)[None, :])
    ).astype(jnp.int32)
    ranking = jnp.sum(jnp.cumsum(member_table, axis=0) * member_table, axis=1) - 1
    slot_index = expert_window * capacity + ranking
    select = (
        (jnp.arange(experts_axis * capacity)[:, None] == slot_index[None, :]) & present[None, :]
    ).astype(jnp.bfloat16)
    select_slots = select.reshape(experts_axis, capacity, -1)
    outgoing = jnp.einsum(
        "jct,td->jcd", select_slots, normed_second, preferred_element_type=jnp.float32
    ).astype(jnp.bfloat16)
    gateup_here = expert_gateup[0]
    down_here = expert_down[0]
    hidden_units = down_here.shape[0]
    slot_items = scatter_blocks(outgoing, experts_axis, 2)
    gate_up = jnp.einsum("jcd,df->jcf", slot_items, gateup_here, preferred_element_type=jnp.float32)
    active = (jax.nn.silu(gate_up[..., :hidden_units]) * gate_up[..., hidden_units:]).astype(
        jnp.bfloat16
    )
    result = jnp.einsum(
        "jcf,fd->jcd", active, down_here, preferred_element_type=jnp.float32
    ).astype(jnp.bfloat16)
    returned = scatter_blocks(result, experts_axis, 3)
    combined = jnp.einsum(
        "jct,jcd->td", select_slots, returned, preferred_element_type=jnp.float32
    )
    expert_mix = (gate_window[:, None] * combined).astype(jnp.bfloat16)
    return (hidden, expert_mix)


def solution(mesh):
    return jax.shard_map(
        per_device,
        mesh=mesh,
        in_specs=(
            P(("group", "expert"), None),
            P(),
            P(),
            P("group", "expert"),
            P(None, "group", None),
            P("expert", "group"),
            P(),
            P(),
            P(),
            P(),
            P("expert", None, None),
            P("expert", None, None),
            P(("group", "expert"), None),
        ),
        out_specs=(P(("group", "expert"), None), P(("group", "expert"), None)),
        check_vma=False,
    )
```

```python
import functools
import math

import jax
import numpy as np
import jax.numpy as jnp
from jax import lax
from jax.experimental import pallas as pl
from jax.experimental.pallas import tpu as pltpu
from jax.sharding import PartitionSpec as P

MESH = pl.DeviceIdType.MESH

QUERY_HEADS = 32
KEY_VALUE_HEADS = 4
HEAD_DIMENSION = 128


epsilon = 1e-06
rope_theta = 1000000.0


def from_partner(block, axis, stride):
    count = lax.axis_size(axis)
    route = []
    for low in range(count):
        high = low | 1 << stride
        if high != low and high < count:
            route += [(low, high), (high, low)]
    return lax.ppermute(block, axis, route)


def gather_kernel(n_group, n_expert, heads_here, q_in, kv_in, o_in, h_in, gain_in, oqkv, oo, oxn, send, recv, xsend, xrecv, local, wqkv, wo, xn):
    e_here = lax.axis_index("expert")
    depth = HEAD_DIMENSION
    column = pl.multiple_of(lax.div(e_here * heads_here, QUERY_HEADS // KEY_VALUE_HEADS) * depth, depth)
    query_width = q_in.shape[1]
    wqkv[:, 0:query_width] = q_in[...].astype(jnp.bfloat16)
    wqkv[:, query_width : query_width + depth] = kv_in[0, :, pl.ds(column, depth)].astype(jnp.bfloat16)
    wqkv[:, query_width + depth : query_width + 2 * depth] = kv_in[1, :, pl.ds(column, depth)].astype(
        jnp.bfloat16
    )
    wo[...] = o_in[...].astype(jnp.bfloat16)
    xn[...] = norm_rows(h_in[...], gain_in[...]).astype(jnp.bfloat16)
    g = lax.axis_index("group")
    e = lax.axis_index("expert")
    columns = n_group // 2
    z = lax.div(g, 2)
    xh = lax.rem(g, 2)
    zp = lax.rem(z + 1, columns)
    zm = lax.rem(z + columns - 1, columns)
    plus_dev = (2 * zp + xh, e)
    minus_dev = (2 * zm + xh, e)
    pair_dev = (g + 1 - 2 * xh, e)
    core = lax.rem(e, 2)
    chip = lax.div(e, 2)
    chips = n_expert // 2
    mate_dev = (g, e + 1 - 2 * core)
    chip_devs = [(g, 2 * lax.rem(chip + j, chips) + core) for j in range(1, chips)]
    barrier = pltpu.get_barrier_semaphore()
    peers = [plus_dev, minus_dev, pair_dev, mate_dev] + chip_devs
    for dev in peers:
        pl.semaphore_signal(barrier, 1, device_id=dev, device_id_type=MESH)
    pl.semaphore_wait(barrier, len(peers))

    def slot(k, origin):
        return (oqkv, oo)[k].at[origin]

    sends = []

    def push(k, origin, src, dev):
        copy = pltpu.make_async_remote_copy(
            src_ref=src,
            dst_ref=slot(k, origin),
            send_sem=send.at[len(sends)],
            recv_sem=recv.at[k, origin],
            device_id=dev,
            device_id_type=MESH,
        )
        copy.start()
        sends.append(copy)

    def forward(origin, dev):
        for k in range(2):
            push(k, origin, slot(k, origin), dev)

    def arrive(origin):
        for k in range(2):
            pltpu.make_async_remote_copy(
                src_ref=slot(k, origin),
                dst_ref=slot(k, origin),
                send_sem=send.at[0],
                recv_sem=recv.at[k, origin],
                device_id=pair_dev,
                device_id_type=MESH,
            ).wait_recv()

    xsends = []

    def xpush(src, origin, dev):
        copy = pltpu.make_async_remote_copy(
            src_ref=src,
            dst_ref=oxn.at[origin],
            send_sem=xsend.at[len(xsends)],
            recv_sem=xrecv.at[origin],
            device_id=dev,
            device_id_type=MESH,
        )
        copy.start()
        xsends.append(copy)

    def xarrive(origin):
        pltpu.make_async_remote_copy(
            src_ref=oxn.at[origin],
            dst_ref=oxn.at[origin],
            send_sem=xsend.at[0],
            recv_sem=xrecv.at[origin],
            device_id=mate_dev,
            device_id_type=MESH,
        ).wait_recv()

    inputs = (wqkv, wo)
    own = [pltpu.make_async_copy(xn, oxn.at[e], local.at[2])]
    own += [pltpu.make_async_copy(inputs[k], slot(k, g), local.at[k]) for k in range(2)]
    for copy in own:
        copy.start()
    xpush(xn, e, mate_dev)
    for dev in chip_devs:
        xpush(xn, e, dev)
    for dev in (pair_dev, plus_dev, minus_dev):
        for k in range(2):
            push(k, g, inputs[k], dev)
    partner = g + 1 - 2 * xh
    arrive(partner)
    forward(partner, plus_dev)
    forward(partner, minus_dev)
    chip_origins = [2 * lax.rem(chip + j, chips) + core for j in range(1, chips)]
    normed_order = [chip_origins[0:2], chip_origins[2:5], chip_origins[5:]]
    for step in range(1, 4):
        behind = lax.rem(z - step + columns, columns)
        ahead = lax.rem(z + step, columns)
        for origin in (2 * behind, 2 * behind + 1):
            arrive(origin)
        for origin in ((2 * behind, 2 * behind + 1) if step < 3 else (2 * behind,)):
            forward(origin, plus_dev)
        for origin in (2 * ahead, 2 * ahead + 1):
            arrive(origin)
        for origin in ((2 * ahead, 2 * ahead + 1) if step < 3 else (2 * ahead + 1,)):
            forward(origin, minus_dev)
        for origin in normed_order[step - 1]:
            xarrive(origin)
            xpush(oxn.at[origin], origin, mate_dev)
    across = lax.rem(z + columns // 2, columns)
    arrive(2 * across)
    arrive(2 * across + 1)
    mate_core = 1 - core
    xarrive(e + 1 - 2 * core)
    for j in range(1, chips):
        xarrive(2 * lax.rem(chip + j, chips) + mate_core)
    for copy in sends + xsends:
        copy.wait_send()
    for copy in own:
        copy.wait()


def gather_all(q_in, kv_in, o_in, h_in, gain_in, n_group, n_expert):
    any_spec = pl.BlockSpec(memory_space=pl.ANY)
    vmem = pl.BlockSpec(memory_space=pltpu.VMEM)
    depth = HEAD_DIMENSION
    joined = (q_in.shape[0], q_in.shape[1] + 2 * depth)
    shapes = [
        jax.ShapeDtypeStruct((n_group,) + joined, jnp.bfloat16),
        jax.ShapeDtypeStruct((n_group,) + o_in.shape, jnp.bfloat16),
        jax.ShapeDtypeStruct((n_expert,) + h_in.shape, jnp.bfloat16),
    ]
    return pl.pallas_call(
        functools.partial(gather_kernel, n_group, n_expert, q_in.shape[1] // depth),
        out_shape=tuple(shapes),
        in_specs=[vmem] * 5,
        out_specs=tuple([any_spec] * 3),
        scratch_shapes=[
            pltpu.SemaphoreType.DMA((32,)),
            pltpu.SemaphoreType.DMA((2, n_group)),
            pltpu.SemaphoreType.DMA((n_expert,)),
            pltpu.SemaphoreType.DMA((n_expert,)),
            pltpu.SemaphoreType.DMA((3,)),
            pltpu.VMEM(joined, jnp.bfloat16),
            pltpu.VMEM(o_in.shape, jnp.bfloat16),
            pltpu.VMEM(h_in.shape, jnp.bfloat16),
        ],
        compiler_params=pltpu.CompilerParams(collective_id=0, has_side_effects=True),
    )(q_in, kv_in, o_in, h_in, gain_in)


def combine_kernel(blocks, attended_ref, weight_ref, out_ref, outgoing, incoming, send, recv):
    g = lax.axis_index("group")
    e = lax.axis_index("expert")
    core = lax.rem(e, 2)
    mate_dev = (g, e + 1 - 2 * core)
    rows = out_ref.shape[1]
    barrier = pltpu.get_barrier_semaphore()
    pl.semaphore_signal(barrier, 1, device_id=mate_dev, device_id_type=MESH)
    pl.semaphore_wait(barrier, 1)

    def partial(block):
        start = pl.multiple_of(block * rows, rows)
        return jnp.dot(
            attended_ref[pl.ds(start, rows), :], weight_ref[...], preferred_element_type=jnp.float32
        ).astype(jnp.bfloat16)

    for i in range(blocks):
        outgoing[i] = partial(2 * i + 1 - core)
    copy = pltpu.make_async_remote_copy(
        src_ref=outgoing,
        dst_ref=incoming,
        send_sem=send.at[0],
        recv_sem=recv.at[0],
        device_id=mate_dev,
        device_id_type=MESH,
    )
    copy.start()
    for i in range(blocks):
        out_ref[i] = partial(2 * i + core)
    copy.wait()
    for i in range(blocks):
        out_ref[i] = (out_ref[i].astype(jnp.float32) + incoming[i].astype(jnp.float32)).astype(
            jnp.bfloat16
        )


def project_and_combine(attended, weight, experts_axis):
    rows = attended.shape[0] // experts_axis
    blocks = experts_axis // 2
    shape = (blocks, rows, weight.shape[1])
    vmem = pl.BlockSpec(memory_space=pltpu.VMEM)
    return pl.pallas_call(
        functools.partial(combine_kernel, blocks),
        out_shape=jax.ShapeDtypeStruct(shape, jnp.bfloat16),
        in_specs=[vmem, vmem],
        out_specs=vmem,
        scratch_shapes=[
            pltpu.VMEM(shape, jnp.bfloat16),
            pltpu.VMEM(shape, jnp.bfloat16),
            pltpu.SemaphoreType.DMA((1,)),
            pltpu.SemaphoreType.DMA((1,)),
        ],
        compiler_params=pltpu.CompilerParams(collective_id=4, has_side_effects=True),
    )(attended, weight)


def combine_scatter_kernel(blocks, attended_ref, weight_ref, out_ref, outgoing, incoming, combined, send, recv, chip_send, chip_recv, local):
    g = lax.axis_index("group")
    e = lax.axis_index("expert")
    core = lax.rem(e, 2)
    chip = lax.div(e, 2)
    mate_dev = (g, e + 1 - 2 * core)
    chip_devs = [(g, 2 * lax.rem(chip + j, blocks) + core) for j in range(1, blocks)]
    rows = out_ref.shape[1]
    barrier = pltpu.get_barrier_semaphore()
    for dev in [mate_dev] + chip_devs:
        pl.semaphore_signal(barrier, 1, device_id=dev, device_id_type=MESH)
    pl.semaphore_wait(barrier, blocks)

    def partial(block):
        start = pl.multiple_of(block * rows, rows)
        return jnp.dot(
            attended_ref[pl.ds(start, rows), :], weight_ref[...], preferred_element_type=jnp.float32
        ).astype(jnp.bfloat16)

    for i in range(blocks):
        outgoing[i] = partial(2 * i + 1 - core)
    copy = pltpu.make_async_remote_copy(
        src_ref=outgoing,
        dst_ref=incoming,
        send_sem=send.at[0],
        recv_sem=recv.at[0],
        device_id=mate_dev,
        device_id_type=MESH,
    )
    copy.start()
    for i in range(blocks):
        combined[i] = partial(2 * i + core)
    copy.wait()
    pushes = []
    for j in range(1, blocks):
        i = lax.rem(chip + j, blocks)
        combined[i] = (combined[i].astype(jnp.float32) + incoming[i].astype(jnp.float32)).astype(
            jnp.bfloat16
        )
        push = pltpu.make_async_remote_copy(
            src_ref=combined.at[i],
            dst_ref=out_ref.at[chip],
            send_sem=chip_send.at[j],
            recv_sem=chip_recv.at[j],
            device_id=chip_devs[j - 1],
            device_id_type=MESH,
        )
        push.start()
        pushes.append(push)
    combined[chip] = (combined[chip].astype(jnp.float32) + incoming[chip].astype(jnp.float32)).astype(
        jnp.bfloat16
    )
    own = pltpu.make_async_copy(combined.at[chip], out_ref.at[chip], local.at[0])
    own.start()
    for push in pushes:
        push.wait()
    own.wait()


def combine_and_scatter(attended, weight, experts_axis):
    rows = attended.shape[0] // experts_axis
    blocks = experts_axis // 2
    shape = (blocks, rows, weight.shape[1])
    vmem = pl.BlockSpec(memory_space=pltpu.VMEM)
    return pl.pallas_call(
        functools.partial(combine_scatter_kernel, blocks),
        out_shape=jax.ShapeDtypeStruct(shape, jnp.bfloat16),
        in_specs=[vmem, vmem],
        out_specs=pl.BlockSpec(memory_space=pl.ANY),
        scratch_shapes=[
            pltpu.VMEM(shape, jnp.bfloat16),
            pltpu.VMEM(shape, jnp.bfloat16),
            pltpu.VMEM(shape, jnp.bfloat16),
            pltpu.SemaphoreType.DMA((1,)),
            pltpu.SemaphoreType.DMA((1,)),
            pltpu.SemaphoreType.DMA((blocks,)),
            pltpu.SemaphoreType.DMA((blocks,)),
            pltpu.SemaphoreType.DMA((1,)),
        ],
        compiler_params=pltpu.CompilerParams(collective_id=7, has_side_effects=True),
    )(attended, weight)


def mate_kernel(part, out, send, recv):
    g = lax.axis_index("group")
    e = lax.axis_index("expert")
    core = lax.rem(e, 2)
    mate_dev = (g, e + 1 - 2 * core)
    barrier = pltpu.get_barrier_semaphore()
    pl.semaphore_signal(barrier, 1, device_id=mate_dev, device_id_type=MESH)
    pl.semaphore_wait(barrier, 1)
    copy = pltpu.make_async_remote_copy(
        src_ref=part.at[:, 1 - core],
        dst_ref=out,
        send_sem=send.at[0],
        recv_sem=recv.at[0],
        device_id=mate_dev,
        device_id_type=MESH,
    )
    copy.start()
    copy.wait()


def exchange_with_mate(part):
    any_spec = pl.BlockSpec(memory_space=pl.ANY)
    shape = (part.shape[0],) + part.shape[2:]
    return pl.pallas_call(
        mate_kernel,
        out_shape=jax.ShapeDtypeStruct(shape, part.dtype),
        in_specs=[any_spec],
        out_specs=any_spec,
        scratch_shapes=[pltpu.SemaphoreType.DMA((1,)), pltpu.SemaphoreType.DMA((1,))],
        compiler_params=pltpu.CompilerParams(collective_id=4, has_side_effects=True),
    )(part)


def chip_scatter_kernel(chips, part, out, send, recv, local):
    g = lax.axis_index("group")
    e = lax.axis_index("expert")
    core = lax.rem(e, 2)
    chip = lax.div(e, 2)
    devs = [(g, 2 * lax.rem(chip + j, chips) + core) for j in range(1, chips)]
    barrier = pltpu.get_barrier_semaphore()
    for dev in devs:
        pl.semaphore_signal(barrier, 1, device_id=dev, device_id_type=MESH)
    pl.semaphore_wait(barrier, len(devs))
    copies = []
    for j in range(1, chips):
        copy = pltpu.make_async_remote_copy(
            src_ref=part.at[lax.rem(chip + j, chips)],
            dst_ref=out.at[chip],
            send_sem=send.at[j],
            recv_sem=recv.at[j],
            device_id=devs[j - 1],
            device_id_type=MESH,
        )
        copy.start()
        copies.append(copy)
    own = pltpu.make_async_copy(part.at[chip], out.at[chip], local.at[0])
    own.start()
    for copy in copies:
        copy.wait()
    own.wait()


def scatter_to_chips(part):
    chips = part.shape[0]
    any_spec = pl.BlockSpec(memory_space=pl.ANY)
    return pl.pallas_call(
        functools.partial(chip_scatter_kernel, chips),
        out_shape=jax.ShapeDtypeStruct(part.shape, part.dtype),
        in_specs=[any_spec],
        out_specs=any_spec,
        scratch_shapes=[
            pltpu.SemaphoreType.DMA((chips,)),
            pltpu.SemaphoreType.DMA((chips,)),
            pltpu.SemaphoreType.DMA((1,)),
        ],
        compiler_params=pltpu.CompilerParams(collective_id=5, has_side_effects=True),
    )(part)


def scatter_kernel(n_expert, part, out, send, recv, local):
    g = lax.axis_index("group")
    e = lax.axis_index("expert")
    barrier = pltpu.get_barrier_semaphore()
    for j in range(1, n_expert):
        pl.semaphore_signal(barrier, 1, device_id=(g, lax.rem(e + j, n_expert)), device_id_type=MESH)
    pl.semaphore_wait(barrier, n_expert - 1)
    copies = []
    for j in range(1, n_expert):
        peer = lax.rem(e + j, n_expert)
        copy = pltpu.make_async_remote_copy(
            src_ref=part.at[peer],
            dst_ref=out.at[e],
            send_sem=send.at[j],
            recv_sem=recv.at[j],
            device_id=(g, peer),
            device_id_type=MESH,
        )
        copy.start()
        copies.append(copy)
    own = pltpu.make_async_copy(part.at[e], out.at[e], local.at[0])
    own.start()
    for copy in copies:
        copy.wait()
    own.wait()


def scatter_blocks(part, n_expert, collective_id):
    any_spec = pl.BlockSpec(memory_space=pl.ANY)
    return pl.pallas_call(
        functools.partial(scatter_kernel, n_expert),
        out_shape=jax.ShapeDtypeStruct(part.shape, part.dtype),
        in_specs=[any_spec],
        out_specs=any_spec,
        scratch_shapes=[
            pltpu.SemaphoreType.DMA((n_expert,)),
            pltpu.SemaphoreType.DMA((n_expert,)),
            pltpu.SemaphoreType.DMA((1,)),
        ],
        compiler_params=pltpu.CompilerParams(collective_id=collective_id, has_side_effects=True),
    )(part)


def attention_kernel(scale, heads, q_ref, k_ref, v_ref, qpos_ref, kpos_ref, o_ref):
    allowed = kpos_ref[...] <= qpos_ref[...]
    keys = k_ref[...]
    values = v_ref[...]
    depth = keys.shape[1]
    for h in range(heads):
        query = q_ref[:, h * depth : (h + 1) * depth]
        scores = (
            lax.dot_general(
                query, keys, (((1,), (1,)), ((), ())), preferred_element_type=jnp.float32
            )
            * scale
        )
        weights = jnp.where(allowed, jnp.exp(scores), 0.0)
        denominators = jnp.sum(weights, axis=-1, keepdims=True)
        weighted = jnp.dot(
            weights.astype(jnp.bfloat16), values, preferred_element_type=jnp.float32
        )
        o_ref[:, h * depth : (h + 1) * depth] = (weighted / denominators).astype(o_ref.dtype)


def attention(queries, keys, values, query_places, key_places, scale):
    rows, width = queries.shape
    key_rows, depth = keys.shape
    block = min(256, rows)
    return pl.pallas_call(
        functools.partial(attention_kernel, scale, width // depth),
        out_shape=jax.ShapeDtypeStruct((rows, width), jnp.bfloat16),
        grid=(rows // block,),
        in_specs=[
            pl.BlockSpec((block, width), lambda i: (i, 0)),
            pl.BlockSpec((key_rows, depth), lambda i: (0, 0)),
            pl.BlockSpec((key_rows, depth), lambda i: (0, 0)),
            pl.BlockSpec((block, 1), lambda i: (i, 0)),
            pl.BlockSpec((1, key_rows), lambda i: (0, 0)),
        ],
        out_specs=pl.BlockSpec((block, width), lambda i: (i, 0)),
        cost_estimate=pl.CostEstimate(
            flops=4 * rows * key_rows * width,
            transcendentals=rows * key_rows * (width // depth),
            bytes_accessed=2 * (2 * rows * width + 2 * key_rows * depth),
        ),
    )(queries, keys, values, query_places.reshape(rows, 1), key_places.reshape(1, key_rows))


def norm_rows(values, gain_vector):
    widened = values.astype(jnp.float32)
    inverse_rms = lax.rsqrt(jnp.mean(widened * widened, axis=-1, keepdims=True) + epsilon)
    return widened * inverse_rms * gain_vector


def rotate(values, positions):
    half_width = values.shape[-1] // 2
    exponents = jnp.arange(half_width).astype(jnp.float32)
    inverse = jnp.exp(exponents * (-2.0 * math.log(rope_theta) / values.shape[-1]))
    angles = positions[:, None, None] * inverse[None, None, :]
    cosine_values = jnp.cos(angles)
    sine_values = jnp.sin(angles)
    first_half = values[..., :half_width]
    second = values[..., half_width:]
    return jnp.concatenate(
        [
            first_half * cosine_values - second * sine_values,
            second * cosine_values + first_half * sine_values,
        ],
        axis=-1,
    )


def local_positions(parity, row_count):
    indices = jnp.arange(row_count)
    quarter = row_count // 2
    offset = jnp.where(parity == 0, jnp.where(indices < quarter, 0, 2 * quarter), quarter)
    return indices + offset


def prep_kernel(query_width, x_ref, w_ref, table_ref, qg_ref, kg_ref, q_out, k_out, v_out):
    x = x_ref[...]
    block = x.shape[0]
    depth = table_ref.shape[1]
    parity = lax.rem(lax.axis_index("group"), 2)
    start = pl.multiple_of(parity * (table_ref.shape[0] // 2) + pl.program_id(0) * block, block)
    table = table_ref[pl.ds(start, block), :]
    swapped = pltpu.roll(table, depth // 2, 1)
    first_half = lax.broadcasted_iota(jnp.int32, table.shape, 1) < depth // 2
    cosines = jnp.where(first_half, table, swapped)
    sines = jnp.where(first_half, -swapped, table)

    def project(start, stop):
        return jnp.dot(x, w_ref[:, start:stop], preferred_element_type=jnp.float32).astype(jnp.bfloat16)

    def norm_rope(values, gain):
        values = values.astype(jnp.float32)
        inverse_rms = lax.rsqrt(jnp.mean(values * values, axis=-1, keepdims=True) + epsilon)
        normed = values * inverse_rms * gain
        return (normed * cosines + pltpu.roll(normed, depth // 2, 1) * sines).astype(jnp.bfloat16)

    queries = project(0, query_width)
    for h in range(queries.shape[1] // depth):
        q_out[:, h * depth : (h + 1) * depth] = norm_rope(
            queries[:, h * depth : (h + 1) * depth], qg_ref[...]
        )
    k_out[...] = norm_rope(project(query_width, query_width + depth), kg_ref[...])
    v_out[...] = project(query_width + depth, query_width + 2 * depth)


def prep(normed_rows, joined, table, query_gain, key_gain):
    rows, width = normed_rows.shape
    depth = table.shape[1]
    query_width = joined.shape[1] - 2 * depth
    block = min(256, rows)
    whole = lambda shape: pl.BlockSpec(shape, lambda i: (0, 0))
    per_row = lambda cols: pl.BlockSpec((block, cols), lambda i: (i, 0))
    return pl.pallas_call(
        functools.partial(prep_kernel, query_width),
        out_shape=(
            jax.ShapeDtypeStruct((rows, query_width), jnp.bfloat16),
            jax.ShapeDtypeStruct((rows, depth), jnp.bfloat16),
            jax.ShapeDtypeStruct((rows, depth), jnp.bfloat16),
        ),
        grid=(rows // block,),
        in_specs=[
            per_row(width),
            whole(joined.shape),
            whole(table.shape),
            whole((1, depth)),
            whole((1, depth)),
        ],
        out_specs=(per_row(query_width), per_row(depth), per_row(depth)),
        cost_estimate=pl.CostEstimate(
            flops=2 * rows * width * joined.shape[1],
            transcendentals=rows * (query_width // depth + 1),
            bytes_accessed=2 * (rows * width + width * joined.shape[1] + rows * joined.shape[1]),
        ),
    )(normed_rows, joined, table, query_gain.reshape(1, depth), key_gain.reshape(1, depth))


def rope_table(row_count, depth):
    half = depth // 2
    frequencies = rope_theta ** (-2.0 * np.arange(half) / depth)
    indices = np.arange(row_count)
    quarter = row_count // 2
    places = np.concatenate([np.where(indices < quarter, indices, indices + 2 * quarter), indices + quarter])
    angles = places[:, None].astype(np.float64) * frequencies[None, :]
    return jnp.asarray(np.concatenate([np.cos(angles), np.sin(angles)], axis=1), jnp.float32)

def per_device(
    hidden_in,
    norm_attention,
    norm_experts,
    query_master,
    trainer_key_value_weight,
    output_master,
    query_gain,
    key_gain,
    lengths,
    router,
    expert_gateup,
    expert_down,
    routes,
):
    experts_axis = lax.axis_size("expert")
    group_member = lax.axis_index("expert")
    group_index = lax.axis_index("group")
    local_head_count = QUERY_HEADS // experts_axis
    width_here = local_head_count * HEAD_DIMENSION
    common_head = group_member * local_head_count // (QUERY_HEADS // KEY_VALUE_HEADS)
    groups_axis = lax.axis_size("group")
    joined_parts, output_parts, normed_parts = gather_all(
        query_master,
        trainer_key_value_weight,
        output_master,
        hidden_in,
        norm_attention.reshape(1, -1),
        groups_axis,
        experts_axis,
    )
    model_width = hidden_in.shape[1]
    local_rows = normed_parts.shape[0] * normed_parts.shape[1]
    parity = group_index % 2
    own_places = local_positions(parity, local_rows)
    partner_places = local_positions(1 - parity, local_rows)
    query_rows_list, key_rows, value_rows = prep(
        normed_parts.reshape(local_rows, model_width),
        joined_parts.reshape(model_width, -1),
        rope_table(local_rows, HEAD_DIMENSION),
        query_gain,
        key_gain,
    )
    partner = from_partner(jnp.stack([key_rows, value_rows]), "group", 0)
    all_keys = jnp.concatenate([key_rows, partner[0]], axis=0)
    all_values = jnp.concatenate([value_rows, partner[1]], axis=0)
    key_places = jnp.concatenate([own_places, partner_places])
    valid_length = jnp.sum(jnp.where(jnp.arange(lengths.shape[0]) == group_index // 2, lengths, 0))
    past_end = jnp.full_like(key_places, 4 * key_places.shape[0])
    key_limits = jnp.where(key_places < valid_length, key_places, past_end)
    attended = attention(
        query_rows_list,
        all_keys,
        all_values,
        own_places,
        key_limits,
        HEAD_DIMENSION ** (-0.5),
    )
    output_weight = jnp.transpose(output_parts, (1, 0, 2)).reshape(output_parts.shape[1], -1)
    owned = combine_and_scatter(attended, output_weight, experts_axis)
    summed = jnp.sum(owned.astype(jnp.float32), axis=0)
    hidden = (hidden_in.astype(jnp.float32) + summed).astype(jnp.bfloat16)
    normed_second = norm_rows(hidden, norm_experts).astype(jnp.bfloat16)
    logits = jnp.dot(normed_second, router, preferred_element_type=jnp.float32)
    route_table = routes[:, :, None] == jnp.arange(logits.shape[1])[None, None, :]
    picked = jnp.sum(jnp.where(route_table, logits[:, None, :], 0.0), axis=-1)
    raised = jnp.exp(picked)
    gate_values = raised / jnp.sum(raised, axis=1, keepdims=True)
    inside = routes < experts_axis
    gate_window = jnp.sum(jnp.where(inside, gate_values, 0.0), axis=1)
    expert_window = jnp.sum(jnp.where(inside, routes, 0), axis=1)
    present = jnp.any(inside, axis=1)
    capacity = local_rows // (experts_axis * experts_axis)
    member_table = (
        present[:, None] & (expert_window[:, None] == jnp.arange(experts_axis)[None, :])
    ).astype(jnp.int32)
    ranking = jnp.sum(jnp.cumsum(member_table, axis=0) * member_table, axis=1) - 1
    slot_index = expert_window * capacity + ranking
    select = (
        (jnp.arange(experts_axis * capacity)[:, None] == slot_index[None, :]) & present[None, :]
    ).astype(jnp.bfloat16)
    select_slots = select.reshape(experts_axis, capacity, -1)
    outgoing = jnp.einsum(
        "jct,td->jcd", select_slots, normed_second, preferred_element_type=jnp.float32
    ).astype(jnp.bfloat16)
    gateup_here = expert_gateup[0]
    down_here = expert_down[0]
    hidden_units = down_here.shape[0]
    slot_items = scatter_blocks(outgoing, experts_axis, 2)
    gate_up = jnp.einsum("jcd,df->jcf", slot_items, gateup_here, preferred_element_type=jnp.float32)
    active = (jax.nn.silu(gate_up[..., :hidden_units]) * gate_up[..., hidden_units:]).astype(
        jnp.bfloat16
    )
    result = jnp.einsum(
        "jcf,fd->jcd", active, down_here, preferred_element_type=jnp.float32
    ).astype(jnp.bfloat16)
    returned = scatter_blocks(result, experts_axis, 3)
    combined = jnp.einsum(
        "jct,jcd->td", select_slots, returned, preferred_element_type=jnp.float32
    )
    expert_mix = (gate_window[:, None] * combined).astype(jnp.bfloat16)
    return (hidden, expert_mix)


def solution(mesh):
    return jax.shard_map(
        per_device,
        mesh=mesh,
        in_specs=(
            P(("group", "expert"), None),
            P(),
            P(),
            P("group", "expert"),
            P(None, "group", None),
            P("expert", "group"),
            P(),
            P(),
            P(),
            P(),
            P("expert", None, None),
            P("expert", None, None),
            P(("group", "expert"), None),
        ),
        out_specs=(P(("group", "expert"), None), P(("group", "expert"), None)),
        check_vma=False,
    )
```

```python
import functools
import math

import jax
import numpy as np
import jax.numpy as jnp
from jax import lax
from jax.experimental import pallas as pl
from jax.experimental.pallas import tpu as pltpu
from jax.sharding import PartitionSpec as P

MESH = pl.DeviceIdType.MESH

QUERY_HEADS = 32
KEY_VALUE_HEADS = 4
HEAD_DIMENSION = 128


epsilon = 1e-06
rope_theta = 1000000.0


def from_partner(block, axis, stride):
    count = lax.axis_size(axis)
    route = []
    for low in range(count):
        high = low | 1 << stride
        if high != low and high < count:
            route += [(low, high), (high, low)]
    return lax.ppermute(block, axis, route)


def gather_kernel(n_group, n_expert, heads_here, q_in, kv_in, o_in, h_in, gain_in, oqkv, oo, oxn, send, recv, xsend, xrecv, local, wqkv, wo, xn):
    e_here = lax.axis_index("expert")
    depth = HEAD_DIMENSION
    column = pl.multiple_of(lax.div(e_here * heads_here, QUERY_HEADS // KEY_VALUE_HEADS) * depth, depth)
    query_width = q_in.shape[1]
    wqkv[:, 0:query_width] = q_in[...].astype(jnp.bfloat16)
    wqkv[:, query_width : query_width + depth] = kv_in[0, :, pl.ds(column, depth)].astype(jnp.bfloat16)
    wqkv[:, query_width + depth : query_width + 2 * depth] = kv_in[1, :, pl.ds(column, depth)].astype(
        jnp.bfloat16
    )
    wo[...] = o_in[...].astype(jnp.bfloat16)
    xn[...] = norm_rows(h_in[...], gain_in[...]).astype(jnp.bfloat16)
    g = lax.axis_index("group")
    e = lax.axis_index("expert")
    columns = n_group // 2
    z = lax.div(g, 2)
    xh = lax.rem(g, 2)
    zp = lax.rem(z + 1, columns)
    zm = lax.rem(z + columns - 1, columns)
    plus_dev = (2 * zp + xh, e)
    minus_dev = (2 * zm + xh, e)
    pair_dev = (g + 1 - 2 * xh, e)
    core = lax.rem(e, 2)
    chip = lax.div(e, 2)
    chips = n_expert // 2
    mate_dev = (g, e + 1 - 2 * core)
    chip_devs = [(g, 2 * lax.rem(chip + j, chips) + core) for j in range(1, chips)]
    barrier = pltpu.get_barrier_semaphore()
    peers = [plus_dev, minus_dev, pair_dev, mate_dev] + chip_devs
    for dev in peers:
        pl.semaphore_signal(barrier, 1, device_id=dev, device_id_type=MESH)
    pl.semaphore_wait(barrier, len(peers))

    def slot(k, origin):
        return (oqkv, oo)[k].at[origin]

    sends = []

    def push(k, origin, src, dev):
        copy = pltpu.make_async_remote_copy(
            src_ref=src,
            dst_ref=slot(k, origin),
            send_sem=send.at[len(sends)],
            recv_sem=recv.at[k, origin],
            device_id=dev,
            device_id_type=MESH,
        )
        copy.start()
        sends.append(copy)

    def forward(origin, dev):
        for k in range(2):
            push(k, origin, slot(k, origin), dev)

    def arrive(origin):
        for k in range(2):
            pltpu.make_async_remote_copy(
                src_ref=slot(k, origin),
                dst_ref=slot(k, origin),
                send_sem=send.at[0],
                recv_sem=recv.at[k, origin],
                device_id=pair_dev,
                device_id_type=MESH,
            ).wait_recv()

    xsends = []

    def xpush(src, origin, dev):
        copy = pltpu.make_async_remote_copy(
            src_ref=src,
            dst_ref=oxn.at[origin],
            send_sem=xsend.at[len(xsends)],
            recv_sem=xrecv.at[origin],
            device_id=dev,
            device_id_type=MESH,
        )
        copy.start()
        xsends.append(copy)

    def xarrive(origin):
        pltpu.make_async_remote_copy(
            src_ref=oxn.at[origin],
            dst_ref=oxn.at[origin],
            send_sem=xsend.at[0],
            recv_sem=xrecv.at[origin],
            device_id=mate_dev,
            device_id_type=MESH,
        ).wait_recv()

    inputs = (wqkv, wo)
    own = [pltpu.make_async_copy(xn, oxn.at[e], local.at[2])]
    own += [pltpu.make_async_copy(inputs[k], slot(k, g), local.at[k]) for k in range(2)]
    for copy in own:
        copy.start()
    xpush(xn, e, mate_dev)
    for dev in chip_devs:
        xpush(xn, e, dev)
    for dev in (pair_dev, plus_dev, minus_dev):
        for k in range(2):
            push(k, g, inputs[k], dev)
    partner = g + 1 - 2 * xh
    arrive(partner)
    forward(partner, plus_dev)
    forward(partner, minus_dev)
    chip_origins = [2 * lax.rem(chip + j, chips) + core for j in range(1, chips)]
    normed_order = [chip_origins[0:2], chip_origins[2:5], chip_origins[5:]]
    for step in range(1, 4):
        behind = lax.rem(z - step + columns, columns)
        ahead = lax.rem(z + step, columns)
        for origin in (2 * behind, 2 * behind + 1):
            arrive(origin)
        for origin in ((2 * behind, 2 * behind + 1) if step < 3 else (2 * behind,)):
            forward(origin, plus_dev)
        for origin in (2 * ahead, 2 * ahead + 1):
            arrive(origin)
        for origin in ((2 * ahead, 2 * ahead + 1) if step < 3 else (2 * ahead + 1,)):
            forward(origin, minus_dev)
        for origin in normed_order[step - 1]:
            xarrive(origin)
            xpush(oxn.at[origin], origin, mate_dev)
    across = lax.rem(z + columns // 2, columns)
    arrive(2 * across)
    arrive(2 * across + 1)
    mate_core = 1 - core
    xarrive(e + 1 - 2 * core)
    for j in range(1, chips):
        xarrive(2 * lax.rem(chip + j, chips) + mate_core)
    for copy in sends + xsends:
        copy.wait_send()
    for copy in own:
        copy.wait()


def gather_all(q_in, kv_in, o_in, h_in, gain_in, n_group, n_expert):
    any_spec = pl.BlockSpec(memory_space=pl.ANY)
    vmem = pl.BlockSpec(memory_space=pltpu.VMEM)
    depth = HEAD_DIMENSION
    joined = (q_in.shape[0], q_in.shape[1] + 2 * depth)
    shapes = [
        jax.ShapeDtypeStruct((n_group,) + joined, jnp.bfloat16),
        jax.ShapeDtypeStruct((n_group,) + o_in.shape, jnp.bfloat16),
        jax.ShapeDtypeStruct((n_expert,) + h_in.shape, jnp.bfloat16),
    ]
    return pl.pallas_call(
        functools.partial(gather_kernel, n_group, n_expert, q_in.shape[1] // depth),
        out_shape=tuple(shapes),
        in_specs=[vmem] * 5,
        out_specs=tuple([any_spec] * 3),
        scratch_shapes=[
            pltpu.SemaphoreType.DMA((32,)),
            pltpu.SemaphoreType.DMA((2, n_group)),
            pltpu.SemaphoreType.DMA((n_expert,)),
            pltpu.SemaphoreType.DMA((n_expert,)),
            pltpu.SemaphoreType.DMA((3,)),
            pltpu.VMEM(joined, jnp.bfloat16),
            pltpu.VMEM(o_in.shape, jnp.bfloat16),
            pltpu.VMEM(h_in.shape, jnp.bfloat16),
        ],
        compiler_params=pltpu.CompilerParams(collective_id=0, has_side_effects=True),
    )(q_in, kv_in, o_in, h_in, gain_in)


def combine_kernel(blocks, attended_ref, weight_ref, out_ref, outgoing, incoming, send, recv):
    g = lax.axis_index("group")
    e = lax.axis_index("expert")
    core = lax.rem(e, 2)
    mate_dev = (g, e + 1 - 2 * core)
    rows = out_ref.shape[1]
    barrier = pltpu.get_barrier_semaphore()
    pl.semaphore_signal(barrier, 1, device_id=mate_dev, device_id_type=MESH)
    pl.semaphore_wait(barrier, 1)

    def partial(block):
        start = pl.multiple_of(block * rows, rows)
        return jnp.dot(
            attended_ref[pl.ds(start, rows), :], weight_ref[...], preferred_element_type=jnp.float32
        ).astype(jnp.bfloat16)

    for i in range(blocks):
        outgoing[i] = partial(2 * i + 1 - core)
    copy = pltpu.make_async_remote_copy(
        src_ref=outgoing,
        dst_ref=incoming,
        send_sem=send.at[0],
        recv_sem=recv.at[0],
        device_id=mate_dev,
        device_id_type=MESH,
    )
    copy.start()
    for i in range(blocks):
        out_ref[i] = partial(2 * i + core)
    copy.wait()
    for i in range(blocks):
        out_ref[i] = (out_ref[i].astype(jnp.float32) + incoming[i].astype(jnp.float32)).astype(
            jnp.bfloat16
        )


def project_and_combine(attended, weight, experts_axis):
    rows = attended.shape[0] // experts_axis
    blocks = experts_axis // 2
    shape = (blocks, rows, weight.shape[1])
    vmem = pl.BlockSpec(memory_space=pltpu.VMEM)
    return pl.pallas_call(
        functools.partial(combine_kernel, blocks),
        out_shape=jax.ShapeDtypeStruct(shape, jnp.bfloat16),
        in_specs=[vmem, vmem],
        out_specs=vmem,
        scratch_shapes=[
            pltpu.VMEM(shape, jnp.bfloat16),
            pltpu.VMEM(shape, jnp.bfloat16),
            pltpu.SemaphoreType.DMA((1,)),
            pltpu.SemaphoreType.DMA((1,)),
        ],
        compiler_params=pltpu.CompilerParams(collective_id=4, has_side_effects=True),
    )(attended, weight)


def combine_scatter_kernel(blocks, attended_ref, weight_ref, out_ref, outgoing, incoming, combined, send, recv, chip_send, chip_recv, local):
    g = lax.axis_index("group")
    e = lax.axis_index("expert")
    core = lax.rem(e, 2)
    chip = lax.div(e, 2)
    mate_dev = (g, e + 1 - 2 * core)
    chip_devs = [(g, 2 * lax.rem(chip + j, blocks) + core) for j in range(1, blocks)]
    rows = out_ref.shape[1]
    barrier = pltpu.get_barrier_semaphore()
    for dev in [mate_dev] + chip_devs:
        pl.semaphore_signal(barrier, 1, device_id=dev, device_id_type=MESH)
    pl.semaphore_wait(barrier, blocks)

    def partial(block):
        start = pl.multiple_of(block * rows, rows)
        return jnp.dot(
            attended_ref[pl.ds(start, rows), :], weight_ref[...], preferred_element_type=jnp.float32
        ).astype(jnp.bfloat16)

    for i in range(blocks):
        outgoing[i] = partial(2 * i + 1 - core)
    copy = pltpu.make_async_remote_copy(
        src_ref=outgoing,
        dst_ref=incoming,
        send_sem=send.at[0],
        recv_sem=recv.at[0],
        device_id=mate_dev,
        device_id_type=MESH,
    )
    copy.start()
    for i in range(blocks):
        combined[i] = partial(2 * i + core)
    copy.wait()
    pushes = []
    for j in range(1, blocks):
        i = lax.rem(chip + j, blocks)
        combined[i] = (combined[i].astype(jnp.float32) + incoming[i].astype(jnp.float32)).astype(
            jnp.bfloat16
        )
        push = pltpu.make_async_remote_copy(
            src_ref=combined.at[i],
            dst_ref=out_ref.at[chip],
            send_sem=chip_send.at[j],
            recv_sem=chip_recv.at[j],
            device_id=chip_devs[j - 1],
            device_id_type=MESH,
        )
        push.start()
        pushes.append(push)
    combined[chip] = (combined[chip].astype(jnp.float32) + incoming[chip].astype(jnp.float32)).astype(
        jnp.bfloat16
    )
    own = pltpu.make_async_copy(combined.at[chip], out_ref.at[chip], local.at[0])
    own.start()
    for push in pushes:
        push.wait()
    own.wait()


def combine_and_scatter(attended, weight, experts_axis):
    rows = attended.shape[0] // experts_axis
    blocks = experts_axis // 2
    shape = (blocks, rows, weight.shape[1])
    vmem = pl.BlockSpec(memory_space=pltpu.VMEM)
    return pl.pallas_call(
        functools.partial(combine_scatter_kernel, blocks),
        out_shape=jax.ShapeDtypeStruct(shape, jnp.bfloat16),
        in_specs=[vmem, vmem],
        out_specs=pl.BlockSpec(memory_space=pl.ANY),
        scratch_shapes=[
            pltpu.VMEM(shape, jnp.bfloat16),
            pltpu.VMEM(shape, jnp.bfloat16),
            pltpu.VMEM(shape, jnp.bfloat16),
            pltpu.SemaphoreType.DMA((1,)),
            pltpu.SemaphoreType.DMA((1,)),
            pltpu.SemaphoreType.DMA((blocks,)),
            pltpu.SemaphoreType.DMA((blocks,)),
            pltpu.SemaphoreType.DMA((1,)),
        ],
        compiler_params=pltpu.CompilerParams(collective_id=7, has_side_effects=True),
    )(attended, weight)


def mate_kernel(part, out, send, recv):
    g = lax.axis_index("group")
    e = lax.axis_index("expert")
    core = lax.rem(e, 2)
    mate_dev = (g, e + 1 - 2 * core)
    barrier = pltpu.get_barrier_semaphore()
    pl.semaphore_signal(barrier, 1, device_id=mate_dev, device_id_type=MESH)
    pl.semaphore_wait(barrier, 1)
    copy = pltpu.make_async_remote_copy(
        src_ref=part.at[:, 1 - core],
        dst_ref=out,
        send_sem=send.at[0],
        recv_sem=recv.at[0],
        device_id=mate_dev,
        device_id_type=MESH,
    )
    copy.start()
    copy.wait()


def exchange_with_mate(part):
    any_spec = pl.BlockSpec(memory_space=pl.ANY)
    shape = (part.shape[0],) + part.shape[2:]
    return pl.pallas_call(
        mate_kernel,
        out_shape=jax.ShapeDtypeStruct(shape, part.dtype),
        in_specs=[any_spec],
        out_specs=any_spec,
        scratch_shapes=[pltpu.SemaphoreType.DMA((1,)), pltpu.SemaphoreType.DMA((1,))],
        compiler_params=pltpu.CompilerParams(collective_id=4, has_side_effects=True),
    )(part)


def chip_scatter_kernel(chips, part, out, send, recv, local):
    g = lax.axis_index("group")
    e = lax.axis_index("expert")
    core = lax.rem(e, 2)
    chip = lax.div(e, 2)
    devs = [(g, 2 * lax.rem(chip + j, chips) + core) for j in range(1, chips)]
    barrier = pltpu.get_barrier_semaphore()
    for dev in devs:
        pl.semaphore_signal(barrier, 1, device_id=dev, device_id_type=MESH)
    pl.semaphore_wait(barrier, len(devs))
    copies = []
    for j in range(1, chips):
        copy = pltpu.make_async_remote_copy(
            src_ref=part.at[lax.rem(chip + j, chips)],
            dst_ref=out.at[chip],
            send_sem=send.at[j],
            recv_sem=recv.at[j],
            device_id=devs[j - 1],
            device_id_type=MESH,
        )
        copy.start()
        copies.append(copy)
    own = pltpu.make_async_copy(part.at[chip], out.at[chip], local.at[0])
    own.start()
    for copy in copies:
        copy.wait()
    own.wait()


def scatter_to_chips(part):
    chips = part.shape[0]
    any_spec = pl.BlockSpec(memory_space=pl.ANY)
    return pl.pallas_call(
        functools.partial(chip_scatter_kernel, chips),
        out_shape=jax.ShapeDtypeStruct(part.shape, part.dtype),
        in_specs=[any_spec],
        out_specs=any_spec,
        scratch_shapes=[
            pltpu.SemaphoreType.DMA((chips,)),
            pltpu.SemaphoreType.DMA((chips,)),
            pltpu.SemaphoreType.DMA((1,)),
        ],
        compiler_params=pltpu.CompilerParams(collective_id=5, has_side_effects=True),
    )(part)


def scatter_kernel(n_expert, part, out, send, recv, local):
    g = lax.axis_index("group")
    e = lax.axis_index("expert")
    barrier = pltpu.get_barrier_semaphore()
    for j in range(1, n_expert):
        pl.semaphore_signal(barrier, 1, device_id=(g, lax.rem(e + j, n_expert)), device_id_type=MESH)
    pl.semaphore_wait(barrier, n_expert - 1)
    copies = []
    for j in range(1, n_expert):
        peer = lax.rem(e + j, n_expert)
        copy = pltpu.make_async_remote_copy(
            src_ref=part.at[peer],
            dst_ref=out.at[e],
            send_sem=send.at[j],
            recv_sem=recv.at[j],
            device_id=(g, peer),
            device_id_type=MESH,
        )
        copy.start()
        copies.append(copy)
    own = pltpu.make_async_copy(part.at[e], out.at[e], local.at[0])
    own.start()
    for copy in copies:
        copy.wait()
    own.wait()


def scatter_blocks(part, n_expert, collective_id):
    any_spec = pl.BlockSpec(memory_space=pl.ANY)
    return pl.pallas_call(
        functools.partial(scatter_kernel, n_expert),
        out_shape=jax.ShapeDtypeStruct(part.shape, part.dtype),
        in_specs=[any_spec],
        out_specs=any_spec,
        scratch_shapes=[
            pltpu.SemaphoreType.DMA((n_expert,)),
            pltpu.SemaphoreType.DMA((n_expert,)),
            pltpu.SemaphoreType.DMA((1,)),
        ],
        compiler_params=pltpu.CompilerParams(collective_id=collective_id, has_side_effects=True),
    )(part)


def attention_kernel(scale, heads, q_ref, own_ref, far_ref, length_ref, o_ref):
    block = q_ref.shape[0]
    rows = own_ref.shape[1]
    half = rows // 2
    parity = lax.rem(lax.axis_index("group"), 2)

    def places(side, shape, axis, start):
        indices = lax.broadcasted_iota(jnp.int32, shape, axis) + start
        return indices + jnp.where(side == 0, jnp.where(indices < half, 0, rows), half)

    query_places = places(parity, (block, 1), 0, pl.program_id(0) * block)
    length = length_ref[0, 0]
    own_places = places(parity, (1, rows), 1, 0)
    far_places = places(1 - parity, (1, rows), 1, 0)
    own_allowed = (own_places <= query_places) & (own_places < length)
    far_allowed = (far_places <= query_places) & (far_places < length)
    own_keys, own_values = own_ref[0], own_ref[1]
    far_keys, far_values = far_ref[0], far_ref[1]
    depth = own_keys.shape[1]
    contract = (((1,), (1,)), ((), ()))
    for h in range(heads):
        query = q_ref[:, h * depth : (h + 1) * depth]
        own_weights = jnp.where(
            own_allowed,
            jnp.exp(lax.dot_general(query, own_keys, contract, preferred_element_type=jnp.float32) * scale),
            0.0,
        )
        far_weights = jnp.where(
            far_allowed,
            jnp.exp(lax.dot_general(query, far_keys, contract, preferred_element_type=jnp.float32) * scale),
            0.0,
        )
        denominators = jnp.sum(own_weights, axis=-1, keepdims=True) + jnp.sum(
            far_weights, axis=-1, keepdims=True
        )
        weighted = jnp.dot(
            own_weights.astype(jnp.bfloat16), own_values, preferred_element_type=jnp.float32
        ) + jnp.dot(far_weights.astype(jnp.bfloat16), far_values, preferred_element_type=jnp.float32)
        o_ref[:, h * depth : (h + 1) * depth] = (weighted / denominators).astype(o_ref.dtype)


def attention(queries, own_kv, far_kv, length, scale):
    rows, width = queries.shape
    key_rows, depth = own_kv.shape[1:]
    block = min(256, rows)
    pair = pl.BlockSpec((2, key_rows, depth), lambda i: (0, 0, 0))
    return pl.pallas_call(
        functools.partial(attention_kernel, scale, width // depth),
        out_shape=jax.ShapeDtypeStruct((rows, width), jnp.bfloat16),
        grid=(rows // block,),
        in_specs=[
            pl.BlockSpec((block, width), lambda i: (i, 0)),
            pair,
            pair,
            pl.BlockSpec(memory_space=pltpu.SMEM),
        ],
        out_specs=pl.BlockSpec((block, width), lambda i: (i, 0)),
        cost_estimate=pl.CostEstimate(
            flops=8 * rows * key_rows * width,
            transcendentals=2 * rows * key_rows * (width // depth),
            bytes_accessed=2 * (2 * rows * width + 4 * key_rows * depth),
        ),
    )(queries, own_kv, far_kv, length.reshape(1, 1))

def norm_rows(values, gain_vector):
    widened = values.astype(jnp.float32)
    inverse_rms = lax.rsqrt(jnp.mean(widened * widened, axis=-1, keepdims=True) + epsilon)
    return widened * inverse_rms * gain_vector


def rotate(values, positions):
    half_width = values.shape[-1] // 2
    exponents = jnp.arange(half_width).astype(jnp.float32)
    inverse = jnp.exp(exponents * (-2.0 * math.log(rope_theta) / values.shape[-1]))
    angles = positions[:, None, None] * inverse[None, None, :]
    cosine_values = jnp.cos(angles)
    sine_values = jnp.sin(angles)
    first_half = values[..., :half_width]
    second = values[..., half_width:]
    return jnp.concatenate(
        [
            first_half * cosine_values - second * sine_values,
            second * cosine_values + first_half * sine_values,
        ],
        axis=-1,
    )


def local_positions(parity, row_count):
    indices = jnp.arange(row_count)
    quarter = row_count // 2
    offset = jnp.where(parity == 0, jnp.where(indices < quarter, 0, 2 * quarter), quarter)
    return indices + offset


def prep_kernel(query_width, x_ref, w_ref, table_ref, qg_ref, kg_ref, q_out, kv_out):
    x = x_ref[...]
    block = x.shape[0]
    depth = table_ref.shape[1]
    parity = lax.rem(lax.axis_index("group"), 2)
    start = pl.multiple_of(parity * (table_ref.shape[0] // 2) + pl.program_id(0) * block, block)
    table = table_ref[pl.ds(start, block), :]
    swapped = pltpu.roll(table, depth // 2, 1)
    first_half = lax.broadcasted_iota(jnp.int32, table.shape, 1) < depth // 2
    cosines = jnp.where(first_half, table, swapped)
    sines = jnp.where(first_half, -swapped, table)

    def project(start, stop):
        return jnp.dot(x, w_ref[:, start:stop], preferred_element_type=jnp.float32).astype(jnp.bfloat16)

    def norm_rope(values, gain):
        values = values.astype(jnp.float32)
        inverse_rms = lax.rsqrt(jnp.mean(values * values, axis=-1, keepdims=True) + epsilon)
        normed = values * inverse_rms * gain
        return (normed * cosines + pltpu.roll(normed, depth // 2, 1) * sines).astype(jnp.bfloat16)

    queries = project(0, query_width)
    for h in range(queries.shape[1] // depth):
        q_out[:, h * depth : (h + 1) * depth] = norm_rope(
            queries[:, h * depth : (h + 1) * depth], qg_ref[...]
        )
    kv_out[0] = norm_rope(project(query_width, query_width + depth), kg_ref[...])
    kv_out[1] = project(query_width + depth, query_width + 2 * depth)


def prep(normed_rows, joined, table, query_gain, key_gain):
    rows, width = normed_rows.shape
    depth = table.shape[1]
    query_width = joined.shape[1] - 2 * depth
    block = min(256, rows)
    whole = lambda shape: pl.BlockSpec(shape, lambda i: (0, 0))
    per_row = lambda cols: pl.BlockSpec((block, cols), lambda i: (i, 0))
    return pl.pallas_call(
        functools.partial(prep_kernel, query_width),
        out_shape=(
            jax.ShapeDtypeStruct((rows, query_width), jnp.bfloat16),
            jax.ShapeDtypeStruct((2, rows, depth), jnp.bfloat16),
        ),
        grid=(rows // block,),
        in_specs=[
            per_row(width),
            whole(joined.shape),
            whole(table.shape),
            whole((1, depth)),
            whole((1, depth)),
        ],
        out_specs=(per_row(query_width), pl.BlockSpec((2, block, depth), lambda i: (0, i, 0))),
        cost_estimate=pl.CostEstimate(
            flops=2 * rows * width * joined.shape[1],
            transcendentals=rows * (query_width // depth + 1),
            bytes_accessed=2 * (rows * width + width * joined.shape[1] + rows * joined.shape[1]),
        ),
    )(normed_rows, joined, table, query_gain.reshape(1, depth), key_gain.reshape(1, depth))


def rope_table(row_count, depth):
    half = depth // 2
    frequencies = rope_theta ** (-2.0 * np.arange(half) / depth)
    indices = np.arange(row_count)
    quarter = row_count // 2
    places = np.concatenate([np.where(indices < quarter, indices, indices + 2 * quarter), indices + quarter])
    angles = places[:, None].astype(np.float64) * frequencies[None, :]
    return jnp.asarray(np.concatenate([np.cos(angles), np.sin(angles)], axis=1), jnp.float32)

def per_device(
    hidden_in,
    norm_attention,
    norm_experts,
    query_master,
    trainer_key_value_weight,
    output_master,
    query_gain,
    key_gain,
    lengths,
    router,
    expert_gateup,
    expert_down,
    routes,
):
    experts_axis = lax.axis_size("expert")
    group_member = lax.axis_index("expert")
    group_index = lax.axis_index("group")
    local_head_count = QUERY_HEADS // experts_axis
    width_here = local_head_count * HEAD_DIMENSION
    common_head = group_member * local_head_count // (QUERY_HEADS // KEY_VALUE_HEADS)
    groups_axis = lax.axis_size("group")
    joined_parts, output_parts, normed_parts = gather_all(
        query_master,
        trainer_key_value_weight,
        output_master,
        hidden_in,
        norm_attention.reshape(1, -1),
        groups_axis,
        experts_axis,
    )
    model_width = hidden_in.shape[1]
    local_rows = normed_parts.shape[0] * normed_parts.shape[1]
    parity = group_index % 2
    query_rows_list, key_values = prep(
        normed_parts.reshape(local_rows, model_width),
        joined_parts.reshape(model_width, -1),
        rope_table(local_rows, HEAD_DIMENSION),
        query_gain,
        key_gain,
    )
    partner = from_partner(key_values, "group", 0)
    valid_length = jnp.sum(jnp.where(jnp.arange(lengths.shape[0]) == group_index // 2, lengths, 0))
    attended = attention(
        query_rows_list,
        key_values,
        partner,
        valid_length.astype(jnp.int32),
        HEAD_DIMENSION ** (-0.5),
    )
    output_weight = jnp.transpose(output_parts, (1, 0, 2)).reshape(output_parts.shape[1], -1)
    owned = combine_and_scatter(attended, output_weight, experts_axis)
    summed = jnp.sum(owned.astype(jnp.float32), axis=0)
    hidden = (hidden_in.astype(jnp.float32) + summed).astype(jnp.bfloat16)
    normed_second = norm_rows(hidden, norm_experts).astype(jnp.bfloat16)
    logits = jnp.dot(normed_second, router, preferred_element_type=jnp.float32)
    route_table = routes[:, :, None] == jnp.arange(logits.shape[1])[None, None, :]
    picked = jnp.sum(jnp.where(route_table, logits[:, None, :], 0.0), axis=-1)
    raised = jnp.exp(picked)
    gate_values = raised / jnp.sum(raised, axis=1, keepdims=True)
    inside = routes < experts_axis
    gate_window = jnp.sum(jnp.where(inside, gate_values, 0.0), axis=1)
    expert_window = jnp.sum(jnp.where(inside, routes, 0), axis=1)
    present = jnp.any(inside, axis=1)
    capacity = local_rows // (experts_axis * experts_axis)
    member_table = (
        present[:, None] & (expert_window[:, None] == jnp.arange(experts_axis)[None, :])
    ).astype(jnp.int32)
    ranking = jnp.sum(jnp.cumsum(member_table, axis=0) * member_table, axis=1) - 1
    slot_index = expert_window * capacity + ranking
    select = (
        (jnp.arange(experts_axis * capacity)[:, None] == slot_index[None, :]) & present[None, :]
    ).astype(jnp.bfloat16)
    select_slots = select.reshape(experts_axis, capacity, -1)
    outgoing = jnp.einsum(
        "jct,td->jcd", select_slots, normed_second, preferred_element_type=jnp.float32
    ).astype(jnp.bfloat16)
    gateup_here = expert_gateup[0]
    down_here = expert_down[0]
    hidden_units = down_here.shape[0]
    slot_items = scatter_blocks(outgoing, experts_axis, 2)
    gate_up = jnp.einsum("jcd,df->jcf", slot_items, gateup_here, preferred_element_type=jnp.float32)
    active = (jax.nn.silu(gate_up[..., :hidden_units]) * gate_up[..., hidden_units:]).astype(
        jnp.bfloat16
    )
    result = jnp.einsum(
        "jcf,fd->jcd", active, down_here, preferred_element_type=jnp.float32
    ).astype(jnp.bfloat16)
    returned = scatter_blocks(result, experts_axis, 3)
    combined = jnp.einsum(
        "jct,jcd->td", select_slots, returned, preferred_element_type=jnp.float32
    )
    expert_mix = (gate_window[:, None] * combined).astype(jnp.bfloat16)
    return (hidden, expert_mix)


def solution(mesh):
    return jax.shard_map(
        per_device,
        mesh=mesh,
        in_specs=(
            P(("group", "expert"), None),
            P(),
            P(),
            P("group", "expert"),
            P(None, "group", None),
            P("expert", "group"),
            P(),
            P(),
            P(),
            P(),
            P("expert", None, None),
            P("expert", None, None),
            P(("group", "expert"), None),
        ),
        out_specs=(P(("group", "expert"), None), P(("group", "expert"), None)),
        check_vma=False,
    )
```

```python
import functools
import math

import jax
import numpy as np
import jax.numpy as jnp
from jax import lax
from jax.experimental import pallas as pl
from jax.experimental.pallas import tpu as pltpu
from jax.sharding import PartitionSpec as P

MESH = pl.DeviceIdType.MESH

QUERY_HEADS = 32
KEY_VALUE_HEADS = 4
HEAD_DIMENSION = 128


epsilon = 1e-06
rope_theta = 1000000.0


def from_partner(block, axis, stride):
    count = lax.axis_size(axis)
    route = []
    for low in range(count):
        high = low | 1 << stride
        if high != low and high < count:
            route += [(low, high), (high, low)]
    return lax.ppermute(block, axis, route)


def gather_kernel(n_group, n_expert, heads_here, q_in, kv_in, o_in, h_in, gain_in, oqkv, oo, oxn, send, recv, xsend, xrecv, local, wqkv, wo, xn):
    e_here = lax.axis_index("expert")
    depth = HEAD_DIMENSION
    column = pl.multiple_of(lax.div(e_here * heads_here, QUERY_HEADS // KEY_VALUE_HEADS) * depth, depth)
    query_width = q_in.shape[1]
    wqkv[:, 0:query_width] = q_in[...].astype(jnp.bfloat16)
    wqkv[:, query_width : query_width + depth] = kv_in[0, :, pl.ds(column, depth)].astype(jnp.bfloat16)
    wqkv[:, query_width + depth : query_width + 2 * depth] = kv_in[1, :, pl.ds(column, depth)].astype(
        jnp.bfloat16
    )
    wo[...] = o_in[...].astype(jnp.bfloat16)
    xn[...] = norm_rows(h_in[...], gain_in[...]).astype(jnp.bfloat16)
    g = lax.axis_index("group")
    e = lax.axis_index("expert")
    columns = n_group // 2
    z = lax.div(g, 2)
    xh = lax.rem(g, 2)
    zp = lax.rem(z + 1, columns)
    zm = lax.rem(z + columns - 1, columns)
    plus_dev = (2 * zp + xh, e)
    minus_dev = (2 * zm + xh, e)
    pair_dev = (g + 1 - 2 * xh, e)
    core = lax.rem(e, 2)
    chip = lax.div(e, 2)
    chips = n_expert // 2
    mate_dev = (g, e + 1 - 2 * core)
    chip_devs = [(g, 2 * lax.rem(chip + j, chips) + core) for j in range(1, chips)]
    barrier = pltpu.get_barrier_semaphore()
    peers = [plus_dev, minus_dev, pair_dev, mate_dev] + chip_devs
    for dev in peers:
        pl.semaphore_signal(barrier, 1, device_id=dev, device_id_type=MESH)
    pl.semaphore_wait(barrier, len(peers))

    def slot(k, origin):
        return (oqkv, oo)[k].at[origin]

    sends = []

    def push(k, origin, src, dev):
        copy = pltpu.make_async_remote_copy(
            src_ref=src,
            dst_ref=slot(k, origin),
            send_sem=send.at[len(sends)],
            recv_sem=recv.at[k, origin],
            device_id=dev,
            device_id_type=MESH,
        )
        copy.start()
        sends.append(copy)

    def forward(origin, dev):
        for k in range(2):
            push(k, origin, slot(k, origin), dev)

    def arrive(origin):
        for k in range(2):
            pltpu.make_async_remote_copy(
                src_ref=slot(k, origin),
                dst_ref=slot(k, origin),
                send_sem=send.at[0],
                recv_sem=recv.at[k, origin],
                device_id=pair_dev,
                device_id_type=MESH,
            ).wait_recv()

    xsends = []

    def xpush(src, origin, dev):
        copy = pltpu.make_async_remote_copy(
            src_ref=src,
            dst_ref=oxn.at[origin],
            send_sem=xsend.at[len(xsends)],
            recv_sem=xrecv.at[origin],
            device_id=dev,
            device_id_type=MESH,
        )
        copy.start()
        xsends.append(copy)

    def xarrive(origin):
        pltpu.make_async_remote_copy(
            src_ref=oxn.at[origin],
            dst_ref=oxn.at[origin],
            send_sem=xsend.at[0],
            recv_sem=xrecv.at[origin],
            device_id=mate_dev,
            device_id_type=MESH,
        ).wait_recv()

    inputs = (wqkv, wo)
    own = [pltpu.make_async_copy(xn, oxn.at[e], local.at[2])]
    own += [pltpu.make_async_copy(inputs[k], slot(k, g), local.at[k]) for k in range(2)]
    for copy in own:
        copy.start()
    xpush(xn, e, mate_dev)
    for dev in chip_devs:
        xpush(xn, e, dev)
    for dev in (pair_dev, plus_dev, minus_dev):
        for k in range(2):
            push(k, g, inputs[k], dev)
    partner = g + 1 - 2 * xh
    arrive(partner)
    forward(partner, plus_dev)
    forward(partner, minus_dev)
    chip_origins = [2 * lax.rem(chip + j, chips) + core for j in range(1, chips)]
    normed_order = [chip_origins[0:2], chip_origins[2:5], chip_origins[5:]]
    for step in range(1, 4):
        behind = lax.rem(z - step + columns, columns)
        ahead = lax.rem(z + step, columns)
        for origin in (2 * behind, 2 * behind + 1):
            arrive(origin)
        for origin in ((2 * behind, 2 * behind + 1) if step < 3 else (2 * behind,)):
            forward(origin, plus_dev)
        for origin in (2 * ahead, 2 * ahead + 1):
            arrive(origin)
        for origin in ((2 * ahead, 2 * ahead + 1) if step < 3 else (2 * ahead + 1,)):
            forward(origin, minus_dev)
        for origin in normed_order[step - 1]:
            xarrive(origin)
            xpush(oxn.at[origin], origin, mate_dev)
    across = lax.rem(z + columns // 2, columns)
    arrive(2 * across)
    arrive(2 * across + 1)
    mate_core = 1 - core
    xarrive(e + 1 - 2 * core)
    for j in range(1, chips):
        xarrive(2 * lax.rem(chip + j, chips) + mate_core)
    for copy in sends + xsends:
        copy.wait_send()
    for copy in own:
        copy.wait()


def gather_all(q_in, kv_in, o_in, h_in, gain_in, n_group, n_expert):
    any_spec = pl.BlockSpec(memory_space=pl.ANY)
    vmem = pl.BlockSpec(memory_space=pltpu.VMEM)
    depth = HEAD_DIMENSION
    joined = (q_in.shape[0], q_in.shape[1] + 2 * depth)
    shapes = [
        jax.ShapeDtypeStruct((n_group,) + joined, jnp.bfloat16),
        jax.ShapeDtypeStruct((n_group,) + o_in.shape, jnp.bfloat16),
        jax.ShapeDtypeStruct((n_expert,) + h_in.shape, jnp.bfloat16),
    ]
    return pl.pallas_call(
        functools.partial(gather_kernel, n_group, n_expert, q_in.shape[1] // depth),
        out_shape=tuple(shapes),
        in_specs=[vmem] * 5,
        out_specs=tuple([any_spec] * 3),
        scratch_shapes=[
            pltpu.SemaphoreType.DMA((32,)),
            pltpu.SemaphoreType.DMA((2, n_group)),
            pltpu.SemaphoreType.DMA((n_expert,)),
            pltpu.SemaphoreType.DMA((n_expert,)),
            pltpu.SemaphoreType.DMA((3,)),
            pltpu.VMEM(joined, jnp.bfloat16),
            pltpu.VMEM(o_in.shape, jnp.bfloat16),
            pltpu.VMEM(h_in.shape, jnp.bfloat16),
        ],
        compiler_params=pltpu.CompilerParams(collective_id=0, has_side_effects=True),
    )(q_in, kv_in, o_in, h_in, gain_in)


def combine_kernel(blocks, attended_ref, weight_ref, out_ref, outgoing, incoming, send, recv):
    g = lax.axis_index("group")
    e = lax.axis_index("expert")
    core = lax.rem(e, 2)
    mate_dev = (g, e + 1 - 2 * core)
    rows = out_ref.shape[1]
    barrier = pltpu.get_barrier_semaphore()
    pl.semaphore_signal(barrier, 1, device_id=mate_dev, device_id_type=MESH)
    pl.semaphore_wait(barrier, 1)

    def partial(block):
        start = pl.multiple_of(block * rows, rows)
        return jnp.dot(
            attended_ref[pl.ds(start, rows), :], weight_ref[...], preferred_element_type=jnp.float32
        ).astype(jnp.bfloat16)

    for i in range(blocks):
        outgoing[i] = partial(2 * i + 1 - core)
    copy = pltpu.make_async_remote_copy(
        src_ref=outgoing,
        dst_ref=incoming,
        send_sem=send.at[0],
        recv_sem=recv.at[0],
        device_id=mate_dev,
        device_id_type=MESH,
    )
    copy.start()
    for i in range(blocks):
        out_ref[i] = partial(2 * i + core)
    copy.wait()
    for i in range(blocks):
        out_ref[i] = (out_ref[i].astype(jnp.float32) + incoming[i].astype(jnp.float32)).astype(
            jnp.bfloat16
        )


def project_and_combine(attended, weight, experts_axis):
    rows = attended.shape[0] // experts_axis
    blocks = experts_axis // 2
    shape = (blocks, rows, weight.shape[1])
    vmem = pl.BlockSpec(memory_space=pltpu.VMEM)
    return pl.pallas_call(
        functools.partial(combine_kernel, blocks),
        out_shape=jax.ShapeDtypeStruct(shape, jnp.bfloat16),
        in_specs=[vmem, vmem],
        out_specs=vmem,
        scratch_shapes=[
            pltpu.VMEM(shape, jnp.bfloat16),
            pltpu.VMEM(shape, jnp.bfloat16),
            pltpu.SemaphoreType.DMA((1,)),
            pltpu.SemaphoreType.DMA((1,)),
        ],
        compiler_params=pltpu.CompilerParams(collective_id=4, has_side_effects=True),
    )(attended, weight)


def combine_scatter_kernel(blocks, attended_ref, weight_ref, out_ref, outgoing, incoming, combined, send, recv, chip_send, chip_recv, local):
    g = lax.axis_index("group")
    e = lax.axis_index("expert")
    core = lax.rem(e, 2)
    chip = lax.div(e, 2)
    mate_dev = (g, e + 1 - 2 * core)
    chip_devs = [(g, 2 * lax.rem(chip + j, blocks) + core) for j in range(1, blocks)]
    rows = out_ref.shape[1]
    barrier = pltpu.get_barrier_semaphore()
    for dev in [mate_dev] + chip_devs:
        pl.semaphore_signal(barrier, 1, device_id=dev, device_id_type=MESH)
    pl.semaphore_wait(barrier, blocks)

    def partial(block):
        start = pl.multiple_of(block * rows, rows)
        return jnp.dot(
            attended_ref[pl.ds(start, rows), :], weight_ref[...], preferred_element_type=jnp.float32
        ).astype(jnp.bfloat16)

    for i in range(blocks):
        outgoing[i] = partial(2 * i + 1 - core)
    copy = pltpu.make_async_remote_copy(
        src_ref=outgoing,
        dst_ref=incoming,
        send_sem=send.at[0],
        recv_sem=recv.at[0],
        device_id=mate_dev,
        device_id_type=MESH,
    )
    copy.start()
    for i in range(blocks):
        combined[i] = partial(2 * i + core)
    copy.wait()
    pushes = []
    for j in range(1, blocks):
        i = lax.rem(chip + j, blocks)
        combined[i] = (combined[i].astype(jnp.float32) + incoming[i].astype(jnp.float32)).astype(
            jnp.bfloat16
        )
        push = pltpu.make_async_remote_copy(
            src_ref=combined.at[i],
            dst_ref=out_ref.at[chip],
            send_sem=chip_send.at[j],
            recv_sem=chip_recv.at[j],
            device_id=chip_devs[j - 1],
            device_id_type=MESH,
        )
        push.start()
        pushes.append(push)
    combined[chip] = (combined[chip].astype(jnp.float32) + incoming[chip].astype(jnp.float32)).astype(
        jnp.bfloat16
    )
    own = pltpu.make_async_copy(combined.at[chip], out_ref.at[chip], local.at[0])
    own.start()
    for push in pushes:
        push.wait()
    own.wait()


def combine_and_scatter(attended, weight, experts_axis):
    rows = attended.shape[0] // experts_axis
    blocks = experts_axis // 2
    shape = (blocks, rows, weight.shape[1])
    vmem = pl.BlockSpec(memory_space=pltpu.VMEM)
    return pl.pallas_call(
        functools.partial(combine_scatter_kernel, blocks),
        out_shape=jax.ShapeDtypeStruct(shape, jnp.bfloat16),
        in_specs=[vmem, vmem],
        out_specs=pl.BlockSpec(memory_space=pl.ANY),
        scratch_shapes=[
            pltpu.VMEM(shape, jnp.bfloat16),
            pltpu.VMEM(shape, jnp.bfloat16),
            pltpu.VMEM(shape, jnp.bfloat16),
            pltpu.SemaphoreType.DMA((1,)),
            pltpu.SemaphoreType.DMA((1,)),
            pltpu.SemaphoreType.DMA((blocks,)),
            pltpu.SemaphoreType.DMA((blocks,)),
            pltpu.SemaphoreType.DMA((1,)),
        ],
        compiler_params=pltpu.CompilerParams(collective_id=7, has_side_effects=True),
    )(attended, weight)


def mate_kernel(part, out, send, recv):
    g = lax.axis_index("group")
    e = lax.axis_index("expert")
    core = lax.rem(e, 2)
    mate_dev = (g, e + 1 - 2 * core)
    barrier = pltpu.get_barrier_semaphore()
    pl.semaphore_signal(barrier, 1, device_id=mate_dev, device_id_type=MESH)
    pl.semaphore_wait(barrier, 1)
    copy = pltpu.make_async_remote_copy(
        src_ref=part.at[:, 1 - core],
        dst_ref=out,
        send_sem=send.at[0],
        recv_sem=recv.at[0],
        device_id=mate_dev,
        device_id_type=MESH,
    )
    copy.start()
    copy.wait()


def exchange_with_mate(part):
    any_spec = pl.BlockSpec(memory_space=pl.ANY)
    shape = (part.shape[0],) + part.shape[2:]
    return pl.pallas_call(
        mate_kernel,
        out_shape=jax.ShapeDtypeStruct(shape, part.dtype),
        in_specs=[any_spec],
        out_specs=any_spec,
        scratch_shapes=[pltpu.SemaphoreType.DMA((1,)), pltpu.SemaphoreType.DMA((1,))],
        compiler_params=pltpu.CompilerParams(collective_id=4, has_side_effects=True),
    )(part)


def chip_scatter_kernel(chips, part, out, send, recv, local):
    g = lax.axis_index("group")
    e = lax.axis_index("expert")
    core = lax.rem(e, 2)
    chip = lax.div(e, 2)
    devs = [(g, 2 * lax.rem(chip + j, chips) + core) for j in range(1, chips)]
    barrier = pltpu.get_barrier_semaphore()
    for dev in devs:
        pl.semaphore_signal(barrier, 1, device_id=dev, device_id_type=MESH)
    pl.semaphore_wait(barrier, len(devs))
    copies = []
    for j in range(1, chips):
        copy = pltpu.make_async_remote_copy(
            src_ref=part.at[lax.rem(chip + j, chips)],
            dst_ref=out.at[chip],
            send_sem=send.at[j],
            recv_sem=recv.at[j],
            device_id=devs[j - 1],
            device_id_type=MESH,
        )
        copy.start()
        copies.append(copy)
    own = pltpu.make_async_copy(part.at[chip], out.at[chip], local.at[0])
    own.start()
    for copy in copies:
        copy.wait()
    own.wait()


def scatter_to_chips(part):
    chips = part.shape[0]
    any_spec = pl.BlockSpec(memory_space=pl.ANY)
    return pl.pallas_call(
        functools.partial(chip_scatter_kernel, chips),
        out_shape=jax.ShapeDtypeStruct(part.shape, part.dtype),
        in_specs=[any_spec],
        out_specs=any_spec,
        scratch_shapes=[
            pltpu.SemaphoreType.DMA((chips,)),
            pltpu.SemaphoreType.DMA((chips,)),
            pltpu.SemaphoreType.DMA((1,)),
        ],
        compiler_params=pltpu.CompilerParams(collective_id=5, has_side_effects=True),
    )(part)


def scatter_kernel(n_expert, part, out, send, recv, local):
    g = lax.axis_index("group")
    e = lax.axis_index("expert")
    barrier = pltpu.get_barrier_semaphore()
    for j in range(1, n_expert):
        pl.semaphore_signal(barrier, 1, device_id=(g, lax.rem(e + j, n_expert)), device_id_type=MESH)
    pl.semaphore_wait(barrier, n_expert - 1)
    copies = []
    for j in range(1, n_expert):
        peer = lax.rem(e + j, n_expert)
        copy = pltpu.make_async_remote_copy(
            src_ref=part.at[peer],
            dst_ref=out.at[e],
            send_sem=send.at[j],
            recv_sem=recv.at[j],
            device_id=(g, peer),
            device_id_type=MESH,
        )
        copy.start()
        copies.append(copy)
    own = pltpu.make_async_copy(part.at[e], out.at[e], local.at[0])
    own.start()
    for copy in copies:
        copy.wait()
    own.wait()


def scatter_blocks(part, n_expert, collective_id):
    any_spec = pl.BlockSpec(memory_space=pl.ANY)
    return pl.pallas_call(
        functools.partial(scatter_kernel, n_expert),
        out_shape=jax.ShapeDtypeStruct(part.shape, part.dtype),
        in_specs=[any_spec],
        out_specs=any_spec,
        scratch_shapes=[
            pltpu.SemaphoreType.DMA((n_expert,)),
            pltpu.SemaphoreType.DMA((n_expert,)),
            pltpu.SemaphoreType.DMA((1,)),
        ],
        compiler_params=pltpu.CompilerParams(collective_id=collective_id, has_side_effects=True),
    )(part)


def attention_kernel(scale, heads, q_ref, own_ref, far_ref, length_ref, o_ref):
    block = q_ref.shape[0]
    rows = own_ref.shape[1]
    half = rows // 2
    parity = lax.rem(lax.axis_index("group"), 2)

    def places(side, shape, axis, start):
        indices = lax.broadcasted_iota(jnp.int32, shape, axis) + start
        return indices + jnp.where(side == 0, jnp.where(indices < half, 0, rows), half)

    query_places = places(parity, (block, 1), 0, pl.program_id(0) * block)
    length = length_ref[0, 0]
    own_places = places(parity, (1, rows), 1, 0)
    far_places = places(1 - parity, (1, rows), 1, 0)
    own_allowed = (own_places <= query_places) & (own_places < length)
    far_allowed = (far_places <= query_places) & (far_places < length)
    own_keys, own_values = own_ref[0], own_ref[1]
    far_keys, far_values = far_ref[0], far_ref[1]
    depth = own_keys.shape[1]
    contract = (((1,), (1,)), ((), ()))
    for h in range(heads):
        query = q_ref[:, h * depth : (h + 1) * depth]
        own_weights = jnp.where(
            own_allowed,
            jnp.exp(lax.dot_general(query, own_keys, contract, preferred_element_type=jnp.float32) * scale),
            0.0,
        )
        far_weights = jnp.where(
            far_allowed,
            jnp.exp(lax.dot_general(query, far_keys, contract, preferred_element_type=jnp.float32) * scale),
            0.0,
        )
        denominators = jnp.sum(own_weights, axis=-1, keepdims=True) + jnp.sum(
            far_weights, axis=-1, keepdims=True
        )
        weighted = jnp.dot(
            own_weights.astype(jnp.bfloat16), own_values, preferred_element_type=jnp.float32
        ) + jnp.dot(far_weights.astype(jnp.bfloat16), far_values, preferred_element_type=jnp.float32)
        o_ref[:, h * depth : (h + 1) * depth] = (weighted / denominators).astype(o_ref.dtype)


def attention(queries, own_kv, far_kv, length, scale):
    rows, width = queries.shape
    key_rows, depth = own_kv.shape[1:]
    block = min(256, rows)
    pair = pl.BlockSpec((2, key_rows, depth), lambda i: (0, 0, 0))
    return pl.pallas_call(
        functools.partial(attention_kernel, scale, width // depth),
        out_shape=jax.ShapeDtypeStruct((rows, width), jnp.bfloat16),
        grid=(rows // block,),
        in_specs=[
            pl.BlockSpec((block, width), lambda i: (i, 0)),
            pair,
            pair,
            pl.BlockSpec(memory_space=pltpu.SMEM),
        ],
        out_specs=pl.BlockSpec((block, width), lambda i: (i, 0)),
        cost_estimate=pl.CostEstimate(
            flops=8 * rows * key_rows * width,
            transcendentals=2 * rows * key_rows * (width // depth),
            bytes_accessed=2 * (2 * rows * width + 4 * key_rows * depth),
        ),
    )(queries, own_kv, far_kv, length.reshape(1, 1))

def norm_rows(values, gain_vector):
    widened = values.astype(jnp.float32)
    inverse_rms = lax.rsqrt(jnp.mean(widened * widened, axis=-1, keepdims=True) + epsilon)
    return widened * inverse_rms * gain_vector


def rotate(values, positions):
    half_width = values.shape[-1] // 2
    exponents = jnp.arange(half_width).astype(jnp.float32)
    inverse = jnp.exp(exponents * (-2.0 * math.log(rope_theta) / values.shape[-1]))
    angles = positions[:, None, None] * inverse[None, None, :]
    cosine_values = jnp.cos(angles)
    sine_values = jnp.sin(angles)
    first_half = values[..., :half_width]
    second = values[..., half_width:]
    return jnp.concatenate(
        [
            first_half * cosine_values - second * sine_values,
            second * cosine_values + first_half * sine_values,
        ],
        axis=-1,
    )


def local_positions(parity, row_count):
    indices = jnp.arange(row_count)
    quarter = row_count // 2
    offset = jnp.where(parity == 0, jnp.where(indices < quarter, 0, 2 * quarter), quarter)
    return indices + offset


def prep_kernel(query_width, for_queries, x_ref, w_ref, table_ref, gain_ref, out_ref):
    x = x_ref[...]
    block = x.shape[0]
    depth = table_ref.shape[1]
    parity = lax.rem(lax.axis_index("group"), 2)
    start = pl.multiple_of(parity * (table_ref.shape[0] // 2) + pl.program_id(0) * block, block)
    table = table_ref[pl.ds(start, block), :]
    swapped = pltpu.roll(table, depth // 2, 1)
    first_half = lax.broadcasted_iota(jnp.int32, table.shape, 1) < depth // 2
    cosines = jnp.where(first_half, table, swapped)
    sines = jnp.where(first_half, -swapped, table)

    def project(start, stop):
        return jnp.dot(x, w_ref[:, start:stop], preferred_element_type=jnp.float32).astype(jnp.bfloat16)

    def norm_rope(values, gain):
        values = values.astype(jnp.float32)
        inverse_rms = lax.rsqrt(jnp.mean(values * values, axis=-1, keepdims=True) + epsilon)
        normed = values * inverse_rms * gain
        return (normed * cosines + pltpu.roll(normed, depth // 2, 1) * sines).astype(jnp.bfloat16)

    if for_queries:
        queries = project(0, query_width)
        for h in range(queries.shape[1] // depth):
            out_ref[:, h * depth : (h + 1) * depth] = norm_rope(
                queries[:, h * depth : (h + 1) * depth], gain_ref[...]
            )
    else:
        out_ref[0] = norm_rope(project(query_width, query_width + depth), gain_ref[...])
        out_ref[1] = project(query_width + depth, query_width + 2 * depth)


def prep(normed_rows, joined, table, gain, for_queries):
    rows, width = normed_rows.shape
    depth = table.shape[1]
    query_width = joined.shape[1] - 2 * depth
    block = min(256, rows)
    whole = lambda shape: pl.BlockSpec(shape, lambda i: (0, 0))
    if for_queries:
        out_shape = jax.ShapeDtypeStruct((rows, query_width), jnp.bfloat16)
        out_spec = pl.BlockSpec((block, query_width), lambda i: (i, 0))
        columns = query_width
    else:
        out_shape = jax.ShapeDtypeStruct((2, rows, depth), jnp.bfloat16)
        out_spec = pl.BlockSpec((2, block, depth), lambda i: (0, i, 0))
        columns = 2 * depth
    return pl.pallas_call(
        functools.partial(prep_kernel, query_width, for_queries),
        out_shape=out_shape,
        grid=(rows // block,),
        in_specs=[
            pl.BlockSpec((block, width), lambda i: (i, 0)),
            whole(joined.shape),
            whole(table.shape),
            whole((1, depth)),
        ],
        out_specs=out_spec,
        cost_estimate=pl.CostEstimate(
            flops=2 * rows * width * columns,
            transcendentals=rows * (columns // depth),
            bytes_accessed=2 * (rows * width + width * columns + rows * columns),
        ),
    )(normed_rows, joined, table, gain.reshape(1, depth))

def rope_table(row_count, depth):
    half = depth // 2
    frequencies = rope_theta ** (-2.0 * np.arange(half) / depth)
    indices = np.arange(row_count)
    quarter = row_count // 2
    places = np.concatenate([np.where(indices < quarter, indices, indices + 2 * quarter), indices + quarter])
    angles = places[:, None].astype(np.float64) * frequencies[None, :]
    return jnp.asarray(np.concatenate([np.cos(angles), np.sin(angles)], axis=1), jnp.float32)

def per_device(
    hidden_in,
    norm_attention,
    norm_experts,
    query_master,
    trainer_key_value_weight,
    output_master,
    query_gain,
    key_gain,
    lengths,
    router,
    expert_gateup,
    expert_down,
    routes,
):
    experts_axis = lax.axis_size("expert")
    group_member = lax.axis_index("expert")
    group_index = lax.axis_index("group")
    local_head_count = QUERY_HEADS // experts_axis
    width_here = local_head_count * HEAD_DIMENSION
    common_head = group_member * local_head_count // (QUERY_HEADS // KEY_VALUE_HEADS)
    groups_axis = lax.axis_size("group")
    joined_parts, output_parts, normed_parts = gather_all(
        query_master,
        trainer_key_value_weight,
        output_master,
        hidden_in,
        norm_attention.reshape(1, -1),
        groups_axis,
        experts_axis,
    )
    model_width = hidden_in.shape[1]
    local_rows = normed_parts.shape[0] * normed_parts.shape[1]
    parity = group_index % 2
    prep_args = (
        normed_parts.reshape(local_rows, model_width),
        joined_parts.reshape(model_width, -1),
        rope_table(local_rows, HEAD_DIMENSION),
    )
    key_values = prep(*prep_args, key_gain, False)
    query_rows_list = prep(*prep_args, query_gain, True)
    partner = from_partner(key_values, "group", 0)
    valid_length = jnp.sum(jnp.where(jnp.arange(lengths.shape[0]) == group_index // 2, lengths, 0))
    attended = attention(
        query_rows_list,
        key_values,
        partner,
        valid_length.astype(jnp.int32),
        HEAD_DIMENSION ** (-0.5),
    )
    output_weight = jnp.transpose(output_parts, (1, 0, 2)).reshape(output_parts.shape[1], -1)
    owned = combine_and_scatter(attended, output_weight, experts_axis)
    summed = jnp.sum(owned.astype(jnp.float32), axis=0)
    hidden = (hidden_in.astype(jnp.float32) + summed).astype(jnp.bfloat16)
    normed_second = norm_rows(hidden, norm_experts).astype(jnp.bfloat16)
    logits = jnp.dot(normed_second, router, preferred_element_type=jnp.float32)
    route_table = routes[:, :, None] == jnp.arange(logits.shape[1])[None, None, :]
    picked = jnp.sum(jnp.where(route_table, logits[:, None, :], 0.0), axis=-1)
    raised = jnp.exp(picked)
    gate_values = raised / jnp.sum(raised, axis=1, keepdims=True)
    inside = routes < experts_axis
    gate_window = jnp.sum(jnp.where(inside, gate_values, 0.0), axis=1)
    expert_window = jnp.sum(jnp.where(inside, routes, 0), axis=1)
    present = jnp.any(inside, axis=1)
    capacity = local_rows // (experts_axis * experts_axis)
    member_table = (
        present[:, None] & (expert_window[:, None] == jnp.arange(experts_axis)[None, :])
    ).astype(jnp.int32)
    ranking = jnp.sum(jnp.cumsum(member_table, axis=0) * member_table, axis=1) - 1
    slot_index = expert_window * capacity + ranking
    select = (
        (jnp.arange(experts_axis * capacity)[:, None] == slot_index[None, :]) & present[None, :]
    ).astype(jnp.bfloat16)
    select_slots = select.reshape(experts_axis, capacity, -1)
    outgoing = jnp.einsum(
        "jct,td->jcd", select_slots, normed_second, preferred_element_type=jnp.float32
    ).astype(jnp.bfloat16)
    gateup_here = expert_gateup[0]
    down_here = expert_down[0]
    hidden_units = down_here.shape[0]
    slot_items = scatter_blocks(outgoing, experts_axis, 2)
    gate_up = jnp.einsum("jcd,df->jcf", slot_items, gateup_here, preferred_element_type=jnp.float32)
    active = (jax.nn.silu(gate_up[..., :hidden_units]) * gate_up[..., hidden_units:]).astype(
        jnp.bfloat16
    )
    result = jnp.einsum(
        "jcf,fd->jcd", active, down_here, preferred_element_type=jnp.float32
    ).astype(jnp.bfloat16)
    returned = scatter_blocks(result, experts_axis, 3)
    combined = jnp.einsum(
        "jct,jcd->td", select_slots, returned, preferred_element_type=jnp.float32
    )
    expert_mix = (gate_window[:, None] * combined).astype(jnp.bfloat16)
    return (hidden, expert_mix)


def solution(mesh):
    return jax.shard_map(
        per_device,
        mesh=mesh,
        in_specs=(
            P(("group", "expert"), None),
            P(),
            P(),
            P("group", "expert"),
            P(None, "group", None),
            P("expert", "group"),
            P(),
            P(),
            P(),
            P(),
            P("expert", None, None),
            P("expert", None, None),
            P(("group", "expert"), None),
        ),
        out_specs=(P(("group", "expert"), None), P(("group", "expert"), None)),
        check_vma=False,
    )
```

```python
import functools
import math

import jax
import numpy as np
import jax.numpy as jnp
from jax import lax
from jax.experimental import pallas as pl
from jax.experimental.pallas import tpu as pltpu
from jax.sharding import PartitionSpec as P

MESH = pl.DeviceIdType.MESH

QUERY_HEADS = 32
KEY_VALUE_HEADS = 4
HEAD_DIMENSION = 128


epsilon = 1e-06
rope_theta = 1000000.0


def from_partner(block, axis, stride):
    count = lax.axis_size(axis)
    route = []
    for low in range(count):
        high = low | 1 << stride
        if high != low and high < count:
            route += [(low, high), (high, low)]
    return lax.ppermute(block, axis, route)


def gather_kernel(n_group, n_expert, heads_here, q_in, kv_in, o_in, h_in, gain_in, oqkv, oo, oxn, send, recv, xsend, xrecv, local, wqkv, wo, xn):
    e_here = lax.axis_index("expert")
    depth = HEAD_DIMENSION
    column = pl.multiple_of(lax.div(e_here * heads_here, QUERY_HEADS // KEY_VALUE_HEADS) * depth, depth)
    query_width = q_in.shape[1]
    wqkv[:, 0:query_width] = q_in[...].astype(jnp.bfloat16)
    wqkv[:, query_width : query_width + depth] = kv_in[0, :, pl.ds(column, depth)].astype(jnp.bfloat16)
    wqkv[:, query_width + depth : query_width + 2 * depth] = kv_in[1, :, pl.ds(column, depth)].astype(
        jnp.bfloat16
    )
    wo[...] = o_in[...].astype(jnp.bfloat16)
    xn[...] = norm_rows(h_in[...], gain_in[...]).astype(jnp.bfloat16)
    g = lax.axis_index("group")
    e = lax.axis_index("expert")
    columns = n_group // 2
    z = lax.div(g, 2)
    xh = lax.rem(g, 2)
    zp = lax.rem(z + 1, columns)
    zm = lax.rem(z + columns - 1, columns)
    plus_dev = (2 * zp + xh, e)
    minus_dev = (2 * zm + xh, e)
    pair_dev = (g + 1 - 2 * xh, e)
    core = lax.rem(e, 2)
    chip = lax.div(e, 2)
    chips = n_expert // 2
    mate_dev = (g, e + 1 - 2 * core)
    chip_devs = [(g, 2 * lax.rem(chip + j, chips) + core) for j in range(1, chips)]
    barrier = pltpu.get_barrier_semaphore()
    peers = [plus_dev, minus_dev, pair_dev, mate_dev] + chip_devs
    for dev in peers:
        pl.semaphore_signal(barrier, 1, device_id=dev, device_id_type=MESH)
    pl.semaphore_wait(barrier, len(peers))

    def slot(k, origin):
        return (oqkv, oo)[k].at[origin]

    sends = []

    def push(k, origin, src, dev):
        copy = pltpu.make_async_remote_copy(
            src_ref=src,
            dst_ref=slot(k, origin),
            send_sem=send.at[len(sends)],
            recv_sem=recv.at[k, origin],
            device_id=dev,
            device_id_type=MESH,
        )
        copy.start()
        sends.append(copy)

    def forward(origin, dev):
        for k in range(2):
            push(k, origin, slot(k, origin), dev)

    def arrive(origin):
        for k in range(2):
            pltpu.make_async_remote_copy(
                src_ref=slot(k, origin),
                dst_ref=slot(k, origin),
                send_sem=send.at[0],
                recv_sem=recv.at[k, origin],
                device_id=pair_dev,
                device_id_type=MESH,
            ).wait_recv()

    xsends = []

    def xpush(src, origin, dev):
        copy = pltpu.make_async_remote_copy(
            src_ref=src,
            dst_ref=oxn.at[origin],
            send_sem=xsend.at[len(xsends)],
            recv_sem=xrecv.at[origin],
            device_id=dev,
            device_id_type=MESH,
        )
        copy.start()
        xsends.append(copy)

    def xarrive(origin):
        pltpu.make_async_remote_copy(
            src_ref=oxn.at[origin],
            dst_ref=oxn.at[origin],
            send_sem=xsend.at[0],
            recv_sem=xrecv.at[origin],
            device_id=mate_dev,
            device_id_type=MESH,
        ).wait_recv()

    inputs = (wqkv, wo)
    own = [pltpu.make_async_copy(xn, oxn.at[e], local.at[2])]
    own += [pltpu.make_async_copy(inputs[k], slot(k, g), local.at[k]) for k in range(2)]
    for copy in own:
        copy.start()
    xpush(xn, e, mate_dev)
    for dev in chip_devs:
        xpush(xn, e, dev)
    for dev in (pair_dev, plus_dev, minus_dev):
        for k in range(2):
            push(k, g, inputs[k], dev)
    partner = g + 1 - 2 * xh
    arrive(partner)
    forward(partner, plus_dev)
    forward(partner, minus_dev)
    chip_origins = [2 * lax.rem(chip + j, chips) + core for j in range(1, chips)]
    normed_order = [chip_origins[0:2], chip_origins[2:5], chip_origins[5:]]
    for step in range(1, 4):
        behind = lax.rem(z - step + columns, columns)
        ahead = lax.rem(z + step, columns)
        for origin in (2 * behind, 2 * behind + 1):
            arrive(origin)
        for origin in ((2 * behind, 2 * behind + 1) if step < 3 else (2 * behind,)):
            forward(origin, plus_dev)
        for origin in (2 * ahead, 2 * ahead + 1):
            arrive(origin)
        for origin in ((2 * ahead, 2 * ahead + 1) if step < 3 else (2 * ahead + 1,)):
            forward(origin, minus_dev)
        for origin in normed_order[step - 1]:
            xarrive(origin)
            xpush(oxn.at[origin], origin, mate_dev)
    across = lax.rem(z + columns // 2, columns)
    arrive(2 * across)
    arrive(2 * across + 1)
    mate_core = 1 - core
    xarrive(e + 1 - 2 * core)
    for j in range(1, chips):
        xarrive(2 * lax.rem(chip + j, chips) + mate_core)
    for copy in sends + xsends:
        copy.wait_send()
    for copy in own:
        copy.wait()


def gather_all(q_in, kv_in, o_in, h_in, gain_in, n_group, n_expert):
    any_spec = pl.BlockSpec(memory_space=pl.ANY)
    vmem = pl.BlockSpec(memory_space=pltpu.VMEM)
    depth = HEAD_DIMENSION
    joined = (q_in.shape[0], q_in.shape[1] + 2 * depth)
    shapes = [
        jax.ShapeDtypeStruct((n_group,) + joined, jnp.bfloat16),
        jax.ShapeDtypeStruct((n_group,) + o_in.shape, jnp.bfloat16),
        jax.ShapeDtypeStruct((n_expert,) + h_in.shape, jnp.bfloat16),
    ]
    return pl.pallas_call(
        functools.partial(gather_kernel, n_group, n_expert, q_in.shape[1] // depth),
        out_shape=tuple(shapes),
        in_specs=[vmem] * 5,
        out_specs=tuple([any_spec] * 3),
        scratch_shapes=[
            pltpu.SemaphoreType.DMA((32,)),
            pltpu.SemaphoreType.DMA((2, n_group)),
            pltpu.SemaphoreType.DMA((n_expert,)),
            pltpu.SemaphoreType.DMA((n_expert,)),
            pltpu.SemaphoreType.DMA((3,)),
            pltpu.VMEM(joined, jnp.bfloat16),
            pltpu.VMEM(o_in.shape, jnp.bfloat16),
            pltpu.VMEM(h_in.shape, jnp.bfloat16),
        ],
        compiler_params=pltpu.CompilerParams(collective_id=0, has_side_effects=True),
    )(q_in, kv_in, o_in, h_in, gain_in)


def combine_kernel(blocks, attended_ref, weight_ref, out_ref, outgoing, incoming, send, recv):
    g = lax.axis_index("group")
    e = lax.axis_index("expert")
    core = lax.rem(e, 2)
    mate_dev = (g, e + 1 - 2 * core)
    rows = out_ref.shape[1]
    barrier = pltpu.get_barrier_semaphore()
    pl.semaphore_signal(barrier, 1, device_id=mate_dev, device_id_type=MESH)
    pl.semaphore_wait(barrier, 1)

    def partial(block):
        start = pl.multiple_of(block * rows, rows)
        return jnp.dot(
            attended_ref[pl.ds(start, rows), :], weight_ref[...], preferred_element_type=jnp.float32
        ).astype(jnp.bfloat16)

    for i in range(blocks):
        outgoing[i] = partial(2 * i + 1 - core)
    copy = pltpu.make_async_remote_copy(
        src_ref=outgoing,
        dst_ref=incoming,
        send_sem=send.at[0],
        recv_sem=recv.at[0],
        device_id=mate_dev,
        device_id_type=MESH,
    )
    copy.start()
    for i in range(blocks):
        out_ref[i] = partial(2 * i + core)
    copy.wait()
    for i in range(blocks):
        out_ref[i] = (out_ref[i].astype(jnp.float32) + incoming[i].astype(jnp.float32)).astype(
            jnp.bfloat16
        )


def project_and_combine(attended, weight, experts_axis):
    rows = attended.shape[0] // experts_axis
    blocks = experts_axis // 2
    shape = (blocks, rows, weight.shape[1])
    vmem = pl.BlockSpec(memory_space=pltpu.VMEM)
    return pl.pallas_call(
        functools.partial(combine_kernel, blocks),
        out_shape=jax.ShapeDtypeStruct(shape, jnp.bfloat16),
        in_specs=[vmem, vmem],
        out_specs=vmem,
        scratch_shapes=[
            pltpu.VMEM(shape, jnp.bfloat16),
            pltpu.VMEM(shape, jnp.bfloat16),
            pltpu.SemaphoreType.DMA((1,)),
            pltpu.SemaphoreType.DMA((1,)),
        ],
        compiler_params=pltpu.CompilerParams(collective_id=4, has_side_effects=True),
    )(attended, weight)


def combine_scatter_kernel(blocks, attended_ref, weight_ref, out_ref, outgoing, incoming, combined, send, recv, chip_send, chip_recv, local):
    g = lax.axis_index("group")
    e = lax.axis_index("expert")
    core = lax.rem(e, 2)
    chip = lax.div(e, 2)
    mate_dev = (g, e + 1 - 2 * core)
    chip_devs = [(g, 2 * lax.rem(chip + j, blocks) + core) for j in range(1, blocks)]
    rows = out_ref.shape[1]
    barrier = pltpu.get_barrier_semaphore()
    for dev in [mate_dev] + chip_devs:
        pl.semaphore_signal(barrier, 1, device_id=dev, device_id_type=MESH)
    pl.semaphore_wait(barrier, blocks)

    def partial(block):
        start = pl.multiple_of(block * rows, rows)
        return jnp.dot(
            attended_ref[pl.ds(start, rows), :], weight_ref[...], preferred_element_type=jnp.float32
        ).astype(jnp.bfloat16)

    for i in range(blocks):
        outgoing[i] = partial(2 * i + 1 - core)
    copy = pltpu.make_async_remote_copy(
        src_ref=outgoing,
        dst_ref=incoming,
        send_sem=send.at[0],
        recv_sem=recv.at[0],
        device_id=mate_dev,
        device_id_type=MESH,
    )
    copy.start()
    for i in range(blocks):
        combined[i] = partial(2 * i + core)
    copy.wait()
    pushes = []
    for j in range(1, blocks):
        i = lax.rem(chip + j, blocks)
        combined[i] = (combined[i].astype(jnp.float32) + incoming[i].astype(jnp.float32)).astype(
            jnp.bfloat16
        )
        push = pltpu.make_async_remote_copy(
            src_ref=combined.at[i],
            dst_ref=out_ref.at[chip],
            send_sem=chip_send.at[j],
            recv_sem=chip_recv.at[j],
            device_id=chip_devs[j - 1],
            device_id_type=MESH,
        )
        push.start()
        pushes.append(push)
    combined[chip] = (combined[chip].astype(jnp.float32) + incoming[chip].astype(jnp.float32)).astype(
        jnp.bfloat16
    )
    own = pltpu.make_async_copy(combined.at[chip], out_ref.at[chip], local.at[0])
    own.start()
    for push in pushes:
        push.wait()
    own.wait()


def combine_and_scatter(attended, weight, experts_axis):
    rows = attended.shape[0] // experts_axis
    blocks = experts_axis // 2
    shape = (blocks, rows, weight.shape[1])
    vmem = pl.BlockSpec(memory_space=pltpu.VMEM)
    return pl.pallas_call(
        functools.partial(combine_scatter_kernel, blocks),
        out_shape=jax.ShapeDtypeStruct(shape, jnp.bfloat16),
        in_specs=[vmem, vmem],
        out_specs=pl.BlockSpec(memory_space=pl.ANY),
        scratch_shapes=[
            pltpu.VMEM(shape, jnp.bfloat16),
            pltpu.VMEM(shape, jnp.bfloat16),
            pltpu.VMEM(shape, jnp.bfloat16),
            pltpu.SemaphoreType.DMA((1,)),
            pltpu.SemaphoreType.DMA((1,)),
            pltpu.SemaphoreType.DMA((blocks,)),
            pltpu.SemaphoreType.DMA((blocks,)),
            pltpu.SemaphoreType.DMA((1,)),
        ],
        compiler_params=pltpu.CompilerParams(collective_id=7, has_side_effects=True),
    )(attended, weight)


def mate_kernel(part, out, send, recv):
    g = lax.axis_index("group")
    e = lax.axis_index("expert")
    core = lax.rem(e, 2)
    mate_dev = (g, e + 1 - 2 * core)
    barrier = pltpu.get_barrier_semaphore()
    pl.semaphore_signal(barrier, 1, device_id=mate_dev, device_id_type=MESH)
    pl.semaphore_wait(barrier, 1)
    copy = pltpu.make_async_remote_copy(
        src_ref=part.at[:, 1 - core],
        dst_ref=out,
        send_sem=send.at[0],
        recv_sem=recv.at[0],
        device_id=mate_dev,
        device_id_type=MESH,
    )
    copy.start()
    copy.wait()


def exchange_with_mate(part):
    any_spec = pl.BlockSpec(memory_space=pl.ANY)
    shape = (part.shape[0],) + part.shape[2:]
    return pl.pallas_call(
        mate_kernel,
        out_shape=jax.ShapeDtypeStruct(shape, part.dtype),
        in_specs=[any_spec],
        out_specs=any_spec,
        scratch_shapes=[pltpu.SemaphoreType.DMA((1,)), pltpu.SemaphoreType.DMA((1,))],
        compiler_params=pltpu.CompilerParams(collective_id=4, has_side_effects=True),
    )(part)


def chip_scatter_kernel(chips, part, out, send, recv, local):
    g = lax.axis_index("group")
    e = lax.axis_index("expert")
    core = lax.rem(e, 2)
    chip = lax.div(e, 2)
    devs = [(g, 2 * lax.rem(chip + j, chips) + core) for j in range(1, chips)]
    barrier = pltpu.get_barrier_semaphore()
    for dev in devs:
        pl.semaphore_signal(barrier, 1, device_id=dev, device_id_type=MESH)
    pl.semaphore_wait(barrier, len(devs))
    copies = []
    for j in range(1, chips):
        copy = pltpu.make_async_remote_copy(
            src_ref=part.at[lax.rem(chip + j, chips)],
            dst_ref=out.at[chip],
            send_sem=send.at[j],
            recv_sem=recv.at[j],
            device_id=devs[j - 1],
            device_id_type=MESH,
        )
        copy.start()
        copies.append(copy)
    own = pltpu.make_async_copy(part.at[chip], out.at[chip], local.at[0])
    own.start()
    for copy in copies:
        copy.wait()
    own.wait()


def scatter_to_chips(part):
    chips = part.shape[0]
    any_spec = pl.BlockSpec(memory_space=pl.ANY)
    return pl.pallas_call(
        functools.partial(chip_scatter_kernel, chips),
        out_shape=jax.ShapeDtypeStruct(part.shape, part.dtype),
        in_specs=[any_spec],
        out_specs=any_spec,
        scratch_shapes=[
            pltpu.SemaphoreType.DMA((chips,)),
            pltpu.SemaphoreType.DMA((chips,)),
            pltpu.SemaphoreType.DMA((1,)),
        ],
        compiler_params=pltpu.CompilerParams(collective_id=5, has_side_effects=True),
    )(part)


def scatter_kernel(n_expert, part, out, send, recv, local):
    g = lax.axis_index("group")
    e = lax.axis_index("expert")
    barrier = pltpu.get_barrier_semaphore()
    for j in range(1, n_expert):
        pl.semaphore_signal(barrier, 1, device_id=(g, lax.rem(e + j, n_expert)), device_id_type=MESH)
    pl.semaphore_wait(barrier, n_expert - 1)
    copies = []
    for j in range(1, n_expert):
        peer = lax.rem(e + j, n_expert)
        copy = pltpu.make_async_remote_copy(
            src_ref=part.at[peer],
            dst_ref=out.at[e],
            send_sem=send.at[j],
            recv_sem=recv.at[j],
            device_id=(g, peer),
            device_id_type=MESH,
        )
        copy.start()
        copies.append(copy)
    own = pltpu.make_async_copy(part.at[e], out.at[e], local.at[0])
    own.start()
    for copy in copies:
        copy.wait()
    own.wait()


def scatter_blocks(part, n_expert, collective_id):
    any_spec = pl.BlockSpec(memory_space=pl.ANY)
    return pl.pallas_call(
        functools.partial(scatter_kernel, n_expert),
        out_shape=jax.ShapeDtypeStruct(part.shape, part.dtype),
        in_specs=[any_spec],
        out_specs=any_spec,
        scratch_shapes=[
            pltpu.SemaphoreType.DMA((n_expert,)),
            pltpu.SemaphoreType.DMA((n_expert,)),
            pltpu.SemaphoreType.DMA((1,)),
        ],
        compiler_params=pltpu.CompilerParams(collective_id=collective_id, has_side_effects=True),
    )(part)


def attention_kernel(scale, heads, q_ref, own_ref, far_ref, length_ref, o_ref):
    block = q_ref.shape[0]
    rows = own_ref.shape[1]
    half = rows // 2
    parity = lax.rem(lax.axis_index("group"), 2)

    def places(side, shape, axis, start):
        indices = lax.broadcasted_iota(jnp.int32, shape, axis) + start
        return indices + jnp.where(side == 0, jnp.where(indices < half, 0, rows), half)

    query_places = places(parity, (block, 1), 0, pl.program_id(0) * block)
    length = length_ref[0, 0]
    own_places = places(parity, (1, rows), 1, 0)
    far_places = places(1 - parity, (1, rows), 1, 0)
    own_allowed = (own_places <= query_places) & (own_places < length)
    far_allowed = (far_places <= query_places) & (far_places < length)
    own_keys, own_values = own_ref[0], own_ref[1]
    far_keys, far_values = far_ref[0], far_ref[1]
    depth = own_keys.shape[1]
    contract = (((1,), (1,)), ((), ()))
    for h in range(heads):
        query = q_ref[:, h * depth : (h + 1) * depth]
        own_weights = jnp.where(
            own_allowed,
            jnp.exp(lax.dot_general(query, own_keys, contract, preferred_element_type=jnp.float32) * scale),
            0.0,
        )
        far_weights = jnp.where(
            far_allowed,
            jnp.exp(lax.dot_general(query, far_keys, contract, preferred_element_type=jnp.float32) * scale),
            0.0,
        )
        denominators = jnp.sum(own_weights, axis=-1, keepdims=True) + jnp.sum(
            far_weights, axis=-1, keepdims=True
        )
        weighted = jnp.dot(
            own_weights.astype(jnp.bfloat16), own_values, preferred_element_type=jnp.float32
        ) + jnp.dot(far_weights.astype(jnp.bfloat16), far_values, preferred_element_type=jnp.float32)
        o_ref[:, h * depth : (h + 1) * depth] = (weighted / denominators).astype(o_ref.dtype)


def attention(queries, own_kv, far_kv, length, scale):
    rows, width = queries.shape
    key_rows, depth = own_kv.shape[1:]
    block = min(256, rows)
    pair = pl.BlockSpec((2, key_rows, depth), lambda i: (0, 0, 0))
    return pl.pallas_call(
        functools.partial(attention_kernel, scale, width // depth),
        out_shape=jax.ShapeDtypeStruct((rows, width), jnp.bfloat16),
        grid=(rows // block,),
        in_specs=[
            pl.BlockSpec((block, width), lambda i: (i, 0)),
            pair,
            pair,
            pl.BlockSpec(memory_space=pltpu.SMEM),
        ],
        out_specs=pl.BlockSpec((block, width), lambda i: (i, 0)),
        cost_estimate=pl.CostEstimate(
            flops=8 * rows * key_rows * width,
            transcendentals=2 * rows * key_rows * (width // depth),
            bytes_accessed=2 * (2 * rows * width + 4 * key_rows * depth),
        ),
    )(queries, own_kv, far_kv, length.reshape(1, 1))

def norm_rows(values, gain_vector):
    widened = values.astype(jnp.float32)
    inverse_rms = lax.rsqrt(jnp.mean(widened * widened, axis=-1, keepdims=True) + epsilon)
    return widened * inverse_rms * gain_vector


def rotate(values, positions):
    half_width = values.shape[-1] // 2
    exponents = jnp.arange(half_width).astype(jnp.float32)
    inverse = jnp.exp(exponents * (-2.0 * math.log(rope_theta) / values.shape[-1]))
    angles = positions[:, None, None] * inverse[None, None, :]
    cosine_values = jnp.cos(angles)
    sine_values = jnp.sin(angles)
    first_half = values[..., :half_width]
    second = values[..., half_width:]
    return jnp.concatenate(
        [
            first_half * cosine_values - second * sine_values,
            second * cosine_values + first_half * sine_values,
        ],
        axis=-1,
    )


def local_positions(parity, row_count):
    indices = jnp.arange(row_count)
    quarter = row_count // 2
    offset = jnp.where(parity == 0, jnp.where(indices < quarter, 0, 2 * quarter), quarter)
    return indices + offset


def prep_kernel(query_width, for_queries, x_ref, w_ref, table_ref, gain_ref, out_ref):
    x = x_ref[...]
    block = x.shape[0]
    depth = table_ref.shape[1]
    parity = lax.rem(lax.axis_index("group"), 2)
    start = pl.multiple_of(parity * (table_ref.shape[0] // 2) + pl.program_id(0) * block, block)
    table = table_ref[pl.ds(start, block), :]
    swapped = pltpu.roll(table, depth // 2, 1)
    first_half = lax.broadcasted_iota(jnp.int32, table.shape, 1) < depth // 2
    cosines = jnp.where(first_half, table, swapped)
    sines = jnp.where(first_half, -swapped, table)

    def project(start, stop):
        return jnp.dot(x, w_ref[:, start:stop], preferred_element_type=jnp.float32).astype(jnp.bfloat16)

    def norm_rope(values, gain):
        values = values.astype(jnp.float32)
        inverse_rms = lax.rsqrt(jnp.mean(values * values, axis=-1, keepdims=True) + epsilon)
        normed = values * inverse_rms * gain
        return (normed * cosines + pltpu.roll(normed, depth // 2, 1) * sines).astype(jnp.bfloat16)

    if for_queries:
        queries = project(0, query_width)
        for h in range(queries.shape[1] // depth):
            out_ref[:, h * depth : (h + 1) * depth] = norm_rope(
                queries[:, h * depth : (h + 1) * depth], gain_ref[...]
            )
    else:
        out_ref[0] = norm_rope(project(0, depth), gain_ref[...])
        out_ref[1] = project(depth, 2 * depth)


def prep(normed_rows, joined, table, gain, for_queries):
    rows, width = normed_rows.shape
    depth = table.shape[1]
    query_width = joined.shape[1] - 2 * depth
    block = min(256, rows)
    whole = lambda shape: pl.BlockSpec(shape, lambda i: (0, 0))
    if for_queries:
        out_shape = jax.ShapeDtypeStruct((rows, query_width), jnp.bfloat16)
        out_spec = pl.BlockSpec((block, query_width), lambda i: (i, 0))
        columns = query_width
    else:
        out_shape = jax.ShapeDtypeStruct((2, rows, depth), jnp.bfloat16)
        out_spec = pl.BlockSpec((2, block, depth), lambda i: (0, i, 0))
        columns = 2 * depth
    return pl.pallas_call(
        functools.partial(prep_kernel, query_width, for_queries),
        out_shape=out_shape,
        grid=(rows // block,),
        in_specs=[
            pl.BlockSpec((block, width), lambda i: (i, 0)),
            pl.BlockSpec((width, columns), lambda i: (0, 0 if for_queries else 1)),
            whole(table.shape),
            whole((1, depth)),
        ],
        out_specs=out_spec,
        cost_estimate=pl.CostEstimate(
            flops=2 * rows * width * columns,
            transcendentals=rows * (columns // depth),
            bytes_accessed=2 * (rows * width + width * columns + rows * columns),
        ),
    )(normed_rows, joined, table, gain.reshape(1, depth))

def rope_table(row_count, depth):
    half = depth // 2
    frequencies = rope_theta ** (-2.0 * np.arange(half) / depth)
    indices = np.arange(row_count)
    quarter = row_count // 2
    places = np.concatenate([np.where(indices < quarter, indices, indices + 2 * quarter), indices + quarter])
    angles = places[:, None].astype(np.float64) * frequencies[None, :]
    return jnp.asarray(np.concatenate([np.cos(angles), np.sin(angles)], axis=1), jnp.float32)

def per_device(
    hidden_in,
    norm_attention,
    norm_experts,
    query_master,
    trainer_key_value_weight,
    output_master,
    query_gain,
    key_gain,
    lengths,
    router,
    expert_gateup,
    expert_down,
    routes,
):
    experts_axis = lax.axis_size("expert")
    group_member = lax.axis_index("expert")
    group_index = lax.axis_index("group")
    local_head_count = QUERY_HEADS // experts_axis
    width_here = local_head_count * HEAD_DIMENSION
    common_head = group_member * local_head_count // (QUERY_HEADS // KEY_VALUE_HEADS)
    groups_axis = lax.axis_size("group")
    joined_parts, output_parts, normed_parts = gather_all(
        query_master,
        trainer_key_value_weight,
        output_master,
        hidden_in,
        norm_attention.reshape(1, -1),
        groups_axis,
        experts_axis,
    )
    model_width = hidden_in.shape[1]
    local_rows = normed_parts.shape[0] * normed_parts.shape[1]
    parity = group_index % 2
    prep_args = (
        normed_parts.reshape(local_rows, model_width),
        joined_parts.reshape(model_width, -1),
        rope_table(local_rows, HEAD_DIMENSION),
    )
    key_values = prep(*prep_args, key_gain, False)
    query_rows_list = prep(*prep_args, query_gain, True)
    partner = from_partner(key_values, "group", 0)
    valid_length = jnp.sum(jnp.where(jnp.arange(lengths.shape[0]) == group_index // 2, lengths, 0))
    attended = attention(
        query_rows_list,
        key_values,
        partner,
        valid_length.astype(jnp.int32),
        HEAD_DIMENSION ** (-0.5),
    )
    output_weight = jnp.transpose(output_parts, (1, 0, 2)).reshape(output_parts.shape[1], -1)
    owned = combine_and_scatter(attended, output_weight, experts_axis)
    summed = jnp.sum(owned.astype(jnp.float32), axis=0)
    hidden = (hidden_in.astype(jnp.float32) + summed).astype(jnp.bfloat16)
    normed_second = norm_rows(hidden, norm_experts).astype(jnp.bfloat16)
    logits = jnp.dot(normed_second, router, preferred_element_type=jnp.float32)
    route_table = routes[:, :, None] == jnp.arange(logits.shape[1])[None, None, :]
    picked = jnp.sum(jnp.where(route_table, logits[:, None, :], 0.0), axis=-1)
    raised = jnp.exp(picked)
    gate_values = raised / jnp.sum(raised, axis=1, keepdims=True)
    inside = routes < experts_axis
    gate_window = jnp.sum(jnp.where(inside, gate_values, 0.0), axis=1)
    expert_window = jnp.sum(jnp.where(inside, routes, 0), axis=1)
    present = jnp.any(inside, axis=1)
    capacity = local_rows // (experts_axis * experts_axis)
    member_table = (
        present[:, None] & (expert_window[:, None] == jnp.arange(experts_axis)[None, :])
    ).astype(jnp.int32)
    ranking = jnp.sum(jnp.cumsum(member_table, axis=0) * member_table, axis=1) - 1
    slot_index = expert_window * capacity + ranking
    select = (
        (jnp.arange(experts_axis * capacity)[:, None] == slot_index[None, :]) & present[None, :]
    ).astype(jnp.bfloat16)
    select_slots = select.reshape(experts_axis, capacity, -1)
    outgoing = jnp.einsum(
        "jct,td->jcd", select_slots, normed_second, preferred_element_type=jnp.float32
    ).astype(jnp.bfloat16)
    gateup_here = expert_gateup[0]
    down_here = expert_down[0]
    hidden_units = down_here.shape[0]
    slot_items = scatter_blocks(outgoing, experts_axis, 2)
    gate_up = jnp.einsum("jcd,df->jcf", slot_items, gateup_here, preferred_element_type=jnp.float32)
    active = (jax.nn.silu(gate_up[..., :hidden_units]) * gate_up[..., hidden_units:]).astype(
        jnp.bfloat16
    )
    result = jnp.einsum(
        "jcf,fd->jcd", active, down_here, preferred_element_type=jnp.float32
    ).astype(jnp.bfloat16)
    returned = scatter_blocks(result, experts_axis, 3)
    combined = jnp.einsum(
        "jct,jcd->td", select_slots, returned, preferred_element_type=jnp.float32
    )
    expert_mix = (gate_window[:, None] * combined).astype(jnp.bfloat16)
    return (hidden, expert_mix)


def solution(mesh):
    return jax.shard_map(
        per_device,
        mesh=mesh,
        in_specs=(
            P(("group", "expert"), None),
            P(),
            P(),
            P("group", "expert"),
            P(None, "group", None),
            P("expert", "group"),
            P(),
            P(),
            P(),
            P(),
            P("expert", None, None),
            P("expert", None, None),
            P(("group", "expert"), None),
        ),
        out_specs=(P(("group", "expert"), None), P(("group", "expert"), None)),
        check_vma=False,
    )
```

```python
import functools
import math

import jax
import numpy as np
import jax.numpy as jnp
from jax import lax
from jax.experimental import pallas as pl
from jax.experimental.pallas import tpu as pltpu
from jax.sharding import PartitionSpec as P

MESH = pl.DeviceIdType.MESH

QUERY_HEADS = 32
KEY_VALUE_HEADS = 4
HEAD_DIMENSION = 128


epsilon = 1e-06
rope_theta = 1000000.0


def from_partner(block, axis, stride):
    count = lax.axis_size(axis)
    route = []
    for low in range(count):
        high = low | 1 << stride
        if high != low and high < count:
            route += [(low, high), (high, low)]
    return lax.ppermute(block, axis, route)


def gather_kernel(n_group, n_expert, heads_here, q_in, kv_in, o_in, h_in, gain_in, oqkv, oo, oxn, send, recv, xsend, xrecv, local, wqkv, wo, xn):
    e_here = lax.axis_index("expert")
    depth = HEAD_DIMENSION
    column = pl.multiple_of(lax.div(e_here * heads_here, QUERY_HEADS // KEY_VALUE_HEADS) * depth, depth)
    query_width = q_in.shape[1]
    wqkv[:, 0:query_width] = q_in[...].astype(jnp.bfloat16)
    wqkv[:, query_width : query_width + depth] = kv_in[0, :, pl.ds(column, depth)].astype(jnp.bfloat16)
    wqkv[:, query_width + depth : query_width + 2 * depth] = kv_in[1, :, pl.ds(column, depth)].astype(
        jnp.bfloat16
    )
    wo[...] = o_in[...].astype(jnp.bfloat16)
    xn[...] = norm_rows(h_in[...], gain_in[...]).astype(jnp.bfloat16)
    g = lax.axis_index("group")
    e = lax.axis_index("expert")
    columns = n_group // 2
    z = lax.div(g, 2)
    xh = lax.rem(g, 2)
    zp = lax.rem(z + 1, columns)
    zm = lax.rem(z + columns - 1, columns)
    plus_dev = (2 * zp + xh, e)
    minus_dev = (2 * zm + xh, e)
    pair_dev = (g + 1 - 2 * xh, e)
    core = lax.rem(e, 2)
    chip = lax.div(e, 2)
    chips = n_expert // 2
    mate_dev = (g, e + 1 - 2 * core)
    chip_devs = [(g, 2 * lax.rem(chip + j, chips) + core) for j in range(1, chips)]
    barrier = pltpu.get_barrier_semaphore()
    peers = [plus_dev, minus_dev, pair_dev, mate_dev] + chip_devs
    for dev in peers:
        pl.semaphore_signal(barrier, 1, device_id=dev, device_id_type=MESH)
    pl.semaphore_wait(barrier, len(peers))

    width = oo.shape[1] // n_group

    def slot(k, origin):
        if k == 1:
            return oo.at[:, pl.ds(pl.multiple_of(origin * width, width), width)]
        return oqkv.at[origin]

    sends = []

    def push(k, origin, src, dev):
        copy = pltpu.make_async_remote_copy(
            src_ref=src,
            dst_ref=slot(k, origin),
            send_sem=send.at[len(sends)],
            recv_sem=recv.at[k, origin],
            device_id=dev,
            device_id_type=MESH,
        )
        copy.start()
        sends.append(copy)

    def forward(origin, dev):
        for k in range(2):
            push(k, origin, slot(k, origin), dev)

    def arrive(origin):
        for k in range(2):
            pltpu.make_async_remote_copy(
                src_ref=slot(k, origin),
                dst_ref=slot(k, origin),
                send_sem=send.at[0],
                recv_sem=recv.at[k, origin],
                device_id=pair_dev,
                device_id_type=MESH,
            ).wait_recv()

    xsends = []

    def xpush(src, origin, dev):
        copy = pltpu.make_async_remote_copy(
            src_ref=src,
            dst_ref=oxn.at[origin],
            send_sem=xsend.at[len(xsends)],
            recv_sem=xrecv.at[origin],
            device_id=dev,
            device_id_type=MESH,
        )
        copy.start()
        xsends.append(copy)

    def xarrive(origin):
        pltpu.make_async_remote_copy(
            src_ref=oxn.at[origin],
            dst_ref=oxn.at[origin],
            send_sem=xsend.at[0],
            recv_sem=xrecv.at[origin],
            device_id=mate_dev,
            device_id_type=MESH,
        ).wait_recv()

    inputs = (wqkv, wo)
    own = [pltpu.make_async_copy(xn, oxn.at[e], local.at[2])]
    own += [pltpu.make_async_copy(inputs[k], slot(k, g), local.at[k]) for k in range(2)]
    for copy in own:
        copy.start()
    xpush(xn, e, mate_dev)
    for dev in chip_devs:
        xpush(xn, e, dev)
    for dev in (pair_dev, plus_dev, minus_dev):
        for k in range(2):
            push(k, g, inputs[k], dev)
    partner = g + 1 - 2 * xh
    arrive(partner)
    forward(partner, plus_dev)
    forward(partner, minus_dev)
    chip_origins = [2 * lax.rem(chip + j, chips) + core for j in range(1, chips)]
    normed_order = [chip_origins[0:2], chip_origins[2:5], chip_origins[5:]]
    for step in range(1, 4):
        behind = lax.rem(z - step + columns, columns)
        ahead = lax.rem(z + step, columns)
        for origin in (2 * behind, 2 * behind + 1):
            arrive(origin)
        for origin in ((2 * behind, 2 * behind + 1) if step < 3 else (2 * behind,)):
            forward(origin, plus_dev)
        for origin in (2 * ahead, 2 * ahead + 1):
            arrive(origin)
        for origin in ((2 * ahead, 2 * ahead + 1) if step < 3 else (2 * ahead + 1,)):
            forward(origin, minus_dev)
        for origin in normed_order[step - 1]:
            xarrive(origin)
            xpush(oxn.at[origin], origin, mate_dev)
    across = lax.rem(z + columns // 2, columns)
    arrive(2 * across)
    arrive(2 * across + 1)
    mate_core = 1 - core
    xarrive(e + 1 - 2 * core)
    for j in range(1, chips):
        xarrive(2 * lax.rem(chip + j, chips) + mate_core)
    for copy in sends + xsends:
        copy.wait_send()
    for copy in own:
        copy.wait()


def gather_all(q_in, kv_in, o_in, h_in, gain_in, n_group, n_expert):
    any_spec = pl.BlockSpec(memory_space=pl.ANY)
    vmem = pl.BlockSpec(memory_space=pltpu.VMEM)
    depth = HEAD_DIMENSION
    joined = (q_in.shape[0], q_in.shape[1] + 2 * depth)
    shapes = [
        jax.ShapeDtypeStruct((n_group,) + joined, jnp.bfloat16),
        jax.ShapeDtypeStruct((o_in.shape[0], n_group * o_in.shape[1]), jnp.bfloat16),
        jax.ShapeDtypeStruct((n_expert,) + h_in.shape, jnp.bfloat16),
    ]
    return pl.pallas_call(
        functools.partial(gather_kernel, n_group, n_expert, q_in.shape[1] // depth),
        out_shape=tuple(shapes),
        in_specs=[vmem] * 5,
        out_specs=tuple([any_spec] * 3),
        scratch_shapes=[
            pltpu.SemaphoreType.DMA((32,)),
            pltpu.SemaphoreType.DMA((2, n_group)),
            pltpu.SemaphoreType.DMA((n_expert,)),
            pltpu.SemaphoreType.DMA((n_expert,)),
            pltpu.SemaphoreType.DMA((3,)),
            pltpu.VMEM(joined, jnp.bfloat16),
            pltpu.VMEM(o_in.shape, jnp.bfloat16),
            pltpu.VMEM(h_in.shape, jnp.bfloat16),
        ],
        compiler_params=pltpu.CompilerParams(collective_id=0, has_side_effects=True),
    )(q_in, kv_in, o_in, h_in, gain_in)


def combine_kernel(blocks, attended_ref, weight_ref, out_ref, outgoing, incoming, send, recv):
    g = lax.axis_index("group")
    e = lax.axis_index("expert")
    core = lax.rem(e, 2)
    mate_dev = (g, e + 1 - 2 * core)
    rows = out_ref.shape[1]
    barrier = pltpu.get_barrier_semaphore()
    pl.semaphore_signal(barrier, 1, device_id=mate_dev, device_id_type=MESH)
    pl.semaphore_wait(barrier, 1)

    def partial(block):
        start = pl.multiple_of(block * rows, rows)
        return jnp.dot(
            attended_ref[pl.ds(start, rows), :], weight_ref[...], preferred_element_type=jnp.float32
        ).astype(jnp.bfloat16)

    for i in range(blocks):
        outgoing[i] = partial(2 * i + 1 - core)
    copy = pltpu.make_async_remote_copy(
        src_ref=outgoing,
        dst_ref=incoming,
        send_sem=send.at[0],
        recv_sem=recv.at[0],
        device_id=mate_dev,
        device_id_type=MESH,
    )
    copy.start()
    for i in range(blocks):
        out_ref[i] = partial(2 * i + core)
    copy.wait()
    for i in range(blocks):
        out_ref[i] = (out_ref[i].astype(jnp.float32) + incoming[i].astype(jnp.float32)).astype(
            jnp.bfloat16
        )


def project_and_combine(attended, weight, experts_axis):
    rows = attended.shape[0] // experts_axis
    blocks = experts_axis // 2
    shape = (blocks, rows, weight.shape[1])
    vmem = pl.BlockSpec(memory_space=pltpu.VMEM)
    return pl.pallas_call(
        functools.partial(combine_kernel, blocks),
        out_shape=jax.ShapeDtypeStruct(shape, jnp.bfloat16),
        in_specs=[vmem, vmem],
        out_specs=vmem,
        scratch_shapes=[
            pltpu.VMEM(shape, jnp.bfloat16),
            pltpu.VMEM(shape, jnp.bfloat16),
            pltpu.SemaphoreType.DMA((1,)),
            pltpu.SemaphoreType.DMA((1,)),
        ],
        compiler_params=pltpu.CompilerParams(collective_id=4, has_side_effects=True),
    )(attended, weight)


def combine_scatter_kernel(blocks, attended_ref, weight_ref, out_ref, outgoing, incoming, combined, send, recv, chip_send, chip_recv, local):
    g = lax.axis_index("group")
    e = lax.axis_index("expert")
    core = lax.rem(e, 2)
    chip = lax.div(e, 2)
    mate_dev = (g, e + 1 - 2 * core)
    chip_devs = [(g, 2 * lax.rem(chip + j, blocks) + core) for j in range(1, blocks)]
    rows = out_ref.shape[1]
    barrier = pltpu.get_barrier_semaphore()
    for dev in [mate_dev] + chip_devs:
        pl.semaphore_signal(barrier, 1, device_id=dev, device_id_type=MESH)
    pl.semaphore_wait(barrier, blocks)

    def partial(block):
        start = pl.multiple_of(block * rows, rows)
        return jnp.dot(
            attended_ref[pl.ds(start, rows), :], weight_ref[...], preferred_element_type=jnp.float32
        ).astype(jnp.bfloat16)

    for i in range(blocks):
        outgoing[i] = partial(2 * i + 1 - core)
    copy = pltpu.make_async_remote_copy(
        src_ref=outgoing,
        dst_ref=incoming,
        send_sem=send.at[0],
        recv_sem=recv.at[0],
        device_id=mate_dev,
        device_id_type=MESH,
    )
    copy.start()
    for i in range(blocks):
        combined[i] = partial(2 * i + core)
    copy.wait()
    pushes = []
    for j in range(1, blocks):
        i = lax.rem(chip + j, blocks)
        combined[i] = (combined[i].astype(jnp.float32) + incoming[i].astype(jnp.float32)).astype(
            jnp.bfloat16
        )
        push = pltpu.make_async_remote_copy(
            src_ref=combined.at[i],
            dst_ref=out_ref.at[chip],
            send_sem=chip_send.at[j],
            recv_sem=chip_recv.at[j],
            device_id=chip_devs[j - 1],
            device_id_type=MESH,
        )
        push.start()
        pushes.append(push)
    combined[chip] = (combined[chip].astype(jnp.float32) + incoming[chip].astype(jnp.float32)).astype(
        jnp.bfloat16
    )
    own = pltpu.make_async_copy(combined.at[chip], out_ref.at[chip], local.at[0])
    own.start()
    for push in pushes:
        push.wait()
    own.wait()


def combine_and_scatter(attended, weight, experts_axis):
    rows = attended.shape[0] // experts_axis
    blocks = experts_axis // 2
    shape = (blocks, rows, weight.shape[1])
    vmem = pl.BlockSpec(memory_space=pltpu.VMEM)
    return pl.pallas_call(
        functools.partial(combine_scatter_kernel, blocks),
        out_shape=jax.ShapeDtypeStruct(shape, jnp.bfloat16),
        in_specs=[vmem, vmem],
        out_specs=pl.BlockSpec(memory_space=pl.ANY),
        scratch_shapes=[
            pltpu.VMEM(shape, jnp.bfloat16),
            pltpu.VMEM(shape, jnp.bfloat16),
            pltpu.VMEM(shape, jnp.bfloat16),
            pltpu.SemaphoreType.DMA((1,)),
            pltpu.SemaphoreType.DMA((1,)),
            pltpu.SemaphoreType.DMA((blocks,)),
            pltpu.SemaphoreType.DMA((blocks,)),
            pltpu.SemaphoreType.DMA((1,)),
        ],
        compiler_params=pltpu.CompilerParams(collective_id=7, has_side_effects=True),
    )(attended, weight)


def mate_kernel(part, out, send, recv):
    g = lax.axis_index("group")
    e = lax.axis_index("expert")
    core = lax.rem(e, 2)
    mate_dev = (g, e + 1 - 2 * core)
    barrier = pltpu.get_barrier_semaphore()
    pl.semaphore_signal(barrier, 1, device_id=mate_dev, device_id_type=MESH)
    pl.semaphore_wait(barrier, 1)
    copy = pltpu.make_async_remote_copy(
        src_ref=part.at[:, 1 - core],
        dst_ref=out,
        send_sem=send.at[0],
        recv_sem=recv.at[0],
        device_id=mate_dev,
        device_id_type=MESH,
    )
    copy.start()
    copy.wait()


def exchange_with_mate(part):
    any_spec = pl.BlockSpec(memory_space=pl.ANY)
    shape = (part.shape[0],) + part.shape[2:]
    return pl.pallas_call(
        mate_kernel,
        out_shape=jax.ShapeDtypeStruct(shape, part.dtype),
        in_specs=[any_spec],
        out_specs=any_spec,
        scratch_shapes=[pltpu.SemaphoreType.DMA((1,)), pltpu.SemaphoreType.DMA((1,))],
        compiler_params=pltpu.CompilerParams(collective_id=4, has_side_effects=True),
    )(part)


def chip_scatter_kernel(chips, part, out, send, recv, local):
    g = lax.axis_index("group")
    e = lax.axis_index("expert")
    core = lax.rem(e, 2)
    chip = lax.div(e, 2)
    devs = [(g, 2 * lax.rem(chip + j, chips) + core) for j in range(1, chips)]
    barrier = pltpu.get_barrier_semaphore()
    for dev in devs:
        pl.semaphore_signal(barrier, 1, device_id=dev, device_id_type=MESH)
    pl.semaphore_wait(barrier, len(devs))
    copies = []
    for j in range(1, chips):
        copy = pltpu.make_async_remote_copy(
            src_ref=part.at[lax.rem(chip + j, chips)],
            dst_ref=out.at[chip],
            send_sem=send.at[j],
            recv_sem=recv.at[j],
            device_id=devs[j - 1],
            device_id_type=MESH,
        )
        copy.start()
        copies.append(copy)
    own = pltpu.make_async_copy(part.at[chip], out.at[chip], local.at[0])
    own.start()
    for copy in copies:
        copy.wait()
    own.wait()


def scatter_to_chips(part):
    chips = part.shape[0]
    any_spec = pl.BlockSpec(memory_space=pl.ANY)
    return pl.pallas_call(
        functools.partial(chip_scatter_kernel, chips),
        out_shape=jax.ShapeDtypeStruct(part.shape, part.dtype),
        in_specs=[any_spec],
        out_specs=any_spec,
        scratch_shapes=[
            pltpu.SemaphoreType.DMA((chips,)),
            pltpu.SemaphoreType.DMA((chips,)),
            pltpu.SemaphoreType.DMA((1,)),
        ],
        compiler_params=pltpu.CompilerParams(collective_id=5, has_side_effects=True),
    )(part)


def scatter_kernel(n_expert, part, out, send, recv, local):
    g = lax.axis_index("group")
    e = lax.axis_index("expert")
    barrier = pltpu.get_barrier_semaphore()
    for j in range(1, n_expert):
        pl.semaphore_signal(barrier, 1, device_id=(g, lax.rem(e + j, n_expert)), device_id_type=MESH)
    pl.semaphore_wait(barrier, n_expert - 1)
    copies = []
    for j in range(1, n_expert):
        peer = lax.rem(e + j, n_expert)
        copy = pltpu.make_async_remote_copy(
            src_ref=part.at[peer],
            dst_ref=out.at[e],
            send_sem=send.at[j],
            recv_sem=recv.at[j],
            device_id=(g, peer),
            device_id_type=MESH,
        )
        copy.start()
        copies.append(copy)
    own = pltpu.make_async_copy(part.at[e], out.at[e], local.at[0])
    own.start()
    for copy in copies:
        copy.wait()
    own.wait()


def scatter_blocks(part, n_expert, collective_id):
    any_spec = pl.BlockSpec(memory_space=pl.ANY)
    return pl.pallas_call(
        functools.partial(scatter_kernel, n_expert),
        out_shape=jax.ShapeDtypeStruct(part.shape, part.dtype),
        in_specs=[any_spec],
        out_specs=any_spec,
        scratch_shapes=[
            pltpu.SemaphoreType.DMA((n_expert,)),
            pltpu.SemaphoreType.DMA((n_expert,)),
            pltpu.SemaphoreType.DMA((1,)),
        ],
        compiler_params=pltpu.CompilerParams(collective_id=collective_id, has_side_effects=True),
    )(part)


def attention_kernel(scale, heads, q_ref, own_ref, far_ref, length_ref, o_ref):
    block = q_ref.shape[0]
    rows = own_ref.shape[1]
    half = rows // 2
    parity = lax.rem(lax.axis_index("group"), 2)

    def places(side, shape, axis, start):
        indices = lax.broadcasted_iota(jnp.int32, shape, axis) + start
        return indices + jnp.where(side == 0, jnp.where(indices < half, 0, rows), half)

    query_places = places(parity, (block, 1), 0, pl.program_id(0) * block)
    length = length_ref[0, 0]
    own_places = places(parity, (1, rows), 1, 0)
    far_places = places(1 - parity, (1, rows), 1, 0)
    own_allowed = (own_places <= query_places) & (own_places < length)
    far_allowed = (far_places <= query_places) & (far_places < length)
    own_keys, own_values = own_ref[0], own_ref[1]
    far_keys, far_values = far_ref[0], far_ref[1]
    depth = own_keys.shape[1]
    contract = (((1,), (1,)), ((), ()))
    for h in range(heads):
        query = q_ref[:, h * depth : (h + 1) * depth]
        own_weights = jnp.where(
            own_allowed,
            jnp.exp(lax.dot_general(query, own_keys, contract, preferred_element_type=jnp.float32) * scale),
            0.0,
        )
        far_weights = jnp.where(
            far_allowed,
            jnp.exp(lax.dot_general(query, far_keys, contract, preferred_element_type=jnp.float32) * scale),
            0.0,
        )
        denominators = jnp.sum(own_weights, axis=-1, keepdims=True) + jnp.sum(
            far_weights, axis=-1, keepdims=True
        )
        weighted = jnp.dot(
            own_weights.astype(jnp.bfloat16), own_values, preferred_element_type=jnp.float32
        ) + jnp.dot(far_weights.astype(jnp.bfloat16), far_values, preferred_element_type=jnp.float32)
        o_ref[:, h * depth : (h + 1) * depth] = (weighted / denominators).astype(o_ref.dtype)


def attention(queries, own_kv, far_kv, length, scale):
    rows, width = queries.shape
    key_rows, depth = own_kv.shape[1:]
    block = min(256, rows)
    pair = pl.BlockSpec((2, key_rows, depth), lambda i: (0, 0, 0))
    return pl.pallas_call(
        functools.partial(attention_kernel, scale, width // depth),
        out_shape=jax.ShapeDtypeStruct((rows, width), jnp.bfloat16),
        grid=(rows // block,),
        in_specs=[
            pl.BlockSpec((block, width), lambda i: (i, 0)),
            pair,
            pair,
            pl.BlockSpec(memory_space=pltpu.SMEM),
        ],
        out_specs=pl.BlockSpec((block, width), lambda i: (i, 0)),
        cost_estimate=pl.CostEstimate(
            flops=8 * rows * key_rows * width,
            transcendentals=2 * rows * key_rows * (width // depth),
            bytes_accessed=2 * (2 * rows * width + 4 * key_rows * depth),
        ),
    )(queries, own_kv, far_kv, length.reshape(1, 1))

def norm_rows(values, gain_vector):
    widened = values.astype(jnp.float32)
    inverse_rms = lax.rsqrt(jnp.mean(widened * widened, axis=-1, keepdims=True) + epsilon)
    return widened * inverse_rms * gain_vector


def rotate(values, positions):
    half_width = values.shape[-1] // 2
    exponents = jnp.arange(half_width).astype(jnp.float32)
    inverse = jnp.exp(exponents * (-2.0 * math.log(rope_theta) / values.shape[-1]))
    angles = positions[:, None, None] * inverse[None, None, :]
    cosine_values = jnp.cos(angles)
    sine_values = jnp.sin(angles)
    first_half = values[..., :half_width]
    second = values[..., half_width:]
    return jnp.concatenate(
        [
            first_half * cosine_values - second * sine_values,
            second * cosine_values + first_half * sine_values,
        ],
        axis=-1,
    )


def local_positions(parity, row_count):
    indices = jnp.arange(row_count)
    quarter = row_count // 2
    offset = jnp.where(parity == 0, jnp.where(indices < quarter, 0, 2 * quarter), quarter)
    return indices + offset


def prep_kernel(query_width, for_queries, x_ref, w_ref, table_ref, gain_ref, out_ref):
    x = x_ref[...]
    block = x.shape[0]
    depth = table_ref.shape[1]
    parity = lax.rem(lax.axis_index("group"), 2)
    start = pl.multiple_of(parity * (table_ref.shape[0] // 2) + pl.program_id(0) * block, block)
    table = table_ref[pl.ds(start, block), :]
    swapped = pltpu.roll(table, depth // 2, 1)
    first_half = lax.broadcasted_iota(jnp.int32, table.shape, 1) < depth // 2
    cosines = jnp.where(first_half, table, swapped)
    sines = jnp.where(first_half, -swapped, table)

    def project(start, stop):
        return jnp.dot(x, w_ref[:, start:stop], preferred_element_type=jnp.float32).astype(jnp.bfloat16)

    def norm_rope(values, gain):
        values = values.astype(jnp.float32)
        inverse_rms = lax.rsqrt(jnp.mean(values * values, axis=-1, keepdims=True) + epsilon)
        normed = values * inverse_rms * gain
        return (normed * cosines + pltpu.roll(normed, depth // 2, 1) * sines).astype(jnp.bfloat16)

    if for_queries:
        queries = project(0, query_width)
        for h in range(queries.shape[1] // depth):
            out_ref[:, h * depth : (h + 1) * depth] = norm_rope(
                queries[:, h * depth : (h + 1) * depth], gain_ref[...]
            )
    else:
        out_ref[0] = norm_rope(project(0, depth), gain_ref[...])
        out_ref[1] = project(depth, 2 * depth)


def prep(normed_rows, joined, table, gain, for_queries):
    rows, width = normed_rows.shape
    depth = table.shape[1]
    query_width = joined.shape[1] - 2 * depth
    block = min(256, rows)
    whole = lambda shape: pl.BlockSpec(shape, lambda i: (0, 0))
    if for_queries:
        out_shape = jax.ShapeDtypeStruct((rows, query_width), jnp.bfloat16)
        out_spec = pl.BlockSpec((block, query_width), lambda i: (i, 0))
        columns = query_width
    else:
        out_shape = jax.ShapeDtypeStruct((2, rows, depth), jnp.bfloat16)
        out_spec = pl.BlockSpec((2, block, depth), lambda i: (0, i, 0))
        columns = 2 * depth
    return pl.pallas_call(
        functools.partial(prep_kernel, query_width, for_queries),
        out_shape=out_shape,
        grid=(rows // block,),
        in_specs=[
            pl.BlockSpec((block, width), lambda i: (i, 0)),
            pl.BlockSpec((width, columns), lambda i: (0, 0 if for_queries else 1)),
            whole(table.shape),
            whole((1, depth)),
        ],
        out_specs=out_spec,
        cost_estimate=pl.CostEstimate(
            flops=2 * rows * width * columns,
            transcendentals=rows * (columns // depth),
            bytes_accessed=2 * (rows * width + width * columns + rows * columns),
        ),
    )(normed_rows, joined, table, gain.reshape(1, depth))

def rope_table(row_count, depth):
    half = depth // 2
    frequencies = rope_theta ** (-2.0 * np.arange(half) / depth)
    indices = np.arange(row_count)
    quarter = row_count // 2
    places = np.concatenate([np.where(indices < quarter, indices, indices + 2 * quarter), indices + quarter])
    angles = places[:, None].astype(np.float64) * frequencies[None, :]
    return jnp.asarray(np.concatenate([np.cos(angles), np.sin(angles)], axis=1), jnp.float32)

def per_device(
    hidden_in,
    norm_attention,
    norm_experts,
    query_master,
    trainer_key_value_weight,
    output_master,
    query_gain,
    key_gain,
    lengths,
    router,
    expert_gateup,
    expert_down,
    routes,
):
    experts_axis = lax.axis_size("expert")
    group_member = lax.axis_index("expert")
    group_index = lax.axis_index("group")
    local_head_count = QUERY_HEADS // experts_axis
    width_here = local_head_count * HEAD_DIMENSION
    common_head = group_member * local_head_count // (QUERY_HEADS // KEY_VALUE_HEADS)
    groups_axis = lax.axis_size("group")
    joined_parts, output_parts, normed_parts = gather_all(
        query_master,
        trainer_key_value_weight,
        output_master,
        hidden_in,
        norm_attention.reshape(1, -1),
        groups_axis,
        experts_axis,
    )
    model_width = hidden_in.shape[1]
    local_rows = normed_parts.shape[0] * normed_parts.shape[1]
    parity = group_index % 2
    prep_args = (
        normed_parts.reshape(local_rows, model_width),
        joined_parts.reshape(model_width, -1),
        rope_table(local_rows, HEAD_DIMENSION),
    )
    key_values = prep(*prep_args, key_gain, False)
    query_rows_list = prep(*prep_args, query_gain, True)
    partner = from_partner(key_values, "group", 0)
    valid_length = jnp.sum(jnp.where(jnp.arange(lengths.shape[0]) == group_index // 2, lengths, 0))
    attended = attention(
        query_rows_list,
        key_values,
        partner,
        valid_length.astype(jnp.int32),
        HEAD_DIMENSION ** (-0.5),
    )
    output_weight = output_parts
    owned = combine_and_scatter(attended, output_weight, experts_axis)
    summed = jnp.sum(owned.astype(jnp.float32), axis=0)
    hidden = (hidden_in.astype(jnp.float32) + summed).astype(jnp.bfloat16)
    normed_second = norm_rows(hidden, norm_experts).astype(jnp.bfloat16)
    logits = jnp.dot(normed_second, router, preferred_element_type=jnp.float32)
    route_table = routes[:, :, None] == jnp.arange(logits.shape[1])[None, None, :]
    picked = jnp.sum(jnp.where(route_table, logits[:, None, :], 0.0), axis=-1)
    raised = jnp.exp(picked)
    gate_values = raised / jnp.sum(raised, axis=1, keepdims=True)
    inside = routes < experts_axis
    gate_window = jnp.sum(jnp.where(inside, gate_values, 0.0), axis=1)
    expert_window = jnp.sum(jnp.where(inside, routes, 0), axis=1)
    present = jnp.any(inside, axis=1)
    capacity = local_rows // (experts_axis * experts_axis)
    member_table = (
        present[:, None] & (expert_window[:, None] == jnp.arange(experts_axis)[None, :])
    ).astype(jnp.int32)
    ranking = jnp.sum(jnp.cumsum(member_table, axis=0) * member_table, axis=1) - 1
    slot_index = expert_window * capacity + ranking
    select = (
        (jnp.arange(experts_axis * capacity)[:, None] == slot_index[None, :]) & present[None, :]
    ).astype(jnp.bfloat16)
    select_slots = select.reshape(experts_axis, capacity, -1)
    outgoing = jnp.einsum(
        "jct,td->jcd", select_slots, normed_second, preferred_element_type=jnp.float32
    ).astype(jnp.bfloat16)
    gateup_here = expert_gateup[0]
    down_here = expert_down[0]
    hidden_units = down_here.shape[0]
    slot_items = scatter_blocks(outgoing, experts_axis, 2)
    gate_up = jnp.einsum("jcd,df->jcf", slot_items, gateup_here, preferred_element_type=jnp.float32)
    active = (jax.nn.silu(gate_up[..., :hidden_units]) * gate_up[..., hidden_units:]).astype(
        jnp.bfloat16
    )
    result = jnp.einsum(
        "jcf,fd->jcd", active, down_here, preferred_element_type=jnp.float32
    ).astype(jnp.bfloat16)
    returned = scatter_blocks(result, experts_axis, 3)
    combined = jnp.einsum(
        "jct,jcd->td", select_slots, returned, preferred_element_type=jnp.float32
    )
    expert_mix = (gate_window[:, None] * combined).astype(jnp.bfloat16)
    return (hidden, expert_mix)


def solution(mesh):
    return jax.shard_map(
        per_device,
        mesh=mesh,
        in_specs=(
            P(("group", "expert"), None),
            P(),
            P(),
            P("group", "expert"),
            P(None, "group", None),
            P("expert", "group"),
            P(),
            P(),
            P(),
            P(),
            P("expert", None, None),
            P("expert", None, None),
            P(("group", "expert"), None),
        ),
        out_specs=(P(("group", "expert"), None), P(("group", "expert"), None)),
        check_vma=False,
    )
```

```python
import functools
import math

import jax
import numpy as np
import jax.numpy as jnp
from jax import lax
from jax.experimental import pallas as pl
from jax.experimental.pallas import tpu as pltpu
from jax.sharding import PartitionSpec as P

MESH = pl.DeviceIdType.MESH

QUERY_HEADS = 32
KEY_VALUE_HEADS = 4
HEAD_DIMENSION = 128


epsilon = 1e-06
rope_theta = 1000000.0


def from_partner(block, axis, stride):
    count = lax.axis_size(axis)
    route = []
    for low in range(count):
        high = low | 1 << stride
        if high != low and high < count:
            route += [(low, high), (high, low)]
    return lax.ppermute(block, axis, route)


def gather_kernel(n_group, n_expert, heads_here, q_in, kv_in, o_in, h_in, gain_in, oqkv, oo, oxn, send, recv, xsend, xrecv, local, wqkv, wo, xn):
    e_here = lax.axis_index("expert")
    depth = HEAD_DIMENSION
    column = pl.multiple_of(lax.div(e_here * heads_here, QUERY_HEADS // KEY_VALUE_HEADS) * depth, depth)
    query_width = q_in.shape[1]
    wqkv[:, 0:query_width] = q_in[...].astype(jnp.bfloat16)
    wqkv[:, query_width : query_width + depth] = kv_in[0, :, pl.ds(column, depth)].astype(jnp.bfloat16)
    wqkv[:, query_width + depth : query_width + 2 * depth] = kv_in[1, :, pl.ds(column, depth)].astype(
        jnp.bfloat16
    )
    wo[...] = o_in[...].astype(jnp.bfloat16)
    xn[...] = norm_rows(h_in[...], gain_in[...]).astype(jnp.bfloat16)
    g = lax.axis_index("group")
    e = lax.axis_index("expert")
    columns = n_group // 2
    z = lax.div(g, 2)
    xh = lax.rem(g, 2)
    zp = lax.rem(z + 1, columns)
    zm = lax.rem(z + columns - 1, columns)
    plus_dev = (2 * zp + xh, e)
    minus_dev = (2 * zm + xh, e)
    pair_dev = (g + 1 - 2 * xh, e)
    core = lax.rem(e, 2)
    chip = lax.div(e, 2)
    chips = n_expert // 2
    mate_dev = (g, e + 1 - 2 * core)
    chip_devs = [(g, 2 * lax.rem(chip + j, chips) + core) for j in range(1, chips)]
    barrier = pltpu.get_barrier_semaphore()
    peers = [plus_dev, minus_dev, pair_dev, mate_dev] + chip_devs
    for dev in peers:
        pl.semaphore_signal(barrier, 1, device_id=dev, device_id_type=MESH)
    pl.semaphore_wait(barrier, len(peers))

    def slot(k, origin):
        return (oqkv, oo)[k].at[origin]

    sends = []

    def push(k, origin, src, dev):
        copy = pltpu.make_async_remote_copy(
            src_ref=src,
            dst_ref=slot(k, origin),
            send_sem=send.at[len(sends)],
            recv_sem=recv.at[k, origin],
            device_id=dev,
            device_id_type=MESH,
        )
        copy.start()
        sends.append(copy)

    def forward(origin, dev):
        for k in range(2):
            push(k, origin, slot(k, origin), dev)

    def arrive(origin):
        for k in range(2):
            pltpu.make_async_remote_copy(
                src_ref=slot(k, origin),
                dst_ref=slot(k, origin),
                send_sem=send.at[0],
                recv_sem=recv.at[k, origin],
                device_id=pair_dev,
                device_id_type=MESH,
            ).wait_recv()

    xsends = []

    def xpush(src, origin, dev):
        copy = pltpu.make_async_remote_copy(
            src_ref=src,
            dst_ref=oxn.at[origin],
            send_sem=xsend.at[len(xsends)],
            recv_sem=xrecv.at[origin],
            device_id=dev,
            device_id_type=MESH,
        )
        copy.start()
        xsends.append(copy)

    def xarrive(origin):
        pltpu.make_async_remote_copy(
            src_ref=oxn.at[origin],
            dst_ref=oxn.at[origin],
            send_sem=xsend.at[0],
            recv_sem=xrecv.at[origin],
            device_id=mate_dev,
            device_id_type=MESH,
        ).wait_recv()

    inputs = (wqkv, wo)
    own = [pltpu.make_async_copy(xn, oxn.at[e], local.at[2])]
    own += [pltpu.make_async_copy(inputs[k], slot(k, g), local.at[k]) for k in range(2)]
    for copy in own:
        copy.start()
    xpush(xn, e, mate_dev)
    for dev in chip_devs:
        xpush(xn, e, dev)
    for dev in (pair_dev, plus_dev, minus_dev):
        for k in range(2):
            push(k, g, inputs[k], dev)
    partner = g + 1 - 2 * xh
    arrive(partner)
    forward(partner, plus_dev)
    forward(partner, minus_dev)
    chip_origins = [2 * lax.rem(chip + j, chips) + core for j in range(1, chips)]
    normed_order = [chip_origins[0:2], chip_origins[2:5], chip_origins[5:]]
    for step in range(1, 4):
        behind = lax.rem(z - step + columns, columns)
        ahead = lax.rem(z + step, columns)
        for origin in (2 * behind, 2 * behind + 1):
            arrive(origin)
        for origin in ((2 * behind, 2 * behind + 1) if step < 3 else (2 * behind,)):
            forward(origin, plus_dev)
        for origin in (2 * ahead, 2 * ahead + 1):
            arrive(origin)
        for origin in ((2 * ahead, 2 * ahead + 1) if step < 3 else (2 * ahead + 1,)):
            forward(origin, minus_dev)
        for origin in normed_order[step - 1]:
            xarrive(origin)
            xpush(oxn.at[origin], origin, mate_dev)
    across = lax.rem(z + columns // 2, columns)
    arrive(2 * across)
    arrive(2 * across + 1)
    mate_core = 1 - core
    xarrive(e + 1 - 2 * core)
    for j in range(1, chips):
        xarrive(2 * lax.rem(chip + j, chips) + mate_core)
    for copy in sends + xsends:
        copy.wait_send()
    for copy in own:
        copy.wait()


def gather_all(q_in, kv_in, o_in, h_in, gain_in, n_group, n_expert):
    any_spec = pl.BlockSpec(memory_space=pl.ANY)
    vmem = pl.BlockSpec(memory_space=pltpu.VMEM)
    depth = HEAD_DIMENSION
    joined = (q_in.shape[0], q_in.shape[1] + 2 * depth)
    shapes = [
        jax.ShapeDtypeStruct((n_group,) + joined, jnp.bfloat16),
        jax.ShapeDtypeStruct((n_group,) + o_in.shape, jnp.bfloat16),
        jax.ShapeDtypeStruct((n_expert,) + h_in.shape, jnp.bfloat16),
    ]
    return pl.pallas_call(
        functools.partial(gather_kernel, n_group, n_expert, q_in.shape[1] // depth),
        out_shape=tuple(shapes),
        in_specs=[vmem] * 5,
        out_specs=tuple([any_spec] * 3),
        scratch_shapes=[
            pltpu.SemaphoreType.DMA((32,)),
            pltpu.SemaphoreType.DMA((2, n_group)),
            pltpu.SemaphoreType.DMA((n_expert,)),
            pltpu.SemaphoreType.DMA((n_expert,)),
            pltpu.SemaphoreType.DMA((3,)),
            pltpu.VMEM(joined, jnp.bfloat16),
            pltpu.VMEM(o_in.shape, jnp.bfloat16),
            pltpu.VMEM(h_in.shape, jnp.bfloat16),
        ],
        compiler_params=pltpu.CompilerParams(collective_id=0, has_side_effects=True),
    )(q_in, kv_in, o_in, h_in, gain_in)


def combine_kernel(blocks, attended_ref, weight_ref, out_ref, outgoing, incoming, send, recv):
    g = lax.axis_index("group")
    e = lax.axis_index("expert")
    core = lax.rem(e, 2)
    mate_dev = (g, e + 1 - 2 * core)
    rows = out_ref.shape[1]
    barrier = pltpu.get_barrier_semaphore()
    pl.semaphore_signal(barrier, 1, device_id=mate_dev, device_id_type=MESH)
    pl.semaphore_wait(barrier, 1)

    def partial(block):
        start = pl.multiple_of(block * rows, rows)
        return jnp.dot(
            attended_ref[pl.ds(start, rows), :], weight_ref[...], preferred_element_type=jnp.float32
        ).astype(jnp.bfloat16)

    for i in range(blocks):
        outgoing[i] = partial(2 * i + 1 - core)
    copy = pltpu.make_async_remote_copy(
        src_ref=outgoing,
        dst_ref=incoming,
        send_sem=send.at[0],
        recv_sem=recv.at[0],
        device_id=mate_dev,
        device_id_type=MESH,
    )
    copy.start()
    for i in range(blocks):
        out_ref[i] = partial(2 * i + core)
    copy.wait()
    for i in range(blocks):
        out_ref[i] = (out_ref[i].astype(jnp.float32) + incoming[i].astype(jnp.float32)).astype(
            jnp.bfloat16
        )


def project_and_combine(attended, weight, experts_axis):
    rows = attended.shape[0] // experts_axis
    blocks = experts_axis // 2
    shape = (blocks, rows, weight.shape[1])
    vmem = pl.BlockSpec(memory_space=pltpu.VMEM)
    return pl.pallas_call(
        functools.partial(combine_kernel, blocks),
        out_shape=jax.ShapeDtypeStruct(shape, jnp.bfloat16),
        in_specs=[vmem, vmem],
        out_specs=vmem,
        scratch_shapes=[
            pltpu.VMEM(shape, jnp.bfloat16),
            pltpu.VMEM(shape, jnp.bfloat16),
            pltpu.SemaphoreType.DMA((1,)),
            pltpu.SemaphoreType.DMA((1,)),
        ],
        compiler_params=pltpu.CompilerParams(collective_id=4, has_side_effects=True),
    )(attended, weight)


def combine_scatter_kernel(blocks, attended_ref, weight_ref, out_ref, outgoing, incoming, combined, send, recv, chip_send, chip_recv, local):
    g = lax.axis_index("group")
    e = lax.axis_index("expert")
    core = lax.rem(e, 2)
    chip = lax.div(e, 2)
    mate_dev = (g, e + 1 - 2 * core)
    chip_devs = [(g, 2 * lax.rem(chip + j, blocks) + core) for j in range(1, blocks)]
    rows = out_ref.shape[1]
    barrier = pltpu.get_barrier_semaphore()
    for dev in [mate_dev] + chip_devs:
        pl.semaphore_signal(barrier, 1, device_id=dev, device_id_type=MESH)
    pl.semaphore_wait(barrier, blocks)

    def partial(block):
        start = pl.multiple_of(block * rows, rows)
        return jnp.dot(
            attended_ref[pl.ds(start, rows), :], weight_ref[...], preferred_element_type=jnp.float32
        ).astype(jnp.bfloat16)

    for i in range(blocks):
        outgoing[i] = partial(2 * i + 1 - core)
    copy = pltpu.make_async_remote_copy(
        src_ref=outgoing,
        dst_ref=incoming,
        send_sem=send.at[0],
        recv_sem=recv.at[0],
        device_id=mate_dev,
        device_id_type=MESH,
    )
    copy.start()
    for i in range(blocks):
        combined[i] = partial(2 * i + core)
    copy.wait()
    pushes = []
    for j in range(1, blocks):
        i = lax.rem(chip + j, blocks)
        combined[i] = (combined[i].astype(jnp.float32) + incoming[i].astype(jnp.float32)).astype(
            jnp.bfloat16
        )
        push = pltpu.make_async_remote_copy(
            src_ref=combined.at[i],
            dst_ref=out_ref.at[chip],
            send_sem=chip_send.at[j],
            recv_sem=chip_recv.at[j],
            device_id=chip_devs[j - 1],
            device_id_type=MESH,
        )
        push.start()
        pushes.append(push)
    combined[chip] = (combined[chip].astype(jnp.float32) + incoming[chip].astype(jnp.float32)).astype(
        jnp.bfloat16
    )
    own = pltpu.make_async_copy(combined.at[chip], out_ref.at[chip], local.at[0])
    own.start()
    for push in pushes:
        push.wait()
    own.wait()


def combine_and_scatter(attended, weight, experts_axis):
    rows = attended.shape[0] // experts_axis
    blocks = experts_axis // 2
    shape = (blocks, rows, weight.shape[1])
    vmem = pl.BlockSpec(memory_space=pltpu.VMEM)
    return pl.pallas_call(
        functools.partial(combine_scatter_kernel, blocks),
        out_shape=jax.ShapeDtypeStruct(shape, jnp.bfloat16),
        in_specs=[vmem, vmem],
        out_specs=pl.BlockSpec(memory_space=pl.ANY),
        scratch_shapes=[
            pltpu.VMEM(shape, jnp.bfloat16),
            pltpu.VMEM(shape, jnp.bfloat16),
            pltpu.VMEM(shape, jnp.bfloat16),
            pltpu.SemaphoreType.DMA((1,)),
            pltpu.SemaphoreType.DMA((1,)),
            pltpu.SemaphoreType.DMA((blocks,)),
            pltpu.SemaphoreType.DMA((blocks,)),
            pltpu.SemaphoreType.DMA((1,)),
        ],
        compiler_params=pltpu.CompilerParams(collective_id=7, has_side_effects=True),
    )(attended, weight)


def mate_kernel(part, out, send, recv):
    g = lax.axis_index("group")
    e = lax.axis_index("expert")
    core = lax.rem(e, 2)
    mate_dev = (g, e + 1 - 2 * core)
    barrier = pltpu.get_barrier_semaphore()
    pl.semaphore_signal(barrier, 1, device_id=mate_dev, device_id_type=MESH)
    pl.semaphore_wait(barrier, 1)
    copy = pltpu.make_async_remote_copy(
        src_ref=part.at[:, 1 - core],
        dst_ref=out,
        send_sem=send.at[0],
        recv_sem=recv.at[0],
        device_id=mate_dev,
        device_id_type=MESH,
    )
    copy.start()
    copy.wait()


def exchange_with_mate(part):
    any_spec = pl.BlockSpec(memory_space=pl.ANY)
    shape = (part.shape[0],) + part.shape[2:]
    return pl.pallas_call(
        mate_kernel,
        out_shape=jax.ShapeDtypeStruct(shape, part.dtype),
        in_specs=[any_spec],
        out_specs=any_spec,
        scratch_shapes=[pltpu.SemaphoreType.DMA((1,)), pltpu.SemaphoreType.DMA((1,))],
        compiler_params=pltpu.CompilerParams(collective_id=4, has_side_effects=True),
    )(part)


def chip_scatter_kernel(chips, part, out, send, recv, local):
    g = lax.axis_index("group")
    e = lax.axis_index("expert")
    core = lax.rem(e, 2)
    chip = lax.div(e, 2)
    devs = [(g, 2 * lax.rem(chip + j, chips) + core) for j in range(1, chips)]
    barrier = pltpu.get_barrier_semaphore()
    for dev in devs:
        pl.semaphore_signal(barrier, 1, device_id=dev, device_id_type=MESH)
    pl.semaphore_wait(barrier, len(devs))
    copies = []
    for j in range(1, chips):
        copy = pltpu.make_async_remote_copy(
            src_ref=part.at[lax.rem(chip + j, chips)],
            dst_ref=out.at[chip],
            send_sem=send.at[j],
            recv_sem=recv.at[j],
            device_id=devs[j - 1],
            device_id_type=MESH,
        )
        copy.start()
        copies.append(copy)
    own = pltpu.make_async_copy(part.at[chip], out.at[chip], local.at[0])
    own.start()
    for copy in copies:
        copy.wait()
    own.wait()


def scatter_to_chips(part):
    chips = part.shape[0]
    any_spec = pl.BlockSpec(memory_space=pl.ANY)
    return pl.pallas_call(
        functools.partial(chip_scatter_kernel, chips),
        out_shape=jax.ShapeDtypeStruct(part.shape, part.dtype),
        in_specs=[any_spec],
        out_specs=any_spec,
        scratch_shapes=[
            pltpu.SemaphoreType.DMA((chips,)),
            pltpu.SemaphoreType.DMA((chips,)),
            pltpu.SemaphoreType.DMA((1,)),
        ],
        compiler_params=pltpu.CompilerParams(collective_id=5, has_side_effects=True),
    )(part)


def scatter_kernel(n_expert, part, out, send, recv, local):
    g = lax.axis_index("group")
    e = lax.axis_index("expert")
    barrier = pltpu.get_barrier_semaphore()
    for j in range(1, n_expert):
        pl.semaphore_signal(barrier, 1, device_id=(g, lax.rem(e + j, n_expert)), device_id_type=MESH)
    pl.semaphore_wait(barrier, n_expert - 1)
    copies = []
    for j in range(1, n_expert):
        peer = lax.rem(e + j, n_expert)
        copy = pltpu.make_async_remote_copy(
            src_ref=part.at[peer],
            dst_ref=out.at[e],
            send_sem=send.at[j],
            recv_sem=recv.at[j],
            device_id=(g, peer),
            device_id_type=MESH,
        )
        copy.start()
        copies.append(copy)
    own = pltpu.make_async_copy(part.at[e], out.at[e], local.at[0])
    own.start()
    for copy in copies:
        copy.wait()
    own.wait()


def scatter_blocks(part, n_expert, collective_id):
    any_spec = pl.BlockSpec(memory_space=pl.ANY)
    return pl.pallas_call(
        functools.partial(scatter_kernel, n_expert),
        out_shape=jax.ShapeDtypeStruct(part.shape, part.dtype),
        in_specs=[any_spec],
        out_specs=any_spec,
        scratch_shapes=[
            pltpu.SemaphoreType.DMA((n_expert,)),
            pltpu.SemaphoreType.DMA((n_expert,)),
            pltpu.SemaphoreType.DMA((1,)),
        ],
        compiler_params=pltpu.CompilerParams(collective_id=collective_id, has_side_effects=True),
    )(part)


def attention_kernel(scale, heads, q_ref, own_ref, far_ref, length_ref, o_ref):
    block = q_ref.shape[0]
    rows = own_ref.shape[1]
    half = rows // 2
    parity = lax.rem(lax.axis_index("group"), 2)

    def places(side, shape, axis, start):
        indices = lax.broadcasted_iota(jnp.int32, shape, axis) + start
        return indices + jnp.where(side == 0, jnp.where(indices < half, 0, rows), half)

    query_places = places(parity, (block, 1), 0, pl.program_id(0) * block)
    length = length_ref[0, 0]
    own_places = places(parity, (1, rows), 1, 0)
    far_places = places(1 - parity, (1, rows), 1, 0)
    own_allowed = (own_places <= query_places) & (own_places < length)
    far_allowed = (far_places <= query_places) & (far_places < length)
    own_keys, own_values = own_ref[0], own_ref[1]
    far_keys, far_values = far_ref[0], far_ref[1]
    depth = own_keys.shape[1]
    contract = (((1,), (1,)), ((), ()))
    for h in range(heads):
        query = q_ref[:, h * depth : (h + 1) * depth]
        own_weights = jnp.where(
            own_allowed,
            jnp.exp(lax.dot_general(query, own_keys, contract, preferred_element_type=jnp.float32) * scale),
            0.0,
        )
        far_weights = jnp.where(
            far_allowed,
            jnp.exp(lax.dot_general(query, far_keys, contract, preferred_element_type=jnp.float32) * scale),
            0.0,
        )
        denominators = jnp.sum(own_weights, axis=-1, keepdims=True) + jnp.sum(
            far_weights, axis=-1, keepdims=True
        )
        weighted = jnp.dot(
            own_weights.astype(jnp.bfloat16), own_values, preferred_element_type=jnp.float32
        ) + jnp.dot(far_weights.astype(jnp.bfloat16), far_values, preferred_element_type=jnp.float32)
        o_ref[:, h * depth : (h + 1) * depth] = (weighted / denominators).astype(o_ref.dtype)


def attention(queries, own_kv, far_kv, length, scale):
    rows, width = queries.shape
    key_rows, depth = own_kv.shape[1:]
    block = min(512, rows)
    pair = pl.BlockSpec((2, key_rows, depth), lambda i: (0, 0, 0))
    return pl.pallas_call(
        functools.partial(attention_kernel, scale, width // depth),
        out_shape=jax.ShapeDtypeStruct((rows, width), jnp.bfloat16),
        grid=(rows // block,),
        in_specs=[
            pl.BlockSpec((block, width), lambda i: (i, 0)),
            pair,
            pair,
            pl.BlockSpec(memory_space=pltpu.SMEM),
        ],
        out_specs=pl.BlockSpec((block, width), lambda i: (i, 0)),
        cost_estimate=pl.CostEstimate(
            flops=8 * rows * key_rows * width,
            transcendentals=2 * rows * key_rows * (width // depth),
            bytes_accessed=2 * (2 * rows * width + 4 * key_rows * depth),
        ),
    )(queries, own_kv, far_kv, length.reshape(1, 1))

def norm_rows(values, gain_vector):
    widened = values.astype(jnp.float32)
    inverse_rms = lax.rsqrt(jnp.mean(widened * widened, axis=-1, keepdims=True) + epsilon)
    return widened * inverse_rms * gain_vector


def rotate(values, positions):
    half_width = values.shape[-1] // 2
    exponents = jnp.arange(half_width).astype(jnp.float32)
    inverse = jnp.exp(exponents * (-2.0 * math.log(rope_theta) / values.shape[-1]))
    angles = positions[:, None, None] * inverse[None, None, :]
    cosine_values = jnp.cos(angles)
    sine_values = jnp.sin(angles)
    first_half = values[..., :half_width]
    second = values[..., half_width:]
    return jnp.concatenate(
        [
            first_half * cosine_values - second * sine_values,
            second * cosine_values + first_half * sine_values,
        ],
        axis=-1,
    )


def local_positions(parity, row_count):
    indices = jnp.arange(row_count)
    quarter = row_count // 2
    offset = jnp.where(parity == 0, jnp.where(indices < quarter, 0, 2 * quarter), quarter)
    return indices + offset


def prep_kernel(query_width, for_queries, x_ref, w_ref, table_ref, gain_ref, out_ref):
    x = x_ref[...]
    block = x.shape[0]
    depth = table_ref.shape[1]
    parity = lax.rem(lax.axis_index("group"), 2)
    start = pl.multiple_of(parity * (table_ref.shape[0] // 2) + pl.program_id(0) * block, block)
    table = table_ref[pl.ds(start, block), :]
    swapped = pltpu.roll(table, depth // 2, 1)
    first_half = lax.broadcasted_iota(jnp.int32, table.shape, 1) < depth // 2
    cosines = jnp.where(first_half, table, swapped)
    sines = jnp.where(first_half, -swapped, table)

    def project(start, stop):
        return jnp.dot(x, w_ref[:, start:stop], preferred_element_type=jnp.float32).astype(jnp.bfloat16)

    def norm_rope(values, gain):
        values = values.astype(jnp.float32)
        inverse_rms = lax.rsqrt(jnp.mean(values * values, axis=-1, keepdims=True) + epsilon)
        normed = values * inverse_rms * gain
        return (normed * cosines + pltpu.roll(normed, depth // 2, 1) * sines).astype(jnp.bfloat16)

    if for_queries:
        queries = project(0, query_width)
        for h in range(queries.shape[1] // depth):
            out_ref[:, h * depth : (h + 1) * depth] = norm_rope(
                queries[:, h * depth : (h + 1) * depth], gain_ref[...]
            )
    else:
        out_ref[0] = norm_rope(project(0, depth), gain_ref[...])
        out_ref[1] = project(depth, 2 * depth)


def prep(normed_rows, joined, table, gain, for_queries):
    rows, width = normed_rows.shape
    depth = table.shape[1]
    query_width = joined.shape[1] - 2 * depth
    block = min(512, rows)
    whole = lambda shape: pl.BlockSpec(shape, lambda i: (0, 0))
    if for_queries:
        out_shape = jax.ShapeDtypeStruct((rows, query_width), jnp.bfloat16)
        out_spec = pl.BlockSpec((block, query_width), lambda i: (i, 0))
        columns = query_width
    else:
        out_shape = jax.ShapeDtypeStruct((2, rows, depth), jnp.bfloat16)
        out_spec = pl.BlockSpec((2, block, depth), lambda i: (0, i, 0))
        columns = 2 * depth
    return pl.pallas_call(
        functools.partial(prep_kernel, query_width, for_queries),
        out_shape=out_shape,
        grid=(rows // block,),
        in_specs=[
            pl.BlockSpec((block, width), lambda i: (i, 0)),
            pl.BlockSpec((width, columns), lambda i: (0, 0 if for_queries else 1)),
            whole(table.shape),
            whole((1, depth)),
        ],
        out_specs=out_spec,
        cost_estimate=pl.CostEstimate(
            flops=2 * rows * width * columns,
            transcendentals=rows * (columns // depth),
            bytes_accessed=2 * (rows * width + width * columns + rows * columns),
        ),
    )(normed_rows, joined, table, gain.reshape(1, depth))

def rope_table(row_count, depth):
    half = depth // 2
    frequencies = rope_theta ** (-2.0 * np.arange(half) / depth)
    indices = np.arange(row_count)
    quarter = row_count // 2
    places = np.concatenate([np.where(indices < quarter, indices, indices + 2 * quarter), indices + quarter])
    angles = places[:, None].astype(np.float64) * frequencies[None, :]
    return jnp.asarray(np.concatenate([np.cos(angles), np.sin(angles)], axis=1), jnp.float32)

def per_device(
    hidden_in,
    norm_attention,
    norm_experts,
    query_master,
    trainer_key_value_weight,
    output_master,
    query_gain,
    key_gain,
    lengths,
    router,
    expert_gateup,
    expert_down,
    routes,
):
    experts_axis = lax.axis_size("expert")
    group_member = lax.axis_index("expert")
    group_index = lax.axis_index("group")
    local_head_count = QUERY_HEADS // experts_axis
    width_here = local_head_count * HEAD_DIMENSION
    common_head = group_member * local_head_count // (QUERY_HEADS // KEY_VALUE_HEADS)
    groups_axis = lax.axis_size("group")
    joined_parts, output_parts, normed_parts = gather_all(
        query_master,
        trainer_key_value_weight,
        output_master,
        hidden_in,
        norm_attention.reshape(1, -1),
        groups_axis,
        experts_axis,
    )
    model_width = hidden_in.shape[1]
    local_rows = normed_parts.shape[0] * normed_parts.shape[1]
    parity = group_index % 2
    prep_args = (
        normed_parts.reshape(local_rows, model_width),
        joined_parts.reshape(model_width, -1),
        rope_table(local_rows, HEAD_DIMENSION),
    )
    key_values = prep(*prep_args, key_gain, False)
    query_rows_list = prep(*prep_args, query_gain, True)
    partner = from_partner(key_values, "group", 0)
    valid_length = jnp.sum(jnp.where(jnp.arange(lengths.shape[0]) == group_index // 2, lengths, 0))
    attended = attention(
        query_rows_list,
        key_values,
        partner,
        valid_length.astype(jnp.int32),
        HEAD_DIMENSION ** (-0.5),
    )
    output_weight = jnp.transpose(output_parts, (1, 0, 2)).reshape(output_parts.shape[1], -1)
    owned = combine_and_scatter(attended, output_weight, experts_axis)
    summed = jnp.sum(owned.astype(jnp.float32), axis=0)
    hidden = (hidden_in.astype(jnp.float32) + summed).astype(jnp.bfloat16)
    normed_second = norm_rows(hidden, norm_experts).astype(jnp.bfloat16)
    logits = jnp.dot(normed_second, router, preferred_element_type=jnp.float32)
    route_table = routes[:, :, None] == jnp.arange(logits.shape[1])[None, None, :]
    picked = jnp.sum(jnp.where(route_table, logits[:, None, :], 0.0), axis=-1)
    raised = jnp.exp(picked)
    gate_values = raised / jnp.sum(raised, axis=1, keepdims=True)
    inside = routes < experts_axis
    gate_window = jnp.sum(jnp.where(inside, gate_values, 0.0), axis=1)
    expert_window = jnp.sum(jnp.where(inside, routes, 0), axis=1)
    present = jnp.any(inside, axis=1)
    capacity = local_rows // (experts_axis * experts_axis)
    member_table = (
        present[:, None] & (expert_window[:, None] == jnp.arange(experts_axis)[None, :])
    ).astype(jnp.int32)
    ranking = jnp.sum(jnp.cumsum(member_table, axis=0) * member_table, axis=1) - 1
    slot_index = expert_window * capacity + ranking
    select = (
        (jnp.arange(experts_axis * capacity)[:, None] == slot_index[None, :]) & present[None, :]
    ).astype(jnp.bfloat16)
    select_slots = select.reshape(experts_axis, capacity, -1)
    outgoing = jnp.einsum(
        "jct,td->jcd", select_slots, normed_second, preferred_element_type=jnp.float32
    ).astype(jnp.bfloat16)
    gateup_here = expert_gateup[0]
    down_here = expert_down[0]
    hidden_units = down_here.shape[0]
    slot_items = scatter_blocks(outgoing, experts_axis, 2)
    gate_up = jnp.einsum("jcd,df->jcf", slot_items, gateup_here, preferred_element_type=jnp.float32)
    active = (jax.nn.silu(gate_up[..., :hidden_units]) * gate_up[..., hidden_units:]).astype(
        jnp.bfloat16
    )
    result = jnp.einsum(
        "jcf,fd->jcd", active, down_here, preferred_element_type=jnp.float32
    ).astype(jnp.bfloat16)
    returned = scatter_blocks(result, experts_axis, 3)
    combined = jnp.einsum(
        "jct,jcd->td", select_slots, returned, preferred_element_type=jnp.float32
    )
    expert_mix = (gate_window[:, None] * combined).astype(jnp.bfloat16)
    return (hidden, expert_mix)


def solution(mesh):
    return jax.shard_map(
        per_device,
        mesh=mesh,
        in_specs=(
            P(("group", "expert"), None),
            P(),
            P(),
            P("group", "expert"),
            P(None, "group", None),
            P("expert", "group"),
            P(),
            P(),
            P(),
            P(),
            P("expert", None, None),
            P("expert", None, None),
            P(("group", "expert"), None),
        ),
        out_specs=(P(("group", "expert"), None), P(("group", "expert"), None)),
        check_vma=False,
    )
```

```python
import functools
import math

import jax
import numpy as np
import jax.numpy as jnp
from jax import lax
from jax.experimental import pallas as pl
from jax.experimental.pallas import tpu as pltpu
from jax.sharding import PartitionSpec as P

MESH = pl.DeviceIdType.MESH

QUERY_HEADS = 32
KEY_VALUE_HEADS = 4
HEAD_DIMENSION = 128


epsilon = 1e-06
rope_theta = 1000000.0


def from_partner(block, axis, stride):
    count = lax.axis_size(axis)
    route = []
    for low in range(count):
        high = low | 1 << stride
        if high != low and high < count:
            route += [(low, high), (high, low)]
    return lax.ppermute(block, axis, route)


def gather_kernel(n_group, n_expert, heads_here, q_in, kv_in, o_in, h_in, gain_in, oqkv, oo, oxn, send, recv, xsend, xrecv, local, wqkv, wo, xn):
    e_here = lax.axis_index("expert")
    depth = HEAD_DIMENSION
    column = pl.multiple_of(lax.div(e_here * heads_here, QUERY_HEADS // KEY_VALUE_HEADS) * depth, depth)
    query_width = q_in.shape[1]
    wqkv[:, 0:query_width] = q_in[...].astype(jnp.bfloat16)
    wqkv[:, query_width : query_width + depth] = kv_in[0, :, pl.ds(column, depth)].astype(jnp.bfloat16)
    wqkv[:, query_width + depth : query_width + 2 * depth] = kv_in[1, :, pl.ds(column, depth)].astype(
        jnp.bfloat16
    )
    wo[...] = o_in[...].astype(jnp.bfloat16)
    xn[...] = norm_rows(h_in[...], gain_in[...]).astype(jnp.bfloat16)
    g = lax.axis_index("group")
    e = lax.axis_index("expert")
    columns = n_group // 2
    z = lax.div(g, 2)
    xh = lax.rem(g, 2)
    zp = lax.rem(z + 1, columns)
    zm = lax.rem(z + columns - 1, columns)
    plus_dev = (2 * zp + xh, e)
    minus_dev = (2 * zm + xh, e)
    pair_dev = (g + 1 - 2 * xh, e)
    core = lax.rem(e, 2)
    chip = lax.div(e, 2)
    chips = n_expert // 2
    mate_dev = (g, e + 1 - 2 * core)
    chip_devs = [(g, 2 * lax.rem(chip + j, chips) + core) for j in range(1, chips)]
    barrier = pltpu.get_barrier_semaphore()
    peers = [plus_dev, minus_dev, pair_dev, mate_dev] + chip_devs
    for dev in peers:
        pl.semaphore_signal(barrier, 1, device_id=dev, device_id_type=MESH)
    pl.semaphore_wait(barrier, len(peers))

    def slot(k, origin):
        return (oqkv, oo)[k].at[origin]

    sends = []

    def push(k, origin, src, dev):
        copy = pltpu.make_async_remote_copy(
            src_ref=src,
            dst_ref=slot(k, origin),
            send_sem=send.at[len(sends)],
            recv_sem=recv.at[k, origin],
            device_id=dev,
            device_id_type=MESH,
        )
        copy.start()
        sends.append(copy)

    def forward(origin, dev):
        for k in range(2):
            push(k, origin, slot(k, origin), dev)

    def arrive(origin):
        for k in range(2):
            pltpu.make_async_remote_copy(
                src_ref=slot(k, origin),
                dst_ref=slot(k, origin),
                send_sem=send.at[0],
                recv_sem=recv.at[k, origin],
                device_id=pair_dev,
                device_id_type=MESH,
            ).wait_recv()

    xsends = []

    def xpush(src, origin, dev):
        copy = pltpu.make_async_remote_copy(
            src_ref=src,
            dst_ref=oxn.at[origin],
            send_sem=xsend.at[len(xsends)],
            recv_sem=xrecv.at[origin],
            device_id=dev,
            device_id_type=MESH,
        )
        copy.start()
        xsends.append(copy)

    def xarrive(origin):
        pltpu.make_async_remote_copy(
            src_ref=oxn.at[origin],
            dst_ref=oxn.at[origin],
            send_sem=xsend.at[0],
            recv_sem=xrecv.at[origin],
            device_id=mate_dev,
            device_id_type=MESH,
        ).wait_recv()

    inputs = (wqkv, wo)
    own = [pltpu.make_async_copy(xn, oxn.at[e], local.at[2])]
    own += [pltpu.make_async_copy(inputs[k], slot(k, g), local.at[k]) for k in range(2)]
    for copy in own:
        copy.start()
    for dev in (pair_dev, plus_dev, minus_dev):
        for k in range(2):
            push(k, g, inputs[k], dev)
    xpush(xn, e, mate_dev)
    for dev in chip_devs:
        xpush(xn, e, dev)
    partner = g + 1 - 2 * xh
    arrive(partner)
    forward(partner, plus_dev)
    forward(partner, minus_dev)
    chip_origins = [2 * lax.rem(chip + j, chips) + core for j in range(1, chips)]
    normed_order = [chip_origins[0:2], chip_origins[2:5], chip_origins[5:]]
    for step in range(1, 4):
        behind = lax.rem(z - step + columns, columns)
        ahead = lax.rem(z + step, columns)
        for origin in (2 * behind, 2 * behind + 1):
            arrive(origin)
        for origin in ((2 * behind, 2 * behind + 1) if step < 3 else (2 * behind,)):
            forward(origin, plus_dev)
        for origin in (2 * ahead, 2 * ahead + 1):
            arrive(origin)
        for origin in ((2 * ahead, 2 * ahead + 1) if step < 3 else (2 * ahead + 1,)):
            forward(origin, minus_dev)
        for origin in normed_order[step - 1]:
            xarrive(origin)
            xpush(oxn.at[origin], origin, mate_dev)
    across = lax.rem(z + columns // 2, columns)
    arrive(2 * across)
    arrive(2 * across + 1)
    mate_core = 1 - core
    xarrive(e + 1 - 2 * core)
    for j in range(1, chips):
        xarrive(2 * lax.rem(chip + j, chips) + mate_core)
    for copy in sends + xsends:
        copy.wait_send()
    for copy in own:
        copy.wait()


def gather_all(q_in, kv_in, o_in, h_in, gain_in, n_group, n_expert):
    any_spec = pl.BlockSpec(memory_space=pl.ANY)
    vmem = pl.BlockSpec(memory_space=pltpu.VMEM)
    depth = HEAD_DIMENSION
    joined = (q_in.shape[0], q_in.shape[1] + 2 * depth)
    shapes = [
        jax.ShapeDtypeStruct((n_group,) + joined, jnp.bfloat16),
        jax.ShapeDtypeStruct((n_group,) + o_in.shape, jnp.bfloat16),
        jax.ShapeDtypeStruct((n_expert,) + h_in.shape, jnp.bfloat16),
    ]
    return pl.pallas_call(
        functools.partial(gather_kernel, n_group, n_expert, q_in.shape[1] // depth),
        out_shape=tuple(shapes),
        in_specs=[vmem] * 5,
        out_specs=tuple([any_spec] * 3),
        scratch_shapes=[
            pltpu.SemaphoreType.DMA((32,)),
            pltpu.SemaphoreType.DMA((2, n_group)),
            pltpu.SemaphoreType.DMA((n_expert,)),
            pltpu.SemaphoreType.DMA((n_expert,)),
            pltpu.SemaphoreType.DMA((3,)),
            pltpu.VMEM(joined, jnp.bfloat16),
            pltpu.VMEM(o_in.shape, jnp.bfloat16),
            pltpu.VMEM(h_in.shape, jnp.bfloat16),
        ],
        compiler_params=pltpu.CompilerParams(collective_id=0, has_side_effects=True),
    )(q_in, kv_in, o_in, h_in, gain_in)


def combine_kernel(blocks, attended_ref, weight_ref, out_ref, outgoing, incoming, send, recv):
    g = lax.axis_index("group")
    e = lax.axis_index("expert")
    core = lax.rem(e, 2)
    mate_dev = (g, e + 1 - 2 * core)
    rows = out_ref.shape[1]
    barrier = pltpu.get_barrier_semaphore()
    pl.semaphore_signal(barrier, 1, device_id=mate_dev, device_id_type=MESH)
    pl.semaphore_wait(barrier, 1)

    def partial(block):
        start = pl.multiple_of(block * rows, rows)
        return jnp.dot(
            attended_ref[pl.ds(start, rows), :], weight_ref[...], preferred_element_type=jnp.float32
        ).astype(jnp.bfloat16)

    for i in range(blocks):
        outgoing[i] = partial(2 * i + 1 - core)
    copy = pltpu.make_async_remote_copy(
        src_ref=outgoing,
        dst_ref=incoming,
        send_sem=send.at[0],
        recv_sem=recv.at[0],
        device_id=mate_dev,
        device_id_type=MESH,
    )
    copy.start()
    for i in range(blocks):
        out_ref[i] = partial(2 * i + core)
    copy.wait()
    for i in range(blocks):
        out_ref[i] = (out_ref[i].astype(jnp.float32) + incoming[i].astype(jnp.float32)).astype(
            jnp.bfloat16
        )


def project_and_combine(attended, weight, experts_axis):
    rows = attended.shape[0] // experts_axis
    blocks = experts_axis // 2
    shape = (blocks, rows, weight.shape[1])
    vmem = pl.BlockSpec(memory_space=pltpu.VMEM)
    return pl.pallas_call(
        functools.partial(combine_kernel, blocks),
        out_shape=jax.ShapeDtypeStruct(shape, jnp.bfloat16),
        in_specs=[vmem, vmem],
        out_specs=vmem,
        scratch_shapes=[
            pltpu.VMEM(shape, jnp.bfloat16),
            pltpu.VMEM(shape, jnp.bfloat16),
            pltpu.SemaphoreType.DMA((1,)),
            pltpu.SemaphoreType.DMA((1,)),
        ],
        compiler_params=pltpu.CompilerParams(collective_id=4, has_side_effects=True),
    )(attended, weight)


def combine_scatter_kernel(blocks, attended_ref, weight_ref, out_ref, outgoing, incoming, combined, send, recv, chip_send, chip_recv, local):
    g = lax.axis_index("group")
    e = lax.axis_index("expert")
    core = lax.rem(e, 2)
    chip = lax.div(e, 2)
    mate_dev = (g, e + 1 - 2 * core)
    chip_devs = [(g, 2 * lax.rem(chip + j, blocks) + core) for j in range(1, blocks)]
    rows = out_ref.shape[1]
    barrier = pltpu.get_barrier_semaphore()
    for dev in [mate_dev] + chip_devs:
        pl.semaphore_signal(barrier, 1, device_id=dev, device_id_type=MESH)
    pl.semaphore_wait(barrier, blocks)

    def partial(block):
        start = pl.multiple_of(block * rows, rows)
        return jnp.dot(
            attended_ref[pl.ds(start, rows), :], weight_ref[...], preferred_element_type=jnp.float32
        ).astype(jnp.bfloat16)

    for i in range(blocks):
        outgoing[i] = partial(2 * i + 1 - core)
    copy = pltpu.make_async_remote_copy(
        src_ref=outgoing,
        dst_ref=incoming,
        send_sem=send.at[0],
        recv_sem=recv.at[0],
        device_id=mate_dev,
        device_id_type=MESH,
    )
    copy.start()
    for i in range(blocks):
        combined[i] = partial(2 * i + core)
    copy.wait()
    pushes = []
    for j in range(1, blocks):
        i = lax.rem(chip + j, blocks)
        combined[i] = (combined[i].astype(jnp.float32) + incoming[i].astype(jnp.float32)).astype(
            jnp.bfloat16
        )
        push = pltpu.make_async_remote_copy(
            src_ref=combined.at[i],
            dst_ref=out_ref.at[chip],
            send_sem=chip_send.at[j],
            recv_sem=chip_recv.at[j],
            device_id=chip_devs[j - 1],
            device_id_type=MESH,
        )
        push.start()
        pushes.append(push)
    combined[chip] = (combined[chip].astype(jnp.float32) + incoming[chip].astype(jnp.float32)).astype(
        jnp.bfloat16
    )
    own = pltpu.make_async_copy(combined.at[chip], out_ref.at[chip], local.at[0])
    own.start()
    for push in pushes:
        push.wait()
    own.wait()


def combine_and_scatter(attended, weight, experts_axis):
    rows = attended.shape[0] // experts_axis
    blocks = experts_axis // 2
    shape = (blocks, rows, weight.shape[1])
    vmem = pl.BlockSpec(memory_space=pltpu.VMEM)
    return pl.pallas_call(
        functools.partial(combine_scatter_kernel, blocks),
        out_shape=jax.ShapeDtypeStruct(shape, jnp.bfloat16),
        in_specs=[vmem, vmem],
        out_specs=pl.BlockSpec(memory_space=pl.ANY),
        scratch_shapes=[
            pltpu.VMEM(shape, jnp.bfloat16),
            pltpu.VMEM(shape, jnp.bfloat16),
            pltpu.VMEM(shape, jnp.bfloat16),
            pltpu.SemaphoreType.DMA((1,)),
            pltpu.SemaphoreType.DMA((1,)),
            pltpu.SemaphoreType.DMA((blocks,)),
            pltpu.SemaphoreType.DMA((blocks,)),
            pltpu.SemaphoreType.DMA((1,)),
        ],
        compiler_params=pltpu.CompilerParams(collective_id=7, has_side_effects=True),
    )(attended, weight)


def mate_kernel(part, out, send, recv):
    g = lax.axis_index("group")
    e = lax.axis_index("expert")
    core = lax.rem(e, 2)
    mate_dev = (g, e + 1 - 2 * core)
    barrier = pltpu.get_barrier_semaphore()
    pl.semaphore_signal(barrier, 1, device_id=mate_dev, device_id_type=MESH)
    pl.semaphore_wait(barrier, 1)
    copy = pltpu.make_async_remote_copy(
        src_ref=part.at[:, 1 - core],
        dst_ref=out,
        send_sem=send.at[0],
        recv_sem=recv.at[0],
        device_id=mate_dev,
        device_id_type=MESH,
    )
    copy.start()
    copy.wait()


def exchange_with_mate(part):
    any_spec = pl.BlockSpec(memory_space=pl.ANY)
    shape = (part.shape[0],) + part.shape[2:]
    return pl.pallas_call(
        mate_kernel,
        out_shape=jax.ShapeDtypeStruct(shape, part.dtype),
        in_specs=[any_spec],
        out_specs=any_spec,
        scratch_shapes=[pltpu.SemaphoreType.DMA((1,)), pltpu.SemaphoreType.DMA((1,))],
        compiler_params=pltpu.CompilerParams(collective_id=4, has_side_effects=True),
    )(part)


def chip_scatter_kernel(chips, part, out, send, recv, local):
    g = lax.axis_index("group")
    e = lax.axis_index("expert")
    core = lax.rem(e, 2)
    chip = lax.div(e, 2)
    devs = [(g, 2 * lax.rem(chip + j, chips) + core) for j in range(1, chips)]
    barrier = pltpu.get_barrier_semaphore()
    for dev in devs:
        pl.semaphore_signal(barrier, 1, device_id=dev, device_id_type=MESH)
    pl.semaphore_wait(barrier, len(devs))
    copies = []
    for j in range(1, chips):
        copy = pltpu.make_async_remote_copy(
            src_ref=part.at[lax.rem(chip + j, chips)],
            dst_ref=out.at[chip],
            send_sem=send.at[j],
            recv_sem=recv.at[j],
            device_id=devs[j - 1],
            device_id_type=MESH,
        )
        copy.start()
        copies.append(copy)
    own = pltpu.make_async_copy(part.at[chip], out.at[chip], local.at[0])
    own.start()
    for copy in copies:
        copy.wait()
    own.wait()


def scatter_to_chips(part):
    chips = part.shape[0]
    any_spec = pl.BlockSpec(memory_space=pl.ANY)
    return pl.pallas_call(
        functools.partial(chip_scatter_kernel, chips),
        out_shape=jax.ShapeDtypeStruct(part.shape, part.dtype),
        in_specs=[any_spec],
        out_specs=any_spec,
        scratch_shapes=[
            pltpu.SemaphoreType.DMA((chips,)),
            pltpu.SemaphoreType.DMA((chips,)),
            pltpu.SemaphoreType.DMA((1,)),
        ],
        compiler_params=pltpu.CompilerParams(collective_id=5, has_side_effects=True),
    )(part)


def scatter_kernel(n_expert, part, out, send, recv, local):
    g = lax.axis_index("group")
    e = lax.axis_index("expert")
    barrier = pltpu.get_barrier_semaphore()
    for j in range(1, n_expert):
        pl.semaphore_signal(barrier, 1, device_id=(g, lax.rem(e + j, n_expert)), device_id_type=MESH)
    pl.semaphore_wait(barrier, n_expert - 1)
    copies = []
    for j in range(1, n_expert):
        peer = lax.rem(e + j, n_expert)
        copy = pltpu.make_async_remote_copy(
            src_ref=part.at[peer],
            dst_ref=out.at[e],
            send_sem=send.at[j],
            recv_sem=recv.at[j],
            device_id=(g, peer),
            device_id_type=MESH,
        )
        copy.start()
        copies.append(copy)
    own = pltpu.make_async_copy(part.at[e], out.at[e], local.at[0])
    own.start()
    for copy in copies:
        copy.wait()
    own.wait()


def scatter_blocks(part, n_expert, collective_id):
    any_spec = pl.BlockSpec(memory_space=pl.ANY)
    return pl.pallas_call(
        functools.partial(scatter_kernel, n_expert),
        out_shape=jax.ShapeDtypeStruct(part.shape, part.dtype),
        in_specs=[any_spec],
        out_specs=any_spec,
        scratch_shapes=[
            pltpu.SemaphoreType.DMA((n_expert,)),
            pltpu.SemaphoreType.DMA((n_expert,)),
            pltpu.SemaphoreType.DMA((1,)),
        ],
        compiler_params=pltpu.CompilerParams(collective_id=collective_id, has_side_effects=True),
    )(part)


def attention_kernel(scale, heads, q_ref, own_ref, far_ref, length_ref, o_ref):
    block = q_ref.shape[0]
    rows = own_ref.shape[1]
    half = rows // 2
    parity = lax.rem(lax.axis_index("group"), 2)

    def places(side, shape, axis, start):
        indices = lax.broadcasted_iota(jnp.int32, shape, axis) + start
        return indices + jnp.where(side == 0, jnp.where(indices < half, 0, rows), half)

    query_places = places(parity, (block, 1), 0, pl.program_id(0) * block)
    length = length_ref[0, 0]
    own_places = places(parity, (1, rows), 1, 0)
    far_places = places(1 - parity, (1, rows), 1, 0)
    own_allowed = (own_places <= query_places) & (own_places < length)
    far_allowed = (far_places <= query_places) & (far_places < length)
    own_keys, own_values = own_ref[0], own_ref[1]
    far_keys, far_values = far_ref[0], far_ref[1]
    depth = own_keys.shape[1]
    contract = (((1,), (1,)), ((), ()))
    for h in range(heads):
        query = q_ref[:, h * depth : (h + 1) * depth]
        own_weights = jnp.where(
            own_allowed,
            jnp.exp(lax.dot_general(query, own_keys, contract, preferred_element_type=jnp.float32) * scale),
            0.0,
        )
        far_weights = jnp.where(
            far_allowed,
            jnp.exp(lax.dot_general(query, far_keys, contract, preferred_element_type=jnp.float32) * scale),
            0.0,
        )
        denominators = jnp.sum(own_weights, axis=-1, keepdims=True) + jnp.sum(
            far_weights, axis=-1, keepdims=True
        )
        weighted = jnp.dot(
            own_weights.astype(jnp.bfloat16), own_values, preferred_element_type=jnp.float32
        ) + jnp.dot(far_weights.astype(jnp.bfloat16), far_values, preferred_element_type=jnp.float32)
        o_ref[:, h * depth : (h + 1) * depth] = (weighted / denominators).astype(o_ref.dtype)


def attention(queries, own_kv, far_kv, length, scale):
    rows, width = queries.shape
    key_rows, depth = own_kv.shape[1:]
    block = min(512, rows)
    pair = pl.BlockSpec((2, key_rows, depth), lambda i: (0, 0, 0))
    return pl.pallas_call(
        functools.partial(attention_kernel, scale, width // depth),
        out_shape=jax.ShapeDtypeStruct((rows, width), jnp.bfloat16),
        grid=(rows // block,),
        in_specs=[
            pl.BlockSpec((block, width), lambda i: (i, 0)),
            pair,
            pair,
            pl.BlockSpec(memory_space=pltpu.SMEM),
        ],
        out_specs=pl.BlockSpec((block, width), lambda i: (i, 0)),
        cost_estimate=pl.CostEstimate(
            flops=8 * rows * key_rows * width,
            transcendentals=2 * rows * key_rows * (width // depth),
            bytes_accessed=2 * (2 * rows * width + 4 * key_rows * depth),
        ),
    )(queries, own_kv, far_kv, length.reshape(1, 1))

def norm_rows(values, gain_vector):
    widened = values.astype(jnp.float32)
    inverse_rms = lax.rsqrt(jnp.mean(widened * widened, axis=-1, keepdims=True) + epsilon)
    return widened * inverse_rms * gain_vector


def rotate(values, positions):
    half_width = values.shape[-1] // 2
    exponents = jnp.arange(half_width).astype(jnp.float32)
    inverse = jnp.exp(exponents * (-2.0 * math.log(rope_theta) / values.shape[-1]))
    angles = positions[:, None, None] * inverse[None, None, :]
    cosine_values = jnp.cos(angles)
    sine_values = jnp.sin(angles)
    first_half = values[..., :half_width]
    second = values[..., half_width:]
    return jnp.concatenate(
        [
            first_half * cosine_values - second * sine_values,
            second * cosine_values + first_half * sine_values,
        ],
        axis=-1,
    )


def local_positions(parity, row_count):
    indices = jnp.arange(row_count)
    quarter = row_count // 2
    offset = jnp.where(parity == 0, jnp.where(indices < quarter, 0, 2 * quarter), quarter)
    return indices + offset


def prep_kernel(query_width, for_queries, x_ref, w_ref, table_ref, gain_ref, out_ref):
    x = x_ref[...]
    block = x.shape[0]
    depth = table_ref.shape[1]
    parity = lax.rem(lax.axis_index("group"), 2)
    start = pl.multiple_of(parity * (table_ref.shape[0] // 2) + pl.program_id(0) * block, block)
    table = table_ref[pl.ds(start, block), :]
    swapped = pltpu.roll(table, depth // 2, 1)
    first_half = lax.broadcasted_iota(jnp.int32, table.shape, 1) < depth // 2
    cosines = jnp.where(first_half, table, swapped)
    sines = jnp.where(first_half, -swapped, table)

    def project(start, stop):
        return jnp.dot(x, w_ref[:, start:stop], preferred_element_type=jnp.float32).astype(jnp.bfloat16)

    def norm_rope(values, gain):
        values = values.astype(jnp.float32)
        inverse_rms = lax.rsqrt(jnp.mean(values * values, axis=-1, keepdims=True) + epsilon)
        normed = values * inverse_rms * gain
        return (normed * cosines + pltpu.roll(normed, depth // 2, 1) * sines).astype(jnp.bfloat16)

    if for_queries:
        queries = project(0, query_width)
        for h in range(queries.shape[1] // depth):
            out_ref[:, h * depth : (h + 1) * depth] = norm_rope(
                queries[:, h * depth : (h + 1) * depth], gain_ref[...]
            )
    else:
        out_ref[0] = norm_rope(project(0, depth), gain_ref[...])
        out_ref[1] = project(depth, 2 * depth)


def prep(normed_rows, joined, table, gain, for_queries):
    rows, width = normed_rows.shape
    depth = table.shape[1]
    query_width = joined.shape[1] - 2 * depth
    block = min(512, rows)
    whole = lambda shape: pl.BlockSpec(shape, lambda i: (0, 0))
    if for_queries:
        out_shape = jax.ShapeDtypeStruct((rows, query_width), jnp.bfloat16)
        out_spec = pl.BlockSpec((block, query_width), lambda i: (i, 0))
        columns = query_width
    else:
        out_shape = jax.ShapeDtypeStruct((2, rows, depth), jnp.bfloat16)
        out_spec = pl.BlockSpec((2, block, depth), lambda i: (0, i, 0))
        columns = 2 * depth
    return pl.pallas_call(
        functools.partial(prep_kernel, query_width, for_queries),
        out_shape=out_shape,
        grid=(rows // block,),
        in_specs=[
            pl.BlockSpec((block, width), lambda i: (i, 0)),
            pl.BlockSpec((width, columns), lambda i: (0, 0 if for_queries else 1)),
            whole(table.shape),
            whole((1, depth)),
        ],
        out_specs=out_spec,
        cost_estimate=pl.CostEstimate(
            flops=2 * rows * width * columns,
            transcendentals=rows * (columns // depth),
            bytes_accessed=2 * (rows * width + width * columns + rows * columns),
        ),
    )(normed_rows, joined, table, gain.reshape(1, depth))

def rope_table(row_count, depth):
    half = depth // 2
    frequencies = rope_theta ** (-2.0 * np.arange(half) / depth)
    indices = np.arange(row_count)
    quarter = row_count // 2
    places = np.concatenate([np.where(indices < quarter, indices, indices + 2 * quarter), indices + quarter])
    angles = places[:, None].astype(np.float64) * frequencies[None, :]
    return jnp.asarray(np.concatenate([np.cos(angles), np.sin(angles)], axis=1), jnp.float32)

def per_device(
    hidden_in,
    norm_attention,
    norm_experts,
    query_master,
    trainer_key_value_weight,
    output_master,
    query_gain,
    key_gain,
    lengths,
    router,
    expert_gateup,
    expert_down,
    routes,
):
    experts_axis = lax.axis_size("expert")
    group_member = lax.axis_index("expert")
    group_index = lax.axis_index("group")
    local_head_count = QUERY_HEADS // experts_axis
    width_here = local_head_count * HEAD_DIMENSION
    common_head = group_member * local_head_count // (QUERY_HEADS // KEY_VALUE_HEADS)
    groups_axis = lax.axis_size("group")
    joined_parts, output_parts, normed_parts = gather_all(
        query_master,
        trainer_key_value_weight,
        output_master,
        hidden_in,
        norm_attention.reshape(1, -1),
        groups_axis,
        experts_axis,
    )
    model_width = hidden_in.shape[1]
    local_rows = normed_parts.shape[0] * normed_parts.shape[1]
    parity = group_index % 2
    prep_args = (
        normed_parts.reshape(local_rows, model_width),
        joined_parts.reshape(model_width, -1),
        rope_table(local_rows, HEAD_DIMENSION),
    )
    key_values = prep(*prep_args, key_gain, False)
    query_rows_list = prep(*prep_args, query_gain, True)
    partner = from_partner(key_values, "group", 0)
    valid_length = jnp.sum(jnp.where(jnp.arange(lengths.shape[0]) == group_index // 2, lengths, 0))
    attended = attention(
        query_rows_list,
        key_values,
        partner,
        valid_length.astype(jnp.int32),
        HEAD_DIMENSION ** (-0.5),
    )
    output_weight = jnp.transpose(output_parts, (1, 0, 2)).reshape(output_parts.shape[1], -1)
    owned = combine_and_scatter(attended, output_weight, experts_axis)
    summed = jnp.sum(owned.astype(jnp.float32), axis=0)
    hidden = (hidden_in.astype(jnp.float32) + summed).astype(jnp.bfloat16)
    normed_second = norm_rows(hidden, norm_experts).astype(jnp.bfloat16)
    logits = jnp.dot(normed_second, router, preferred_element_type=jnp.float32)
    route_table = routes[:, :, None] == jnp.arange(logits.shape[1])[None, None, :]
    picked = jnp.sum(jnp.where(route_table, logits[:, None, :], 0.0), axis=-1)
    raised = jnp.exp(picked)
    gate_values = raised / jnp.sum(raised, axis=1, keepdims=True)
    inside = routes < experts_axis
    gate_window = jnp.sum(jnp.where(inside, gate_values, 0.0), axis=1)
    expert_window = jnp.sum(jnp.where(inside, routes, 0), axis=1)
    present = jnp.any(inside, axis=1)
    capacity = local_rows // (experts_axis * experts_axis)
    member_table = (
        present[:, None] & (expert_window[:, None] == jnp.arange(experts_axis)[None, :])
    ).astype(jnp.int32)
    ranking = jnp.sum(jnp.cumsum(member_table, axis=0) * member_table, axis=1) - 1
    slot_index = expert_window * capacity + ranking
    select = (
        (jnp.arange(experts_axis * capacity)[:, None] == slot_index[None, :]) & present[None, :]
    ).astype(jnp.bfloat16)
    select_slots = select.reshape(experts_axis, capacity, -1)
    outgoing = jnp.einsum(
        "jct,td->jcd", select_slots, normed_second, preferred_element_type=jnp.float32
    ).astype(jnp.bfloat16)
    gateup_here = expert_gateup[0]
    down_here = expert_down[0]
    hidden_units = down_here.shape[0]
    slot_items = scatter_blocks(outgoing, experts_axis, 2)
    gate_up = jnp.einsum("jcd,df->jcf", slot_items, gateup_here, preferred_element_type=jnp.float32)
    active = (jax.nn.silu(gate_up[..., :hidden_units]) * gate_up[..., hidden_units:]).astype(
        jnp.bfloat16
    )
    result = jnp.einsum(
        "jcf,fd->jcd", active, down_here, preferred_element_type=jnp.float32
    ).astype(jnp.bfloat16)
    returned = scatter_blocks(result, experts_axis, 3)
    combined = jnp.einsum(
        "jct,jcd->td", select_slots, returned, preferred_element_type=jnp.float32
    )
    expert_mix = (gate_window[:, None] * combined).astype(jnp.bfloat16)
    return (hidden, expert_mix)


def solution(mesh):
    return jax.shard_map(
        per_device,
        mesh=mesh,
        in_specs=(
            P(("group", "expert"), None),
            P(),
            P(),
            P("group", "expert"),
            P(None, "group", None),
            P("expert", "group"),
            P(),
            P(),
            P(),
            P(),
            P("expert", None, None),
            P("expert", None, None),
            P(("group", "expert"), None),
        ),
        out_specs=(P(("group", "expert"), None), P(("group", "expert"), None)),
        check_vma=False,
    )
```

```python
import functools
import math

import jax
import numpy as np
import jax.numpy as jnp
from jax import lax
from jax.experimental import pallas as pl
from jax.experimental.pallas import tpu as pltpu
from jax.sharding import PartitionSpec as P

MESH = pl.DeviceIdType.MESH

QUERY_HEADS = 32
KEY_VALUE_HEADS = 4
HEAD_DIMENSION = 128


epsilon = 1e-06
rope_theta = 1000000.0


def from_partner(block, axis, stride):
    count = lax.axis_size(axis)
    route = []
    for low in range(count):
        high = low | 1 << stride
        if high != low and high < count:
            route += [(low, high), (high, low)]
    return lax.ppermute(block, axis, route)


def gather_kernel(n_group, n_expert, heads_here, q_in, kv_in, o_in, h_in, gain_in, oqkv, oo, oxn, send, recv, xsend, xrecv, local, wqkv, wo, xn):
    e_here = lax.axis_index("expert")
    depth = HEAD_DIMENSION
    column = pl.multiple_of(lax.div(e_here * heads_here, QUERY_HEADS // KEY_VALUE_HEADS) * depth, depth)
    query_width = q_in.shape[1]
    wqkv[:, 0:query_width] = q_in[...].astype(jnp.bfloat16)
    wqkv[:, query_width : query_width + depth] = kv_in[0, :, pl.ds(column, depth)].astype(jnp.bfloat16)
    wqkv[:, query_width + depth : query_width + 2 * depth] = kv_in[1, :, pl.ds(column, depth)].astype(
        jnp.bfloat16
    )
    wo[...] = o_in[...].astype(jnp.bfloat16)
    xn[...] = norm_rows(h_in[...], gain_in[...]).astype(jnp.bfloat16)
    g = lax.axis_index("group")
    e = lax.axis_index("expert")
    columns = n_group // 2
    z = lax.div(g, 2)
    xh = lax.rem(g, 2)
    zp = lax.rem(z + 1, columns)
    zm = lax.rem(z + columns - 1, columns)
    plus_dev = (2 * zp + xh, e)
    minus_dev = (2 * zm + xh, e)
    pair_dev = (g + 1 - 2 * xh, e)
    core = lax.rem(e, 2)
    chip = lax.div(e, 2)
    chips = n_expert // 2
    mate_dev = (g, e + 1 - 2 * core)
    chip_devs = [(g, 2 * lax.rem(chip + j, chips) + core) for j in range(1, chips)]
    barrier = pltpu.get_barrier_semaphore()
    peers = [plus_dev, minus_dev, pair_dev, mate_dev] + chip_devs
    for dev in peers:
        pl.semaphore_signal(barrier, 1, device_id=dev, device_id_type=MESH)
    pl.semaphore_wait(barrier, len(peers))

    def slot(k, origin):
        return (oqkv, oo)[k].at[origin]

    sends = []

    def push(k, origin, src, dev):
        copy = pltpu.make_async_remote_copy(
            src_ref=src,
            dst_ref=slot(k, origin),
            send_sem=send.at[len(sends)],
            recv_sem=recv.at[k, origin],
            device_id=dev,
            device_id_type=MESH,
        )
        copy.start()
        sends.append(copy)

    def forward(origin, dev):
        for k in range(2):
            push(k, origin, slot(k, origin), dev)

    def arrive(origin):
        for k in range(2):
            pltpu.make_async_remote_copy(
                src_ref=slot(k, origin),
                dst_ref=slot(k, origin),
                send_sem=send.at[0],
                recv_sem=recv.at[k, origin],
                device_id=pair_dev,
                device_id_type=MESH,
            ).wait_recv()

    xsends = []

    def xpush(src, origin, dev):
        copy = pltpu.make_async_remote_copy(
            src_ref=src,
            dst_ref=oxn.at[origin],
            send_sem=xsend.at[len(xsends)],
            recv_sem=xrecv.at[origin],
            device_id=dev,
            device_id_type=MESH,
        )
        copy.start()
        xsends.append(copy)

    def xarrive(origin):
        pltpu.make_async_remote_copy(
            src_ref=oxn.at[origin],
            dst_ref=oxn.at[origin],
            send_sem=xsend.at[0],
            recv_sem=xrecv.at[origin],
            device_id=mate_dev,
            device_id_type=MESH,
        ).wait_recv()

    inputs = (wqkv, wo)
    own = [pltpu.make_async_copy(xn, oxn.at[e], local.at[2])]
    own += [pltpu.make_async_copy(inputs[k], slot(k, g), local.at[k]) for k in range(2)]
    for copy in own:
        copy.start()
    for dev in (pair_dev, plus_dev, minus_dev):
        for k in range(2):
            push(k, g, inputs[k], dev)
    partner = g + 1 - 2 * xh
    arrive(partner)
    forward(partner, plus_dev)
    forward(partner, minus_dev)
    xpush(xn, e, mate_dev)
    for dev in chip_devs:
        xpush(xn, e, dev)
    chip_origins = [2 * lax.rem(chip + j, chips) + core for j in range(1, chips)]
    normed_order = [chip_origins[0:2], chip_origins[2:5], chip_origins[5:]]
    for step in range(1, 4):
        behind = lax.rem(z - step + columns, columns)
        ahead = lax.rem(z + step, columns)
        for origin in (2 * behind, 2 * behind + 1):
            arrive(origin)
        for origin in ((2 * behind, 2 * behind + 1) if step < 3 else (2 * behind,)):
            forward(origin, plus_dev)
        for origin in (2 * ahead, 2 * ahead + 1):
            arrive(origin)
        for origin in ((2 * ahead, 2 * ahead + 1) if step < 3 else (2 * ahead + 1,)):
            forward(origin, minus_dev)
        for origin in normed_order[step - 1]:
            xarrive(origin)
            xpush(oxn.at[origin], origin, mate_dev)
    across = lax.rem(z + columns // 2, columns)
    arrive(2 * across)
    arrive(2 * across + 1)
    mate_core = 1 - core
    xarrive(e + 1 - 2 * core)
    for j in range(1, chips):
        xarrive(2 * lax.rem(chip + j, chips) + mate_core)
    for copy in sends + xsends:
        copy.wait_send()
    for copy in own:
        copy.wait()


def gather_all(q_in, kv_in, o_in, h_in, gain_in, n_group, n_expert):
    any_spec = pl.BlockSpec(memory_space=pl.ANY)
    vmem = pl.BlockSpec(memory_space=pltpu.VMEM)
    depth = HEAD_DIMENSION
    joined = (q_in.shape[0], q_in.shape[1] + 2 * depth)
    shapes = [
        jax.ShapeDtypeStruct((n_group,) + joined, jnp.bfloat16),
        jax.ShapeDtypeStruct((n_group,) + o_in.shape, jnp.bfloat16),
        jax.ShapeDtypeStruct((n_expert,) + h_in.shape, jnp.bfloat16),
    ]
    return pl.pallas_call(
        functools.partial(gather_kernel, n_group, n_expert, q_in.shape[1] // depth),
        out_shape=tuple(shapes),
        in_specs=[vmem] * 5,
        out_specs=tuple([any_spec] * 3),
        scratch_shapes=[
            pltpu.SemaphoreType.DMA((32,)),
            pltpu.SemaphoreType.DMA((2, n_group)),
            pltpu.SemaphoreType.DMA((n_expert,)),
            pltpu.SemaphoreType.DMA((n_expert,)),
            pltpu.SemaphoreType.DMA((3,)),
            pltpu.VMEM(joined, jnp.bfloat16),
            pltpu.VMEM(o_in.shape, jnp.bfloat16),
            pltpu.VMEM(h_in.shape, jnp.bfloat16),
        ],
        compiler_params=pltpu.CompilerParams(collective_id=0, has_side_effects=True),
    )(q_in, kv_in, o_in, h_in, gain_in)


def combine_kernel(blocks, attended_ref, weight_ref, out_ref, outgoing, incoming, send, recv):
    g = lax.axis_index("group")
    e = lax.axis_index("expert")
    core = lax.rem(e, 2)
    mate_dev = (g, e + 1 - 2 * core)
    rows = out_ref.shape[1]
    barrier = pltpu.get_barrier_semaphore()
    pl.semaphore_signal(barrier, 1, device_id=mate_dev, device_id_type=MESH)
    pl.semaphore_wait(barrier, 1)

    def partial(block):
        start = pl.multiple_of(block * rows, rows)
        return jnp.dot(
            attended_ref[pl.ds(start, rows), :], weight_ref[...], preferred_element_type=jnp.float32
        ).astype(jnp.bfloat16)

    for i in range(blocks):
        outgoing[i] = partial(2 * i + 1 - core)
    copy = pltpu.make_async_remote_copy(
        src_ref=outgoing,
        dst_ref=incoming,
        send_sem=send.at[0],
        recv_sem=recv.at[0],
        device_id=mate_dev,
        device_id_type=MESH,
    )
    copy.start()
    for i in range(blocks):
        out_ref[i] = partial(2 * i + core)
    copy.wait()
    for i in range(blocks):
        out_ref[i] = (out_ref[i].astype(jnp.float32) + incoming[i].astype(jnp.float32)).astype(
            jnp.bfloat16
        )


def project_and_combine(attended, weight, experts_axis):
    rows = attended.shape[0] // experts_axis
    blocks = experts_axis // 2
    shape = (blocks, rows, weight.shape[1])
    vmem = pl.BlockSpec(memory_space=pltpu.VMEM)
    return pl.pallas_call(
        functools.partial(combine_kernel, blocks),
        out_shape=jax.ShapeDtypeStruct(shape, jnp.bfloat16),
        in_specs=[vmem, vmem],
        out_specs=vmem,
        scratch_shapes=[
            pltpu.VMEM(shape, jnp.bfloat16),
            pltpu.VMEM(shape, jnp.bfloat16),
            pltpu.SemaphoreType.DMA((1,)),
            pltpu.SemaphoreType.DMA((1,)),
        ],
        compiler_params=pltpu.CompilerParams(collective_id=4, has_side_effects=True),
    )(attended, weight)


def combine_scatter_kernel(blocks, attended_ref, weight_ref, out_ref, outgoing, incoming, combined, send, recv, chip_send, chip_recv, local):
    g = lax.axis_index("group")
    e = lax.axis_index("expert")
    core = lax.rem(e, 2)
    chip = lax.div(e, 2)
    mate_dev = (g, e + 1 - 2 * core)
    chip_devs = [(g, 2 * lax.rem(chip + j, blocks) + core) for j in range(1, blocks)]
    rows = out_ref.shape[1]
    barrier = pltpu.get_barrier_semaphore()
    for dev in [mate_dev] + chip_devs:
        pl.semaphore_signal(barrier, 1, device_id=dev, device_id_type=MESH)
    pl.semaphore_wait(barrier, blocks)

    def partial(block):
        start = pl.multiple_of(block * rows, rows)
        return jnp.dot(
            attended_ref[pl.ds(start, rows), :], weight_ref[...], preferred_element_type=jnp.float32
        ).astype(jnp.bfloat16)

    for i in range(blocks):
        outgoing[i] = partial(2 * i + 1 - core)
    copy = pltpu.make_async_remote_copy(
        src_ref=outgoing,
        dst_ref=incoming,
        send_sem=send.at[0],
        recv_sem=recv.at[0],
        device_id=mate_dev,
        device_id_type=MESH,
    )
    copy.start()
    for i in range(blocks):
        combined[i] = partial(2 * i + core)
    copy.wait()
    pushes = []
    for j in range(1, blocks):
        i = lax.rem(chip + j, blocks)
        combined[i] = (combined[i].astype(jnp.float32) + incoming[i].astype(jnp.float32)).astype(
            jnp.bfloat16
        )
        push = pltpu.make_async_remote_copy(
            src_ref=combined.at[i],
            dst_ref=out_ref.at[chip],
            send_sem=chip_send.at[j],
            recv_sem=chip_recv.at[j],
            device_id=chip_devs[j - 1],
            device_id_type=MESH,
        )
        push.start()
        pushes.append(push)
    combined[chip] = (combined[chip].astype(jnp.float32) + incoming[chip].astype(jnp.float32)).astype(
        jnp.bfloat16
    )
    own = pltpu.make_async_copy(combined.at[chip], out_ref.at[chip], local.at[0])
    own.start()
    for push in pushes:
        push.wait()
    own.wait()


def combine_and_scatter(attended, weight, experts_axis):
    rows = attended.shape[0] // experts_axis
    blocks = experts_axis // 2
    shape = (blocks, rows, weight.shape[1])
    vmem = pl.BlockSpec(memory_space=pltpu.VMEM)
    return pl.pallas_call(
        functools.partial(combine_scatter_kernel, blocks),
        out_shape=jax.ShapeDtypeStruct(shape, jnp.bfloat16),
        in_specs=[vmem, vmem],
        out_specs=pl.BlockSpec(memory_space=pl.ANY),
        scratch_shapes=[
            pltpu.VMEM(shape, jnp.bfloat16),
            pltpu.VMEM(shape, jnp.bfloat16),
            pltpu.VMEM(shape, jnp.bfloat16),
            pltpu.SemaphoreType.DMA((1,)),
            pltpu.SemaphoreType.DMA((1,)),
            pltpu.SemaphoreType.DMA((blocks,)),
            pltpu.SemaphoreType.DMA((blocks,)),
            pltpu.SemaphoreType.DMA((1,)),
        ],
        compiler_params=pltpu.CompilerParams(collective_id=7, has_side_effects=True),
    )(attended, weight)


def mate_kernel(part, out, send, recv):
    g = lax.axis_index("group")
    e = lax.axis_index("expert")
    core = lax.rem(e, 2)
    mate_dev = (g, e + 1 - 2 * core)
    barrier = pltpu.get_barrier_semaphore()
    pl.semaphore_signal(barrier, 1, device_id=mate_dev, device_id_type=MESH)
    pl.semaphore_wait(barrier, 1)
    copy = pltpu.make_async_remote_copy(
        src_ref=part.at[:, 1 - core],
        dst_ref=out,
        send_sem=send.at[0],
        recv_sem=recv.at[0],
        device_id=mate_dev,
        device_id_type=MESH,
    )
    copy.start()
    copy.wait()


def exchange_with_mate(part):
    any_spec = pl.BlockSpec(memory_space=pl.ANY)
    shape = (part.shape[0],) + part.shape[2:]
    return pl.pallas_call(
        mate_kernel,
        out_shape=jax.ShapeDtypeStruct(shape, part.dtype),
        in_specs=[any_spec],
        out_specs=any_spec,
        scratch_shapes=[pltpu.SemaphoreType.DMA((1,)), pltpu.SemaphoreType.DMA((1,))],
        compiler_params=pltpu.CompilerParams(collective_id=4, has_side_effects=True),
    )(part)


def chip_scatter_kernel(chips, part, out, send, recv, local):
    g = lax.axis_index("group")
    e = lax.axis_index("expert")
    core = lax.rem(e, 2)
    chip = lax.div(e, 2)
    devs = [(g, 2 * lax.rem(chip + j, chips) + core) for j in range(1, chips)]
    barrier = pltpu.get_barrier_semaphore()
    for dev in devs:
        pl.semaphore_signal(barrier, 1, device_id=dev, device_id_type=MESH)
    pl.semaphore_wait(barrier, len(devs))
    copies = []
    for j in range(1, chips):
        copy = pltpu.make_async_remote_copy(
            src_ref=part.at[lax.rem(chip + j, chips)],
            dst_ref=out.at[chip],
            send_sem=send.at[j],
            recv_sem=recv.at[j],
            device_id=devs[j - 1],
            device_id_type=MESH,
        )
        copy.start()
        copies.append(copy)
    own = pltpu.make_async_copy(part.at[chip], out.at[chip], local.at[0])
    own.start()
    for copy in copies:
        copy.wait()
    own.wait()


def scatter_to_chips(part):
    chips = part.shape[0]
    any_spec = pl.BlockSpec(memory_space=pl.ANY)
    return pl.pallas_call(
        functools.partial(chip_scatter_kernel, chips),
        out_shape=jax.ShapeDtypeStruct(part.shape, part.dtype),
        in_specs=[any_spec],
        out_specs=any_spec,
        scratch_shapes=[
            pltpu.SemaphoreType.DMA((chips,)),
            pltpu.SemaphoreType.DMA((chips,)),
            pltpu.SemaphoreType.DMA((1,)),
        ],
        compiler_params=pltpu.CompilerParams(collective_id=5, has_side_effects=True),
    )(part)


def scatter_kernel(n_expert, part, out, send, recv, local):
    g = lax.axis_index("group")
    e = lax.axis_index("expert")
    barrier = pltpu.get_barrier_semaphore()
    for j in range(1, n_expert):
        pl.semaphore_signal(barrier, 1, device_id=(g, lax.rem(e + j, n_expert)), device_id_type=MESH)
    pl.semaphore_wait(barrier, n_expert - 1)
    copies = []
    for j in range(1, n_expert):
        peer = lax.rem(e + j, n_expert)
        copy = pltpu.make_async_remote_copy(
            src_ref=part.at[peer],
            dst_ref=out.at[e],
            send_sem=send.at[j],
            recv_sem=recv.at[j],
            device_id=(g, peer),
            device_id_type=MESH,
        )
        copy.start()
        copies.append(copy)
    own = pltpu.make_async_copy(part.at[e], out.at[e], local.at[0])
    own.start()
    for copy in copies:
        copy.wait()
    own.wait()


def scatter_blocks(part, n_expert, collective_id):
    any_spec = pl.BlockSpec(memory_space=pl.ANY)
    return pl.pallas_call(
        functools.partial(scatter_kernel, n_expert),
        out_shape=jax.ShapeDtypeStruct(part.shape, part.dtype),
        in_specs=[any_spec],
        out_specs=any_spec,
        scratch_shapes=[
            pltpu.SemaphoreType.DMA((n_expert,)),
            pltpu.SemaphoreType.DMA((n_expert,)),
            pltpu.SemaphoreType.DMA((1,)),
        ],
        compiler_params=pltpu.CompilerParams(collective_id=collective_id, has_side_effects=True),
    )(part)


def attention_kernel(scale, heads, q_ref, own_ref, far_ref, length_ref, o_ref):
    block = q_ref.shape[0]
    rows = own_ref.shape[1]
    half = rows // 2
    parity = lax.rem(lax.axis_index("group"), 2)

    def places(side, shape, axis, start):
        indices = lax.broadcasted_iota(jnp.int32, shape, axis) + start
        return indices + jnp.where(side == 0, jnp.where(indices < half, 0, rows), half)

    query_places = places(parity, (block, 1), 0, pl.program_id(0) * block)
    length = length_ref[0, 0]
    own_places = places(parity, (1, rows), 1, 0)
    far_places = places(1 - parity, (1, rows), 1, 0)
    own_allowed = (own_places <= query_places) & (own_places < length)
    far_allowed = (far_places <= query_places) & (far_places < length)
    own_keys, own_values = own_ref[0], own_ref[1]
    far_keys, far_values = far_ref[0], far_ref[1]
    depth = own_keys.shape[1]
    contract = (((1,), (1,)), ((), ()))
    for h in range(heads):
        query = q_ref[:, h * depth : (h + 1) * depth]
        own_weights = jnp.where(
            own_allowed,
            jnp.exp(lax.dot_general(query, own_keys, contract, preferred_element_type=jnp.float32) * scale),
            0.0,
        )
        far_weights = jnp.where(
            far_allowed,
            jnp.exp(lax.dot_general(query, far_keys, contract, preferred_element_type=jnp.float32) * scale),
            0.0,
        )
        denominators = jnp.sum(own_weights, axis=-1, keepdims=True) + jnp.sum(
            far_weights, axis=-1, keepdims=True
        )
        weighted = jnp.dot(
            own_weights.astype(jnp.bfloat16), own_values, preferred_element_type=jnp.float32
        ) + jnp.dot(far_weights.astype(jnp.bfloat16), far_values, preferred_element_type=jnp.float32)
        o_ref[:, h * depth : (h + 1) * depth] = (weighted / denominators).astype(o_ref.dtype)


def attention(queries, own_kv, far_kv, length, scale):
    rows, width = queries.shape
    key_rows, depth = own_kv.shape[1:]
    block = min(512, rows)
    pair = pl.BlockSpec((2, key_rows, depth), lambda i: (0, 0, 0))
    return pl.pallas_call(
        functools.partial(attention_kernel, scale, width // depth),
        out_shape=jax.ShapeDtypeStruct((rows, width), jnp.bfloat16),
        grid=(rows // block,),
        in_specs=[
            pl.BlockSpec((block, width), lambda i: (i, 0)),
            pair,
            pair,
            pl.BlockSpec(memory_space=pltpu.SMEM),
        ],
        out_specs=pl.BlockSpec((block, width), lambda i: (i, 0)),
        cost_estimate=pl.CostEstimate(
            flops=8 * rows * key_rows * width,
            transcendentals=2 * rows * key_rows * (width // depth),
            bytes_accessed=2 * (2 * rows * width + 4 * key_rows * depth),
        ),
    )(queries, own_kv, far_kv, length.reshape(1, 1))

def norm_rows(values, gain_vector):
    widened = values.astype(jnp.float32)
    inverse_rms = lax.rsqrt(jnp.mean(widened * widened, axis=-1, keepdims=True) + epsilon)
    return widened * inverse_rms * gain_vector


def rotate(values, positions):
    half_width = values.shape[-1] // 2
    exponents = jnp.arange(half_width).astype(jnp.float32)
    inverse = jnp.exp(exponents * (-2.0 * math.log(rope_theta) / values.shape[-1]))
    angles = positions[:, None, None] * inverse[None, None, :]
    cosine_values = jnp.cos(angles)
    sine_values = jnp.sin(angles)
    first_half = values[..., :half_width]
    second = values[..., half_width:]
    return jnp.concatenate(
        [
            first_half * cosine_values - second * sine_values,
            second * cosine_values + first_half * sine_values,
        ],
        axis=-1,
    )


def local_positions(parity, row_count):
    indices = jnp.arange(row_count)
    quarter = row_count // 2
    offset = jnp.where(parity == 0, jnp.where(indices < quarter, 0, 2 * quarter), quarter)
    return indices + offset


def prep_kernel(query_width, for_queries, x_ref, w_ref, table_ref, gain_ref, out_ref):
    x = x_ref[...]
    block = x.shape[0]
    depth = table_ref.shape[1]
    parity = lax.rem(lax.axis_index("group"), 2)
    start = pl.multiple_of(parity * (table_ref.shape[0] // 2) + pl.program_id(0) * block, block)
    table = table_ref[pl.ds(start, block), :]
    swapped = pltpu.roll(table, depth // 2, 1)
    first_half = lax.broadcasted_iota(jnp.int32, table.shape, 1) < depth // 2
    cosines = jnp.where(first_half, table, swapped)
    sines = jnp.where(first_half, -swapped, table)

    def project(start, stop):
        return jnp.dot(x, w_ref[:, start:stop], preferred_element_type=jnp.float32).astype(jnp.bfloat16)

    def norm_rope(values, gain):
        values = values.astype(jnp.float32)
        inverse_rms = lax.rsqrt(jnp.mean(values * values, axis=-1, keepdims=True) + epsilon)
        normed = values * inverse_rms * gain
        return (normed * cosines + pltpu.roll(normed, depth // 2, 1) * sines).astype(jnp.bfloat16)

    if for_queries:
        queries = project(0, query_width)
        for h in range(queries.shape[1] // depth):
            out_ref[:, h * depth : (h + 1) * depth] = norm_rope(
                queries[:, h * depth : (h + 1) * depth], gain_ref[...]
            )
    else:
        out_ref[0] = norm_rope(project(0, depth), gain_ref[...])
        out_ref[1] = project(depth, 2 * depth)


def prep(normed_rows, joined, table, gain, for_queries):
    rows, width = normed_rows.shape
    depth = table.shape[1]
    query_width = joined.shape[1] - 2 * depth
    block = min(512, rows)
    whole = lambda shape: pl.BlockSpec(shape, lambda i: (0, 0))
    if for_queries:
        out_shape = jax.ShapeDtypeStruct((rows, query_width), jnp.bfloat16)
        out_spec = pl.BlockSpec((block, query_width), lambda i: (i, 0))
        columns = query_width
    else:
        out_shape = jax.ShapeDtypeStruct((2, rows, depth), jnp.bfloat16)
        out_spec = pl.BlockSpec((2, block, depth), lambda i: (0, i, 0))
        columns = 2 * depth
    return pl.pallas_call(
        functools.partial(prep_kernel, query_width, for_queries),
        out_shape=out_shape,
        grid=(rows // block,),
        in_specs=[
            pl.BlockSpec((block, width), lambda i: (i, 0)),
            pl.BlockSpec((width, columns), lambda i: (0, 0 if for_queries else 1)),
            whole(table.shape),
            whole((1, depth)),
        ],
        out_specs=out_spec,
        cost_estimate=pl.CostEstimate(
            flops=2 * rows * width * columns,
            transcendentals=rows * (columns // depth),
            bytes_accessed=2 * (rows * width + width * columns + rows * columns),
        ),
    )(normed_rows, joined, table, gain.reshape(1, depth))

def rope_table(row_count, depth):
    half = depth // 2
    frequencies = rope_theta ** (-2.0 * np.arange(half) / depth)
    indices = np.arange(row_count)
    quarter = row_count // 2
    places = np.concatenate([np.where(indices < quarter, indices, indices + 2 * quarter), indices + quarter])
    angles = places[:, None].astype(np.float64) * frequencies[None, :]
    return jnp.asarray(np.concatenate([np.cos(angles), np.sin(angles)], axis=1), jnp.float32)

def per_device(
    hidden_in,
    norm_attention,
    norm_experts,
    query_master,
    trainer_key_value_weight,
    output_master,
    query_gain,
    key_gain,
    lengths,
    router,
    expert_gateup,
    expert_down,
    routes,
):
    experts_axis = lax.axis_size("expert")
    group_member = lax.axis_index("expert")
    group_index = lax.axis_index("group")
    local_head_count = QUERY_HEADS // experts_axis
    width_here = local_head_count * HEAD_DIMENSION
    common_head = group_member * local_head_count // (QUERY_HEADS // KEY_VALUE_HEADS)
    groups_axis = lax.axis_size("group")
    joined_parts, output_parts, normed_parts = gather_all(
        query_master,
        trainer_key_value_weight,
        output_master,
        hidden_in,
        norm_attention.reshape(1, -1),
        groups_axis,
        experts_axis,
    )
    model_width = hidden_in.shape[1]
    local_rows = normed_parts.shape[0] * normed_parts.shape[1]
    parity = group_index % 2
    prep_args = (
        normed_parts.reshape(local_rows, model_width),
        joined_parts.reshape(model_width, -1),
        rope_table(local_rows, HEAD_DIMENSION),
    )
    key_values = prep(*prep_args, key_gain, False)
    query_rows_list = prep(*prep_args, query_gain, True)
    partner = from_partner(key_values, "group", 0)
    valid_length = jnp.sum(jnp.where(jnp.arange(lengths.shape[0]) == group_index // 2, lengths, 0))
    attended = attention(
        query_rows_list,
        key_values,
        partner,
        valid_length.astype(jnp.int32),
        HEAD_DIMENSION ** (-0.5),
    )
    output_weight = jnp.transpose(output_parts, (1, 0, 2)).reshape(output_parts.shape[1], -1)
    owned = combine_and_scatter(attended, output_weight, experts_axis)
    summed = jnp.sum(owned.astype(jnp.float32), axis=0)
    hidden = (hidden_in.astype(jnp.float32) + summed).astype(jnp.bfloat16)
    normed_second = norm_rows(hidden, norm_experts).astype(jnp.bfloat16)
    logits = jnp.dot(normed_second, router, preferred_element_type=jnp.float32)
    route_table = routes[:, :, None] == jnp.arange(logits.shape[1])[None, None, :]
    picked = jnp.sum(jnp.where(route_table, logits[:, None, :], 0.0), axis=-1)
    raised = jnp.exp(picked)
    gate_values = raised / jnp.sum(raised, axis=1, keepdims=True)
    inside = routes < experts_axis
    gate_window = jnp.sum(jnp.where(inside, gate_values, 0.0), axis=1)
    expert_window = jnp.sum(jnp.where(inside, routes, 0), axis=1)
    present = jnp.any(inside, axis=1)
    capacity = local_rows // (experts_axis * experts_axis)
    member_table = (
        present[:, None] & (expert_window[:, None] == jnp.arange(experts_axis)[None, :])
    ).astype(jnp.int32)
    ranking = jnp.sum(jnp.cumsum(member_table, axis=0) * member_table, axis=1) - 1
    slot_index = expert_window * capacity + ranking
    select = (
        (jnp.arange(experts_axis * capacity)[:, None] == slot_index[None, :]) & present[None, :]
    ).astype(jnp.bfloat16)
    select_slots = select.reshape(experts_axis, capacity, -1)
    outgoing = jnp.einsum(
        "jct,td->jcd", select_slots, normed_second, preferred_element_type=jnp.float32
    ).astype(jnp.bfloat16)
    gateup_here = expert_gateup[0]
    down_here = expert_down[0]
    hidden_units = down_here.shape[0]
    slot_items = scatter_blocks(outgoing, experts_axis, 2)
    gate_up = jnp.einsum("jcd,df->jcf", slot_items, gateup_here, preferred_element_type=jnp.float32)
    active = (jax.nn.silu(gate_up[..., :hidden_units]) * gate_up[..., hidden_units:]).astype(
        jnp.bfloat16
    )
    result = jnp.einsum(
        "jcf,fd->jcd", active, down_here, preferred_element_type=jnp.float32
    ).astype(jnp.bfloat16)
    returned = scatter_blocks(result, experts_axis, 3)
    combined = jnp.einsum(
        "jct,jcd->td", select_slots, returned, preferred_element_type=jnp.float32
    )
    expert_mix = (gate_window[:, None] * combined).astype(jnp.bfloat16)
    return (hidden, expert_mix)


def solution(mesh):
    return jax.shard_map(
        per_device,
        mesh=mesh,
        in_specs=(
            P(("group", "expert"), None),
            P(),
            P(),
            P("group", "expert"),
            P(None, "group", None),
            P("expert", "group"),
            P(),
            P(),
            P(),
            P(),
            P("expert", None, None),
            P("expert", None, None),
            P(("group", "expert"), None),
        ),
        out_specs=(P(("group", "expert"), None), P(("group", "expert"), None)),
        check_vma=False,
    )
```

```python
import functools
import math

import jax
import numpy as np
import jax.numpy as jnp
from jax import lax
from jax.experimental import pallas as pl
from jax.experimental.pallas import tpu as pltpu
from jax.sharding import PartitionSpec as P

MESH = pl.DeviceIdType.MESH

QUERY_HEADS = 32
KEY_VALUE_HEADS = 4
HEAD_DIMENSION = 128


epsilon = 1e-06
rope_theta = 1000000.0


def from_partner(block, axis, stride):
    count = lax.axis_size(axis)
    route = []
    for low in range(count):
        high = low | 1 << stride
        if high != low and high < count:
            route += [(low, high), (high, low)]
    return lax.ppermute(block, axis, route)


def gather_kernel(n_group, n_expert, heads_here, q_in, kv_in, o_in, h_in, gain_in, oqkv, oo, oxn, send, recv, xsend, xrecv, local, wqkv, wo, xn):
    e_here = lax.axis_index("expert")
    depth = HEAD_DIMENSION
    column = pl.multiple_of(lax.div(e_here * heads_here, QUERY_HEADS // KEY_VALUE_HEADS) * depth, depth)
    query_width = q_in.shape[1]
    wqkv[:, 0:query_width] = q_in[...].astype(jnp.bfloat16)
    wqkv[:, query_width : query_width + depth] = kv_in[0, :, pl.ds(column, depth)].astype(jnp.bfloat16)
    wqkv[:, query_width + depth : query_width + 2 * depth] = kv_in[1, :, pl.ds(column, depth)].astype(
        jnp.bfloat16
    )
    wo[...] = o_in[...].astype(jnp.bfloat16)
    xn[...] = norm_rows(h_in[...], gain_in[...]).astype(jnp.bfloat16)
    g = lax.axis_index("group")
    e = lax.axis_index("expert")
    columns = n_group // 2
    z = lax.div(g, 2)
    xh = lax.rem(g, 2)
    zp = lax.rem(z + 1, columns)
    zm = lax.rem(z + columns - 1, columns)
    plus_dev = (2 * zp + xh, e)
    minus_dev = (2 * zm + xh, e)
    pair_dev = (g + 1 - 2 * xh, e)
    core = lax.rem(e, 2)
    chip = lax.div(e, 2)
    chips = n_expert // 2
    mate_dev = (g, e + 1 - 2 * core)
    chip_devs = [(g, 2 * lax.rem(chip + j, chips) + core) for j in range(1, chips)]
    barrier = pltpu.get_barrier_semaphore()
    peers = [plus_dev, minus_dev, pair_dev, mate_dev] + chip_devs
    for dev in peers:
        pl.semaphore_signal(barrier, 1, device_id=dev, device_id_type=MESH)
    pl.semaphore_wait(barrier, len(peers))

    def slot(k, origin):
        return (oqkv, oo)[k].at[origin]

    sends = []

    def push(k, origin, src, dev):
        copy = pltpu.make_async_remote_copy(
            src_ref=src,
            dst_ref=slot(k, origin),
            send_sem=send.at[len(sends)],
            recv_sem=recv.at[k, origin],
            device_id=dev,
            device_id_type=MESH,
        )
        copy.start()
        sends.append(copy)

    def forward(origin, dev):
        for k in range(2):
            push(k, origin, slot(k, origin), dev)

    def arrive(origin):
        for k in range(2):
            pltpu.make_async_remote_copy(
                src_ref=slot(k, origin),
                dst_ref=slot(k, origin),
                send_sem=send.at[0],
                recv_sem=recv.at[k, origin],
                device_id=pair_dev,
                device_id_type=MESH,
            ).wait_recv()

    xsends = []

    def xpush(src, origin, dev):
        copy = pltpu.make_async_remote_copy(
            src_ref=src,
            dst_ref=oxn.at[origin],
            send_sem=xsend.at[len(xsends)],
            recv_sem=xrecv.at[origin],
            device_id=dev,
            device_id_type=MESH,
        )
        copy.start()
        xsends.append(copy)

    def xarrive(origin):
        pltpu.make_async_remote_copy(
            src_ref=oxn.at[origin],
            dst_ref=oxn.at[origin],
            send_sem=xsend.at[0],
            recv_sem=xrecv.at[origin],
            device_id=mate_dev,
            device_id_type=MESH,
        ).wait_recv()

    inputs = (wqkv, wo)
    own = [pltpu.make_async_copy(xn, oxn.at[e], local.at[2])]
    own += [pltpu.make_async_copy(inputs[k], slot(k, g), local.at[k]) for k in range(2)]
    for copy in own:
        copy.start()
    for dev in (pair_dev, plus_dev, minus_dev):
        for k in range(2):
            push(k, g, inputs[k], dev)
    xpush(xn, e, mate_dev)
    for dev in chip_devs:
        xpush(xn, e, dev)
    partner = g + 1 - 2 * xh
    arrive(partner)
    forward(partner, plus_dev)
    forward(partner, minus_dev)
    chip_origins = [2 * lax.rem(chip + j, chips) + core for j in range(1, chips)]
    normed_order = [chip_origins[0:2], chip_origins[2:5], chip_origins[5:]]
    for step in range(1, 4):
        behind = lax.rem(z - step + columns, columns)
        ahead = lax.rem(z + step, columns)
        for origin in (2 * behind, 2 * behind + 1):
            arrive(origin)
        for origin in ((2 * behind, 2 * behind + 1) if step < 3 else (2 * behind,)):
            forward(origin, plus_dev)
        for origin in (2 * ahead, 2 * ahead + 1):
            arrive(origin)
        for origin in ((2 * ahead, 2 * ahead + 1) if step < 3 else (2 * ahead + 1,)):
            forward(origin, minus_dev)
        for origin in normed_order[step - 1]:
            xarrive(origin)
            xpush(oxn.at[origin], origin, mate_dev)
    across = lax.rem(z + columns // 2, columns)
    arrive(2 * across)
    arrive(2 * across + 1)
    mate_core = 1 - core
    xarrive(e + 1 - 2 * core)
    for j in range(1, chips):
        xarrive(2 * lax.rem(chip + j, chips) + mate_core)
    for copy in sends + xsends:
        copy.wait_send()
    for copy in own:
        copy.wait()


def gather_all(q_in, kv_in, o_in, h_in, gain_in, n_group, n_expert):
    any_spec = pl.BlockSpec(memory_space=pl.ANY)
    vmem = pl.BlockSpec(memory_space=pltpu.VMEM)
    depth = HEAD_DIMENSION
    joined = (q_in.shape[0], q_in.shape[1] + 2 * depth)
    shapes = [
        jax.ShapeDtypeStruct((n_group,) + joined, jnp.bfloat16),
        jax.ShapeDtypeStruct((n_group,) + o_in.shape, jnp.bfloat16),
        jax.ShapeDtypeStruct((n_expert,) + h_in.shape, jnp.bfloat16),
    ]
    return pl.pallas_call(
        functools.partial(gather_kernel, n_group, n_expert, q_in.shape[1] // depth),
        out_shape=tuple(shapes),
        in_specs=[vmem] * 5,
        out_specs=tuple([any_spec] * 3),
        scratch_shapes=[
            pltpu.SemaphoreType.DMA((32,)),
            pltpu.SemaphoreType.DMA((2, n_group)),
            pltpu.SemaphoreType.DMA((n_expert,)),
            pltpu.SemaphoreType.DMA((n_expert,)),
            pltpu.SemaphoreType.DMA((3,)),
            pltpu.VMEM(joined, jnp.bfloat16),
            pltpu.VMEM(o_in.shape, jnp.bfloat16),
            pltpu.VMEM(h_in.shape, jnp.bfloat16),
        ],
        compiler_params=pltpu.CompilerParams(collective_id=0, has_side_effects=True),
    )(q_in, kv_in, o_in, h_in, gain_in)


def combine_kernel(blocks, attended_ref, weight_ref, out_ref, outgoing, incoming, send, recv):
    g = lax.axis_index("group")
    e = lax.axis_index("expert")
    core = lax.rem(e, 2)
    mate_dev = (g, e + 1 - 2 * core)
    rows = out_ref.shape[1]
    barrier = pltpu.get_barrier_semaphore()
    pl.semaphore_signal(barrier, 1, device_id=mate_dev, device_id_type=MESH)
    pl.semaphore_wait(barrier, 1)

    def partial(block):
        start = pl.multiple_of(block * rows, rows)
        return jnp.dot(
            attended_ref[pl.ds(start, rows), :], weight_ref[...], preferred_element_type=jnp.float32
        ).astype(jnp.bfloat16)

    for i in range(blocks):
        outgoing[i] = partial(2 * i + 1 - core)
    copy = pltpu.make_async_remote_copy(
        src_ref=outgoing,
        dst_ref=incoming,
        send_sem=send.at[0],
        recv_sem=recv.at[0],
        device_id=mate_dev,
        device_id_type=MESH,
    )
    copy.start()
    for i in range(blocks):
        out_ref[i] = partial(2 * i + core)
    copy.wait()
    for i in range(blocks):
        out_ref[i] = (out_ref[i].astype(jnp.float32) + incoming[i].astype(jnp.float32)).astype(
            jnp.bfloat16
        )


def project_and_combine(attended, weight, experts_axis):
    rows = attended.shape[0] // experts_axis
    blocks = experts_axis // 2
    shape = (blocks, rows, weight.shape[1])
    vmem = pl.BlockSpec(memory_space=pltpu.VMEM)
    return pl.pallas_call(
        functools.partial(combine_kernel, blocks),
        out_shape=jax.ShapeDtypeStruct(shape, jnp.bfloat16),
        in_specs=[vmem, vmem],
        out_specs=vmem,
        scratch_shapes=[
            pltpu.VMEM(shape, jnp.bfloat16),
            pltpu.VMEM(shape, jnp.bfloat16),
            pltpu.SemaphoreType.DMA((1,)),
            pltpu.SemaphoreType.DMA((1,)),
        ],
        compiler_params=pltpu.CompilerParams(collective_id=4, has_side_effects=True),
    )(attended, weight)


def combine_scatter_kernel(blocks, attended_ref, weight_ref, out_ref, outgoing, incoming, combined, send, recv, chip_send, chip_recv, local):
    g = lax.axis_index("group")
    e = lax.axis_index("expert")
    core = lax.rem(e, 2)
    chip = lax.div(e, 2)
    mate_dev = (g, e + 1 - 2 * core)
    chip_devs = [(g, 2 * lax.rem(chip + j, blocks) + core) for j in range(1, blocks)]
    rows = out_ref.shape[1]
    barrier = pltpu.get_barrier_semaphore()
    for dev in [mate_dev] + chip_devs:
        pl.semaphore_signal(barrier, 1, device_id=dev, device_id_type=MESH)
    pl.semaphore_wait(barrier, blocks)

    def partial(block):
        start = pl.multiple_of(block * rows, rows)
        return jnp.dot(
            attended_ref[pl.ds(start, rows), :], weight_ref[...], preferred_element_type=jnp.float32
        ).astype(jnp.bfloat16)

    for i in range(blocks):
        outgoing[i] = partial(2 * i + 1 - core)
    copy = pltpu.make_async_remote_copy(
        src_ref=outgoing,
        dst_ref=incoming,
        send_sem=send.at[0],
        recv_sem=recv.at[0],
        device_id=mate_dev,
        device_id_type=MESH,
    )
    copy.start()
    for i in range(blocks):
        combined[i] = partial(2 * i + core)
    copy.wait()
    pushes = []
    for j in range(1, blocks):
        i = lax.rem(chip + j, blocks)
        combined[i] = (combined[i].astype(jnp.float32) + incoming[i].astype(jnp.float32)).astype(
            jnp.bfloat16
        )
        push = pltpu.make_async_remote_copy(
            src_ref=combined.at[i],
            dst_ref=out_ref.at[chip],
            send_sem=chip_send.at[j],
            recv_sem=chip_recv.at[j],
            device_id=chip_devs[j - 1],
            device_id_type=MESH,
        )
        push.start()
        pushes.append(push)
    combined[chip] = (combined[chip].astype(jnp.float32) + incoming[chip].astype(jnp.float32)).astype(
        jnp.bfloat16
    )
    own = pltpu.make_async_copy(combined.at[chip], out_ref.at[chip], local.at[0])
    own.start()
    for push in pushes:
        push.wait()
    own.wait()


def combine_and_scatter(attended, weight, experts_axis):
    rows = attended.shape[0] // experts_axis
    blocks = experts_axis // 2
    shape = (blocks, rows, weight.shape[1])
    vmem = pl.BlockSpec(memory_space=pltpu.VMEM)
    return pl.pallas_call(
        functools.partial(combine_scatter_kernel, blocks),
        out_shape=jax.ShapeDtypeStruct(shape, jnp.bfloat16),
        in_specs=[vmem, vmem],
        out_specs=pl.BlockSpec(memory_space=pl.ANY),
        scratch_shapes=[
            pltpu.VMEM(shape, jnp.bfloat16),
            pltpu.VMEM(shape, jnp.bfloat16),
            pltpu.VMEM(shape, jnp.bfloat16),
            pltpu.SemaphoreType.DMA((1,)),
            pltpu.SemaphoreType.DMA((1,)),
            pltpu.SemaphoreType.DMA((blocks,)),
            pltpu.SemaphoreType.DMA((blocks,)),
            pltpu.SemaphoreType.DMA((1,)),
        ],
        compiler_params=pltpu.CompilerParams(collective_id=7, has_side_effects=True),
    )(attended, weight)


def mate_kernel(part, out, send, recv):
    g = lax.axis_index("group")
    e = lax.axis_index("expert")
    core = lax.rem(e, 2)
    mate_dev = (g, e + 1 - 2 * core)
    barrier = pltpu.get_barrier_semaphore()
    pl.semaphore_signal(barrier, 1, device_id=mate_dev, device_id_type=MESH)
    pl.semaphore_wait(barrier, 1)
    copy = pltpu.make_async_remote_copy(
        src_ref=part.at[:, 1 - core],
        dst_ref=out,
        send_sem=send.at[0],
        recv_sem=recv.at[0],
        device_id=mate_dev,
        device_id_type=MESH,
    )
    copy.start()
    copy.wait()


def exchange_with_mate(part):
    any_spec = pl.BlockSpec(memory_space=pl.ANY)
    shape = (part.shape[0],) + part.shape[2:]
    return pl.pallas_call(
        mate_kernel,
        out_shape=jax.ShapeDtypeStruct(shape, part.dtype),
        in_specs=[any_spec],
        out_specs=any_spec,
        scratch_shapes=[pltpu.SemaphoreType.DMA((1,)), pltpu.SemaphoreType.DMA((1,))],
        compiler_params=pltpu.CompilerParams(collective_id=4, has_side_effects=True),
    )(part)


def chip_scatter_kernel(chips, part, out, send, recv, local):
    g = lax.axis_index("group")
    e = lax.axis_index("expert")
    core = lax.rem(e, 2)
    chip = lax.div(e, 2)
    devs = [(g, 2 * lax.rem(chip + j, chips) + core) for j in range(1, chips)]
    barrier = pltpu.get_barrier_semaphore()
    for dev in devs:
        pl.semaphore_signal(barrier, 1, device_id=dev, device_id_type=MESH)
    pl.semaphore_wait(barrier, len(devs))
    copies = []
    for j in range(1, chips):
        copy = pltpu.make_async_remote_copy(
            src_ref=part.at[lax.rem(chip + j, chips)],
            dst_ref=out.at[chip],
            send_sem=send.at[j],
            recv_sem=recv.at[j],
            device_id=devs[j - 1],
            device_id_type=MESH,
        )
        copy.start()
        copies.append(copy)
    own = pltpu.make_async_copy(part.at[chip], out.at[chip], local.at[0])
    own.start()
    for copy in copies:
        copy.wait()
    own.wait()


def scatter_to_chips(part):
    chips = part.shape[0]
    any_spec = pl.BlockSpec(memory_space=pl.ANY)
    return pl.pallas_call(
        functools.partial(chip_scatter_kernel, chips),
        out_shape=jax.ShapeDtypeStruct(part.shape, part.dtype),
        in_specs=[any_spec],
        out_specs=any_spec,
        scratch_shapes=[
            pltpu.SemaphoreType.DMA((chips,)),
            pltpu.SemaphoreType.DMA((chips,)),
            pltpu.SemaphoreType.DMA((1,)),
        ],
        compiler_params=pltpu.CompilerParams(collective_id=5, has_side_effects=True),
    )(part)


def scatter_kernel(n_expert, part, out, send, recv, local):
    g = lax.axis_index("group")
    e = lax.axis_index("expert")
    barrier = pltpu.get_barrier_semaphore()
    for j in range(1, n_expert):
        pl.semaphore_signal(barrier, 1, device_id=(g, lax.rem(e + j, n_expert)), device_id_type=MESH)
    pl.semaphore_wait(barrier, n_expert - 1)
    copies = []
    for j in range(1, n_expert):
        peer = lax.rem(e + j, n_expert)
        copy = pltpu.make_async_remote_copy(
            src_ref=part.at[peer],
            dst_ref=out.at[e],
            send_sem=send.at[j],
            recv_sem=recv.at[j],
            device_id=(g, peer),
            device_id_type=MESH,
        )
        copy.start()
        copies.append(copy)
    own = pltpu.make_async_copy(part.at[e], out.at[e], local.at[0])
    own.start()
    for copy in copies:
        copy.wait()
    own.wait()


def scatter_blocks(part, n_expert, collective_id):
    any_spec = pl.BlockSpec(memory_space=pl.ANY)
    return pl.pallas_call(
        functools.partial(scatter_kernel, n_expert),
        out_shape=jax.ShapeDtypeStruct(part.shape, part.dtype),
        in_specs=[any_spec],
        out_specs=any_spec,
        scratch_shapes=[
            pltpu.SemaphoreType.DMA((n_expert,)),
            pltpu.SemaphoreType.DMA((n_expert,)),
            pltpu.SemaphoreType.DMA((1,)),
        ],
        compiler_params=pltpu.CompilerParams(collective_id=collective_id, has_side_effects=True),
    )(part)


def attention_kernel(scale, heads, q_ref, own_ref, far_ref, length_ref, o_ref):
    block = q_ref.shape[0]
    rows = own_ref.shape[1]
    half = rows // 2
    parity = lax.rem(lax.axis_index("group"), 2)

    def places(side, shape, axis, start):
        indices = lax.broadcasted_iota(jnp.int32, shape, axis) + start
        return indices + jnp.where(side == 0, jnp.where(indices < half, 0, rows), half)

    query_places = places(parity, (block, 1), 0, pl.program_id(0) * block)
    length = length_ref[0, 0]
    own_places = places(parity, (1, rows), 1, 0)
    far_places = places(1 - parity, (1, rows), 1, 0)
    own_allowed = (own_places <= query_places) & (own_places < length)
    far_allowed = (far_places <= query_places) & (far_places < length)
    own_keys, own_values = own_ref[0], own_ref[1]
    far_keys, far_values = far_ref[0], far_ref[1]
    depth = own_keys.shape[1]
    contract = (((1,), (1,)), ((), ()))
    for h in range(heads):
        query = q_ref[:, h * depth : (h + 1) * depth]
        own_weights = jnp.where(
            own_allowed,
            jnp.exp(lax.dot_general(query, own_keys, contract, preferred_element_type=jnp.float32) * scale),
            0.0,
        )
        far_weights = jnp.where(
            far_allowed,
            jnp.exp(lax.dot_general(query, far_keys, contract, preferred_element_type=jnp.float32) * scale),
            0.0,
        )
        denominators = jnp.sum(own_weights, axis=-1, keepdims=True) + jnp.sum(
            far_weights, axis=-1, keepdims=True
        )
        weighted = jnp.dot(
            own_weights.astype(jnp.bfloat16), own_values, preferred_element_type=jnp.float32
        ) + jnp.dot(far_weights.astype(jnp.bfloat16), far_values, preferred_element_type=jnp.float32)
        o_ref[:, h * depth : (h + 1) * depth] = (weighted / denominators).astype(o_ref.dtype)


def attention(queries, own_kv, far_kv, length, scale):
    rows, width = queries.shape
    key_rows, depth = own_kv.shape[1:]
    block = rows
    pair = pl.BlockSpec((2, key_rows, depth), lambda i: (0, 0, 0))
    return pl.pallas_call(
        functools.partial(attention_kernel, scale, width // depth),
        out_shape=jax.ShapeDtypeStruct((rows, width), jnp.bfloat16),
        grid=(rows // block,),
        in_specs=[
            pl.BlockSpec((block, width), lambda i: (i, 0)),
            pair,
            pair,
            pl.BlockSpec(memory_space=pltpu.SMEM),
        ],
        out_specs=pl.BlockSpec((block, width), lambda i: (i, 0)),
        cost_estimate=pl.CostEstimate(
            flops=8 * rows * key_rows * width,
            transcendentals=2 * rows * key_rows * (width // depth),
            bytes_accessed=2 * (2 * rows * width + 4 * key_rows * depth),
        ),
    )(queries, own_kv, far_kv, length.reshape(1, 1))

def norm_rows(values, gain_vector):
    widened = values.astype(jnp.float32)
    inverse_rms = lax.rsqrt(jnp.mean(widened * widened, axis=-1, keepdims=True) + epsilon)
    return widened * inverse_rms * gain_vector


def rotate(values, positions):
    half_width = values.shape[-1] // 2
    exponents = jnp.arange(half_width).astype(jnp.float32)
    inverse = jnp.exp(exponents * (-2.0 * math.log(rope_theta) / values.shape[-1]))
    angles = positions[:, None, None] * inverse[None, None, :]
    cosine_values = jnp.cos(angles)
    sine_values = jnp.sin(angles)
    first_half = values[..., :half_width]
    second = values[..., half_width:]
    return jnp.concatenate(
        [
            first_half * cosine_values - second * sine_values,
            second * cosine_values + first_half * sine_values,
        ],
        axis=-1,
    )


def local_positions(parity, row_count):
    indices = jnp.arange(row_count)
    quarter = row_count // 2
    offset = jnp.where(parity == 0, jnp.where(indices < quarter, 0, 2 * quarter), quarter)
    return indices + offset


def prep_kernel(query_width, for_queries, x_ref, w_ref, table_ref, gain_ref, out_ref):
    x = x_ref[...]
    block = x.shape[0]
    depth = table_ref.shape[1]
    parity = lax.rem(lax.axis_index("group"), 2)
    start = pl.multiple_of(parity * (table_ref.shape[0] // 2) + pl.program_id(0) * block, block)
    table = table_ref[pl.ds(start, block), :]
    swapped = pltpu.roll(table, depth // 2, 1)
    first_half = lax.broadcasted_iota(jnp.int32, table.shape, 1) < depth // 2
    cosines = jnp.where(first_half, table, swapped)
    sines = jnp.where(first_half, -swapped, table)

    def project(start, stop):
        return jnp.dot(x, w_ref[:, start:stop], preferred_element_type=jnp.float32).astype(jnp.bfloat16)

    def norm_rope(values, gain):
        values = values.astype(jnp.float32)
        inverse_rms = lax.rsqrt(jnp.mean(values * values, axis=-1, keepdims=True) + epsilon)
        normed = values * inverse_rms * gain
        return (normed * cosines + pltpu.roll(normed, depth // 2, 1) * sines).astype(jnp.bfloat16)

    if for_queries:
        queries = project(0, query_width)
        for h in range(queries.shape[1] // depth):
            out_ref[:, h * depth : (h + 1) * depth] = norm_rope(
                queries[:, h * depth : (h + 1) * depth], gain_ref[...]
            )
    else:
        out_ref[0] = norm_rope(project(0, depth), gain_ref[...])
        out_ref[1] = project(depth, 2 * depth)


def prep(normed_rows, joined, table, gain, for_queries):
    rows, width = normed_rows.shape
    depth = table.shape[1]
    query_width = joined.shape[1] - 2 * depth
    block = min(512, rows)
    whole = lambda shape: pl.BlockSpec(shape, lambda i: (0, 0))
    if for_queries:
        out_shape = jax.ShapeDtypeStruct((rows, query_width), jnp.bfloat16)
        out_spec = pl.BlockSpec((block, query_width), lambda i: (i, 0))
        columns = query_width
    else:
        out_shape = jax.ShapeDtypeStruct((2, rows, depth), jnp.bfloat16)
        out_spec = pl.BlockSpec((2, block, depth), lambda i: (0, i, 0))
        columns = 2 * depth
    return pl.pallas_call(
        functools.partial(prep_kernel, query_width, for_queries),
        out_shape=out_shape,
        grid=(rows // block,),
        in_specs=[
            pl.BlockSpec((block, width), lambda i: (i, 0)),
            pl.BlockSpec((width, columns), lambda i: (0, 0 if for_queries else 1)),
            whole(table.shape),
            whole((1, depth)),
        ],
        out_specs=out_spec,
        cost_estimate=pl.CostEstimate(
            flops=2 * rows * width * columns,
            transcendentals=rows * (columns // depth),
            bytes_accessed=2 * (rows * width + width * columns + rows * columns),
        ),
    )(normed_rows, joined, table, gain.reshape(1, depth))

def rope_table(row_count, depth):
    half = depth // 2
    frequencies = rope_theta ** (-2.0 * np.arange(half) / depth)
    indices = np.arange(row_count)
    quarter = row_count // 2
    places = np.concatenate([np.where(indices < quarter, indices, indices + 2 * quarter), indices + quarter])
    angles = places[:, None].astype(np.float64) * frequencies[None, :]
    return jnp.asarray(np.concatenate([np.cos(angles), np.sin(angles)], axis=1), jnp.float32)

def per_device(
    hidden_in,
    norm_attention,
    norm_experts,
    query_master,
    trainer_key_value_weight,
    output_master,
    query_gain,
    key_gain,
    lengths,
    router,
    expert_gateup,
    expert_down,
    routes,
):
    experts_axis = lax.axis_size("expert")
    group_member = lax.axis_index("expert")
    group_index = lax.axis_index("group")
    local_head_count = QUERY_HEADS // experts_axis
    width_here = local_head_count * HEAD_DIMENSION
    common_head = group_member * local_head_count // (QUERY_HEADS // KEY_VALUE_HEADS)
    groups_axis = lax.axis_size("group")
    joined_parts, output_parts, normed_parts = gather_all(
        query_master,
        trainer_key_value_weight,
        output_master,
        hidden_in,
        norm_attention.reshape(1, -1),
        groups_axis,
        experts_axis,
    )
    model_width = hidden_in.shape[1]
    local_rows = normed_parts.shape[0] * normed_parts.shape[1]
    parity = group_index % 2
    prep_args = (
        normed_parts.reshape(local_rows, model_width),
        joined_parts.reshape(model_width, -1),
        rope_table(local_rows, HEAD_DIMENSION),
    )
    key_values = prep(*prep_args, key_gain, False)
    query_rows_list = prep(*prep_args, query_gain, True)
    partner = from_partner(key_values, "group", 0)
    valid_length = jnp.sum(jnp.where(jnp.arange(lengths.shape[0]) == group_index // 2, lengths, 0))
    attended = attention(
        query_rows_list,
        key_values,
        partner,
        valid_length.astype(jnp.int32),
        HEAD_DIMENSION ** (-0.5),
    )
    output_weight = jnp.transpose(output_parts, (1, 0, 2)).reshape(output_parts.shape[1], -1)
    owned = combine_and_scatter(attended, output_weight, experts_axis)
    summed = jnp.sum(owned.astype(jnp.float32), axis=0)
    hidden = (hidden_in.astype(jnp.float32) + summed).astype(jnp.bfloat16)
    normed_second = norm_rows(hidden, norm_experts).astype(jnp.bfloat16)
    logits = jnp.dot(normed_second, router, preferred_element_type=jnp.float32)
    route_table = routes[:, :, None] == jnp.arange(logits.shape[1])[None, None, :]
    picked = jnp.sum(jnp.where(route_table, logits[:, None, :], 0.0), axis=-1)
    raised = jnp.exp(picked)
    gate_values = raised / jnp.sum(raised, axis=1, keepdims=True)
    inside = routes < experts_axis
    gate_window = jnp.sum(jnp.where(inside, gate_values, 0.0), axis=1)
    expert_window = jnp.sum(jnp.where(inside, routes, 0), axis=1)
    present = jnp.any(inside, axis=1)
    capacity = local_rows // (experts_axis * experts_axis)
    member_table = (
        present[:, None] & (expert_window[:, None] == jnp.arange(experts_axis)[None, :])
    ).astype(jnp.int32)
    ranking = jnp.sum(jnp.cumsum(member_table, axis=0) * member_table, axis=1) - 1
    slot_index = expert_window * capacity + ranking
    select = (
        (jnp.arange(experts_axis * capacity)[:, None] == slot_index[None, :]) & present[None, :]
    ).astype(jnp.bfloat16)
    select_slots = select.reshape(experts_axis, capacity, -1)
    outgoing = jnp.einsum(
        "jct,td->jcd", select_slots, normed_second, preferred_element_type=jnp.float32
    ).astype(jnp.bfloat16)
    gateup_here = expert_gateup[0]
    down_here = expert_down[0]
    hidden_units = down_here.shape[0]
    slot_items = scatter_blocks(outgoing, experts_axis, 2)
    gate_up = jnp.einsum("jcd,df->jcf", slot_items, gateup_here, preferred_element_type=jnp.float32)
    active = (jax.nn.silu(gate_up[..., :hidden_units]) * gate_up[..., hidden_units:]).astype(
        jnp.bfloat16
    )
    result = jnp.einsum(
        "jcf,fd->jcd", active, down_here, preferred_element_type=jnp.float32
    ).astype(jnp.bfloat16)
    returned = scatter_blocks(result, experts_axis, 3)
    combined = jnp.einsum(
        "jct,jcd->td", select_slots, returned, preferred_element_type=jnp.float32
    )
    expert_mix = (gate_window[:, None] * combined).astype(jnp.bfloat16)
    return (hidden, expert_mix)


def solution(mesh):
    return jax.shard_map(
        per_device,
        mesh=mesh,
        in_specs=(
            P(("group", "expert"), None),
            P(),
            P(),
            P("group", "expert"),
            P(None, "group", None),
            P("expert", "group"),
            P(),
            P(),
            P(),
            P(),
            P("expert", None, None),
            P("expert", None, None),
            P(("group", "expert"), None),
        ),
        out_specs=(P(("group", "expert"), None), P(("group", "expert"), None)),
        check_vma=False,
    )
```
